32 devices in a mesh: dp: 8 (over z, x), tensor: 4 (over y, core).
Axes of the slice: x: 2, y: 2, z: 4, core: 2. Of those that a mesh axis runs over, the one named last changes fastest.
Arguments:
- tokens: bfloat16 [16384, 768], P(('dp', 'tensor')), may hold values from -6 to 6
- lengths: int32 [16], P('dp'), may hold values from 256 to 1024, as said below
- w_qkv: bfloat16 [3, 768, 768], P(None, 'dp', 'tensor'), may hold values from -0.21875 to 0.21875
- b_qv: float32 [2, 768], P(None, 'tensor'), may hold values from -3 to 3
- w_out: bfloat16 [768, 768], P('tensor', 'dp'), may hold values from -0.875 to 0.875
- b_out: float32 [768], replicated, may hold values from -3 to 3
- w_up: bfloat16 [768, 3072], P('dp', 'tensor'), may hold values from -0.21875 to 0.21875
- b_up: float32 [3072], P('tensor'), may hold values from -3 to 3
- w_down: bfloat16 [3072, 768], P('tensor', 'dp'), may hold values from -0.109375 to 0.109375
- b_down: float32 [768], replicated, may hold values from -3 to 3
- g_one: float32 [768], replicated, may hold values from 0.25 to 1.75
- c_one: float32 [768], replicated, may hold values from -3 to 3
- g_two: float32 [768], replicated, may hold values from 0.25 to 1.75
- c_two: float32 [768], replicated, may hold values from -3 to 3
- out_grad: bfloat16 [16384, 768], P(('dp', 'tensor')), may hold values from -6 to 6
Outputs:
- result: float32 [16384, 768], P(('dp', 'tensor'))
- tokens_grad: float32 [16384, 768], P(('dp', 'tensor'))
- w_qkv_grad: float32 [3, 768, 768], P(None, 'dp', 'tensor')
- b_qv_grad: float32 [2, 768], P(None, 'tensor')
- w_out_grad: float32 [768, 768], P('tensor', 'dp')
- b_out_grad: float32 [768], replicated
- w_up_grad: float32 [768, 3072], P('dp', 'tensor')
- b_up_grad: float32 [3072], P('tensor')
- w_down_grad: float32 [3072, 768], P('tensor', 'dp')
- b_down_grad: float32 [768], replicated
- g_one_grad: float32 [768], replicated
- c_one_grad: float32 [768], replicated
- g_two_grad: float32 [768], replicated
- c_two_grad: float32 [768], replicated
The draws below stay inside these ranges and needn't reach their ends.
Inputs may be any that keep to these rules, and one draw needn't show every extreme that they name: `lengths`: every draw has one sequence with exactly 1024 valid patches and one with exactly 256.
All inputs are finite; a program needn't handle non-finite values.
Results may differ from the reference program's by a relative error of at most 0.01.
Values may be sent and summed in bfloat16 or wider, within the bound.
A program may use at most 192 MiB of HBM per device.

```python
import jax
import jax.numpy as jnp
from jax import lax

D = 768
HEADS = 12
HEAD_DIM = 64
FF = 3072
LEN = 1024
MIN_LEN = 256
SEQS = 16
TOKENS = 16384


def draw_lengths(key, part):
    first_key, second_key = jax.random.split(jax.random.fold_in(key, 11))
    lengths_drawn = jax.random.randint(first_key, (SEQS,), MIN_LEN, LEN + 1, dtype=jnp.int32)
    shuffled = jax.random.permutation(second_key, SEQS)
    lengths_drawn = lengths_drawn.at[shuffled[0]].set(LEN)
    lengths_drawn = lengths_drawn.at[shuffled[1]].set(MIN_LEN)
    return lengths_drawn


def raised(drawn, key, source, target, blocks, factor):
    owner, partner = [(jnp.arange(drawn.shape[axis_at]) // (drawn.shape[axis_at] // blocks)).reshape([-1 if axis == axis_at else 1 for axis in range(drawn.ndim)]) for axis_at in (source, target)]
    chosen = jax.random.permutation(key, blocks)[partner]
    strong = (owner == chosen) | (owner == (partner + blocks // 2) % blocks)
    return jnp.where(strong, factor * drawn, drawn)


def block_scale(stream_key, dims, cuts, least, high):
    level, own = 1.0, jax.random.fold_in(stream_key, 6)
    for position, shards_of in cuts:
        heights = jnp.exp(jax.random.uniform(jax.random.fold_in(own, position), (shards_of,), jnp.float32, least / len(cuts), high / len(cuts)))
        level = level * jnp.repeat(heights, dims[position] // shards_of).reshape([-1 if axis == position else 1 for axis in range(len(dims))])
    return level


def noise(rng, dims, scale, limit, shards=(), kind=jnp.bfloat16):
    result = jax.random.normal(rng, dims, jnp.float32) * scale
    if len(shards) > 0:
        result = block_scale(rng, dims, shards, -0.22, 0.18) * result
    return jnp.clip(result, min=-limit, max=limit).astype(kind)


def bell_draw_with(own_key, shape, scale, reach, pieces, heavy, kind=jnp.bfloat16):
    array = scale * jax.random.normal(own_key, shape, jnp.float32)
    if pieces:
        array = array * block_scale(own_key, shape, pieces, -0.22, 0.18)
    return jnp.clip(raised(array, jax.random.fold_in(own_key, 3), *heavy), -reach, reach).astype(kind)


def setup_inputs(seed: int = 0) -> dict:
    keys = jax.random.split(jax.random.key(seed), 16)
    tokens = noise(keys[0], (TOKENS, D), 1.0, 6.0, ((0, 32),))
    lengths = draw_lengths(jax.random.fold_in(keys[15], 71), 0)
    w_qkv = noise(keys[2], (3, D, D), D ** -0.5, 0.21875, ((1, 8), (2, 4)))
    b_qv = noise(keys[3], (2, D), 0.5, 3.0, ((1, 4),), jnp.float32)
    w_out = noise(keys[4], (D, D), (D // 16) ** -0.5, 0.875, ((0, 4), (1, 8)))
    b_out = noise(keys[5], (D,), 0.5, 3.0, (), jnp.float32)
    w_up = noise(keys[6], (D, FF), D ** -0.5, 0.21875, ((0, 8), (1, 4)))
    b_up = noise(keys[7], (FF,), 0.5, 3.0, ((0, 4),), jnp.float32)
    w_down = noise(keys[8], (FF, D), FF ** -0.5, 0.109375, ((0, 4), (1, 8)))
    b_down = noise(keys[9], (D,), 0.5, 3.0, (), jnp.float32)
    g_one = jnp.clip(1.0 + 0.15 * jax.random.normal(keys[10], (D,), jnp.float32), 0.25, 1.75)
    c_one = noise(keys[11], (D,), 0.5, 3.0, (), jnp.float32)
    g_two = jnp.clip(1.0 + 0.15 * jax.random.normal(keys[12], (D,), jnp.float32), 0.25, 1.75)
    c_two = noise(keys[13], (D,), 0.5, 3.0, (), jnp.float32)
    out_grad = bell_draw_with(keys[14], (TOKENS, D), 1.0, 6.0, ((0, 32),), (0, 1, 32, 2.75))
    return dict(tokens=tokens, lengths=lengths, w_qkv=w_qkv, b_qv=b_qv, w_out=w_out, b_out=b_out, w_up=w_up, b_up=b_up, w_down=w_down, b_down=b_down, g_one=g_one, c_one=c_one, g_two=g_two, c_two=c_two, out_grad=out_grad)


@jax.custom_vjp
def low(v):
    return lax.optimization_barrier(v.astype(jnp.bfloat16)).astype(jnp.float32)

@jax.custom_vjp
def low_back(v):
    return v

def low_keep(v):
    return (low(v), None)

def low_pass(kept, grad):
    return (grad,)

def back_keep(v):
    return (v, None)

def back_low(kept, grad):
    return (low(grad),)
low.defvjp(low_keep, low_pass)
low_back.defvjp(back_keep, back_low)
EPSILON = 1e-05
HIGHEST_PRECISION = lax.Precision.HIGHEST

def normalize(values, gain, shift):
    center = values - lax.optimization_barrier(jnp.mean(values, axis=-1, keepdims=True))
    spread = lax.optimization_barrier(jnp.mean(center * center, axis=-1, keepdims=True))
    return center * lax.rsqrt(spread + EPSILON) * gain + shift

def product(left, right):
    return jnp.dot(left, right, precision=HIGHEST_PRECISION, preferred_element_type=jnp.float32)

def forward_one(params, inputs, length):
    w_qkv, b_qv, w_out, b_out, w_up, b_up, w_down, b_down, g_one, c_one, g_two, c_two = params
    score_scale = HEAD_DIM ** (-0.5)
    first = low(normalize(inputs, g_one, c_one))
    query_rows = low(low_back(product(first, w_qkv[0]) + b_qv[0]))
    key_rows = low(low_back(product(first, w_qkv[1])))
    value_rows = low(low_back(product(first, w_qkv[2]) + b_qv[1]))
    query_heads = query_rows.reshape(LEN, HEADS, HEAD_DIM)
    key_heads = key_rows.reshape(LEN, HEADS, HEAD_DIM)
    value_heads = value_rows.reshape(LEN, HEADS, HEAD_DIM)
    block_rows = min(512, LEN)
    positions = jnp.arange(LEN, dtype=jnp.int32)

    def one_block(offset):
        query_block = lax.dynamic_slice_in_dim(query_heads, offset, block_rows, 0)
        scores = jnp.einsum('qhd,khd->hqk', query_block, key_heads, precision=HIGHEST_PRECISION) * score_scale
        query_pos = offset + jnp.arange(block_rows, dtype=jnp.int32)
        allowed = (positions[None, :] <= query_pos[:, None]) & (positions[None, :] < length)
        scores = low_back(jnp.where(allowed[None], scores, -1e+30))
        weights = low(jax.nn.softmax(scores, axis=-1))
        return jnp.einsum('hqk,khd->qhd', weights, value_heads, precision=HIGHEST_PRECISION)
    offsets = (jnp.arange(LEN // block_rows) * block_rows).astype(jnp.int32)
    blocks = lax.map(jax.checkpoint(one_block), offsets)
    mixed = low(low_back(blocks.reshape(LEN, HEADS * HEAD_DIM)))
    hidden = inputs + low_back(product(mixed, w_out)) + b_out
    second = low(normalize(hidden, g_two, c_two))
    pre_act = low_back(product(second, w_up) + b_up)
    activated = low(jax.nn.gelu(pre_act, approximate=True))
    outcome = hidden + low_back(product(activated, w_down)) + b_down
    row_valid = (positions < length).astype(jnp.float32)[:, None]
    return outcome * row_valid

def reference(tokens, lengths, w_qkv, b_qv, w_out, b_out, w_up, b_up, w_down, b_down, g_one, c_one, g_two, c_two, out_grad):
    params = tuple((item.astype(jnp.float32) for item in (w_qkv, b_qv, w_out, b_out, w_up, b_up, w_down, b_down, g_one, c_one, g_two, c_two)))
    inputs_all = tokens.astype(jnp.float32).reshape(SEQS, LEN, D)
    cotangents = out_grad.astype(jnp.float32).reshape(SEQS, LEN, D)

    def one_sequence(totals, item):
        inputs, length, cotangent = item

        def forward(param_set, values):
            return forward_one(param_set, values, length)
        outcome, pull = jax.vjp(forward, params, inputs)
        grad_params, grad_inputs = pull(cotangent)
        summed = tuple((left + right for left, right in zip(totals, grad_params)))
        return (summed, (outcome, grad_inputs))
    zeros = tuple((jnp.zeros_like(item) for item in params))
    totals, (outcomes, input_grads) = lax.scan(one_sequence, zeros, (inputs_all, lengths, cotangents))
    return (outcomes.reshape(TOKENS, D), input_grads.reshape(TOKENS, D), totals[0], totals[1], totals[2], totals[3], totals[4], totals[5], totals[6], totals[7], totals[8], totals[9], totals[10], totals[11])
```

```python
import functools
import math

import jax
import jax.numpy as jnp
from jax import lax
from jax.experimental import pallas as pl
from jax.experimental.pallas import tpu as pltpu
from jax.sharding import Mesh
from jax.sharding import PartitionSpec as P

HEAD_DIM = 64
EPSILON = 1e-05
MESH = pl.DeviceIdType.MESH
NX = 2
NK = 3

class Place:
    def __init__(self, nz):
        self.nz = nz
        self.e = lax.axis_index("e"); self.y = lax.axis_index("y")
        self.z = self.e // NX; self.x = self.e % NX
        self.xn = {"e": self.e + 1 - 2 * self.x}
        self.yn = {"y": 1 - self.y}
        self.up = {"e": self.e + NX}
        self.dn = {"e": self.e - NX}
        self.core = {"c": 1 - lax.axis_index("c")}

def barrier(p, with_core=False):
    bar = pltpu.get_barrier_semaphore()
    nbrs = [p.xn, p.yn] + ([p.core] if with_core else [])
    for n in nbrs:
        pl.semaphore_signal(bar, 1, device_id=n, device_id_type=MESH)
    @pl.when(p.z < p.nz - 1)
    def _(): pl.semaphore_signal(bar, 1, device_id=p.up, device_id_type=MESH)
    @pl.when(p.z > 0)
    def _(): pl.semaphore_signal(bar, 1, device_id=p.dn, device_id_type=MESH)
    inner = (p.z > 0) & (p.z < p.nz - 1)
    @pl.when(inner)
    def _(): pl.semaphore_wait(bar, len(nbrs) + 2)
    @pl.when(jnp.logical_not(inner))
    def _(): pl.semaphore_wait(bar, len(nbrs) + 1)

class Gather:
    def __init__(self, p, own, full, ssem, rsem):
        self.p, self.own, self.full, self.ssem, self.rsem = p, own, full, ssem, rsem
        self.rows = own.shape[1]
    def piece(self, yq, k, e, half=None):
        r = self.rows
        if half is None: return self.full.at[yq, k, pl.ds(pl.multiple_of(e * r, 16), r)]
        h = r // 2
        return self.full.at[yq, k, pl.ds(pl.multiple_of(e * r + half * h, 16), h)]
    def copy(self, kind, k, src, own=False):
        p = self.p
        half = None
        if kind < 4: yq, e = p.y, src * NX + p.x
        elif kind == 4: yq, e, half = p.y, src * NX + 1 - p.x, 0
        else: yq, e, half = 1 - p.y, src * NX + p.x, 1
        ref = self.piece(yq, k, e, half)
        dev = (p.up, p.dn, p.xn, p.yn, p.yn, p.xn)[kind]
        rk = (0, 0, 1, 2, 3, 4)[kind]
        s = self.own.at[k] if own else ref
        return pltpu.make_async_remote_copy(s, ref, self.ssem.at[kind, k, src], self.rsem.at[rk, k, src],
                                            device_id=dev, device_id_type=MESH)
    def recv(self, rk, k, src):
        p = self.p
        half = None
        if rk == 0: yq, e = p.y, src * NX + p.x
        elif rk == 1: yq, e = p.y, src * NX + 1 - p.x
        elif rk == 2: yq, e = 1 - p.y, src * NX + p.x
        elif rk == 3: yq, e, half = 1 - p.y, src * NX + 1 - p.x, 0
        else: yq, e, half = 1 - p.y, src * NX + 1 - p.x, 1
        ref = self.piece(yq, k, e, half)
        pltpu.make_async_remote_copy(ref, ref, self.ssem.at[0, k, src], self.rsem.at[rk, k, src],
                                     device_id=p.xn, device_id_type=MESH).wait_recv()
    def send_all(self, kind, k, src, own=False):
        self.copy(kind, k, src, own).start()
    def tick(self, k, s):
        p = self.p
        if s == 0:
            self.full[p.y, k, pl.ds(pl.multiple_of(p.e * self.rows, 16), self.rows)] = self.own[k]
            @pl.when(p.z < p.nz - 1)
            def _(): self.copy(0, k, p.z, True).start()
            @pl.when(p.z > 0)
            def _(): self.copy(1, k, p.z, True).start()
            self.copy(2, k, p.z, True).start(); self.copy(3, k, p.z, True).start()
            return
        @pl.when(p.z - s >= 0)
        def _():
            src = p.z - s
            self.recv(0, k, src)
            @pl.when(p.z < p.nz - 1)
            def _(): self.copy(0, k, src).start()
            self.copy(2, k, src).start(); self.copy(3, k, src).start()
        @pl.when(p.z + s < p.nz)
        def _():
            src = p.z + s
            self.recv(0, k, src)
            @pl.when(p.z > 0)
            def _(): self.copy(1, k, src).start()
            self.copy(2, k, src).start(); self.copy(3, k, src).start()
    def turn_one(self, k, src):
        self.recv(1, k, src); self.copy(4, k, src).start()
        self.recv(2, k, src); self.copy(5, k, src).start()
    def turn(self, k, s):
        p = self.p
        if s == 0: return self.turn_one(k, p.z)
        @pl.when(p.z - s >= 0)
        def _(): self.turn_one(k, p.z - s)
        @pl.when(p.z + s < p.nz)
        def _(): self.turn_one(k, p.z + s)
    def final(self, k):
        for src in range(self.p.nz):
            self.recv(3, k, src); self.recv(4, k, src)
    def drain(self, k):
        p = self.p
        for src in range(p.nz):
            own = p.z == src
            @pl.when((p.z < p.nz - 1) & (src <= p.z))
            def _(): self.copy(0, k, src).wait_send()
            @pl.when((p.z > 0) & (src >= p.z))
            def _(): self.copy(1, k, src).wait_send()
            for kind in (2, 3, 4, 5): self.copy(kind, k, src).wait_send()

def gather_sems(nz):
    return [pltpu.SemaphoreType.DMA((6, NK, nz)), pltpu.SemaphoreType.DMA((5, NK, nz))]

class Scatter:
    def __init__(self, p, full, bd, bxy, bz, out, ssem, rsem):
        self.p, self.full, self.bd, self.bxy, self.bz, self.out, self.ssem, self.rsem = p, full, bd, bxy, bz, out, ssem, rsem
        self.rows = full.shape[2] // (p.nz * NX)
        self.order = []
        for j in range(p.nz // 2): self.order += [p.nz - 1 - j, j]
    def piece(self, yq, k, e, half=None):
        r = self.rows
        if half is None: return self.full.at[yq, k, pl.ds(pl.multiple_of(e * r, 16), r)]
        h = r // 2
        return self.full.at[yq, k, pl.ds(pl.multiple_of(e * r + half * h, 16), h)]
    def copy(self, kind, k, d):
        p = self.p
        if kind == 0: s, t, dev = self.piece(1 - p.y, k, d * NX + 1 - p.x, 0), self.bd.at[0, k, d], p.yn
        elif kind == 1: s, t, dev = self.piece(1 - p.y, k, d * NX + 1 - p.x, 1), self.bd.at[1, k, d], p.xn
        elif kind == 2: s, t, dev = self.piece(p.y, k, d * NX + 1 - p.x), self.bxy.at[0, k, d], p.xn
        elif kind == 3: s, t, dev = self.piece(1 - p.y, k, d * NX + p.x), self.bxy.at[1, k, d], p.yn
        elif kind == 4: s, t, dev = self.piece(p.y, k, d * NX + p.x), self.bz.at[0, k, d], p.up
        else: s, t, dev = self.piece(p.y, k, d * NX + p.x), self.bz.at[1, k, d], p.dn
        return pltpu.make_async_remote_copy(s, t, self.ssem.at[kind, k, d], self.rsem.at[kind, k, d],
                                            device_id=dev, device_id_type=MESH)
    def first(self, k):
        for d in self.order:
            self.copy(0, k, d).start(); self.copy(1, k, d).start()
    def second(self, k, d):
        p = self.p
        self.copy(0, k, d).wait_recv()
        ref = self.piece(p.y, k, d * NX + 1 - p.x, 0)
        ref[...] = (ref[...].astype(jnp.float32) + self.bd[0, k, d].astype(jnp.float32)).astype(jnp.bfloat16)
        self.copy(2, k, d).start()
        self.copy(1, k, d).wait_recv()
        ref = self.piece(1 - p.y, k, d * NX + p.x, 1)
        ref[...] = (ref[...].astype(jnp.float32) + self.bd[1, k, d].astype(jnp.float32)).astype(jnp.bfloat16)
        self.copy(3, k, d).start()
    def third(self, k, d):
        p = self.p
        ref = self.piece(p.y, k, d * NX + p.x)
        self.copy(2, k, d).wait_recv(); self.copy(3, k, d).wait_recv()
        def total():
            return ref[...].astype(jnp.float32) + self.bxy[0, k, d].astype(jnp.float32) + self.bxy[1, k, d].astype(jnp.float32)
        @pl.when(d > p.z)
        def _():
            @pl.when(p.z > 0)
            def _():
                self.copy(4, k, d).wait_recv()
                ref[...] = (total() + self.bz[0, k, d].astype(jnp.float32)).astype(jnp.bfloat16)
            @pl.when(p.z == 0)
            def _(): ref[...] = total().astype(jnp.bfloat16)
            self.copy(4, k, d).start()
        @pl.when(d < p.z)
        def _():
            @pl.when(p.z < p.nz - 1)
            def _():
                self.copy(5, k, d).wait_recv()
                ref[...] = (total() + self.bz[1, k, d].astype(jnp.float32)).astype(jnp.bfloat16)
            @pl.when(p.z == p.nz - 1)
            def _(): ref[...] = total().astype(jnp.bfloat16)
            self.copy(5, k, d).start()
        @pl.when(d == p.z)
        def _(): self.out[k] = total()
    def final(self, k):
        p = self.p
        @pl.when(p.z > 0)
        def _():
            self.copy(4, k, p.z).wait_recv()
            self.out[k] = self.out[k] + self.bz[0, k, p.z].astype(jnp.float32)
        @pl.when(p.z < p.nz - 1)
        def _():
            self.copy(5, k, p.z).wait_recv()
            self.out[k] = self.out[k] + self.bz[1, k, p.z].astype(jnp.float32)
    def drain(self, k):
        p = self.p
        for d in range(p.nz):
            for kind in (0, 1, 2, 3): self.copy(kind, k, d).wait_send()
            @pl.when(d > p.z)
            def _(): self.copy(4, k, d).wait_send()
            @pl.when(d < p.z)
            def _(): self.copy(5, k, d).wait_send()

def scatter_bufs(nz, rows, cols):
    b = jnp.bfloat16
    return [pltpu.VMEM((2, NK, nz, rows // 2, cols), b), pltpu.VMEM((2, NK, nz, rows, cols), b), pltpu.VMEM((2, NK, nz, rows, cols), b)]
def scatter_sems(nz):
    return [pltpu.SemaphoreType.DMA((6, NK, nz)), pltpu.SemaphoreType.DMA((6, NK, nz))]


VM = pl.BlockSpec(memory_space=pltpu.VMEM)


def gather_kernel(own, full, ssem, rsem):
    nz = ssem.shape[2]
    p = Place(nz)
    barrier(p)
    g = Gather(p, own, full, ssem, rsem)
    for k in range(NK):
        for s in range(nz):
            g.tick(k, s)
            if s >= 1:
                g.turn(k, s - 1)
        g.turn(k, nz - 1)
    for k in range(NK):
        g.final(k)
    for k in range(NK):
        g.drain(k)


def gather(own, nz):
    nk, rows, cols = own.shape
    return pl.pallas_call(
        gather_kernel,
        out_shape=jax.ShapeDtypeStruct((2, nk, rows * nz * NX, cols), jnp.bfloat16),
        in_specs=[VM],
        out_specs=VM,
        scratch_shapes=gather_sems(nz),
        compiler_params=pltpu.CompilerParams(collective_id=0, has_side_effects=True, vmem_limit_bytes=60 << 20),
    )(own)


def scatter_kernel(full_in, out, full, bd, bxy, bz, ssem, rsem):
    nz = ssem.shape[2]
    p = Place(nz)
    barrier(p)
    full[...] = full_in[...]
    r = Scatter(p, full, bd, bxy, bz, out, ssem, rsem)
    for k in range(NK):
        r.first(k)
    for k in range(NK):
        for i, d in enumerate(r.order):
            r.second(k, d)
            if i >= 1:
                r.third(k, r.order[i - 1])
        r.third(k, r.order[-1])
    for k in range(NK):
        r.final(k)
    for k in range(NK):
        r.drain(k)


def scatter(full, nz):
    _, nk, d, cols = full.shape
    rows = d // (nz * NX)
    return pl.pallas_call(
        scatter_kernel,
        out_shape=jax.ShapeDtypeStruct((nk, rows, cols), jnp.float32),
        in_specs=[VM],
        out_specs=VM,
        scratch_shapes=[pltpu.VMEM(full.shape, jnp.bfloat16)] + scatter_bufs(nz, rows, cols) + scatter_sems(nz),
        compiler_params=pltpu.CompilerParams(collective_id=1, has_side_effects=True, vmem_limit_bytes=62 << 20),
    )(full)


def normalize(values, gain, shift):
    center = values - jnp.mean(values, axis=-1, keepdims=True)
    spread = jnp.mean(center * center, axis=-1, keepdims=True)
    return center * lax.rsqrt(spread + EPSILON) * gain + shift


def matmul(left, right):
    return jnp.dot(left, right, preferred_element_type=jnp.float32)


def transposed_left(left, right):
    return lax.dot_general(left, right, (((0,), (0,)), ((), ())), preferred_element_type=jnp.float32)


def transposed_right(left, right):
    return lax.dot_general(left, right, (((1,), (1,)), ((), ())), preferred_element_type=jnp.float32)


def allowed(seq_len, length):
    at = jnp.arange(seq_len, dtype=jnp.int32)
    return ((at[None, :] <= at[:, None]) & (at[None, :] < length))[None]


def heads(m):
    return m.reshape(m.shape[0], -1, HEAD_DIM)


def per_device(tokens, lengths, w_qkv, b_qv, w_out, b_out, w_up, b_up, w_down, b_down, g_one, c_one, g_two, c_two, out_grad, *, nz, sub):
    f32, bf16 = jnp.float32, jnp.bfloat16
    local = tokens.shape[0]
    seq_len = 2 * local
    y, c = lax.axis_index("y"), lax.axis_index("c")
    length = lengths[y]
    scale = HEAD_DIM ** -0.5
    hw = w_qkv.shape[2]
    d_model = tokens.shape[1]
    packed = jnp.concatenate([w_qkv[0], w_qkv[1], w_qkv[2], w_out.T, w_up, w_down.T], axis=1)
    if sub > 1:
        packed = lax.all_gather(packed, "r", axis=0, tiled=True)
    packed = jnp.stack([packed[:, i * d_model : (i + 1) * d_model] for i in range(NK)])
    full = gather(packed, nz)

    def both(k, lo, hi):
        return jnp.concatenate([full[0, k, :, lo:hi], full[1, k, :, lo:hi]], axis=1)

    wq, wk, wv, wot = [both(0, i * hw, (i + 1) * hw) for i in range(4)]
    w_up_c, w_down_t = both(1, 0, d_model), both(2, 0, d_model)

    def cols(b):
        return lax.all_gather(b, "y", axis=b.ndim - 1, tiled=True)

    bqv = cols(b_qv)
    bup = cols(b_up)
    rows_valid = (jnp.arange(local) + c * local < length).astype(f32)[:, None]
    x = tokens.astype(f32)
    first = normalize(x, g_one, c_one).astype(bf16)
    pair = lambda v: lax.all_gather(v, "c", axis=0, tiled=True)
    unpair = lambda v: lax.psum_scatter(v, "c", scatter_dimension=0, tiled=True)
    first_all = pair(first)
    q = (matmul(first_all, wq) + bqv[0]).astype(bf16)
    kk = matmul(first_all, wk).astype(bf16)
    v = (matmul(first_all, wv) + bqv[1]).astype(bf16)
    mask = allowed(seq_len, length)
    s = jnp.where(mask, jnp.einsum("qhd,khd->hqk", heads(q), heads(kk), preferred_element_type=f32) * scale, -1e30)
    m = jnp.max(s, -1, keepdims=True)
    ex = jnp.exp(s - m)
    tot = jnp.sum(ex, -1, keepdims=True)
    w = ex / tot
    mixed = jnp.einsum("hqk,khd->qhd", w.astype(bf16), heads(v), preferred_element_type=f32).reshape(seq_len, -1).astype(bf16)
    hidden = x + unpair(transposed_right(mixed, wot)) + b_out
    second = normalize(hidden, g_two, c_two).astype(bf16)
    second_all = pair(second)
    pre = matmul(second_all, w_up_c) + bup
    act, gpull = jax.vjp(functools.partial(jax.nn.gelu, approximate=True), pre)
    act = act.astype(bf16)
    result = rows_valid * (hidden + unpair(transposed_right(act, w_down_t)) + b_down)
    dres = rows_valid * out_grad.astype(f32)
    b_down_grad = jnp.sum(dres, 0)
    dres_all = pair(dres.astype(bf16))
    g_down = transposed_left(dres_all, act)
    dpre = gpull(matmul(dres_all, w_down_t))[0].astype(bf16)
    b_up_grad = jnp.sum(dpre.astype(f32), 0)
    g_up = transposed_left(second_all, dpre)
    dsecond = unpair(transposed_right(dpre, w_up_c))
    _, pull2 = jax.vjp(normalize, hidden, g_two, c_two)
    dh, g_two_grad, c_two_grad = pull2(dsecond)
    dhidden = dres + dh
    b_out_grad = jnp.sum(dhidden, 0)
    dh_all = pair(dhidden.astype(bf16))
    g_out = transposed_left(dh_all, mixed)
    dmixed = heads(matmul(dh_all, wot).astype(bf16))
    dv = jnp.einsum("hqk,qhd->khd", w.astype(bf16), dmixed, preferred_element_type=f32)
    dp = jnp.einsum("qhd,khd->hqk", dmixed, heads(v), preferred_element_type=f32)
    ds = (w * (dp - jnp.sum(w * dp, -1, keepdims=True))).astype(bf16)
    dq = jnp.einsum("hqk,khd->qhd", ds, heads(kk), preferred_element_type=f32) * scale
    dk = jnp.einsum("hqk,qhd->khd", ds, heads(q), preferred_element_type=f32) * scale
    dq, dk, dv = [a.reshape(seq_len, -1).astype(bf16) for a in (dq, dk, dv)]
    b_qv_grad = jnp.stack([jnp.sum(dq.astype(f32), 0), jnp.sum(dv.astype(f32), 0)])
    gq, gk, gv = [transposed_left(first_all, a) for a in (dq, dk, dv)]
    dfirst = unpair(transposed_right(dq, wq) + transposed_right(dk, wk) + transposed_right(dv, wv))
    _, pull1 = jax.vjp(normalize, x, g_one, c_one)
    dx, g_one_grad, c_one_grad = pull1(dfirst)
    tokens_grad = dhidden + dx

    def half(g, i):
        n = g.shape[1] // 2
        return g[:, i * n : (i + 1) * n]

    partial = jnp.stack(
        [
            jnp.stack([jnp.concatenate([half(g, i) for g in (gq, gk, gv, g_out)], axis=1), half(g_up, i), half(g_down, i)])
            for i in range(2)
        ]
    ).astype(bf16)
    mine = scatter(partial, nz)
    if sub > 1:
        mine = lax.psum_scatter(mine, "r", scatter_dimension=1, tiled=True)
    qkv_grad = jnp.stack([mine[0, :, i * hw : (i + 1) * hw] for i in range(3)])
    out_grad_w = mine[0, :, 3 * hw : 4 * hw].T
    up_grad = mine[1]
    down_grad = mine[2].T
    bqv_all, bup_all = lax.psum((b_qv_grad, b_up_grad), ("e", "r", "y"))
    bqv_out = lax.dynamic_slice_in_dim(bqv_all, y * hw, hw, 1)
    bup_out = lax.dynamic_slice_in_dim(bup_all, y * b_up.shape[0], b_up.shape[0], 0)
    small = lax.psum((b_out_grad, b_down_grad, g_one_grad, c_one_grad, g_two_grad, c_two_grad), ("e", "r", "y", "c"))
    return (result, tokens_grad, qkv_grad, bqv_out, out_grad_w, small[0], up_grad, bup_out, down_grad, small[1], small[2], small[3], small[4], small[5])


def solution(mesh):
    dp, tensor = mesh.shape["dp"], mesh.shape["tensor"]
    line = min(dp, 8)
    nz, sub = line // NX, dp // line
    grid = Mesh(mesh.devices.reshape(line, sub, tensor // 2, 2), ("e", "r", "y", "c"))
    dpx, tx = ("e", "r"), ("y", "c")
    rows = P(dpx + tx, None)
    return jax.shard_map(
        functools.partial(per_device, nz=nz, sub=sub),
        mesh=grid,
        in_specs=(rows, P(dpx), P(None, dpx, tx), P(None, tx), P(tx, dpx), P(), P(dpx, tx), P(tx), P(tx, dpx), P(), P(), P(), P(), P(), rows),
        out_specs=(rows, rows, P(None, dpx, tx), P(None, tx), P(tx, dpx), P(), P(dpx, tx), P(tx), P(tx, dpx), P(), P(), P(), P(), P()),
        check_vma=False,
    )
```

```python
import functools
import math

import jax
import jax.numpy as jnp
from jax import lax
from jax.experimental import pallas as pl
from jax.experimental.pallas import tpu as pltpu
from jax.sharding import Mesh
from jax.sharding import PartitionSpec as P

HEAD_DIM = 64
EPSILON = 1e-05
MESH = pl.DeviceIdType.MESH
NX = 2
NK = 3

class Place:
    def __init__(self, nz):
        self.nz = nz
        self.e = lax.axis_index("e"); self.y = lax.axis_index("y")
        self.z = self.e // NX; self.x = self.e % NX
        self.xn = {"e": self.e + 1 - 2 * self.x}
        self.yn = {"y": 1 - self.y}
        self.up = {"e": self.e + NX}
        self.dn = {"e": self.e - NX}
        self.core = {"c": 1 - lax.axis_index("c")}

class Gather:
    def __init__(self, p, own, full, ssem, rsem):
        self.p, self.own, self.full, self.ssem, self.rsem = p, own, full, ssem, rsem
        self.rows = own.shape[1]
    def piece(self, yq, k, e, half=None):
        r = self.rows
        if half is None: return self.full.at[yq, k, pl.ds(pl.multiple_of(e * r, 16), r)]
        h = r // 2
        return self.full.at[yq, k, pl.ds(pl.multiple_of(e * r + half * h, 16), h)]
    def copy(self, kind, k, src, own=False):
        p = self.p
        half = None
        if kind < 4: yq, e = p.y, src * NX + p.x
        elif kind == 4: yq, e, half = p.y, src * NX + 1 - p.x, 0
        else: yq, e, half = 1 - p.y, src * NX + p.x, 1
        ref = self.piece(yq, k, e, half)
        dev = (p.up, p.dn, p.xn, p.yn, p.yn, p.xn)[kind]
        rk = (0, 0, 1, 2, 3, 4)[kind]
        s = self.own.at[k] if own else ref
        return pltpu.make_async_remote_copy(s, ref, self.ssem.at[kind, k, src], self.rsem.at[rk, k, src],
                                            device_id=dev, device_id_type=MESH)
    def recv(self, rk, k, src):
        p = self.p
        half = None
        if rk == 0: yq, e = p.y, src * NX + p.x
        elif rk == 1: yq, e = p.y, src * NX + 1 - p.x
        elif rk == 2: yq, e = 1 - p.y, src * NX + p.x
        elif rk == 3: yq, e, half = 1 - p.y, src * NX + 1 - p.x, 0
        else: yq, e, half = 1 - p.y, src * NX + 1 - p.x, 1
        ref = self.piece(yq, k, e, half)
        pltpu.make_async_remote_copy(ref, ref, self.ssem.at[0, k, src], self.rsem.at[rk, k, src],
                                     device_id=p.xn, device_id_type=MESH).wait_recv()
    def send_all(self, kind, k, src, own=False):
        self.copy(kind, k, src, own).start()
    def tick(self, k, s):
        p = self.p
        if s == 0:
            self.full[p.y, k, pl.ds(pl.multiple_of(p.e * self.rows, 16), self.rows)] = self.own[k]
            @pl.when(p.z < p.nz - 1)
            def _(): self.copy(0, k, p.z, True).start()
            @pl.when(p.z > 0)
            def _(): self.copy(1, k, p.z, True).start()
            self.copy(2, k, p.z, True).start(); self.copy(3, k, p.z, True).start()
            return
        @pl.when(p.z - s >= 0)
        def _():
            src = p.z - s
            self.recv(0, k, src)
            @pl.when(p.z < p.nz - 1)
            def _(): self.copy(0, k, src).start()
            self.copy(2, k, src).start(); self.copy(3, k, src).start()
        @pl.when(p.z + s < p.nz)
        def _():
            src = p.z + s
            self.recv(0, k, src)
            @pl.when(p.z > 0)
            def _(): self.copy(1, k, src).start()
            self.copy(2, k, src).start(); self.copy(3, k, src).start()
    def turn_one(self, k, src):
        self.recv(1, k, src); self.copy(4, k, src).start()
        self.recv(2, k, src); self.copy(5, k, src).start()
    def turn(self, k, s):
        p = self.p
        if s == 0: return self.turn_one(k, p.z)
        @pl.when(p.z - s >= 0)
        def _(): self.turn_one(k, p.z - s)
        @pl.when(p.z + s < p.nz)
        def _(): self.turn_one(k, p.z + s)
    def final(self, k):
        for src in range(self.p.nz):
            self.recv(3, k, src); self.recv(4, k, src)
    def drain(self, k):
        p = self.p
        for src in range(p.nz):
            own = p.z == src
            @pl.when((p.z < p.nz - 1) & (src <= p.z))
            def _(): self.copy(0, k, src).wait_send()
            @pl.when((p.z > 0) & (src >= p.z))
            def _(): self.copy(1, k, src).wait_send()
            for kind in (2, 3, 4, 5): self.copy(kind, k, src).wait_send()

BQ = 256
NEG = -1e30
f32, bf16 = jnp.float32, jnp.bfloat16
def dot_nt(a, b): return lax.dot_general(a, b, (((1,), (1,)), ((), ())), preferred_element_type=f32)
def dot_nn(a, b): return lax.dot_general(a, b, (((1,), (0,)), ((), ())), preferred_element_type=f32)
def flip(a): return a.astype(f32).T.astype(bf16)

def pair_cols(p, group, width):
    return pl.ds(pl.multiple_of(group * width + p * 128, 128), 128)

def masked_keys(k, j, length):
    n = k.shape[0]
    lane = lax.broadcasted_iota(jnp.int32, (n, 128), 1)
    row = lax.broadcasted_iota(jnp.int32, (n, 128), 0)
    out = jnp.where((lane == 64 * (1 - j)) & (row >= length), NEG, 0.0)
    return jnp.where(lane // 64 == j, k.astype(f32), out).astype(bf16)

def with_one(q, j):
    lane = lax.broadcasted_iota(jnp.int32, q.shape, 1)
    return jnp.where(lane == 64 * (1 - j), 1.0, q.astype(f32)).astype(bf16)

def only(a, h):
    lane = lax.broadcasted_iota(jnp.int32, a.shape, 1)
    return jnp.where(lane // 64 == h, a.astype(f32), 0.0).astype(bf16)

def causal(s, i):
    n = s.shape[0] - BQ
    row = lax.broadcasted_iota(jnp.int32, (BQ, BQ), 0)
    col = lax.broadcasted_iota(jnp.int32, (BQ, BQ), 1)
    d = jnp.where(row <= col, s[n:], NEG)
    return d if n == 0 else jnp.concatenate([s[:n], d], axis=0)

def attn_fwd_pair(p, width, length, qkv, mixed, lse):
    n = qkv.shape[0]
    k = qkv[:, pair_cols(p, 1, width)]
    vt = flip(qkv[:, pair_cols(p, 2, width)])
    kp = [masked_keys(k, j, length) for j in (0, 1)]
    for i in range(n // BQ):
        hi = (i + 1) * BQ
        q = qkv[i * BQ:hi, pair_cols(p, 0, width)]
        outs = []
        for j in (0, 1):
            s = causal(dot_nt(kp[j][:hi], with_one(q, j)), i)
            m = jnp.max(s, axis=0, keepdims=True)
            e = jnp.exp(s - m)
            l = jnp.sum(e, axis=0, keepdims=True)
            o = dot_nn(vt[64 * (1 - j):64 * (2 - j), :hi], e.astype(bf16))
            outs.append(o * (1.0 / l))
            lse[2 * p + j, :, i * BQ:hi] = m + jnp.log(l)
        mixed[i * BQ:hi, pair_cols(p, 0, width)] = jnp.concatenate(outs[::-1], axis=0).T.astype(bf16)

def attn_bwd_pair(p, width, length, qkv, mixed, lse, dmixed, dk_acc, dv_acc):
    n = qkv.shape[0]
    c0, c1, c2 = [pair_cols(p, g, width) for g in range(3)]
    k = qkv[:, c1]
    kt = flip(k)
    v = qkv[:, c2]
    kp = [masked_keys(k, j, length) for j in (0, 1)]
    dk_acc[...] = jnp.zeros_like(dk_acc); dv_acc[...] = jnp.zeros_like(dv_acc)
    for i in range(n // BQ):
        hi = (i + 1) * BQ
        q = qkv[i * BQ:hi, c0]
        do = dmixed[i * BQ:hi, c0]
        prod = (do.astype(f32) * mixed[i * BQ:hi, c0].astype(f32)).T
        dq = []
        for j in (0, 1):
            vh = 1 - j
            delta = jnp.sum(prod[64 * vh:64 * (vh + 1)], axis=0, keepdims=True)
            dom = only(do, vh)
            s = causal(dot_nt(kp[j][:hi], with_one(q, j)), i)
            w = jnp.exp(s - lse[2 * p + j, :, i * BQ:hi])
            dw = dot_nt(v[:hi], dom)
            ds = (w * (dw - delta)).astype(bf16)
            dv_acc[:hi] += dot_nn(w.astype(bf16), dom)
            dk_acc[:hi] += dot_nn(ds, only(q, j))
            dq.append(dot_nn(kt[64 * j:64 * (j + 1), :hi], ds))
        qkv[i * BQ:hi, c0] = (jnp.concatenate(dq, axis=0).T * 0.125).astype(bf16)
    qkv[:, c1] = dk_acc[...].astype(bf16)
    qkv[:, c2] = dv_acc[...].astype(bf16)


class Scatter:
    def __init__(self, p, full, bd, bxy, bz, out, ssem, rsem):
        self.p, self.full, self.bd, self.bxy, self.bz, self.out, self.ssem, self.rsem = p, full, bd, bxy, bz, out, ssem, rsem
        self.rows = full.shape[2] // (p.nz * NX)
        self.order = []
        for j in range(p.nz // 2):
            self.order += [p.nz - 1 - j, j]

    def piece(self, yq, k, e, half=None):
        r = self.rows
        if half is None:
            return self.full.at[yq, k, pl.ds(pl.multiple_of(e * r, 16), r)]
        h = r // 2
        return self.full.at[yq, k, pl.ds(pl.multiple_of(e * r + half * h, 16), h)]

    def copy(self, kind, k, d):
        p = self.p
        if kind == 0:
            s, t, dev = self.piece(1 - p.y, k, d * NX + 1 - p.x, 0), self.bd.at[0, k, d], p.yn
        elif kind == 1:
            s, t, dev = self.piece(1 - p.y, k, d * NX + 1 - p.x, 1), self.bd.at[1, k, d], p.xn
        elif kind == 2:
            s, t, dev = self.piece(p.y, k, d * NX + 1 - p.x), self.bxy.at[0, k, d], p.xn
        elif kind == 3:
            s, t, dev = self.piece(1 - p.y, k, d * NX + p.x), self.bxy.at[1, k, d], p.yn
        elif kind == 4:
            s, t, dev = self.piece(p.y, k, d * NX + p.x), self.bz.at[0, k, d], p.up
        else:
            s, t, dev = self.piece(p.y, k, d * NX + p.x), self.bz.at[1, k, d], p.dn
        return remote(s, t, self.ssem.at[kind, k, d], self.rsem.at[kind, k, d], dev)

    def first(self, k):
        for d in self.order:
            self.copy(0, k, d).start()
            self.copy(1, k, d).start()

    def second(self, k, d):
        p = self.p
        self.copy(0, k, d).wait_recv()
        ref = self.piece(p.y, k, d * NX + 1 - p.x, 0)
        ref[...] = (ref[...].astype(f32) + self.bd[0, k, d].astype(f32)).astype(bf16)
        self.copy(2, k, d).start()
        self.copy(1, k, d).wait_recv()
        ref = self.piece(1 - p.y, k, d * NX + p.x, 1)
        ref[...] = (ref[...].astype(f32) + self.bd[1, k, d].astype(f32)).astype(bf16)
        self.copy(3, k, d).start()

    def third(self, k, d):
        p = self.p
        ref = self.piece(p.y, k, d * NX + p.x)
        self.copy(2, k, d).wait_recv()
        self.copy(3, k, d).wait_recv()

        def total():
            return ref[...].astype(f32) + self.bxy[0, k, d].astype(f32) + self.bxy[1, k, d].astype(f32)

        for kind, ahead, start in ((4, d > p.z, p.z == 0), (5, d < p.z, p.z == p.nz - 1)):

            @pl.when(ahead)
            def _():
                @pl.when(jnp.logical_not(start))
                def _():
                    self.copy(kind, k, d).wait_recv()
                    ref[...] = (total() + self.bz[kind - 4, k, d].astype(f32)).astype(bf16)

                @pl.when(start)
                def _():
                    ref[...] = total().astype(bf16)

                self.copy(kind, k, d).start()

        @pl.when(d == p.z)
        def _():
            self.out[k] = total()

    def step(self, k, s):
        nz = self.p.nz
        if s == 0:
            self.first(k)
        if 1 <= s <= nz:
            self.second(k, self.order[s - 1])
        if 3 <= s:
            self.third(k, self.order[s - 3])

    def final(self, k):
        p = self.p

        @pl.when(p.z > 0)
        def _():
            self.copy(4, k, p.z).wait_recv()
            self.out[k] = self.out[k] + self.bz[0, k, p.z].astype(f32)

        @pl.when(p.z < p.nz - 1)
        def _():
            self.copy(5, k, p.z).wait_recv()
            self.out[k] = self.out[k] + self.bz[1, k, p.z].astype(f32)

    def drain(self, k):
        p = self.p
        for d in range(p.nz):
            for kind in (0, 1, 2, 3):
                self.copy(kind, k, d).wait_send()

            @pl.when(d > p.z)
            def _():
                self.copy(4, k, d).wait_send()

            @pl.when(d < p.z)
            def _():
                self.copy(5, k, d).wait_send()


def remote(src, dst, ssem, rsem, dev):
    return pltpu.make_async_remote_copy(src, dst, ssem, rsem, device_id=dev, device_id_type=MESH)


def loop(n, fn):
    def body(i, carry):
        fn(i)
        return carry

    lax.fori_loop(0, n, body, 0)


def at(i, steps):
    for j, todo in enumerate(steps):
        if todo:

            @pl.when(i == j)
            def _(todo=todo):
                for f in todo:
                    f()


def pick(a, b):
    lane = lax.broadcasted_iota(jnp.int32, a.shape, 1)
    return jnp.where(lane % 128 < 64, a.astype(f32), b.astype(f32))


def norm_parts(v):
    center = v - jnp.mean(v, axis=-1, keepdims=True)
    r = lax.rsqrt(jnp.mean(center * center, axis=-1, keepdims=True) + EPSILON)
    return center * r, r


def norm_back(n, r, d, gain):
    q = d * gain
    return r * (q - jnp.mean(q, axis=-1, keepdims=True) - n * jnp.mean(q * n, axis=-1, keepdims=True))


def gelu_both(u):
    a, b = math.sqrt(2.0 / math.pi), 0.044715
    u2 = u * u
    t = jnp.tanh(a * u * (1.0 + b * u2))
    h = 0.5 + 0.5 * t
    return u * h, h + (0.5 * a) * u * (1.0 - t * t) * (1.0 + (3.0 * b) * u2)


def valid(shape, base, length):
    return base + lax.broadcasted_iota(jnp.int32, shape, 0) < length


ROW_B_UP, ROW_B_QV, N_SUM = 6, 8, 16


def block_kernel(
    lens, shard, tokens, ograd, vec,
    result, tgrad, outf, outp, sums,
    w, wc, wo, x_all, sec, dr, t1, t2, ft, qkv, mixed, lse, act, gp, dmx, go,
    r1, r2, r3, r4, s1, s2, part, dk_acc, dv_acc, bias, sm, ar1, ar2,
    grf, grp, fd, fxy, fz, pd, pxy, pz,
    g_ss, g_rs, f_ss, f_rs, p_ss, p_rs, sib_ss, sib_rs, ar_ss, ar_rs,
):
    nz = g_ss.shape[2]
    p = Place(nz)
    c = lax.axis_index("c")
    half, d_model = tokens.shape
    seq = 2 * half
    hw = mixed.shape[1]
    TR = 256
    nt = half // TR
    length = lens[p.y]
    own0, sib0 = c * half, (1 - c) * half

    def rows(base, i, n=TR):
        return pl.ds(pl.multiple_of(base + i * n, n), n)

    peers = []
    for dx in (0, 1):
        for dy in (0, 1):
            for dc in (0, 1):
                if dx + dy + dc:
                    peers.append((4 * dx + 2 * dy + dc, {"e": p.e + dx * (1 - 2 * p.x), "y": p.y + dy * (1 - 2 * p.y), "c": c + dc * (1 - 2 * c)}))
    column = [(r, {"e": ((p.z + r) % nz) * NX + p.x}) for r in range(1, nz)]
    bar = pltpu.get_barrier_semaphore()
    for _, dev in peers + column:
        pl.semaphore_signal(bar, 1, device_id=dev, device_id_type=MESH)
    pl.semaphore_wait(bar, len(peers) + len(column))

    def sib(i, src, dst):
        return remote(src, dst, sib_ss.at[i], sib_rs.at[i], p.core)

    g = Gather(p, shard, w, g_ss, g_rs)
    rf = Scatter(p, grf, fd, fxy, fz, outf, f_ss, f_rs)
    rp = Scatter(p, grp, pd, pxy, pz, outp, p_ss, p_rs)

    x_own, x_sib = x_all.at[rows(own0, 0, half)], x_all.at[rows(sib0, 0, half)]
    send_x = sib(0, tokens, x_own)
    send_x.start()
    g.tick(0, 0)
    send_b = remote(vec.at[pl.ds(0, 8)], bias.at[p.y], sib_ss.at[8], sib_rs.at[8], p.yn)
    send_b.start()
    send_dr = sib(1, ograd, dr.at[rows(own0, 0, half)])
    send_dr.start()
    bias[p.y] = vec[0:8]
    sm[...] = jnp.zeros_like(sm)

    def norm_one(base, src, lo):
        def one(i):
            v = src[rows(lo, i, 128)].astype(f32)
            n, _ = norm_parts(v)
            f = n * vec[2:3] + vec[3:4]
            sec[rows(base, i, 128)] = f.astype(bf16)
            ft[:, rows(base, i, 128)] = f.astype(bf16).astype(f32).T.astype(bf16)

        loop(half // 128, one)

    def mask_rows(base, src, lo):
        def one(i):
            v = jnp.where(valid((128, d_model), base + i * 128, length), src[rows(lo, i, 128)].astype(f32), 0.0)
            dr[rows(base, i, 128)] = v.astype(bf16)
            t1[:, rows(base, i, 128)] = v.T.astype(bf16)

        loop(half // 128, one)

    norm_one(own0, tokens, 0)
    g.tick(0, 1)
    g.turn(0, 0)
    g.tick(1, 0)
    send_x.wait_recv()
    norm_one(sib0, x_all, sib0)
    g.tick(0, 2)
    g.turn(0, 1)
    mask_rows(own0, ograd, 0)
    g.tick(0, 3)
    g.turn(0, 2)
    send_dr.wait_recv()
    mask_rows(sib0, dr, sib0)
    g.turn(0, 3)
    g.final(0)

    def collect(i):
        r = rows(0, i)
        for q in range(hw // 128):
            a = [w[yq, 0, r, q * 256 : q * 256 + 128] for yq in (0, 1)]
            b = [w[yq, 0, r, q * 256 + 128 : q * 256 + 256] for yq in (0, 1)]
            for group, v in enumerate((pick(a[0], a[1]), pick(b[0], b[1]), pick(a[1], a[0]), pick(b[1], b[0]))):
                wc[r, group * hw + q * 128 : group * hw + q * 128 + 128] = v.astype(bf16)
                if group == 3:
                    wo[q * 128 : q * 128 + 128, r] = v.T.astype(bf16)

    loop(d_model // TR, collect)
    g.tick(1, 1)
    g.turn(1, 0)
    send_b.wait_recv()
    ba, bb = bias[0, 7:8], bias[1, 7:8]
    bq = jnp.concatenate([pick(ba[:, q * 256 : q * 256 + 128], bb[:, q * 256 : q * 256 + 128]) for q in range(hw // 128)], axis=1)
    bv = jnp.concatenate([pick(bb[:, q * 256 : q * 256 + 128], ba[:, q * 256 : q * 256 + 128]) for q in range(hw // 128)], axis=1)

    def project(i):
        h = sec[rows(0, i)]
        qkv[rows(0, i), 0:hw] = ((dot_nn(h, wc[:, 0:hw]) + bq).astype(bf16).astype(f32) * 0.125).astype(bf16)
        qkv[rows(0, i), hw : 2 * hw] = dot_nn(h, wc[:, hw : 2 * hw]).astype(bf16)
        qkv[rows(0, i), 2 * hw : 3 * hw] = (dot_nn(h, wc[:, 2 * hw : 3 * hw]) + bv).astype(bf16)

    loop(seq // TR, project)
    g.tick(1, 2)
    g.turn(1, 1)
    g.tick(2, 0)

    def attend(i):
        attn_fwd_pair(i, hw, length, qkv, mixed, lse)
        at(
            i,
            [
                [lambda: g.tick(1, 3), lambda: g.turn(1, 2), lambda: g.tick(2, 1), lambda: g.turn(2, 0)],
                [lambda: g.turn(1, 3), lambda: g.tick(2, 2), lambda: g.turn(2, 1)],
                [lambda: g.tick(2, 3), lambda: g.turn(2, 2)],
            ],
        )

    loop(hw // 128, attend)

    def out_sib(i):
        s1[rows(0, i)] = dot_nn(mixed[rows(sib0, i)], wo[...]).astype(bf16)

    loop(nt, out_sib)
    send_h = sib(2, s1, r1)
    send_h.start()

    def out_own(i):
        result[rows(0, i)] = tokens[rows(0, i)].astype(f32) + dot_nn(mixed[rows(own0, i)], wo[...]) + vec[0:1]

    loop(nt, out_own)
    g.turn(2, 3)
    send_h.wait_recv()

    def norm_two(i):
        h = result[rows(0, i, 128)] + r1[rows(0, i, 128)].astype(f32)
        result[rows(0, i, 128)] = h
        n, _ = norm_parts(h)
        sec[rows(own0, i, 128)] = (n * vec[4:5] + vec[5:6]).astype(bf16)

    loop(half // 128, norm_two)
    send_s = sib(3, sec.at[rows(own0, 0, half)], sec.at[rows(own0, 0, half)])
    send_s.start()
    g.final(1)

    ffq = w.shape[3]

    def up(base):
        def one(i):
            r = rows(base, i)
            h = sec[r]
            t2[:, r] = h.astype(f32).T.astype(bf16)
            for yq in (0, 1):
                u = dot_nn(h, w[yq, 1]) + bias[yq, 6:7]
                a, s = gelu_both(u)
                act[r, yq * ffq : (yq + 1) * ffq] = a.astype(bf16)
                gp[r, yq * ffq : (yq + 1) * ffq] = s.astype(bf16)

        loop(nt, one)

    up(own0)
    send_s.wait_recv()
    up(sib0)

    def down_grad(i):
        r = rows(0, i)
        for yq in (0, 1):
            grf[yq, 1, r] = dot_nn(t1[r], act[:, yq * ffq : (yq + 1) * ffq]).astype(bf16)

    loop(d_model // TR, down_grad)
    rf.step(1, 0)
    g.final(2)

    def pre_grad(i):
        r = rows(0, i)
        for yq in (0, 1):
            cols = slice(yq * ffq, (yq + 1) * ffq)
            v = (dot_nn(dr[r], w[yq, 2]) * gp[r, cols].astype(f32)).astype(bf16)
            gp[r, cols] = v
            sm[ROW_B_UP + yq : ROW_B_UP + yq + 1] += jnp.sum(v.astype(f32), axis=0, keepdims=True)

    loop(seq // TR, pre_grad)
    rf.step(1, 1)
    rf.step(1, 2)

    def up_back(i, base):
        return dot_nt(gp[rows(base, i), 0:ffq], w[0, 1]) + dot_nt(gp[rows(base, i), ffq : 2 * ffq], w[1, 1])

    send_h.wait_send()

    def second_sib(i):
        s1[rows(0, i)] = up_back(i, sib0).astype(bf16)

    loop(nt, second_sib)
    send_d = sib(4, s1, r3)
    send_d.start()

    def second_own(i):
        part[rows(0, i)] = up_back(i, own0)

    loop(nt, second_own)
    rf.step(1, 3)

    def up_grad(i):
        r = rows(0, i)
        for yq in (0, 1):
            grf[yq, 0, r] = dot_nn(t2[r], gp[:, yq * ffq : (yq + 1) * ffq]).astype(bf16)

    send_d.wait_recv()

    def back_two(i):
        r = rows(0, i, 128)
        n, rr = norm_parts(result[r])
        ds = part[r] + r3[r].astype(f32)
        dres = jnp.where(valid((128, d_model), own0 + i * 128, length), ograd[r].astype(f32), 0.0)
        dh = dres + norm_back(n, rr, ds, vec[4:5])
        tgrad[r] = dh
        x_all[rows(own0, i, 128)] = dh.astype(bf16)
        for row, v in ((0, dh), (1, dres), (4, ds * n), (5, ds)):
            sm[row : row + 1] += jnp.sum(v, axis=0, keepdims=True)

    loop(half // 128, back_two)
    send_dh = sib(5, x_own, x_own)
    send_dh.start()
    loop(d_model // TR, up_grad)
    rf.step(0, 0)
    rf.step(1, 4)
    send_dh.wait_recv()

    def mixed_grad(i):
        r = rows(0, i)
        h = x_all[r]
        t1[:, r] = h.astype(f32).T.astype(bf16)
        dmx[r] = dot_nn(h, wc[:, 3 * hw : 4 * hw]).astype(bf16)

    loop(seq // TR, mixed_grad)
    rf.step(1, 5)

    def out_grad_w(i):
        go[rows(0, i)] = dot_nn(t1[rows(0, i)], mixed[...]).astype(bf16)

    loop(d_model // TR, out_grad_w)
    rf.step(0, 1)
    rf.step(1, 6)

    def attend_back(i):
        attn_bwd_pair(i, hw, length, qkv, mixed, lse, dmx, dk_acc, dv_acc)
        cq, ck, cv = [pair_cols(i, group, hw) for group in range(3)]

        def grads(t):
            r = rows(0, t)
            gq, gk, gv = [dot_nn(ft[r], qkv[:, cc]) for cc in (cq, ck, cv)]
            o = go[r, cq].astype(f32)
            grp[0, i, r, 0:128] = pick(gq, gv).astype(bf16)
            grp[0, i, r, 128:256] = pick(gk, o).astype(bf16)
            grp[1, i, r, 0:128] = pick(gv, gq).astype(bf16)
            grp[1, i, r, 128:256] = pick(o, gk).astype(bf16)

        loop(d_model // TR, grads)
        rp.step(i, 0)
        for cc, lo in ((cq, 0), (cv, hw)):
            to = pl.ds(pl.multiple_of(lo + i * 128, 128), 128)
            sm[ROW_B_QV : ROW_B_QV + 1, to] = jnp.sum(qkv[:, cc].astype(f32), axis=0, keepdims=True)
        at(
            i,
            [
                [lambda s=s: rf.step(0, s) for s in (2, 3, 4)],
                [lambda s=s: rf.step(0, s) for s in (5, 6)] + [lambda: rf.final(1)] + [lambda s=s: rp.step(0, s) for s in (1, 2, 3)],
                [lambda: rf.final(0)] + [lambda s=s: rp.step(0, s) for s in (4, 5, 6)] + [lambda s=s: rp.step(1, s) for s in (1, 2, 3)],
            ],
        )

    loop(hw // 128, attend_back)

    def first_back(i, base):
        return dot_nt(qkv[rows(base, i)], wc[:, 0 : 3 * hw])

    def first_sib(i):
        s2[rows(0, i)] = first_back(i, sib0).astype(bf16)

    loop(nt, first_sib)
    send_f = sib(6, s2, r4)
    send_f.start()

    def first_own(i):
        part[rows(0, i)] = first_back(i, own0)

    loop(nt, first_own)
    for s in (4, 5, 6):
        rp.step(1, s)
    for s in (1, 2):
        rp.step(2, s)
    send_f.wait_recv()

    def back_one(i):
        r = rows(0, i, 128)
        n, rr = norm_parts(tokens[r].astype(f32))
        df = part[r] + r4[r].astype(f32)
        tgrad[r] = tgrad[r] + norm_back(n, rr, df, vec[2:3])
        for row, v in ((2, df * n), (3, df)):
            sm[row : row + 1] += jnp.sum(v, axis=0, keepdims=True)

    loop(half // 128, back_one)

    plane = [remote(sm, ar1.at[i], ar_ss.at[i], ar_rs.at[i], dev) for i, dev in peers]
    for cp in plane:
        cp.start()
    for s in (3, 4):
        rp.step(2, s)

    def down(i, base):
        return dot_nt(act[rows(base, i), 0:ffq], w[0, 2]) + dot_nt(act[rows(base, i), ffq : 2 * ffq], w[1, 2])

    send_d.wait_send()

    def down_sib(i):
        s1[rows(0, i)] = down(i, sib0).astype(bf16)

    loop(nt, down_sib)
    send_r = sib(7, s1, r2)
    send_r.start()
    for cp in plane:
        cp.wait()
    lane_row = lax.broadcasted_iota(jnp.int32, (N_SUM, d_model), 0)
    total = sm[...]
    for i, _ in peers:
        total = total + (jnp.where(lane_row < ROW_B_UP, ar1[i], 0.0) if i % 2 else ar1[i])
    sums[...] = total
    line = [remote(sums, ar2.at[r], ar_ss.at[8 + r], ar_rs.at[8 + r], dev) for r, dev in column]
    for cp in line:
        cp.start()
    for s in (5, 6):
        rp.step(2, s)

    def down_own(i):
        part[rows(0, i)] = down(i, own0)

    loop(nt, down_own)
    send_r.wait_recv()

    def finish(i):
        r = rows(0, i, 128)
        v = result[r] + part[r] + r2[r].astype(f32) + vec[1:2]
        result[r] = jnp.where(valid((128, d_model), own0 + i * 128, length), v, 0.0)

    loop(half // 128, finish)
    for cp in line:
        cp.wait()
    for r, _ in column:
        total = total + ar2[r]
    sums[...] = total
    for k in range(3):
        rp.final(k)

    for k in range(NK):
        g.drain(k)
    for k in range(2):
        rf.drain(k)
    for k in range(3):
        rp.drain(k)
    for cp in (send_x, send_b, send_dr, send_s, send_dh, send_f, send_r):
        cp.wait_send()


def block(lens, shard, tokens, ograd, vec, nz):
    half, d = tokens.shape
    seq = 2 * half
    nk, rows, ffq = shard.shape
    hw = d // 2
    pw = 256
    npair = hw // 128

    def V(shape, t=bf16):
        return pltpu.VMEM(shape, t)

    scratch = [
        V((2, nk, d, ffq)), V((d, 4 * hw)), V((hw, d)), V((seq, d)), V((seq, d)), V((seq, d)), V((d, seq)), V((d, seq)), V((d, seq)),
        V((seq, 3 * hw)), V((seq, hw)), V((2 * npair, 1, seq), f32), V((seq, 2 * ffq)), V((seq, 2 * ffq)), V((seq, hw)), V((d, hw)),
        V((half, d)), V((half, d)), V((half, d)), V((half, d)), V((half, d)), V((half, d)), V((half, d), f32),
        V((seq, 128), f32), V((seq, 128), f32), V((2, 8, d), f32), V((N_SUM, d), f32), V((8, N_SUM, d), f32), V((nz, N_SUM, d), f32),
        V((2, 2, d, ffq)), V((2, npair, d, pw)),
        V((2, 2, nz, rows // 2, ffq)), V((2, 2, nz, rows, ffq)), V((2, 2, nz, rows, ffq)),
        V((2, npair, nz, rows // 2, pw)), V((2, npair, nz, rows, pw)), V((2, npair, nz, rows, pw)),
    ]
    dma = pltpu.SemaphoreType.DMA
    sems = [dma((6, nk, nz)), dma((5, nk, nz)), dma((6, 2, nz)), dma((6, 2, nz)), dma((6, npair, nz)), dma((6, npair, nz)), dma((9,)), dma((9,)), dma((8 + nz,)), dma((8 + nz,))]
    vm = pl.BlockSpec(memory_space=pltpu.VMEM)
    return pl.pallas_call(
        block_kernel,
        out_shape=(
            jax.ShapeDtypeStruct((half, d), f32),
            jax.ShapeDtypeStruct((half, d), f32),
            jax.ShapeDtypeStruct((2, rows, ffq), f32),
            jax.ShapeDtypeStruct((npair, rows, pw), f32),
            jax.ShapeDtypeStruct((N_SUM, d), f32),
        ),
        in_specs=[pl.BlockSpec(memory_space=pltpu.SMEM), vm, vm, vm, vm],
        out_specs=(vm,) * 5,
        scratch_shapes=scratch + sems,
        compiler_params=pltpu.CompilerParams(collective_id=0, has_side_effects=True, vmem_limit_bytes=64 << 20),
    )(lens, shard, tokens, ograd, vec)


def per_device(tokens, lengths, w_qkv, b_qv, w_out, b_out, w_up, b_up, w_down, b_down, g_one, c_one, g_two, c_two, out_grad, *, nz, sub):
    y = lax.axis_index("y")
    d = tokens.shape[1]
    heads = w_qkv.shape[2] // HEAD_DIM
    first = y == 0

    def lanes(a):
        return a[..., :HEAD_DIM], a[..., HEAD_DIM:]

    def swap(a, b):
        return [jnp.where(first, a, b), jnp.where(first, b, a)]

    pieces = []
    bias = []
    w_out_t = w_out.T
    for h in range(heads):
        s = slice(h * HEAD_DIM, (h + 1) * HEAD_DIM)
        pieces += swap(w_qkv[0][:, s], w_qkv[2][:, s]) + swap(w_qkv[1][:, s], w_out_t[:, s])
        bias += swap(b_qv[0, s], b_qv[1, s]) + [jnp.zeros((2 * HEAD_DIM,), f32)]
    packed = jnp.stack([jnp.concatenate(pieces, axis=1), w_up, w_down.T])
    if sub > 1:
        packed = lax.all_gather(packed, "r", axis=1, tiled=True)
    vec = jnp.stack([b_out, b_down, g_one, c_one, g_two, c_two, b_up, jnp.concatenate(bias)])
    result, tokens_grad, outf, outp, sums = block(lengths, packed, tokens, out_grad, vec, nz)
    if sub > 1:
        outf, outp = [lax.psum_scatter(a, "r", scatter_dimension=1, tiled=True) for a in (outf, outp)]
        sums = lax.psum(sums, "r")
    qs, ks, vs, os_ = [], [], [], []
    for h in range(heads):
        a = lanes(outp[h][:, : 2 * HEAD_DIM])
        b = lanes(outp[h][:, 2 * HEAD_DIM :])
        q, v = swap(*a)
        k, o = swap(*b)
        qs.append(q), ks.append(k), vs.append(v), os_.append(o)
    qkv_grad = jnp.stack([jnp.concatenate(a, axis=1) for a in (qs, ks, vs)])
    out_grad_w = jnp.concatenate(os_, axis=1).T
    bq, bv = [sums[ROW_B_QV, i * d // 2 : (i + 1) * d // 2].reshape(heads, 2, HEAD_DIM) for i in (0, 1)]
    b_qv_grad = jnp.stack([jnp.where(first, bq[:, 0], bq[:, 1]).reshape(-1), jnp.where(first, bv[:, 1], bv[:, 0]).reshape(-1)])
    b_up_grad = jnp.where(first, sums[ROW_B_UP], sums[ROW_B_UP + 1])
    return (result, tokens_grad, qkv_grad, b_qv_grad, out_grad_w, sums[0], outf[0], b_up_grad, outf[1].T, sums[1], sums[2], sums[3], sums[4], sums[5])


def solution(mesh):
    dp, tensor = mesh.shape["dp"], mesh.shape["tensor"]
    line = 4 * NX
    nz, sub = line // NX, dp // line
    grid = Mesh(mesh.devices.reshape(line, sub, tensor // 2, 2), ("e", "r", "y", "c"))
    dpx, tx = ("e", "r"), ("y", "c")
    rows = P(dpx + tx, None)
    return jax.shard_map(
        functools.partial(per_device, nz=nz, sub=sub),
        mesh=grid,
        in_specs=(rows, P(dpx), P(None, dpx, tx), P(None, tx), P(tx, dpx), P(), P(dpx, tx), P(tx), P(tx, dpx), P(), P(), P(), P(), P(), rows),
        out_specs=(rows, rows, P(None, dpx, tx), P(None, tx), P(tx, dpx), P(), P(dpx, tx), P(tx), P(tx, dpx), P(), P(), P(), P(), P()),
        check_vma=False,
    )
```

```python
import functools
import math

import jax
import jax.numpy as jnp
from jax import lax
from jax.experimental import pallas as pl
from jax.experimental.pallas import tpu as pltpu
from jax.sharding import Mesh
from jax.sharding import PartitionSpec as P

HEAD_DIM = 64
EPSILON = 1e-05
MESH = pl.DeviceIdType.MESH
NX = 2
NK = 3

class Place:
    def __init__(self, nz):
        self.nz = nz
        self.e = lax.axis_index("e"); self.y = lax.axis_index("y")
        self.z = self.e // NX; self.x = self.e % NX
        self.xn = {"e": self.e + 1 - 2 * self.x}
        self.yn = {"y": 1 - self.y}
        self.up = {"e": self.e + NX}
        self.dn = {"e": self.e - NX}
        self.core = {"c": 1 - lax.axis_index("c")}

BQ = 256
NEG = -1e30
f32, bf16 = jnp.float32, jnp.bfloat16
def dot_nt(a, b): return lax.dot_general(a, b, (((1,), (1,)), ((), ())), preferred_element_type=f32)
def dot_nn(a, b): return lax.dot_general(a, b, (((1,), (0,)), ((), ())), preferred_element_type=f32)
def flip(a): return a.astype(f32).T.astype(bf16)

def pair_cols(p, group, width):
    return pl.ds(pl.multiple_of(group * width + p * 128, 128), 128)

def masked_keys(k, j, length):
    n = k.shape[0]
    lane = lax.broadcasted_iota(jnp.int32, (n, 128), 1)
    row = lax.broadcasted_iota(jnp.int32, (n, 128), 0)
    out = jnp.where((lane == 64 * (1 - j)) & (row >= length), NEG, 0.0)
    return jnp.where(lane // 64 == j, k.astype(f32), out).astype(bf16)

def with_one(q, j):
    lane = lax.broadcasted_iota(jnp.int32, q.shape, 1)
    return jnp.where(lane == 64 * (1 - j), 1.0, q.astype(f32)).astype(bf16)

def only(a, h):
    lane = lax.broadcasted_iota(jnp.int32, a.shape, 1)
    return jnp.where(lane // 64 == h, a.astype(f32), 0.0).astype(bf16)

def causal(s, i):
    n = s.shape[0] - BQ
    row = lax.broadcasted_iota(jnp.int32, (BQ, BQ), 0)
    col = lax.broadcasted_iota(jnp.int32, (BQ, BQ), 1)
    d = jnp.where(row <= col, s[n:], NEG)
    return d if n == 0 else jnp.concatenate([s[:n], d], axis=0)

def attn_fwd_pair(p, width, length, qkv, mixed, lse, hook):
    n = qkv.shape[0]
    k = qkv[:, pair_cols(p, 1, width)]
    vt = flip(qkv[:, pair_cols(p, 2, width)])
    kp = [masked_keys(k, j, length) for j in (0, 1)]
    for i in range(n // BQ):
        hi = (i + 1) * BQ
        q = qkv[i * BQ:hi, pair_cols(p, 0, width)]
        outs = []
        for j in (0, 1):
            s = causal(dot_nt(kp[j][:hi], with_one(q, j)), i)
            m = jnp.max(s, axis=0, keepdims=True)
            e = jnp.exp(s - m)
            l = jnp.sum(e, axis=0, keepdims=True)
            o = dot_nn(vt[64 * (1 - j):64 * (2 - j), :hi], e.astype(bf16))
            outs.append(o * (1.0 / l))
            lse[2 * p + j, :, i * BQ:hi] = m + jnp.log(l)
        mixed[i * BQ:hi, pair_cols(p, 0, width)] = jnp.concatenate(outs[::-1], axis=0).T.astype(bf16)
        hook(i)

def attn_bwd_pair(p, width, length, qkv, mixed, lse, dmixed, dk_acc, dv_acc, hook):
    n = qkv.shape[0]
    c0, c1, c2 = [pair_cols(p, g, width) for g in range(3)]
    k = qkv[:, c1]
    kt = flip(k)
    v = qkv[:, c2]
    kp = [masked_keys(k, j, length) for j in (0, 1)]
    dk_acc[...] = jnp.zeros_like(dk_acc); dv_acc[...] = jnp.zeros_like(dv_acc)
    for i in range(n // BQ):
        hi = (i + 1) * BQ
        q = qkv[i * BQ:hi, c0]
        do = dmixed[i * BQ:hi, c0]
        prod = (do.astype(f32) * mixed[i * BQ:hi, c0].astype(f32)).T
        dq = []
        for j in (0, 1):
            vh = 1 - j
            delta = jnp.sum(prod[64 * vh:64 * (vh + 1)], axis=0, keepdims=True)
            dom = only(do, vh)
            s = causal(dot_nt(kp[j][:hi], with_one(q, j)), i)
            w = jnp.exp(s - lse[2 * p + j, :, i * BQ:hi])
            dw = dot_nt(v[:hi], dom)
            ds = (w * (dw - delta)).astype(bf16)
            dv_acc[:hi] += dot_nn(w.astype(bf16), dom)
            dk_acc[:hi] += dot_nn(ds, only(q, j))
            dq.append(dot_nn(kt[64 * j:64 * (j + 1), :hi], ds))
        qkv[i * BQ:hi, c0] = (jnp.concatenate(dq, axis=0).T * 0.125).astype(bf16)
        hook(i)
    qkv[:, c1] = dk_acc[...].astype(bf16)
    qkv[:, c2] = dv_acc[...].astype(bf16)


class Gather:
    def __init__(self, p, own, full, ssem, rsem):
        self.p, self.own, self.full, self.ssem, self.rsem = p, own, full, ssem, rsem
        self.rows = own.shape[1]

    def piece(self, yq, k, e, half=None):
        r = self.rows
        if half is None:
            return self.full.at[yq, k, pl.ds(pl.multiple_of(e * r, 16), r)]
        h = r // 2
        return self.full.at[yq, k, pl.ds(pl.multiple_of(e * r + half * h, 16), h)]

    def z(self, r):
        return (self.p.z + r + self.p.nz) % self.p.nz

    def copy(self, kind, k, r):
        p = self.p
        back = self.z(-r)
        if kind == 0:
            s, t, dev = self.own.at[k], self.piece(p.y, k, p.e), {"e": self.z(r) * NX + p.x}
        elif kind in (1, 2):
            t = self.piece(p.y, k, back * NX + p.x)
            s, dev = (t if r else self.own.at[k]), (p.xn, p.yn)[kind - 1]
        elif kind == 3:
            s = t = self.piece(p.y, k, back * NX + 1 - p.x, 0)
            dev = p.yn
        else:
            s = t = self.piece(1 - p.y, k, back * NX + p.x, 1)
            dev = p.xn
        return remote(s, t, self.ssem.at[kind, k, r], self.rsem.at[kind, k, r], dev)

    def got(self, kind, k, r):
        p = self.p
        back = self.z(-r) * NX
        yq = p.y if kind < 2 else 1 - p.y
        e = back + (p.x if kind in (0, 2) else 1 - p.x)
        ref = self.piece(yq, k, e, None if kind < 3 else kind - 3)
        remote(ref, ref, self.ssem.at[kind, k, r], self.rsem.at[kind, k, r], p.xn).wait_recv()

    def own_z(self, k):
        nz = self.p.nz
        for r in [1, nz - 1] + list(range(2, nz - 1)):
            self.copy(0, k, r).start()

    def own_xy(self, k):
        self.copy(1, k, 0).start()
        self.copy(2, k, 0).start()

    def pass_on(self, k, r):
        self.got(0, k, r)
        self.copy(1, k, r).start()
        self.copy(2, k, r).start()

    def turn(self, k, r):
        self.got(1, k, r)
        self.copy(3, k, r).start()
        self.got(2, k, r)
        self.copy(4, k, r).start()

    def final(self, k):
        for r in range(self.p.nz):
            self.got(3, k, r)
            self.got(4, k, r)

    def drain(self, k):
        for r in range(self.p.nz):
            for kind in range(5):
                if kind or r:
                    self.copy(kind, k, r).wait_send()


class Scatter:
    def __init__(self, p, full, bd, bxy, bz, out, ssem, rsem):
        self.p, self.full, self.bd, self.bxy, self.bz, self.out, self.ssem, self.rsem = p, full, bd, bxy, bz, out, ssem, rsem
        self.rows = full.shape[2] // (p.nz * NX)

    def piece(self, yq, k, e, half=None):
        r = self.rows
        if half is None:
            return self.full.at[yq, k, pl.ds(pl.multiple_of(e * r, 16), r)]
        h = r // 2
        return self.full.at[yq, k, pl.ds(pl.multiple_of(e * r + half * h, 16), h)]

    def copy(self, kind, k, d):
        p = self.p
        if kind == 0:
            s, t, dev = self.piece(1 - p.y, k, d * NX + 1 - p.x, 0), self.bd.at[0, k, d], p.yn
        elif kind == 1:
            s, t, dev = self.piece(1 - p.y, k, d * NX + 1 - p.x, 1), self.bd.at[1, k, d], p.xn
        elif kind == 2:
            s, t, dev = self.piece(p.y, k, d * NX + 1 - p.x), self.bxy.at[0, k, d], p.xn
        elif kind == 3:
            s, t, dev = self.piece(1 - p.y, k, d * NX + p.x), self.bxy.at[1, k, d], p.yn
        else:
            e = ((p.z + d) % p.nz) * NX + p.x
            s, t, dev = self.piece(p.y, k, e), self.bz.at[k, d - 1], {"e": e}
        return remote(s, t, self.ssem.at[kind, k, d], self.rsem.at[kind, k, d], dev)

    def first(self, k, d):
        self.copy(0, k, d).start()
        self.copy(1, k, d).start()

    def second(self, k, d):
        p = self.p
        self.copy(0, k, d).wait_recv()
        ref = self.piece(p.y, k, d * NX + 1 - p.x, 0)
        ref[...] = (ref[...].astype(f32) + self.bd[0, k, d].astype(f32)).astype(bf16)
        self.copy(2, k, d).start()
        self.copy(1, k, d).wait_recv()
        ref = self.piece(1 - p.y, k, d * NX + p.x, 1)
        ref[...] = (ref[...].astype(f32) + self.bd[1, k, d].astype(f32)).astype(bf16)
        self.copy(3, k, d).start()

    def third(self, k):
        p = self.p
        for d in range(p.nz):
            self.copy(2, k, d).wait_recv()
            self.copy(3, k, d).wait_recv()
        for r in list(range(1, p.nz)) + [0]:
            d = (p.z + r) % p.nz
            ref = self.piece(p.y, k, d * NX + p.x)
            total = ref[...].astype(f32) + self.bxy[0, k, d].astype(f32) + self.bxy[1, k, d].astype(f32)
            if r == 0:
                self.out[k] = total
            else:
                ref[...] = total.astype(bf16)
                self.copy(4, k, r).start()

    def final(self, k):
        total = self.out[k]
        for r in range(1, self.p.nz):
            self.copy(4, k, r).wait_recv()
            total = total + self.bz[k, r - 1].astype(f32)
        self.out[k] = total

    def drain(self, k):
        for d in range(self.p.nz):
            for kind in (0, 1, 2, 3):
                self.copy(kind, k, d).wait_send()
            if d:
                self.copy(4, k, d).wait_send()


def remote(src, dst, ssem, rsem, dev):
    return pltpu.make_async_remote_copy(src, dst, ssem, rsem, device_id=dev, device_id_type=MESH)


def loop(n, fn, after=()):
    def body(i, carry):
        fn(i)
        at(i, after)
        return carry

    lax.fori_loop(0, n, body, 0)


def at(i, steps):
    for j, todo in enumerate(steps):
        if todo:

            @pl.when(i == j)
            def _(todo=todo):
                for f in todo:
                    f()


def pick(a, b):
    lane = lax.broadcasted_iota(jnp.int32, a.shape, 1)
    return jnp.where(lane % 128 < 64, a.astype(f32), b.astype(f32))


def norm_parts(v):
    center = v - jnp.mean(v, axis=-1, keepdims=True)
    r = lax.rsqrt(jnp.mean(center * center, axis=-1, keepdims=True) + EPSILON)
    return center * r, r


def norm_back(n, r, d, gain):
    q = d * gain
    return r * (q - jnp.mean(q, axis=-1, keepdims=True) - n * jnp.mean(q * n, axis=-1, keepdims=True))


def gelu_both(u):
    a, b = math.sqrt(2.0 / math.pi), 0.044715
    u2 = u * u
    t = jnp.tanh(a * u * (1.0 + b * u2))
    h = 0.5 + 0.5 * t
    return u * h, h + (0.5 * a) * u * (1.0 - t * t) * (1.0 + (3.0 * b) * u2)


def valid(shape, base, length):
    return base + lax.broadcasted_iota(jnp.int32, shape, 0) < length


ROW_B_UP, ROW_B_QV, N_SUM = 6, 8, 16


def block_kernel(
    lens, shard, tokens, ograd, vec,
    result_hbm, tgrad_hbm, outf, outp, sums,
    result, tgrad, tok, og, w, wc, wo, x_all, sec, dr, t1, t2, ft, qkv, mixed, lse, act, gp, dmx, go,
    r1, r2, r3, r4, s1, s2, part, dk_acc, dv_acc, bias, sm, ar1, ar2,
    grf, grp, fd, fxy, fz, pd, pxy, pz,
    g_ss, g_rs, f_ss, f_rs, p_ss, p_rs, sib_ss, sib_rs, ar_ss, ar_rs, loc,
):
    nz = g_ss.shape[2]
    p = Place(nz)
    c = lax.axis_index("c")
    half, d_model = tokens.shape
    seq = 2 * half
    hw = mixed.shape[1]
    TR = 256
    nt = half // TR
    length = lens[p.y]
    own0, sib0 = c * half, (1 - c) * half

    def rows(base, i, n=TR):
        return pl.ds(pl.multiple_of(base + i * n, n), n)

    load_t = pltpu.make_async_copy(tokens, tok, loc.at[0])
    load_g = pltpu.make_async_copy(ograd, og, loc.at[1])
    load_t.start()
    load_g.start()
    peers = []
    for dx in (0, 1):
        for dy in (0, 1):
            for dc in (0, 1):
                if dx + dy + dc:
                    peers.append((4 * dx + 2 * dy + dc, {"e": p.e + dx * (1 - 2 * p.x), "y": p.y + dy * (1 - 2 * p.y), "c": c + dc * (1 - 2 * c)}))
    column = [(r, {"e": ((p.z + r) % nz) * NX + p.x}) for r in range(1, nz)]
    bar = pltpu.get_barrier_semaphore()
    for _, dev in peers + column:
        pl.semaphore_signal(bar, 1, device_id=dev, device_id_type=MESH)
    pl.semaphore_wait(bar, len(peers) + len(column))

    def sib(i, src, dst):
        return remote(src, dst, sib_ss.at[i], sib_rs.at[i], p.core)

    g = Gather(p, shard, w, g_ss, g_rs)
    rf = Scatter(p, grf, fd, fxy, fz, outf, f_ss, f_rs)
    rp = Scatter(p, grp, pd, pxy, pz, outp, p_ss, p_rs)
    DOWN, UP = 1, 0

    x_own, x_sib = x_all.at[rows(own0, 0, half)], x_all.at[rows(sib0, 0, half)]
    g.own_xy(0)
    g.own_z(0)
    send_x = sib(0, tokens, x_own)
    send_x.start()
    g.own_z(1)
    send_dr = sib(1, ograd, dr.at[rows(own0, 0, half)])
    send_dr.start()
    send_b = remote(vec.at[pl.ds(0, 8)], bias.at[p.y], sib_ss.at[8], sib_rs.at[8], p.yn)
    send_b.start()
    keep = [pltpu.make_async_copy(shard.at[k], g.piece(p.y, k, p.e), loc.at[2 + k]) for k in range(NK)]
    for cp in keep:
        cp.start()
    bias[p.y] = vec[0:8]
    sm[...] = jnp.zeros_like(sm)

    def norm_one(base, src, lo):
        def one(i):
            v = src[rows(lo, i, 128)].astype(f32)
            n, _ = norm_parts(v)
            f = n * vec[2:3] + vec[3:4]
            sec[rows(base, i, 128)] = f.astype(bf16)
            ft[:, rows(base, i, 128)] = f.astype(bf16).astype(f32).T.astype(bf16)

        loop(half // 128, one)

    def mask_rows(base, src, lo):
        def one(i):
            v = jnp.where(valid((128, d_model), base + i * 128, length), src[rows(lo, i, 128)].astype(f32), 0.0)
            dr[rows(base, i, 128)] = v.astype(bf16)
            t1[:, rows(base, i, 128)] = v.T.astype(bf16)

        loop(half // 128, one)

    load_t.wait()
    norm_one(own0, tok, 0)
    g.pass_on(0, 1)
    send_x.wait_recv()
    norm_one(sib0, x_all, sib0)
    g.pass_on(0, 3)
    g.turn(0, 0)
    g.pass_on(0, 2)
    load_g.wait()
    mask_rows(own0, og, 0)
    g.own_xy(1)
    g.turn(0, 1)
    g.pass_on(1, 1)
    send_dr.wait_recv()
    mask_rows(sib0, dr, sib0)
    g.turn(0, 3)
    g.pass_on(1, 3)
    g.turn(0, 2)
    g.pass_on(1, 2)
    for cp in keep:
        cp.wait()
    g.final(0)

    def collect(i):
        r = rows(0, i)
        for q in range(hw // 128):
            a = [w[yq, 0, r, q * 256 : q * 256 + 128] for yq in (0, 1)]
            b = [w[yq, 0, r, q * 256 + 128 : q * 256 + 256] for yq in (0, 1)]
            for group, v in enumerate((pick(a[0], a[1]), pick(b[0], b[1]), pick(a[1], a[0]), pick(b[1], b[0]))):
                wc[r, group * hw + q * 128 : group * hw + q * 128 + 128] = v.astype(bf16)
                if group == 3:
                    wo[q * 128 : q * 128 + 128, r] = v.T.astype(bf16)

    loop(d_model // TR, collect)
    send_b.wait_recv()
    ba, bb = bias[0, 7:8], bias[1, 7:8]
    bq = jnp.concatenate([pick(ba[:, q * 256 : q * 256 + 128], bb[:, q * 256 : q * 256 + 128]) for q in range(hw // 128)], axis=1)
    bv = jnp.concatenate([pick(bb[:, q * 256 : q * 256 + 128], ba[:, q * 256 : q * 256 + 128]) for q in range(hw // 128)], axis=1)

    def project(i):
        h = sec[rows(0, i)]
        qkv[rows(0, i), 0:hw] = ((dot_nn(h, wc[:, 0:hw]) + bq).astype(bf16).astype(f32) * 0.125).astype(bf16)
        qkv[rows(0, i), hw : 2 * hw] = dot_nn(h, wc[:, hw : 2 * hw]).astype(bf16)
        qkv[rows(0, i), 2 * hw : 3 * hw] = (dot_nn(h, wc[:, 2 * hw : 3 * hw]) + bv).astype(bf16)

    loop(seq // TR, project, [[], [lambda: g.turn(1, 0)], [], [lambda: g.own_z(2)]])

    fwd_steps = {
        (0, 2): [lambda: g.turn(1, 1)],
        (1, 1): [lambda: g.own_xy(2)],
        (1, 2): [lambda: g.turn(1, 3)],
        (2, 1): [lambda: g.turn(1, 2)],
        (2, 2): [lambda: g.pass_on(2, 1)],
        (2, 3): [lambda: g.pass_on(2, 3)],
    }

    def attend(i):
        attn_fwd_pair(i, hw, length, qkv, mixed, lse, lambda b: at(i, [fwd_steps.get((j, b), []) for j in range(hw // 128)]))

    loop(hw // 128, attend)

    def out_sib(i):
        s1[rows(0, i)] = dot_nn(mixed[rows(sib0, i)], wo[...]).astype(bf16)

    loop(nt, out_sib)
    send_h = sib(2, s1, r1)
    send_h.start()

    def out_own(i):
        result[rows(0, i)] = tok[rows(0, i)].astype(f32) + dot_nn(mixed[rows(own0, i)], wo[...]) + vec[0:1]

    loop(nt, out_own)
    g.pass_on(2, 2)
    send_h.wait_recv()

    def norm_two(i):
        h = result[rows(0, i, 128)] + r1[rows(0, i, 128)].astype(f32)
        result[rows(0, i, 128)] = h
        n, _ = norm_parts(h)
        sec[rows(own0, i, 128)] = (n * vec[4:5] + vec[5:6]).astype(bf16)

    loop(half // 128, norm_two)
    send_s = sib(3, sec.at[rows(own0, 0, half)], sec.at[rows(own0, 0, half)])
    send_s.start()
    g.turn(2, 0)
    g.final(1)

    ffq = w.shape[3]

    def up(base, after):
        def one(i):
            r = rows(base, i)
            h = sec[r]
            t2[:, r] = h.astype(f32).T.astype(bf16)
            for yq in (0, 1):
                u = dot_nn(h, w[yq, 1]) + bias[yq, 6:7]
                a, s = gelu_both(u)
                act[r, yq * ffq : (yq + 1) * ffq] = a.astype(bf16)
                gp[r, yq * ffq : (yq + 1) * ffq] = s.astype(bf16)

        loop(nt, one, after)

    up(own0, [[], [lambda: g.turn(2, 1)]])
    send_s.wait_recv()
    up(sib0, [[], [lambda: g.turn(2, 3)]])

    ZR = d_model // nz

    def down_grad(i):
        r = rows(0, i, ZR)
        for yq in (0, 1):
            grf[yq, DOWN, r] = dot_nn(t1[r], act[:, yq * ffq : (yq + 1) * ffq]).astype(bf16)

    loop(nz, down_grad, [[], [lambda: g.turn(2, 2)], [lambda d=d: rf.first(DOWN, d) for d in range(3)], [lambda: rf.first(DOWN, 3)]])
    g.final(2)

    def pre_grad(i):
        r = rows(0, i)
        for yq in (0, 1):
            cols = slice(yq * ffq, (yq + 1) * ffq)
            v = (dot_nn(dr[r], w[yq, 2]) * gp[r, cols].astype(f32)).astype(bf16)
            gp[r, cols] = v
            sm[ROW_B_UP + yq : ROW_B_UP + yq + 1] += jnp.sum(v.astype(f32), axis=0, keepdims=True)

    loop(seq // TR, pre_grad, [[lambda d=d: rf.second(DOWN, d)] for d in range(nz)])

    def up_back(i, base):
        return dot_nt(gp[rows(base, i), 0:ffq], w[0, 1]) + dot_nt(gp[rows(base, i), ffq : 2 * ffq], w[1, 1])

    send_h.wait_send()

    def second_sib(i):
        s1[rows(0, i)] = up_back(i, sib0).astype(bf16)

    loop(nt, second_sib)
    send_d = sib(4, s1, r3)
    send_d.start()

    def second_own(i):
        part[rows(0, i)] = up_back(i, own0)

    loop(nt, second_own)

    def up_grad(i):
        r = rows(0, i, ZR)
        for yq in (0, 1):
            grf[yq, UP, r] = dot_nn(t2[r], gp[:, yq * ffq : (yq + 1) * ffq]).astype(bf16)
        rf.first(UP, i)

    loop(nz, up_grad)
    send_d.wait_recv()

    def back_two(i):
        r = rows(0, i, 128)
        n, rr = norm_parts(result[r])
        ds = part[r] + r3[r].astype(f32)
        dres = jnp.where(valid((128, d_model), own0 + i * 128, length), og[r].astype(f32), 0.0)
        dh = dres + norm_back(n, rr, ds, vec[4:5])
        tgrad[r] = dh
        x_all[rows(own0, i, 128)] = dh.astype(bf16)
        for row, v in ((0, dh), (1, dres), (4, ds * n), (5, ds)):
            sm[row : row + 1] += jnp.sum(v, axis=0, keepdims=True)

    loop(half // 128, back_two)
    send_dh = sib(5, x_own, x_own)
    send_dh.start()
    send_dh.wait_recv()

    def mixed_grad(i):
        r = rows(0, i)
        h = x_all[r]
        t1[:, r] = h.astype(f32).T.astype(bf16)
        dmx[r] = dot_nn(h, wc[:, 3 * hw : 4 * hw]).astype(bf16)

    loop(seq // TR, mixed_grad)

    def out_grad_w(i):
        go[rows(0, i)] = dot_nn(t1[rows(0, i)], mixed[...]).astype(bf16)

    loop(d_model // TR, out_grad_w)

    bwd_steps = {
        (0, 0): [lambda: rf.third(DOWN)],
        (0, 2): [lambda: rf.second(UP, 0), lambda: rf.second(UP, 1)],
        (0, 3): [lambda: rf.second(UP, 2), lambda: rf.second(UP, 3)],
        (1, 1): [lambda: rp.second(0, 0), lambda: rp.second(0, 1)],
        (1, 2): [lambda: rp.second(0, 2), lambda: rp.second(0, 3)],
        (1, 3): [lambda: rf.third(UP)],
        (2, 0): [lambda: rf.final(DOWN)],
        (2, 1): [lambda: rp.second(1, 0), lambda: rp.second(1, 1)],
        (2, 2): [lambda: rp.second(1, 2), lambda: rp.second(1, 3)],
        (2, 3): [lambda: rp.third(0)],
    }

    def attend_back(i):
        attn_bwd_pair(
            i, hw, length, qkv, mixed, lse, dmx, dk_acc, dv_acc, lambda b: at(i, [bwd_steps.get((j, b), []) for j in range(hw // 128)])
        )
        cq, ck, cv = [pair_cols(i, group, hw) for group in range(3)]

        def grads(t):
            r = rows(0, t, ZR)
            gq, gk, gv = [dot_nn(ft[r], qkv[:, cc]) for cc in (cq, ck, cv)]
            o = go[r, cq].astype(f32)
            grp[0, i, r, 0:128] = pick(gq, gv).astype(bf16)
            grp[0, i, r, 128:256] = pick(gk, o).astype(bf16)
            grp[1, i, r, 0:128] = pick(gv, gq).astype(bf16)
            grp[1, i, r, 128:256] = pick(o, gk).astype(bf16)
            rp.first(i, t)

        loop(nz, grads)
        for cc, lo in ((cq, 0), (cv, hw)):
            to = pl.ds(pl.multiple_of(lo + i * 128, 128), 128)
            sm[ROW_B_QV : ROW_B_QV + 1, to] = jnp.sum(qkv[:, cc].astype(f32), axis=0, keepdims=True)

    loop(hw // 128, attend_back)

    def first_back(i, base):
        return dot_nt(qkv[rows(base, i)], wc[:, 0 : 3 * hw])

    def first_sib(i):
        s2[rows(0, i)] = first_back(i, sib0).astype(bf16)

    loop(nt, first_sib)
    send_f = sib(6, s2, r4)
    send_f.start()

    def first_own(i):
        part[rows(0, i)] = first_back(i, own0)

    loop(nt, first_own)
    rp.second(2, 0)
    rp.second(2, 1)
    send_f.wait_recv()

    def back_one(i):
        r = rows(0, i, 128)
        n, rr = norm_parts(tok[r].astype(f32))
        df = part[r] + r4[r].astype(f32)
        tgrad[r] = tgrad[r] + norm_back(n, rr, df, vec[2:3])
        for row, v in ((2, df * n), (3, df)):
            sm[row : row + 1] += jnp.sum(v, axis=0, keepdims=True)

    loop(half // 128, back_one)
    store_t = pltpu.make_async_copy(tgrad, tgrad_hbm, loc.at[0])
    store_t.start()

    plane = [remote(sm, ar1.at[i], ar_ss.at[i], ar_rs.at[i], dev) for i, dev in peers]
    for cp in plane:
        cp.start()
    rp.second(2, 2)
    rp.second(2, 3)
    rp.third(1)

    def down(i, base):
        return dot_nt(act[rows(base, i), 0:ffq], w[0, 2]) + dot_nt(act[rows(base, i), ffq : 2 * ffq], w[1, 2])

    send_d.wait_send()

    def down_sib(i):
        s1[rows(0, i)] = down(i, sib0).astype(bf16)

    loop(nt, down_sib)
    send_r = sib(7, s1, r2)
    send_r.start()
    for cp in plane:
        cp.wait()
    lane_row = lax.broadcasted_iota(jnp.int32, (N_SUM, d_model), 0)
    total = sm[...]
    for i, _ in peers:
        total = total + (jnp.where(lane_row < ROW_B_UP, ar1[i], 0.0) if i % 2 else ar1[i])
    sums[...] = total
    line = [remote(sums, ar2.at[r], ar_ss.at[8 + r], ar_rs.at[8 + r], dev) for r, dev in column]
    for cp in line:
        cp.start()
    rp.third(2)

    def down_own(i):
        part[rows(0, i)] = down(i, own0)

    loop(nt, down_own)
    send_r.wait_recv()

    def finish(i):
        r = rows(0, i, 128)
        v = result[r] + part[r] + r2[r].astype(f32) + vec[1:2]
        result[r] = jnp.where(valid((128, d_model), own0 + i * 128, length), v, 0.0)

    loop(half // 128, finish)
    store_r = pltpu.make_async_copy(result, result_hbm, loc.at[1])
    store_r.start()
    rf.final(UP)
    for cp in line:
        cp.wait()
    for r, _ in column:
        total = total + ar2[r]
    sums[...] = total
    for k in range(3):
        rp.final(k)

    for k in range(NK):
        g.drain(k)
    for k in range(2):
        rf.drain(k)
    for k in range(3):
        rp.drain(k)
    for cp in (send_x, send_b, send_dr, send_s, send_dh, send_f, send_r):
        cp.wait_send()
    store_t.wait()
    store_r.wait()


def block(lens, shard, tokens, ograd, vec, nz):
    half, d = tokens.shape
    seq = 2 * half
    nk, rows, ffq = shard.shape
    hw = d // 2
    pw = 256
    npair = hw // 128

    def V(shape, t=bf16):
        return pltpu.VMEM(shape, t)

    scratch = [
        V((half, d), f32), V((half, d), f32), V((half, d)), V((half, d)),
        V((2, nk, d, ffq)), V((d, 4 * hw)), V((hw, d)), V((seq, d)), V((seq, d)), V((seq, d)), V((d, seq)), V((d, seq)), V((d, seq)),
        V((seq, 3 * hw)), V((seq, hw)), V((2 * npair, 1, seq), f32), V((seq, 2 * ffq)), V((seq, 2 * ffq)), V((seq, hw)), V((d, hw)),
        V((half, d)), V((half, d)), V((half, d)), V((half, d)), V((half, d)), V((half, d)), V((half, d), f32),
        V((seq, 128), f32), V((seq, 128), f32), V((2, 8, d), f32), V((N_SUM, d), f32), V((8, N_SUM, d), f32), V((nz, N_SUM, d), f32),
        V((2, 2, d, ffq)), V((2, npair, d, pw)),
        V((2, 2, nz, rows // 2, ffq)), V((2, 2, nz, rows, ffq)), V((2, nz - 1, rows, ffq)),
        V((2, npair, nz, rows // 2, pw)), V((2, npair, nz, rows, pw)), V((npair, nz - 1, rows, pw)),
    ]
    dma = pltpu.SemaphoreType.DMA
    sems = [dma((5, nk, nz)), dma((5, nk, nz)), dma((5, 2, nz)), dma((5, 2, nz)), dma((5, npair, nz)), dma((5, npair, nz)), dma((9,)), dma((9,)), dma((8 + nz,)), dma((8 + nz,)), dma((2 + nk,))]
    vm = pl.BlockSpec(memory_space=pltpu.VMEM)
    anywhere = pl.BlockSpec(memory_space=pl.ANY)
    return pl.pallas_call(
        block_kernel,
        out_shape=(
            jax.ShapeDtypeStruct((half, d), f32),
            jax.ShapeDtypeStruct((half, d), f32),
            jax.ShapeDtypeStruct((2, rows, ffq), f32),
            jax.ShapeDtypeStruct((npair, rows, pw), f32),
            jax.ShapeDtypeStruct((N_SUM, d), f32),
        ),
        in_specs=[pl.BlockSpec(memory_space=pltpu.SMEM), anywhere, anywhere, anywhere, vm],
        out_specs=(anywhere, anywhere, vm, vm, vm),
        scratch_shapes=scratch + sems,
        compiler_params=pltpu.CompilerParams(collective_id=0, has_side_effects=True, vmem_limit_bytes=64 << 20),
    )(lens, shard, tokens, ograd, vec)


def per_device(tokens, lengths, w_qkv, b_qv, w_out, b_out, w_up, b_up, w_down, b_down, g_one, c_one, g_two, c_two, out_grad, *, nz, sub):
    y = lax.axis_index("y")
    d = tokens.shape[1]
    heads = w_qkv.shape[2] // HEAD_DIM
    first = y == 0

    def lanes(a):
        return a[..., :HEAD_DIM], a[..., HEAD_DIM:]

    def swap(a, b):
        return [jnp.where(first, a, b), jnp.where(first, b, a)]

    pieces = []
    bias = []
    w_out_t = w_out.T
    for h in range(heads):
        s = slice(h * HEAD_DIM, (h + 1) * HEAD_DIM)
        pieces += swap(w_qkv[0][:, s], w_qkv[2][:, s]) + swap(w_qkv[1][:, s], w_out_t[:, s])
        bias += swap(b_qv[0, s], b_qv[1, s]) + [jnp.zeros((2 * HEAD_DIM,), f32)]
    packed = jnp.stack([jnp.concatenate(pieces, axis=1), w_up, w_down.T])
    if sub > 1:
        packed = lax.all_gather(packed, "r", axis=1, tiled=True)
    vec = jnp.stack([b_out, b_down, g_one, c_one, g_two, c_two, b_up, jnp.concatenate(bias)])
    result, tokens_grad, outf, outp, sums = block(lengths, packed, tokens, out_grad, vec, nz)
    if sub > 1:
        outf, outp = [lax.psum_scatter(a, "r", scatter_dimension=1, tiled=True) for a in (outf, outp)]
        sums = lax.psum(sums, "r")
    qs, ks, vs, os_ = [], [], [], []
    for h in range(heads):
        a = lanes(outp[h][:, : 2 * HEAD_DIM])
        b = lanes(outp[h][:, 2 * HEAD_DIM :])
        q, v = swap(*a)
        k, o = swap(*b)
        qs.append(q), ks.append(k), vs.append(v), os_.append(o)
    qkv_grad = jnp.stack([jnp.concatenate(a, axis=1) for a in (qs, ks, vs)])
    out_grad_w = jnp.concatenate(os_, axis=1).T
    bq, bv = [sums[ROW_B_QV, i * d // 2 : (i + 1) * d // 2].reshape(heads, 2, HEAD_DIM) for i in (0, 1)]
    b_qv_grad = jnp.stack([jnp.where(first, bq[:, 0], bq[:, 1]).reshape(-1), jnp.where(first, bv[:, 1], bv[:, 0]).reshape(-1)])
    b_up_grad = jnp.where(first, sums[ROW_B_UP], sums[ROW_B_UP + 1])
    return (result, tokens_grad, qkv_grad, b_qv_grad, out_grad_w, sums[0], outf[0], b_up_grad, outf[1].T, sums[1], sums[2], sums[3], sums[4], sums[5])


def solution(mesh):
    dp, tensor = mesh.shape["dp"], mesh.shape["tensor"]
    line = 4 * NX
    nz, sub = line // NX, dp // line
    grid = Mesh(mesh.devices.reshape(line, sub, tensor // 2, 2), ("e", "r", "y", "c"))
    dpx, tx = ("e", "r"), ("y", "c")
    rows = P(dpx + tx, None)
    return jax.shard_map(
        functools.partial(per_device, nz=nz, sub=sub),
        mesh=grid,
        in_specs=(rows, P(dpx), P(None, dpx, tx), P(None, tx), P(tx, dpx), P(), P(dpx, tx), P(tx), P(tx, dpx), P(), P(), P(), P(), P(), rows),
        out_specs=(rows, rows, P(None, dpx, tx), P(None, tx), P(tx, dpx), P(), P(dpx, tx), P(tx), P(tx, dpx), P(), P(), P(), P(), P()),
        check_vma=False,
    )
```

```python
import functools
import math

import jax
import jax.numpy as jnp
from jax import lax
from jax.experimental import pallas as pl
from jax.experimental.pallas import tpu as pltpu
from jax.sharding import Mesh
from jax.sharding import PartitionSpec as P

HEAD_DIM = 64
EPSILON = 1e-05
MESH = pl.DeviceIdType.MESH
NX = 2
NK = 3

class Place:
    def __init__(self, nz):
        self.nz = nz
        self.e = lax.axis_index("e"); self.y = lax.axis_index("y")
        self.z = self.e // NX; self.x = self.e % NX
        self.xn = {"e": self.e + 1 - 2 * self.x}
        self.yn = {"y": 1 - self.y}
        self.up = {"e": self.e + NX}
        self.dn = {"e": self.e - NX}
        self.core = {"c": 1 - lax.axis_index("c")}

BQ = 256
NEG = -1e30
f32, bf16 = jnp.float32, jnp.bfloat16
def dot_nt(a, b): return lax.dot_general(a, b, (((1,), (1,)), ((), ())), preferred_element_type=f32)
def dot_nn(a, b): return lax.dot_general(a, b, (((1,), (0,)), ((), ())), preferred_element_type=f32)
def flip(a): return a.astype(f32).T.astype(bf16)

def pair_cols(p, group, width):
    return pl.ds(pl.multiple_of(group * width + p * 128, 128), 128)

def masked_keys(k, j, length):
    n = k.shape[0]
    lane = lax.broadcasted_iota(jnp.int32, (n, 128), 1)
    row = lax.broadcasted_iota(jnp.int32, (n, 128), 0)
    out = jnp.where((lane == 64 * (1 - j)) & (row >= length), NEG, 0.0)
    return jnp.where(lane // 64 == j, k.astype(f32), out).astype(bf16)

def with_one(q, j):
    lane = lax.broadcasted_iota(jnp.int32, q.shape, 1)
    return jnp.where(lane == 64 * (1 - j), 1.0, q.astype(f32)).astype(bf16)

def only(a, h):
    lane = lax.broadcasted_iota(jnp.int32, a.shape, 1)
    return jnp.where(lane // 64 == h, a.astype(f32), 0.0).astype(bf16)

def causal(s, i):
    n = s.shape[0] - BQ
    row = lax.broadcasted_iota(jnp.int32, (BQ, BQ), 0)
    col = lax.broadcasted_iota(jnp.int32, (BQ, BQ), 1)
    d = jnp.where(row <= col, s[n:], NEG)
    return d if n == 0 else jnp.concatenate([s[:n], d], axis=0)

def attn_fwd_pair(p, width, length, qkv, mixed, lse, hook):
    n = qkv.shape[0]
    k = qkv[:, pair_cols(p, 1, width)]
    vt = flip(qkv[:, pair_cols(p, 2, width)])
    kp = [masked_keys(k, j, length) for j in (0, 1)]
    for i in range(n // BQ):
        hi = (i + 1) * BQ
        q = qkv[i * BQ:hi, pair_cols(p, 0, width)]
        outs = []
        for j in (0, 1):
            s = causal(dot_nt(kp[j][:hi], with_one(q, j)), i)
            m = jnp.max(s, axis=0, keepdims=True)
            e = jnp.exp(s - m)
            l = jnp.sum(e, axis=0, keepdims=True)
            o = dot_nn(vt[64 * (1 - j):64 * (2 - j), :hi], e.astype(bf16))
            outs.append(o * (1.0 / l))
            lse[2 * p + j, :, i * BQ:hi] = m + jnp.log(l)
        mixed[i * BQ:hi, pair_cols(p, 0, width)] = jnp.concatenate(outs[::-1], axis=0).T.astype(bf16)
        hook(i)

def attn_bwd_pair(p, width, length, qkv, mixed, lse, dmixed, dk_acc, dv_acc, hook):
    n = qkv.shape[0]
    c0, c1, c2 = [pair_cols(p, g, width) for g in range(3)]
    k = qkv[:, c1]
    kt = flip(k)
    v = qkv[:, c2]
    kp = [masked_keys(k, j, length) for j in (0, 1)]
    dk_acc[...] = jnp.zeros_like(dk_acc); dv_acc[...] = jnp.zeros_like(dv_acc)
    for i in range(n // BQ):
        hi = (i + 1) * BQ
        q = qkv[i * BQ:hi, c0]
        do = dmixed[i * BQ:hi, c0]
        prod = (do.astype(f32) * mixed[i * BQ:hi, c0].astype(f32)).T
        dq = []
        for j in (0, 1):
            vh = 1 - j
            delta = jnp.sum(prod[64 * vh:64 * (vh + 1)], axis=0, keepdims=True)
            dom = only(do, vh)
            s = causal(dot_nt(kp[j][:hi], with_one(q, j)), i)
            w = jnp.exp(s - lse[2 * p + j, :, i * BQ:hi])
            dw = dot_nt(v[:hi], dom)
            ds = (w * (dw - delta)).astype(bf16)
            dv_acc[:hi] += dot_nn(w.astype(bf16), dom)
            dk_acc[:hi] += dot_nn(ds, only(q, j))
            dq.append(dot_nn(kt[64 * j:64 * (j + 1), :hi], ds))
        qkv[i * BQ:hi, c0] = (jnp.concatenate(dq, axis=0).T * 0.125).astype(bf16)
        hook(i)
    qkv[:, c1] = dk_acc[...].astype(bf16)
    qkv[:, c2] = dv_acc[...].astype(bf16)


class Pieces:
    def __init__(self, p, full, lo, width, ssem, rsem):
        self.p, self.full, self.lo, self.width, self.ssem, self.rsem = p, full, lo, width, ssem, rsem
        self.rows = full.shape[2] // (p.nz * NX)

    def piece(self, yq, k, e, half=None):
        n = self.rows if half is None else self.rows // 2
        at_row = e * self.rows + (half or 0) * n
        return self.full.at[yq, k, pl.ds(pl.multiple_of(at_row, 16), n), pl.ds(self.lo, self.width)]

    def z(self, r):
        return (self.p.z + r + self.p.nz) % self.p.nz

    def wire(self, s, t, dev, *sem):
        return remote(s, t, self.ssem.at[sem], self.rsem.at[sem], dev)


class Gather(Pieces):
    def __init__(self, p, own, *rest):
        super().__init__(p, *rest)
        self.own = own

    def mine(self, k):
        return self.own.at[k, :, pl.ds(self.lo, self.width)]

    def copy(self, kind, k, r):
        p = self.p
        back = self.z(-r)
        if kind == 0:
            s, t, dev = self.mine(k), self.piece(p.y, k, p.e), {"e": self.z(r) * NX + p.x}
        elif kind in (1, 2):
            t = self.piece(p.y, k, back * NX + p.x)
            s, dev = (t if r else self.mine(k)), (p.xn, p.yn)[kind - 1]
        elif kind == 3:
            s = t = self.piece(p.y, k, back * NX + 1 - p.x, 0)
            dev = p.yn
        else:
            s = t = self.piece(1 - p.y, k, back * NX + p.x, 1)
            dev = p.xn
        return self.wire(s, t, dev, kind, k, r)

    def got(self, kind, k, r):
        p = self.p
        back = self.z(-r) * NX
        yq = p.y if kind < 2 else 1 - p.y
        e = back + (p.x if kind in (0, 2) else 1 - p.x)
        ref = self.piece(yq, k, e, None if kind < 3 else kind - 3)
        self.wire(ref, ref, p.xn, kind, k, r).wait_recv()

    def own_z(self, k):
        nz = self.p.nz
        for r in [1, nz - 1] + list(range(2, nz - 1)):
            self.copy(0, k, r).start()

    def own_xy(self, k):
        self.copy(1, k, 0).start()
        self.copy(2, k, 0).start()

    def pass_on(self, k, r):
        self.got(0, k, r)
        self.copy(1, k, r).start()
        self.copy(2, k, r).start()

    def turn(self, k, r):
        self.got(1, k, r)
        self.copy(3, k, r).start()
        self.got(2, k, r)
        self.copy(4, k, r).start()

    def final(self, k):
        for r in range(self.p.nz):
            self.got(3, k, r)
            self.got(4, k, r)

    def drain(self, k):
        for r in range(self.p.nz):
            for kind in range(5):
                if kind or r:
                    self.copy(kind, k, r).wait_send()


class PlaneGather(Pieces):
    def __init__(self, p, own, k, *rest):
        super().__init__(p, *rest)
        self.own, self.k = own, k

    def spot(self, q, z):
        p = self.p
        return self.piece(1 - p.y if q >= 2 else p.y, self.k, z * NX + (1 - p.x if q % 2 else p.x))

    def mine(self):
        return self.own.at[self.k, :, pl.ds(self.lo, self.width)]

    def copy(self, q, r):
        p = self.p
        if r:
            t = self.spot(q, p.z)
            return self.wire(t if q else self.mine(), t, {"e": self.z(r) * NX + p.x}, q, r)
        if q == 3:
            t = self.spot(1, p.z)
            return self.wire(t, t, p.yn, q, 0)
        return self.wire(self.mine(), self.spot(0, p.z), (p.xn, p.yn)[q - 1], q, 0)

    def got(self, q, r):
        ref = self.spot(q, self.z(-r))
        self.wire(ref, ref, self.p.xn, q, r).wait_recv()

    def spread(self, q):
        if q:
            self.got(q, 0)
            if q == 1:
                self.copy(3, 0).start()
        else:
            self.copy(1, 0).start()
            self.copy(2, 0).start()
        for r in range(1, self.p.nz):
            self.copy(q, r).start()

    def final(self):
        for r in range(1, self.p.nz):
            for q in range(4):
                self.got(q, r)

    def drain(self):
        for q in range(4):
            for r in range(self.p.nz):
                if q or r:
                    self.copy(q, r).wait_send()


class Scatter(Pieces):
    def __init__(self, p, bd, bxy, bz, out, *rest):
        super().__init__(p, *rest)
        self.bd, self.bxy, self.bz, self.out = bd, bxy, bz, out

    def copy(self, kind, k, d):
        p, b = self.p, k if self.bd.shape[1] > 1 else 0
        if kind == 0:
            s, t, dev = self.piece(1 - p.y, k, d * NX + 1 - p.x, 0), self.bd.at[0, b, d], p.yn
        elif kind == 1:
            s, t, dev = self.piece(1 - p.y, k, d * NX + 1 - p.x, 1), self.bd.at[1, b, d], p.xn
        elif kind == 2:
            s, t, dev = self.piece(p.y, k, d * NX + 1 - p.x), self.bxy.at[0, b, d], p.xn
        elif kind == 3:
            s, t, dev = self.piece(1 - p.y, k, d * NX + p.x), self.bxy.at[1, b, d], p.yn
        else:
            e = self.z(d) * NX + p.x
            s, t, dev = self.piece(p.y, k, e), self.bz.at[b, d - 1], {"e": e}
        return self.wire(s, t, dev, kind, b, d)

    def first(self, k, d):
        self.copy(0, k, d).start()
        self.copy(1, k, d).start()

    def second(self, k, r):
        p, b, d = self.p, k if self.bd.shape[1] > 1 else 0, self.z(r)
        self.copy(0, k, d).wait_recv()
        ref = self.piece(p.y, k, d * NX + 1 - p.x, 0)
        ref[...] = (ref[...].astype(f32) + self.bd[0, b, d].astype(f32)).astype(bf16)
        self.copy(2, k, d).start()
        self.copy(1, k, d).wait_recv()
        ref = self.piece(1 - p.y, k, d * NX + p.x, 1)
        ref[...] = (ref[...].astype(f32) + self.bd[1, b, d].astype(f32)).astype(bf16)
        self.copy(3, k, d).start()

    def third(self, k, r):
        p, b, d = self.p, k if self.bd.shape[1] > 1 else 0, self.z(r)
        self.copy(2, k, d).wait_recv()
        self.copy(3, k, d).wait_recv()
        ref = self.piece(p.y, k, d * NX + p.x)
        total = ref[...].astype(f32) + self.bxy[0, b, d].astype(f32) + self.bxy[1, b, d].astype(f32)
        if r == 0:
            self.out[k, :, self.lo : self.lo + self.width] = total
        else:
            ref[...] = total.astype(bf16)
            self.copy(4, k, r).start()

    def final(self, k):
        b = k if self.bd.shape[1] > 1 else 0
        cols = slice(self.lo, self.lo + self.width)
        total = self.out[k, :, cols]
        for r in range(1, self.p.nz):
            self.copy(4, k, r).wait_recv()
            total = total + self.bz[b, r - 1].astype(f32)
        self.out[k, :, cols] = total

    def drain(self, k):
        for d in range(self.p.nz):
            for kind in (0, 1, 2, 3):
                self.copy(kind, k, d).wait_send()
            if d:
                self.copy(4, k, d).wait_send()


class PlaneScatter(Pieces):
    def __init__(self, p, k, bz, bq, out, *rest):
        super().__init__(p, *rest)
        self.k, self.bz, self.bq, self.out = k, bz, bq, out

    def spot(self, q, z):
        p = self.p
        return self.piece(1 - p.y if q >= 2 else p.y, self.k, z * NX + (1 - p.x if q % 2 else p.x))

    def copy(self, q, r):
        p = self.p
        if r:
            return self.wire(self.spot(q, self.z(r)), self.bz.at[r - 1, q], {"e": self.z(r) * NX + p.x}, q, r)
        return self.wire(self.spot(q, p.z), self.bq.at[q - 1], p.yn if q == 2 else p.xn, q, 0)

    def first(self):
        for r in range(1, self.p.nz):
            for q in (3, 2, 1, 0):
                self.copy(q, r).start()

    def plane_sum(self, q):
        for r in range(1, self.p.nz):
            self.copy(q, r).wait_recv()
        total = self.spot(q, self.p.z)[...].astype(f32)
        for r in range(1, self.p.nz):
            total = total + self.bz[r - 1, q].astype(f32)
        return total

    def second(self):
        for q in (3, 1):
            self.spot(q, self.p.z)[...] = self.plane_sum(q).astype(bf16)
            self.copy(q, 0).start()

    def third(self):
        total = self.plane_sum(2)
        self.copy(3, 0).wait_recv()
        self.spot(2, self.p.z)[...] = (total + self.bq[2].astype(f32)).astype(bf16)
        self.copy(2, 0).start()

    def final(self):
        total = self.plane_sum(0)
        for q in (1, 2):
            self.copy(q, 0).wait_recv()
            total = total + self.bq[q - 1].astype(f32)
        self.out[self.k, :, self.lo : self.lo + self.width] = total

    def drain(self):
        for q in range(4):
            for r in range(self.p.nz):
                if q or r:
                    self.copy(q, r).wait_send()


class Sums:
    def __init__(self, p, own, plane_buf, line_buf, out, peers, column, ssem, rsem):
        self.p, self.own, self.plane_buf, self.line_buf, self.out = p, own, plane_buf, line_buf, out
        self.peers, self.column, self.ssem, self.rsem = peers, column, ssem, rsem

    def tile(self, ref, t):
        return ref.at[pl.ds(8 * t, 8)]

    def plane_copy(self, t, i, dev):
        return remote(self.tile(self.own, t), self.plane_buf.at[t, i], self.ssem.at[t, i], self.rsem.at[t, i], dev)

    def line_copy(self, t, r, dev):
        return remote(self.tile(self.out, t), self.line_buf.at[t, r], self.ssem.at[t, 8 + r], self.rsem.at[t, 8 + r], dev)

    def plane(self, t):
        for i, dev in self.peers:
            self.plane_copy(t, i, dev).start()

    def line(self, t):
        row = lax.broadcasted_iota(jnp.int32, self.plane_buf.shape[2:], 0)
        lo, hi = SPLIT_ROWS[t]
        total = self.own[8 * t : 8 * t + 8]
        for i, dev in self.peers:
            self.plane_copy(t, i, dev).wait_recv()
            part = self.plane_buf[t, i]
            total = total + (jnp.where((row >= lo) & (row < hi), 0.0, part) if i % 2 else part)
        self.out[8 * t : 8 * t + 8] = total
        for r, dev in self.column:
            self.line_copy(t, r, dev).start()

    def done(self, t):
        total = self.out[8 * t : 8 * t + 8]
        for r, dev in self.column:
            self.line_copy(t, r, dev).wait()
            total = total + self.line_buf[t, r]
        self.out[8 * t : 8 * t + 8] = total

    def drain(self, t):
        for i, dev in self.peers:
            self.plane_copy(t, i, dev).wait_send()


def remote(src, dst, ssem, rsem, dev):
    return pltpu.make_async_remote_copy(src, dst, ssem, rsem, device_id=dev, device_id_type=MESH)


def loop(n, fn, after=()):
    def body(i, carry):
        fn(i)
        at(i, after)
        return carry

    lax.fori_loop(0, n, body, 0)


def at(i, steps):
    for j, todo in enumerate(steps):
        if todo:

            @pl.when(i == j)
            def _(todo=todo):
                for f in todo:
                    f()


def pick(a, b):
    lane = lax.broadcasted_iota(jnp.int32, a.shape, 1)
    return jnp.where(lane % 128 < 64, a.astype(f32), b.astype(f32))


def norm_parts(v):
    center = v - jnp.mean(v, axis=-1, keepdims=True)
    r = lax.rsqrt(jnp.mean(center * center, axis=-1, keepdims=True) + EPSILON)
    return center * r, r


def norm_back(n, r, d, gain):
    q = d * gain
    return r * (q - jnp.mean(q, axis=-1, keepdims=True) - n * jnp.mean(q * n, axis=-1, keepdims=True))


def gelu_both(u):
    a, b = math.sqrt(2.0 / math.pi), 0.044715
    u2 = u * u
    t = jnp.tanh(a * u * (1.0 + b * u2))
    h = 0.5 + 0.5 * t
    return u * h, h + (0.5 * a) * u * (1.0 - t * t) * (1.0 + (3.0 * b) * u2)


def valid(shape, base, length):
    return base + lax.broadcasted_iota(jnp.int32, shape, 0) < length


N_SUM = 16
ROW_B_OUT, ROW_B_DOWN, ROW_G_TWO, ROW_C_TWO, ROW_B_UP, ROW_G_ONE, ROW_C_ONE, ROW_B_QV = 0, 1, 2, 3, 4, 8, 9, 10
SPLIT_ROWS = ((4, 6), (2, 3))
PLANE_GATHER, PLANE_SCATTER = 256, 256
PLAN = {
    ("begin", 0): (("g", "own_z", 0), ("gp", "spread", 0)),
    ("norm_a", 1): (("g", "own_xy", 1), ("g", "own_z", 1)),
    ("norm_b", 0): (("g", "own_xy", 0), ("gp", "spread", 1)),
    ("norm_b", 1): (("gd", "own_z", 2),),
    ("mask_a", 2): (("gp", "spread", 2),),
    ("mask_b", 1): (("g", "turn", 1, 0),),
    ("wait_0", 0): (("g", "pass_on", 0, 3), ("g", "turn", 0, 0), ("gp", "spread", 3), ("g", "turn", 0, 3), ("g", "pass_on", 0, 2), ("g", "pass_on", 0, 1), ("g", "turn", 0, 2), ("g", "turn", 0, 1)),
    ("collect", 0): (("g", "pass_on", 1, 3),),
    ("project", 3): (("gd", "own_xy", 2),),
    ("attend", 1): (("g", "turn", 1, 3),),
    ("attend", 3): (("g", "pass_on", 1, 2), ("gd", "turn", 2, 0)),
    ("attend", 6): (("g", "pass_on", 1, 1),),
    ("attend", 9): (("g", "turn", 1, 2),),
    ("out_sib", 0): (("gd", "pass_on", 2, 3),),
    ("out_own", 0): (("g", "turn", 1, 1),),
    ("norm_two", 2): (("gd", "pass_on", 2, 2),),
    ("up_a", 0): (("gd", "pass_on", 2, 1), ("gd", "turn", 2, 3)),
    ("up_a", 1): (("gd", "turn", 2, 2),),
    ("up_b", 1): (("gd", "turn", 2, 1),),
    ("down_grad", 1): (("rd", "first", 1, 1),),
    ("down_grad", 2): (("rd", "first", 1, 2),),
    ("down_grad", 3): (("rq", "first"), ("rd", "first", 1, 3)),
    ("wait_2", 0): (("rd", "first", 1, 0),),
    ("pre_grad", 2): (("rd", "second", 1, 0), ("rd", "second", 1, 2), ("rd", "second", 1, 1)),
    ("second_sib", 1): (("rd", "second", 1, 3),),
    ("second_own", 0): (("rd", "third", 1, 0),),
    ("second_own", 1): (("rd", "third", 1, 2),),
    ("up_grad", 2): (("rd", "third", 1, 1),),
    ("back_two", 1): (("rd", "third", 1, 3),),
    ("mixed_grad", 0): (("ar", "plane", 0),),
    ("mixed_grad", 2): (("ru", "second", 0, 0), ("ru", "second", 0, 2), ("ru", "second", 0, 1), ("ru", "second", 0, 3)),
    ("attend_back", 1): (("ar", "line", 0),),
    ("attend_back", 2): (("rq", "second"),),
    ("attend_back", 3): (("ru", "third", 0, 0),),
    ("attend_back", 4): (("ru", "third", 0, 2),),
    ("attend_back", 7): (("ar", "done", 0), ("rd", "final", 1), ("ru", "third", 0, 1)),
    ("grads", 1): (("rq", "third"), ("ru", "third", 0, 3)),
    ("attend_back", 10): (("rp", "second", 0, 3), ("rp", "second", 0, 2)),
    ("attend_back", 11): (("rq", "final"), ("rp", "second", 0, 0), ("rp", "second", 1, 3), ("rp", "second", 1, 1), ("rp", "second", 1, 0), ("rp", "second", 0, 1), ("rp", "third", 0, 3), ("rp", "third", 0, 2)),
    ("grads", 2): (("rp", "third", 0, 0), ("ru", "final", 0)),
    ("first_own", 0): (("rp", "second", 1, 2), ("rp", "third", 1, 1), ("rp", "third", 1, 3)),
    ("first_own", 1): (("rp", "third", 1, 0),),
    ("back_one", 0): (("rp", "third", 0, 1),),
    ("back_one", 1): (("rp", "second", 2, 3), ("rp", "second", 2, 1), ("rp", "second", 2, 2), ("rp", "second", 2, 0)),
    ("back_one", 2): (("rp", "third", 1, 2),),
    ("back_one", 3): (("rp", "third", 2, 3), ("ar", "plane", 1), ("rp", "final", 0)),
    ("down_sib", 0): (("rp", "third", 2, 1),),
    ("down_own", 0): (("rp", "third", 2, 2), ("rp", "third", 2, 0), ("rp", "final", 1)),
    ("end", 0): (("ar", "line", 1), ("rp", "final", 2), ("ar", "done", 1)),
}


def block_kernel(
    lens, shard, tokens, ograd, vec,
    result_hbm, tgrad_hbm, outf, outp, sums,
    result, tgrad, tok, og, w, wc, wo, x_all, sec, dr, t1, t2, ft, qkv, mixed, lse, act, gp, dmx, go,
    r1, r2, r3, r4, s1, s2, part, dk_acc, dv_acc, bias, sm, ar1, ar2,
    grf, grp, dd, dxy, dz, ud, uxy, uz, pd, pxy, pz, qz, qq,
    g_ss, g_rs, h_ss, h_rs, q_ss, q_rs, d_ss, d_rs, u_ss, u_rs, v_ss, v_rs, p_ss, p_rs, sib_ss, sib_rs, ar_ss, ar_rs, loc,
):
    nz = g_ss.shape[2]
    p = Place(nz)
    c = lax.axis_index("c")
    half, d_model = tokens.shape
    seq = 2 * half
    hw = mixed.shape[1]
    TR = 256
    nt = half // TR
    length = lens[p.y]
    own0, sib0 = c * half, (1 - c) * half

    def rows(base, i, n=TR):
        return pl.ds(pl.multiple_of(base + i * n, n), n)

    load_t = pltpu.make_async_copy(tokens, tok, loc.at[0])
    load_g = pltpu.make_async_copy(ograd, og, loc.at[1])
    load_t.start()
    load_g.start()
    peers = []
    for dx in (0, 1):
        for dy in (0, 1):
            for dc in (0, 1):
                if dx + dy + dc:
                    peers.append((4 * dx + 2 * dy + dc, {"e": p.e + dx * (1 - 2 * p.x), "y": p.y + dy * (1 - 2 * p.y), "c": c + dc * (1 - 2 * c)}))
    column = [(r, {"e": ((p.z + r) % nz) * NX + p.x}) for r in range(1, nz)]
    bar = pltpu.get_barrier_semaphore()
    for _, dev in peers + column:
        pl.semaphore_signal(bar, 1, device_id=dev, device_id_type=MESH)
    pl.semaphore_wait(bar, len(peers) + len(column))

    def sib(i, src, dst):
        return remote(src, dst, sib_ss.at[i], sib_rs.at[i], p.core)

    DOWN, UP = 1, 0
    ffq = w.shape[3]
    gcut, rcut = ffq - PLANE_GATHER, ffq - PLANE_SCATTER
    g = Gather(p, shard, w, 0, ffq, g_ss, g_rs)
    gd = Gather(p, shard, w, 0, gcut, h_ss, h_rs)
    gp2 = PlaneGather(p, shard, 2, w, gcut, ffq - gcut, q_ss, q_rs)
    ru = Scatter(p, ud, uxy, uz, outf, grf, 0, ffq, u_ss, u_rs)
    rd = Scatter(p, dd, dxy, dz, outf, grf, 0, rcut, d_ss, d_rs)
    rq = PlaneScatter(p, DOWN, qz, qq, outf, grf, rcut, ffq - rcut, v_ss, v_rs)
    rp = Scatter(p, pd, pxy, pz, outp, grp, 0, grp.shape[3], p_ss, p_rs)
    ar = Sums(p, sm, ar1, ar2, sums, peers, column, ar_ss, ar_rs)
    parts = {"g": g, "gd": gd, "gp": gp2, "rd": rd, "rq": rq, "ru": ru, "rp": rp, "ar": ar}

    def steps(name, i=0):
        return [lambda t=t: getattr(parts[t[0]], t[1])(*t[2:]) for t in PLAN.get((name, i), ())]

    def mark(name):
        for f in steps(name):
            f()

    def tiled(name, n, fn):
        loop(n, fn, [steps(name, i) for i in range(n)])

    x_own, x_sib = x_all.at[rows(own0, 0, half)], x_all.at[rows(sib0, 0, half)]
    mark("begin")
    send_x = sib(0, tokens, x_own)
    send_x.start()
    send_dr = sib(1, ograd, dr.at[rows(own0, 0, half)])
    send_dr.start()
    send_b = remote(vec.at[pl.ds(0, 8)], bias.at[p.y], sib_ss.at[8], sib_rs.at[8], p.yn)
    send_b.start()
    keep = [pltpu.make_async_copy(shard.at[k], w.at[p.y, k, pl.ds(pl.multiple_of(p.e * shard.shape[1], 16), shard.shape[1])], loc.at[2 + k]) for k in range(NK)]
    for cp in keep:
        cp.start()
    bias[p.y] = vec[0:8]
    sm[...] = jnp.zeros_like(sm)

    def norm_one(name, base, src, lo):
        def one(i):
            v = src[rows(lo, i, 128)].astype(f32)
            n, _ = norm_parts(v)
            f = n * vec[2:3] + vec[3:4]
            sec[rows(base, i, 128)] = f.astype(bf16)
            ft[:, rows(base, i, 128)] = f.astype(bf16).astype(f32).T.astype(bf16)

        tiled(name, half // 128, one)

    def mask_rows(name, base, src, lo):
        def one(i):
            v = jnp.where(valid((128, d_model), base + i * 128, length), src[rows(lo, i, 128)].astype(f32), 0.0)
            dr[rows(base, i, 128)] = v.astype(bf16)
            t1[:, rows(base, i, 128)] = v.T.astype(bf16)

        tiled(name, half // 128, one)

    load_t.wait()
    norm_one("norm_a", own0, tok, 0)
    send_x.wait_recv()
    norm_one("norm_b", sib0, x_all, sib0)
    load_g.wait()
    mask_rows("mask_a", own0, og, 0)
    send_dr.wait_recv()
    mask_rows("mask_b", sib0, dr, sib0)
    for cp in keep:
        cp.wait()
    mark("wait_0")
    g.final(0)

    def collect(i):
        r = rows(0, i)
        for q in range(hw // 128):
            a = [w[yq, 0, r, q * 256 : q * 256 + 128] for yq in (0, 1)]
            b = [w[yq, 0, r, q * 256 + 128 : q * 256 + 256] for yq in (0, 1)]
            for group, v in enumerate((pick(a[0], a[1]), pick(b[0], b[1]), pick(a[1], a[0]), pick(b[1], b[0]))):
                wc[r, group * hw + q * 128 : group * hw + q * 128 + 128] = v.astype(bf16)
                if group == 3:
                    wo[q * 128 : q * 128 + 128, r] = v.T.astype(bf16)

    tiled("collect", d_model // TR, collect)
    send_b.wait_recv()
    ba, bb = bias[0, 7:8], bias[1, 7:8]
    bq = jnp.concatenate([pick(ba[:, q * 256 : q * 256 + 128], bb[:, q * 256 : q * 256 + 128]) for q in range(hw // 128)], axis=1)
    bv = jnp.concatenate([pick(bb[:, q * 256 : q * 256 + 128], ba[:, q * 256 : q * 256 + 128]) for q in range(hw // 128)], axis=1)

    def project(i):
        h = sec[rows(0, i)]
        qkv[rows(0, i), 0:hw] = ((dot_nn(h, wc[:, 0:hw]) + bq).astype(bf16).astype(f32) * 0.125).astype(bf16)
        qkv[rows(0, i), hw : 2 * hw] = dot_nn(h, wc[:, hw : 2 * hw]).astype(bf16)
        qkv[rows(0, i), 2 * hw : 3 * hw] = (dot_nn(h, wc[:, 2 * hw : 3 * hw]) + bv).astype(bf16)

    tiled("project", seq // TR, project)
    pairs, blocks = hw // 128, seq // BQ

    def attend(i):
        attn_fwd_pair(i, hw, length, qkv, mixed, lse, lambda b: at(i, [steps("attend", j * blocks + b) for j in range(pairs)]))

    loop(pairs, attend)

    def out_sib(i):
        s1[rows(0, i)] = dot_nn(mixed[rows(sib0, i)], wo[...]).astype(bf16)

    tiled("out_sib", nt, out_sib)
    send_h = sib(2, s1, r1)
    send_h.start()

    def out_own(i):
        result[rows(0, i)] = tok[rows(0, i)].astype(f32) + dot_nn(mixed[rows(own0, i)], wo[...]) + vec[0:1]

    tiled("out_own", nt, out_own)
    send_h.wait_recv()

    def norm_two(i):
        h = result[rows(0, i, 128)] + r1[rows(0, i, 128)].astype(f32)
        result[rows(0, i, 128)] = h
        n, _ = norm_parts(h)
        sec[rows(own0, i, 128)] = (n * vec[4:5] + vec[5:6]).astype(bf16)

    tiled("norm_two", half // 128, norm_two)
    send_s = sib(3, sec.at[rows(own0, 0, half)], sec.at[rows(own0, 0, half)])
    send_s.start()
    mark("wait_1")
    g.final(1)

    def up(name, base):
        def one(i):
            r = rows(base, i)
            h = sec[r]
            t2[:, r] = h.astype(f32).T.astype(bf16)
            for yq in (0, 1):
                u = dot_nn(h, w[yq, 1]) + bias[yq, 6:7]
                a, s = gelu_both(u)
                act[r, yq * ffq : (yq + 1) * ffq] = a.astype(bf16)
                gp[r, yq * ffq : (yq + 1) * ffq] = s.astype(bf16)

        tiled(name, nt, one)

    up("up_a", own0)
    send_s.wait_recv()
    up("up_b", sib0)
    ZR = d_model // nz

    def down_grad(i):
        r = rows(0, i, ZR)
        for yq in (0, 1):
            grf[yq, DOWN, r] = dot_nn(t1[r], act[:, yq * ffq : (yq + 1) * ffq]).astype(bf16)

    tiled("down_grad", nz, down_grad)
    mark("wait_2")
    gd.final(2)
    gp2.final()

    def pre_grad(i):
        r = rows(0, i)
        for yq in (0, 1):
            cols = slice(yq * ffq, (yq + 1) * ffq)
            v = (dot_nn(dr[r], w[yq, 2]) * gp[r, cols].astype(f32)).astype(bf16)
            gp[r, cols] = v
            sm[ROW_B_UP + yq : ROW_B_UP + yq + 1] += jnp.sum(v.astype(f32), axis=0, keepdims=True)

    tiled("pre_grad", seq // TR, pre_grad)

    def up_back(i, base):
        return dot_nt(gp[rows(base, i), 0:ffq], w[0, 1]) + dot_nt(gp[rows(base, i), ffq : 2 * ffq], w[1, 1])

    send_h.wait_send()

    def second_sib(i):
        s1[rows(0, i)] = up_back(i, sib0).astype(bf16)

    tiled("second_sib", nt, second_sib)
    send_d = sib(4, s1, r3)
    send_d.start()

    def second_own(i):
        part[rows(0, i)] = up_back(i, own0)

    tiled("second_own", nt, second_own)

    def up_grad(i):
        r = rows(0, i, ZR)
        for yq in (0, 1):
            grf[yq, UP, r] = dot_nn(t2[r], gp[:, yq * ffq : (yq + 1) * ffq]).astype(bf16)
        ru.first(UP, i)

    tiled("up_grad", nz, up_grad)
    send_d.wait_recv()

    def back_two(i):
        r = rows(0, i, 128)
        n, rr = norm_parts(result[r])
        ds = part[r] + r3[r].astype(f32)
        dres = jnp.where(valid((128, d_model), own0 + i * 128, length), og[r].astype(f32), 0.0)
        dh = dres + norm_back(n, rr, ds, vec[4:5])
        tgrad[r] = dh
        x_all[rows(own0, i, 128)] = dh.astype(bf16)
        for row, v in ((ROW_B_OUT, dh), (ROW_B_DOWN, dres), (ROW_G_TWO, ds * n), (ROW_C_TWO, ds)):
            sm[row : row + 1] += jnp.sum(v, axis=0, keepdims=True)

    tiled("back_two", half // 128, back_two)
    send_dh = sib(5, x_own, x_own)
    send_dh.start()
    send_dh.wait_recv()

    def mixed_grad(i):
        r = rows(0, i)
        h = x_all[r]
        t1[:, r] = h.astype(f32).T.astype(bf16)
        dmx[r] = dot_nn(h, wc[:, 3 * hw : 4 * hw]).astype(bf16)

    tiled("mixed_grad", seq // TR, mixed_grad)

    def out_grad_w(i):
        go[rows(0, i)] = dot_nn(t1[rows(0, i)], mixed[...]).astype(bf16)

    tiled("out_grad_w", d_model // TR, out_grad_w)

    def attend_back(i):
        attn_bwd_pair(
            i, hw, length, qkv, mixed, lse, dmx, dk_acc, dv_acc, lambda b: at(i, [steps("attend_back", j * blocks + b) for j in range(pairs)])
        )
        cq, ck, cv = [pair_cols(i, group, hw) for group in range(3)]

        def grads(t):
            r = rows(0, t, ZR)
            gq, gk, gv = [dot_nn(ft[r], qkv[:, cc]) for cc in (cq, ck, cv)]
            o = go[r, cq].astype(f32)
            grp[0, i, r, 0:128] = pick(gq, gv).astype(bf16)
            grp[0, i, r, 128:256] = pick(gk, o).astype(bf16)
            grp[1, i, r, 0:128] = pick(gv, gq).astype(bf16)
            grp[1, i, r, 128:256] = pick(o, gk).astype(bf16)
            rp.first(i, t)

        loop(nz, grads)
        at(i, [steps("grads", j) for j in range(pairs)])
        for cc, lo in ((cq, 0), (cv, hw)):
            to = pl.ds(pl.multiple_of(lo + i * 128, 128), 128)
            sm[ROW_B_QV : ROW_B_QV + 1, to] = jnp.sum(qkv[:, cc].astype(f32), axis=0, keepdims=True)

    loop(pairs, attend_back)

    def first_back(i, base):
        return dot_nt(qkv[rows(base, i)], wc[:, 0 : 3 * hw])

    def first_sib(i):
        s2[rows(0, i)] = first_back(i, sib0).astype(bf16)

    tiled("first_sib", nt, first_sib)
    send_f = sib(6, s2, r4)
    send_f.start()

    def first_own(i):
        part[rows(0, i)] = first_back(i, own0)

    tiled("first_own", nt, first_own)
    send_f.wait_recv()

    def back_one(i):
        r = rows(0, i, 128)
        n, rr = norm_parts(tok[r].astype(f32))
        df = part[r] + r4[r].astype(f32)
        tgrad[r] = tgrad[r] + norm_back(n, rr, df, vec[2:3])
        for row, v in ((ROW_G_ONE, df * n), (ROW_C_ONE, df)):
            sm[row : row + 1] += jnp.sum(v, axis=0, keepdims=True)

    tiled("back_one", half // 128, back_one)
    store_t = pltpu.make_async_copy(tgrad, tgrad_hbm, loc.at[0])
    store_t.start()

    def down(i, base):
        return dot_nt(act[rows(base, i), 0:ffq], w[0, 2]) + dot_nt(act[rows(base, i), ffq : 2 * ffq], w[1, 2])

    send_d.wait_send()

    def down_sib(i):
        s1[rows(0, i)] = down(i, sib0).astype(bf16)

    tiled("down_sib", nt, down_sib)
    send_r = sib(7, s1, r2)
    send_r.start()
    def down_own(i):
        part[rows(0, i)] = down(i, own0)

    tiled("down_own", nt, down_own)
    send_r.wait_recv()

    def finish(i):
        r = rows(0, i, 128)
        v = result[r] + part[r] + r2[r].astype(f32) + vec[1:2]
        result[r] = jnp.where(valid((128, d_model), own0 + i * 128, length), v, 0.0)

    tiled("finish", half // 128, finish)
    store_r = pltpu.make_async_copy(result, result_hbm, loc.at[1])
    store_r.start()
    mark("end")

    for k in range(2):
        g.drain(k)
    gd.drain(2)
    gp2.drain()
    ar.drain(0)
    ar.drain(1)
    rd.drain(DOWN)
    rq.drain()
    ru.drain(UP)
    for k in range(3):
        rp.drain(k)
    for cp in (send_x, send_b, send_dr, send_s, send_dh, send_f, send_r):
        cp.wait_send()
    store_t.wait()
    store_r.wait()


def block(lens, shard, tokens, ograd, vec, nz):
    half, d = tokens.shape
    seq = 2 * half
    nk, rows, ffq = shard.shape
    hw = d // 2
    pw = 256
    npair = hw // 128

    def V(shape, t=bf16):
        return pltpu.VMEM(shape, t)

    scratch = [
        V((half, d), f32), V((half, d), f32), V((half, d)), V((half, d)),
        V((2, nk, d, ffq)), V((d, 4 * hw)), V((hw, d)), V((seq, d)), V((seq, d)), V((seq, d)), V((d, seq)), V((d, seq)), V((d, seq)),
        V((seq, 3 * hw)), V((seq, hw)), V((2 * npair, 1, seq), f32), V((seq, 2 * ffq)), V((seq, 2 * ffq)), V((seq, hw)), V((d, hw)),
        V((half, d)), V((half, d)), V((half, d)), V((half, d)), V((half, d)), V((half, d)), V((half, d), f32),
        V((seq, 128), f32), V((seq, 128), f32), V((2, 8, d), f32), V((N_SUM, d), f32), V((2, 8, 8, d), f32), V((2, nz, 8, d), f32),
        V((2, 2, d, ffq)), V((2, npair, d, pw)),
        V((2, 1, nz, rows // 2, ffq - PLANE_SCATTER)), V((2, 1, nz, rows, ffq - PLANE_SCATTER)), V((1, nz - 1, rows, ffq - PLANE_SCATTER)),
        V((2, 1, nz, rows // 2, ffq)), V((2, 1, nz, rows, ffq)), V((1, nz - 1, rows, ffq)),
        V((2, npair, nz, rows // 2, pw)), V((2, npair, nz, rows, pw)), V((npair, nz - 1, rows, pw)),
        V((nz - 1, 4, rows, PLANE_SCATTER)), V((3, rows, PLANE_SCATTER)),
    ]
    dma = pltpu.SemaphoreType.DMA
    sems = [dma((5, nk, nz))] * 4 + [dma((4, nz))] * 2 + [dma((5, 1, nz))] * 4 + [dma((4, nz))] * 2 + [dma((5, npair, nz))] * 2
    sems += [dma((9,)), dma((9,)), dma((2, 8 + nz)), dma((2, 8 + nz)), dma((2 + nk,))]
    vm = pl.BlockSpec(memory_space=pltpu.VMEM)
    anywhere = pl.BlockSpec(memory_space=pl.ANY)
    return pl.pallas_call(
        block_kernel,
        out_shape=(
            jax.ShapeDtypeStruct((half, d), f32),
            jax.ShapeDtypeStruct((half, d), f32),
            jax.ShapeDtypeStruct((2, rows, ffq), f32),
            jax.ShapeDtypeStruct((npair, rows, pw), f32),
            jax.ShapeDtypeStruct((N_SUM, d), f32),
        ),
        in_specs=[pl.BlockSpec(memory_space=pltpu.SMEM), anywhere, anywhere, anywhere, vm],
        out_specs=(anywhere, anywhere, vm, vm, vm),
        scratch_shapes=scratch + sems,
        compiler_params=pltpu.CompilerParams(collective_id=0, has_side_effects=True, vmem_limit_bytes=64 << 20),
    )(lens, shard, tokens, ograd, vec)


def per_device(tokens, lengths, w_qkv, b_qv, w_out, b_out, w_up, b_up, w_down, b_down, g_one, c_one, g_two, c_two, out_grad, *, nz, sub):
    y = lax.axis_index("y")
    d = tokens.shape[1]
    heads = w_qkv.shape[2] // HEAD_DIM
    first = y == 0

    def lanes(a):
        return a[..., :HEAD_DIM], a[..., HEAD_DIM:]

    def swap(a, b):
        return [jnp.where(first, a, b), jnp.where(first, b, a)]

    pieces = []
    bias = []
    w_out_t = w_out.T
    for h in range(heads):
        s = slice(h * HEAD_DIM, (h + 1) * HEAD_DIM)
        pieces += swap(w_qkv[0][:, s], w_qkv[2][:, s]) + swap(w_qkv[1][:, s], w_out_t[:, s])
        bias += swap(b_qv[0, s], b_qv[1, s]) + [jnp.zeros((2 * HEAD_DIM,), f32)]
    packed = jnp.stack([jnp.concatenate(pieces, axis=1), w_up, w_down.T])
    if sub > 1:
        packed = lax.all_gather(packed, "r", axis=1, tiled=True)
    vec = jnp.stack([b_out, b_down, g_one, c_one, g_two, c_two, b_up, jnp.concatenate(bias)])
    result, tokens_grad, outf, outp, sums = block(lengths, packed, tokens, out_grad, vec, nz)
    if sub > 1:
        outf, outp = [lax.psum_scatter(a, "r", scatter_dimension=1, tiled=True) for a in (outf, outp)]
        sums = lax.psum(sums, "r")
    qs, ks, vs, os_ = [], [], [], []
    for h in range(heads):
        a = lanes(outp[h][:, : 2 * HEAD_DIM])
        b = lanes(outp[h][:, 2 * HEAD_DIM :])
        q, v = swap(*a)
        k, o = swap(*b)
        qs.append(q), ks.append(k), vs.append(v), os_.append(o)
    qkv_grad = jnp.stack([jnp.concatenate(a, axis=1) for a in (qs, ks, vs)])
    out_grad_w = jnp.concatenate(os_, axis=1).T
    bq, bv = [sums[ROW_B_QV, i * d // 2 : (i + 1) * d // 2].reshape(heads, 2, HEAD_DIM) for i in (0, 1)]
    b_qv_grad = jnp.stack([jnp.where(first, bq[:, 0], bq[:, 1]).reshape(-1), jnp.where(first, bv[:, 1], bv[:, 0]).reshape(-1)])
    b_up_grad = jnp.where(first, sums[ROW_B_UP], sums[ROW_B_UP + 1])
    return (result, tokens_grad, qkv_grad, b_qv_grad, out_grad_w, sums[ROW_B_OUT], outf[0], b_up_grad, outf[1].T, sums[ROW_B_DOWN], sums[ROW_G_ONE], sums[ROW_C_ONE], sums[ROW_G_TWO], sums[ROW_C_TWO])


def solution(mesh):
    dp, tensor = mesh.shape["dp"], mesh.shape["tensor"]
    line = 4 * NX
    nz, sub = line // NX, dp // line
    grid = Mesh(mesh.devices.reshape(line, sub, tensor // 2, 2), ("e", "r", "y", "c"))
    dpx, tx = ("e", "r"), ("y", "c")
    rows = P(dpx + tx, None)
    return jax.shard_map(
        functools.partial(per_device, nz=nz, sub=sub),
        mesh=grid,
        in_specs=(rows, P(dpx), P(None, dpx, tx), P(None, tx), P(tx, dpx), P(), P(dpx, tx), P(tx), P(tx, dpx), P(), P(), P(), P(), P(), rows),
        out_specs=(rows, rows, P(None, dpx, tx), P(None, tx), P(tx, dpx), P(), P(dpx, tx), P(tx), P(tx, dpx), P(), P(), P(), P(), P()),
        check_vma=False,
    )
```

```python
import functools
import math

import jax
import jax.numpy as jnp
from jax import lax
from jax.experimental import pallas as pl
from jax.experimental.pallas import tpu as pltpu
from jax.sharding import Mesh
from jax.sharding import PartitionSpec as P

HEAD_DIM = 64
EPSILON = 1e-05
MESH = pl.DeviceIdType.MESH
NX = 2
NK = 3

class Place:
    def __init__(self, nz):
        self.nz = nz
        self.e = lax.axis_index("e"); self.y = lax.axis_index("y")
        self.z = self.e // NX; self.x = self.e % NX
        self.xn = {"e": self.e + 1 - 2 * self.x}
        self.yn = {"y": 1 - self.y}
        self.up = {"e": self.e + NX}
        self.dn = {"e": self.e - NX}
        self.core = {"c": 1 - lax.axis_index("c")}

BQ = 256
NEG = -1e30
f32, bf16 = jnp.float32, jnp.bfloat16
def dot_nt(a, b): return lax.dot_general(a, b, (((1,), (1,)), ((), ())), preferred_element_type=f32)
def dot_nn(a, b): return lax.dot_general(a, b, (((1,), (0,)), ((), ())), preferred_element_type=f32)
def flip(a): return a.astype(f32).T.astype(bf16)

def pair_cols(p, group, width):
    return pl.ds(pl.multiple_of(group * width + p * 128, 128), 128)

def masked_keys(k, j, length):
    n = k.shape[0]
    lane = lax.broadcasted_iota(jnp.int32, (n, 128), 1)
    row = lax.broadcasted_iota(jnp.int32, (n, 128), 0)
    out = jnp.where((lane == 64 * (1 - j)) & (row >= length), NEG, 0.0)
    return jnp.where(lane // 64 == j, k.astype(f32), out).astype(bf16)

def with_one(q, j):
    lane = lax.broadcasted_iota(jnp.int32, q.shape, 1)
    return jnp.where(lane == 64 * (1 - j), 1.0, q.astype(f32)).astype(bf16)

def only(a, h):
    lane = lax.broadcasted_iota(jnp.int32, a.shape, 1)
    return jnp.where(lane // 64 == h, a.astype(f32), 0.0).astype(bf16)

def causal(s, i):
    n = s.shape[0] - BQ
    row = lax.broadcasted_iota(jnp.int32, (BQ, BQ), 0)
    col = lax.broadcasted_iota(jnp.int32, (BQ, BQ), 1)
    d = jnp.where(row <= col, s[n:], NEG)
    return d if n == 0 else jnp.concatenate([s[:n], d], axis=0)

def attn_fwd_pair(p, width, length, qkv, mixed, lse, hook):
    n = qkv.shape[0]
    k = qkv[:, pair_cols(p, 1, width)]
    vt = flip(qkv[:, pair_cols(p, 2, width)])
    kp = [masked_keys(k, j, length) for j in (0, 1)]
    for i in range(n // BQ):
        hi = (i + 1) * BQ
        q = qkv[i * BQ:hi, pair_cols(p, 0, width)]
        outs = []
        for j in (0, 1):
            s = causal(dot_nt(kp[j][:hi], with_one(q, j)), i)
            m = jnp.max(s, axis=0, keepdims=True)
            e = jnp.exp(s - m)
            l = jnp.sum(e, axis=0, keepdims=True)
            o = dot_nn(vt[64 * (1 - j):64 * (2 - j), :hi], e.astype(bf16))
            outs.append(o * (1.0 / l))
            lse[2 * p + j, :, i * BQ:hi] = m + jnp.log(l)
        mixed[i * BQ:hi, pair_cols(p, 0, width)] = jnp.concatenate(outs[::-1], axis=0).T.astype(bf16)
        hook(i)

def attn_bwd_pair(p, width, length, qkv, mixed, lse, dmixed, dk_acc, dv_acc, hook):
    n = qkv.shape[0]
    c0, c1, c2 = [pair_cols(p, g, width) for g in range(3)]
    k = qkv[:, c1]
    kt = flip(k)
    v = qkv[:, c2]
    kp = [masked_keys(k, j, length) for j in (0, 1)]
    dk_acc[...] = jnp.zeros_like(dk_acc); dv_acc[...] = jnp.zeros_like(dv_acc)
    for i in range(n // BQ):
        hi = (i + 1) * BQ
        q = qkv[i * BQ:hi, c0]
        do = dmixed[i * BQ:hi, c0]
        prod = (do.astype(f32) * mixed[i * BQ:hi, c0].astype(f32)).T
        dq = []
        for j in (0, 1):
            vh = 1 - j
            delta = jnp.sum(prod[64 * vh:64 * (vh + 1)], axis=0, keepdims=True)
            dom = only(do, vh)
            s = causal(dot_nt(kp[j][:hi], with_one(q, j)), i)
            w = jnp.exp(s - lse[2 * p + j, :, i * BQ:hi])
            dw = dot_nt(v[:hi], dom)
            ds = (w * (dw - delta)).astype(bf16)
            dv_acc[:hi] += dot_nn(w.astype(bf16), dom)
            dk_acc[:hi] += dot_nn(ds, only(q, j))
            dq.append(dot_nn(kt[64 * j:64 * (j + 1), :hi], ds))
        qkv[i * BQ:hi, c0] = (jnp.concatenate(dq, axis=0).T * 0.125).astype(bf16)
        hook(i)
    qkv[:, c1] = dk_acc[...].astype(bf16)
    qkv[:, c2] = dv_acc[...].astype(bf16)


class Pieces:
    def __init__(self, p, full, lo, width, ssem, rsem):
        self.p, self.full, self.lo, self.width, self.ssem, self.rsem = p, full, lo, width, ssem, rsem
        self.rows = full.shape[2] // (p.nz * NX)

    def piece(self, yq, k, e, half=None):
        n = self.rows if half is None else self.rows // 2
        at_row = e * self.rows + (half or 0) * n
        return self.full.at[yq, k, pl.ds(pl.multiple_of(at_row, 16), n), pl.ds(self.lo, self.width)]

    def z(self, r):
        return (self.p.z + r + self.p.nz) % self.p.nz

    def home(self, k):
        return self.out[k] if isinstance(self.out, tuple) else self.out.at[k]

    def wire(self, s, t, dev, *sem):
        return remote(s, t, self.ssem.at[sem], self.rsem.at[sem], dev)


class Gather(Pieces):
    def __init__(self, p, own, *rest):
        super().__init__(p, *rest)
        self.own = own

    def mine(self, k):
        return self.own[k].at[:, pl.ds(self.lo, self.width)]

    def copy(self, kind, k, r):
        p = self.p
        back = self.z(-r)
        if kind == 0:
            s, t, dev = self.mine(k), self.piece(p.y, k, p.e), {"e": self.z(r) * NX + p.x}
        elif kind in (1, 2):
            t = self.piece(p.y, k, back * NX + p.x)
            s, dev = (t if r else self.mine(k)), (p.xn, p.yn)[kind - 1]
        elif kind == 3:
            s = t = self.piece(p.y, k, back * NX + 1 - p.x, 0)
            dev = p.yn
        else:
            s = t = self.piece(1 - p.y, k, back * NX + p.x, 1)
            dev = p.xn
        return self.wire(s, t, dev, kind, k, r)

    def got(self, kind, k, r):
        p = self.p
        back = self.z(-r) * NX
        yq = p.y if kind < 2 else 1 - p.y
        e = back + (p.x if kind in (0, 2) else 1 - p.x)
        ref = self.piece(yq, k, e, None if kind < 3 else kind - 3)
        self.wire(ref, ref, p.xn, kind, k, r).wait_recv()

    def own_z(self, k):
        nz = self.p.nz
        for r in [1, nz - 1] + list(range(2, nz - 1)):
            self.copy(0, k, r).start()

    def own_xy(self, k):
        self.copy(1, k, 0).start()
        self.copy(2, k, 0).start()

    def pass_on(self, k, r):
        self.got(0, k, r)
        self.copy(1, k, r).start()
        self.copy(2, k, r).start()

    def turn(self, k, r):
        self.got(1, k, r)
        self.copy(3, k, r).start()
        self.got(2, k, r)
        self.copy(4, k, r).start()

    def final(self, k):
        for r in range(self.p.nz):
            self.got(3, k, r)
            self.got(4, k, r)

    def drain(self, k):
        for r in range(self.p.nz):
            for kind in range(5):
                if kind or r:
                    self.copy(kind, k, r).wait_send()


class PlaneGather(Pieces):
    def __init__(self, p, own, k, *rest):
        super().__init__(p, *rest)
        self.own, self.k = own, k

    def spot(self, q, z):
        p = self.p
        return self.piece(1 - p.y if q >= 2 else p.y, self.k, z * NX + (1 - p.x if q % 2 else p.x))

    def mine(self):
        return self.own[self.k].at[:, pl.ds(self.lo, self.width)]

    def copy(self, q, r):
        p = self.p
        if r:
            t = self.spot(q, p.z)
            return self.wire(t if q else self.mine(), t, {"e": self.z(r) * NX + p.x}, q, r)
        if q == 3:
            t = self.spot(1, p.z)
            return self.wire(t, t, p.yn, q, 0)
        return self.wire(self.mine(), self.spot(0, p.z), (p.xn, p.yn)[q - 1], q, 0)

    def got(self, q, r):
        ref = self.spot(q, self.z(-r))
        self.wire(ref, ref, self.p.xn, q, r).wait_recv()

    def spread(self, q):
        if q:
            self.got(q, 0)
            if q == 1:
                self.copy(3, 0).start()
        else:
            self.copy(1, 0).start()
            self.copy(2, 0).start()
        for r in range(1, self.p.nz):
            self.copy(q, r).start()

    def final(self):
        for r in range(1, self.p.nz):
            for q in range(4):
                self.got(q, r)

    def drain(self):
        for q in range(4):
            for r in range(self.p.nz):
                if q or r:
                    self.copy(q, r).wait_send()


class Scatter(Pieces):
    def __init__(self, p, bd, bxy, bz, out, *rest):
        super().__init__(p, *rest)
        self.bd, self.bxy, self.bz, self.out = bd, bxy, bz, out

    def copy(self, kind, k, d):
        p, b = self.p, k if self.bd.shape[1] > 1 else 0
        if kind == 0:
            s, t, dev = self.piece(1 - p.y, k, d * NX + 1 - p.x, 0), self.bd.at[0, b, d], p.yn
        elif kind == 1:
            s, t, dev = self.piece(1 - p.y, k, d * NX + 1 - p.x, 1), self.bd.at[1, b, d], p.xn
        elif kind == 2:
            s, t, dev = self.piece(p.y, k, d * NX + 1 - p.x), self.bxy.at[0, b, d], p.xn
        elif kind == 3:
            s, t, dev = self.piece(1 - p.y, k, d * NX + p.x), self.bxy.at[1, b, d], p.yn
        else:
            e = self.z(d) * NX + p.x
            s, t, dev = self.piece(p.y, k, e), self.bz.at[b, d - 1], {"e": e}
        return self.wire(s, t, dev, kind, b, d)

    def first(self, k, d):
        self.copy(0, k, d).start()
        self.copy(1, k, d).start()

    def second(self, k, r):
        p, b, d = self.p, k if self.bd.shape[1] > 1 else 0, self.z(r)
        self.copy(0, k, d).wait_recv()
        ref = self.piece(p.y, k, d * NX + 1 - p.x, 0)
        ref[...] = (ref[...].astype(f32) + self.bd[0, b, d].astype(f32)).astype(bf16)
        self.copy(2, k, d).start()
        self.copy(1, k, d).wait_recv()
        ref = self.piece(1 - p.y, k, d * NX + p.x, 1)
        ref[...] = (ref[...].astype(f32) + self.bd[1, b, d].astype(f32)).astype(bf16)
        self.copy(3, k, d).start()

    def third(self, k, r):
        p, b, d = self.p, k if self.bd.shape[1] > 1 else 0, self.z(r)
        self.copy(2, k, d).wait_recv()
        self.copy(3, k, d).wait_recv()
        ref = self.piece(p.y, k, d * NX + p.x)
        total = ref[...].astype(f32) + self.bxy[0, b, d].astype(f32) + self.bxy[1, b, d].astype(f32)
        if r == 0:
            self.home(k)[:, self.lo : self.lo + self.width] = total
        else:
            ref[...] = total.astype(bf16)
            self.copy(4, k, r).start()

    def final(self, k):
        b = k if self.bd.shape[1] > 1 else 0
        cols = slice(self.lo, self.lo + self.width)
        total = self.home(k)[:, cols]
        for r in range(1, self.p.nz):
            self.copy(4, k, r).wait_recv()
            total = total + self.bz[b, r - 1].astype(f32)
        self.home(k)[:, cols] = total

    def drain(self, k):
        for d in range(self.p.nz):
            for kind in (0, 1, 2, 3):
                self.copy(kind, k, d).wait_send()
            if d:
                self.copy(4, k, d).wait_send()


class PlaneScatter(Pieces):
    def __init__(self, p, k, bz, bq, out, *rest):
        super().__init__(p, *rest)
        self.k, self.bz, self.bq, self.out = k, bz, bq, out

    def spot(self, q, z):
        p = self.p
        return self.piece(1 - p.y if q >= 2 else p.y, self.k, z * NX + (1 - p.x if q % 2 else p.x))

    def copy(self, q, r):
        p = self.p
        if r:
            return self.wire(self.spot(q, self.z(r)), self.bz.at[r - 1, q], {"e": self.z(r) * NX + p.x}, q, r)
        return self.wire(self.spot(q, p.z), self.bq.at[q - 1], p.yn if q == 2 else p.xn, q, 0)

    def first(self):
        for r in range(1, self.p.nz):
            for q in (3, 2, 1, 0):
                self.copy(q, r).start()

    def plane_sum(self, q):
        for r in range(1, self.p.nz):
            self.copy(q, r).wait_recv()
        total = self.spot(q, self.p.z)[...].astype(f32)
        for r in range(1, self.p.nz):
            total = total + self.bz[r - 1, q].astype(f32)
        return total

    def second(self):
        for q in (3, 1):
            self.spot(q, self.p.z)[...] = self.plane_sum(q).astype(bf16)
            self.copy(q, 0).start()

    def third(self):
        total = self.plane_sum(2)
        self.copy(3, 0).wait_recv()
        self.spot(2, self.p.z)[...] = (total + self.bq[2].astype(f32)).astype(bf16)
        self.copy(2, 0).start()

    def final(self):
        total = self.plane_sum(0)
        for q in (1, 2):
            self.copy(q, 0).wait_recv()
            total = total + self.bq[q - 1].astype(f32)
        self.home(self.k)[:, self.lo : self.lo + self.width] = total

    def drain(self):
        for q in range(4):
            for r in range(self.p.nz):
                if q or r:
                    self.copy(q, r).wait_send()


class Sums:
    def __init__(self, p, own, plane_buf, line_buf, out, peers, column, ssem, rsem):
        self.p, self.own, self.plane_buf, self.line_buf, self.out = p, own, plane_buf, line_buf, out
        self.peers, self.column, self.ssem, self.rsem = peers, column, ssem, rsem

    def tile(self, ref, t):
        return ref.at[pl.ds(8 * t, 8)]

    def plane_copy(self, t, i, dev):
        return remote(self.tile(self.own, t), self.plane_buf.at[t, i], self.ssem.at[t, i], self.rsem.at[t, i], dev)

    def line_copy(self, t, r, dev):
        return remote(self.tile(self.out, t), self.line_buf.at[t, r], self.ssem.at[t, 8 + r], self.rsem.at[t, 8 + r], dev)

    def plane(self, t):
        for i, dev in self.peers:
            self.plane_copy(t, i, dev).start()

    def line(self, t):
        row = lax.broadcasted_iota(jnp.int32, self.plane_buf.shape[2:], 0)
        lo, hi = SPLIT_ROWS[t]
        total = self.own[8 * t : 8 * t + 8]
        for i, dev in self.peers:
            self.plane_copy(t, i, dev).wait_recv()
            part = self.plane_buf[t, i]
            total = total + (jnp.where((row >= lo) & (row < hi), 0.0, part) if i % 2 else part)
        self.out[8 * t : 8 * t + 8] = total
        for r, dev in self.column:
            self.line_copy(t, r, dev).start()

    def done(self, t):
        total = self.out[8 * t : 8 * t + 8]
        for r, dev in self.column:
            self.line_copy(t, r, dev).wait()
            total = total + self.line_buf[t, r]
        self.out[8 * t : 8 * t + 8] = total

    def drain(self, t):
        for i, dev in self.peers:
            self.plane_copy(t, i, dev).wait_send()


def remote(src, dst, ssem, rsem, dev):
    return pltpu.make_async_remote_copy(src, dst, ssem, rsem, device_id=dev, device_id_type=MESH)


def loop(n, fn, after=()):
    def body(i, carry):
        fn(i)
        at(i, after)
        return carry

    lax.fori_loop(0, n, body, 0)


def at(i, steps):
    for j, todo in enumerate(steps):
        if todo:

            @pl.when(i == j)
            def _(todo=todo):
                for f in todo:
                    f()


def pick(a, b):
    lane = lax.broadcasted_iota(jnp.int32, a.shape, 1)
    return jnp.where(lane % 128 < 64, a.astype(f32), b.astype(f32))


def norm_parts(v):
    center = v - jnp.mean(v, axis=-1, keepdims=True)
    r = lax.rsqrt(jnp.mean(center * center, axis=-1, keepdims=True) + EPSILON)
    return center * r, r


def norm_back(n, r, d, gain):
    q = d * gain
    return r * (q - jnp.mean(q, axis=-1, keepdims=True) - n * jnp.mean(q * n, axis=-1, keepdims=True))


def gelu_both(u):
    a, b = math.sqrt(2.0 / math.pi), 0.044715
    u2 = u * u
    t = jnp.tanh(a * u * (1.0 + b * u2))
    h = 0.5 + 0.5 * t
    return u * h, h + (0.5 * a) * u * (1.0 - t * t) * (1.0 + (3.0 * b) * u2)


def valid(shape, base, length):
    return base + lax.broadcasted_iota(jnp.int32, shape, 0) < length


N_SUM = 16
ROW_B_OUT, ROW_B_DOWN, ROW_G_TWO, ROW_C_TWO, ROW_B_UP, ROW_G_ONE, ROW_C_ONE, ROW_B_QV = 0, 1, 2, 3, 4, 8, 9, 10
SPLIT_ROWS = ((4, 6), (2, 3))
PLANE_GATHER, PLANE_SCATTER = 256, 256
AT_BEGIN, AT_NORM_A, AT_NORM_B, AT_MASK_A, AT_MASK_B, AT_WAIT_0, AT_COLLECT, AT_PROJECT, AT_ATTEND, AT_OUT_SIB, AT_OUT_OWN, AT_NORM_TWO, AT_WAIT_1, AT_UP_A, AT_UP_B, AT_DOWN_GRAD, AT_WAIT_2, AT_PRE_GRAD, AT_SECOND_SIB, AT_SECOND_OWN, AT_UP_GRAD, AT_BACK_TWO, AT_MIXED_GRAD, AT_OUT_GRAD_W, AT_ATTEND_BACK, AT_GRADS, AT_FIRST_SIB, AT_FIRST_OWN, AT_BACK_ONE, AT_DOWN_SIB, AT_DOWN_OWN, AT_FINISH, AT_END = range(33)
IN_G, IN_GD, IN_GP, IN_RD, IN_RQ, IN_RU, IN_RP, IN_AR = range(8)
DO_OWN_XY, DO_OWN_Z, DO_PASS_ON, DO_TURN, DO_SPREAD, DO_FIRST, DO_SECOND, DO_THIRD, DO_FINAL, DO_PLANE, DO_LINE, DO_DONE = range(12)
METHODS = (
    lambda part: part.own_xy,
    lambda part: part.own_z,
    lambda part: part.pass_on,
    lambda part: part.turn,
    lambda part: part.spread,
    lambda part: part.first,
    lambda part: part.second,
    lambda part: part.third,
    lambda part: part.final,
    lambda part: part.plane,
    lambda part: part.line,
    lambda part: part.done,
)
PLAN = {
    (AT_BEGIN, 0): ((IN_G, DO_OWN_Z, 0), (IN_GP, DO_SPREAD, 0),),
    (AT_NORM_A, 1): ((IN_G, DO_OWN_XY, 1), (IN_G, DO_OWN_Z, 1),),
    (AT_NORM_B, 0): ((IN_G, DO_OWN_XY, 0), (IN_GP, DO_SPREAD, 1),),
    (AT_NORM_B, 1): ((IN_GD, DO_OWN_Z, 2),),
    (AT_MASK_A, 2): ((IN_GP, DO_SPREAD, 2),),
    (AT_MASK_B, 1): ((IN_G, DO_TURN, 1, 0),),
    (AT_WAIT_0, 0): ((IN_G, DO_PASS_ON, 0, 3), (IN_G, DO_TURN, 0, 0), (IN_GP, DO_SPREAD, 3), (IN_G, DO_TURN, 0, 3), (IN_G, DO_PASS_ON, 0, 2), (IN_G, DO_PASS_ON, 0, 1), (IN_G, DO_TURN, 0, 2), (IN_G, DO_TURN, 0, 1),),
    (AT_COLLECT, 0): ((IN_G, DO_PASS_ON, 1, 3),),
    (AT_PROJECT, 3): ((IN_GD, DO_OWN_XY, 2),),
    (AT_ATTEND, 1): ((IN_G, DO_TURN, 1, 3),),
    (AT_ATTEND, 3): ((IN_G, DO_PASS_ON, 1, 2), (IN_GD, DO_TURN, 2, 0),),
    (AT_ATTEND, 6): ((IN_G, DO_PASS_ON, 1, 1),),
    (AT_ATTEND, 9): ((IN_G, DO_TURN, 1, 2),),
    (AT_OUT_SIB, 0): ((IN_GD, DO_PASS_ON, 2, 3),),
    (AT_OUT_OWN, 0): ((IN_G, DO_TURN, 1, 1),),
    (AT_NORM_TWO, 2): ((IN_GD, DO_PASS_ON, 2, 2),),
    (AT_UP_A, 0): ((IN_GD, DO_PASS_ON, 2, 1), (IN_GD, DO_TURN, 2, 3),),
    (AT_UP_A, 1): ((IN_GD, DO_TURN, 2, 2),),
    (AT_UP_B, 1): ((IN_GD, DO_TURN, 2, 1),),
    (AT_DOWN_GRAD, 1): ((IN_RD, DO_FIRST, 1, 1),),
    (AT_DOWN_GRAD, 2): ((IN_RD, DO_FIRST, 1, 2),),
    (AT_DOWN_GRAD, 3): ((IN_RQ, DO_FIRST), (IN_RD, DO_FIRST, 1, 3),),
    (AT_WAIT_2, 0): ((IN_RD, DO_FIRST, 1, 0),),
    (AT_PRE_GRAD, 2): ((IN_RD, DO_SECOND, 1, 0), (IN_RD, DO_SECOND, 1, 2), (IN_RD, DO_SECOND, 1, 1),),
    (AT_SECOND_SIB, 1): ((IN_RD, DO_SECOND, 1, 3),),
    (AT_SECOND_OWN, 0): ((IN_RD, DO_THIRD, 1, 0),),
    (AT_SECOND_OWN, 1): ((IN_RD, DO_THIRD, 1, 2),),
    (AT_UP_GRAD, 2): ((IN_RD, DO_THIRD, 1, 1),),
    (AT_BACK_TWO, 1): ((IN_RD, DO_THIRD, 1, 3),),
    (AT_MIXED_GRAD, 0): ((IN_AR, DO_PLANE, 0),),
    (AT_MIXED_GRAD, 2): ((IN_RU, DO_SECOND, 0, 0), (IN_RU, DO_SECOND, 0, 2), (IN_RU, DO_SECOND, 0, 1), (IN_RU, DO_SECOND, 0, 3),),
    (AT_ATTEND_BACK, 1): ((IN_AR, DO_LINE, 0),),
    (AT_ATTEND_BACK, 2): ((IN_RQ, DO_SECOND),),
    (AT_ATTEND_BACK, 3): ((IN_RU, DO_THIRD, 0, 0),),
    (AT_ATTEND_BACK, 4): ((IN_RU, DO_THIRD, 0, 2),),
    (AT_ATTEND_BACK, 7): ((IN_AR, DO_DONE, 0), (IN_RD, DO_FINAL, 1), (IN_RU, DO_THIRD, 0, 1),),
    (AT_GRADS, 1): ((IN_RQ, DO_THIRD), (IN_RU, DO_THIRD, 0, 3),),
    (AT_ATTEND_BACK, 10): ((IN_RP, DO_SECOND, 0, 3), (IN_RP, DO_SECOND, 0, 2),),
    (AT_ATTEND_BACK, 11): ((IN_RQ, DO_FINAL), (IN_RP, DO_SECOND, 0, 0), (IN_RP, DO_SECOND, 1, 3), (IN_RP, DO_SECOND, 1, 1), (IN_RP, DO_SECOND, 1, 0), (IN_RP, DO_SECOND, 0, 1), (IN_RP, DO_THIRD, 0, 3), (IN_RP, DO_THIRD, 0, 2),),
    (AT_GRADS, 2): ((IN_RP, DO_THIRD, 0, 0), (IN_RU, DO_FINAL, 0),),
    (AT_FIRST_OWN, 0): ((IN_RP, DO_SECOND, 1, 2), (IN_RP, DO_THIRD, 1, 1), (IN_RP, DO_THIRD, 1, 3),),
    (AT_FIRST_OWN, 1): ((IN_RP, DO_THIRD, 1, 0),),
    (AT_BACK_ONE, 0): ((IN_RP, DO_THIRD, 0, 1),),
    (AT_BACK_ONE, 1): ((IN_RP, DO_SECOND, 2, 3), (IN_RP, DO_SECOND, 2, 1), (IN_RP, DO_SECOND, 2, 2), (IN_RP, DO_SECOND, 2, 0),),
    (AT_BACK_ONE, 2): ((IN_RP, DO_THIRD, 1, 2),),
    (AT_BACK_ONE, 3): ((IN_RP, DO_THIRD, 2, 3), (IN_AR, DO_PLANE, 1), (IN_RP, DO_FINAL, 0),),
    (AT_DOWN_SIB, 0): ((IN_RP, DO_THIRD, 2, 1),),
    (AT_DOWN_OWN, 0): ((IN_RP, DO_THIRD, 2, 2), (IN_RP, DO_THIRD, 2, 0), (IN_RP, DO_FINAL, 1),),
    (AT_END, 0): ((IN_AR, DO_LINE, 1), (IN_RP, DO_FINAL, 2), (IN_AR, DO_DONE, 1),),
}


def block_kernel(
    lens, tokens, ograd, w_qkv, w_out, w_up, w_down, b_qv, b_up, b_out, b_down, g_one, c_one, g_two, c_two,
    result_hbm, tgrad_hbm, up_out, down_out, outp, sums,
    result, tgrad, tok, og, packed, w, wc, wo, x_all, sec, dr, t1, t2, ft, qkv, mixed, lse, act, gp, dmx, go,
    r1, r2, r3, r4, s1, s2, part, dk_acc, dv_acc, bias, bias_up, vec, sm, ar1, ar2,
    grf, grp, dd, dxy, dz, ud, uxy, uz, pd, pxy, pz, qz, qq,
    g_ss, g_rs, h_ss, h_rs, q_ss, q_rs, d_ss, d_rs, u_ss, u_rs, v_ss, v_rs, p_ss, p_rs, sib_ss, sib_rs, ar_ss, ar_rs, loc,
):
    nz = g_ss.shape[2]
    p = Place(nz)
    c = lax.axis_index("c")
    half, d_model = tokens.shape
    seq = 2 * half
    hw = mixed.shape[1]
    TR = 256
    nt = half // TR
    length = lens[p.y]
    own0, sib0 = c * half, (1 - c) * half

    def rows(base, i, n=TR):
        return pl.ds(pl.multiple_of(base + i * n, n), n)

    load_t = pltpu.make_async_copy(tokens, tok, loc.at[0])
    load_g = pltpu.make_async_copy(ograd, og, loc.at[1])
    load_t.start()
    load_g.start()
    peers = []
    for dx in (0, 1):
        for dy in (0, 1):
            for dc in (0, 1):
                if dx + dy + dc:
                    peers.append((4 * dx + 2 * dy + dc, {"e": p.e + dx * (1 - 2 * p.x), "y": p.y + dy * (1 - 2 * p.y), "c": c + dc * (1 - 2 * c)}))
    column = [(r, {"e": ((p.z + r) % nz) * NX + p.x}) for r in range(1, nz)]
    bar = pltpu.get_barrier_semaphore()
    for _, dev in peers + column:
        pl.semaphore_signal(bar, 1, device_id=dev, device_id_type=MESH)
    for j, ref in enumerate((b_up, b_out, b_down, g_one, c_one, g_two, c_two)):
        vec[j] = ref[...]

    flip_lanes = p.y == 1
    for h in range(hw // 128):
        s = slice(HEAD_DIM * h, HEAD_DIM * (h + 1))
        q, k, v = [w_qkv[j][:, s].astype(f32) for j in range(3)]
        o = w_out[s, :].astype(f32).T
        for j, (lo, hi) in enumerate(((q, v), (k, o))):
            put = jnp.where(flip_lanes, jnp.concatenate([hi, lo], axis=1), jnp.concatenate([lo, hi], axis=1))
            packed[:, 256 * h + 128 * j : 256 * h + 128 * j + 128] = put.astype(bf16)
    pl.semaphore_wait(bar, len(peers) + len(column))

    def sib(i, src, dst):
        return remote(src, dst, sib_ss.at[i], sib_rs.at[i], p.core)

    DOWN, UP = 1, 0
    ffq = w.shape[3]
    gcut, rcut = ffq - PLANE_GATHER, ffq - PLANE_SCATTER
    shard = (packed, w_up, w_down)
    g = Gather(p, shard, w, 0, ffq, g_ss, g_rs)
    gd = Gather(p, shard, w, 0, gcut, h_ss, h_rs)
    gp2 = PlaneGather(p, shard, 2, w, gcut, ffq - gcut, q_ss, q_rs)
    outf = (up_out, down_out)
    ru = Scatter(p, ud, uxy, uz, outf, grf, 0, ffq, u_ss, u_rs)
    rd = Scatter(p, dd, dxy, dz, outf, grf, 0, rcut, d_ss, d_rs)
    rq = PlaneScatter(p, DOWN, qz, qq, outf, grf, rcut, ffq - rcut, v_ss, v_rs)
    rp = Scatter(p, pd, pxy, pz, outp, grp, 0, grp.shape[3], p_ss, p_rs)
    ar = Sums(p, sm, ar1, ar2, sums, peers, column, ar_ss, ar_rs)
    parts = (g, gd, gp2, rd, rq, ru, rp, ar)

    def steps(name, i=0):
        return [lambda t=t: METHODS[t[1]](parts[t[0]])(*t[2:]) for t in PLAN.get((name, i), ())]

    def mark(name):
        for f in steps(name):
            f()

    def tiled(name, n, fn):
        loop(n, fn, [steps(name, i) for i in range(n)])

    x_own, x_sib = x_all.at[rows(own0, 0, half)], x_all.at[rows(sib0, 0, half)]
    mark(AT_BEGIN)
    send_x = sib(0, tokens, x_own)
    send_x.start()
    send_dr = sib(1, ograd, dr.at[rows(own0, 0, half)])
    send_dr.start()
    send_b = remote(b_qv, bias.at[p.y], sib_ss.at[8], sib_rs.at[8], p.yn)
    send_u = remote(vec, bias_up.at[p.y], sib_ss.at[9], sib_rs.at[9], p.yn)
    send_b.start()
    send_u.start()
    keep = [pltpu.make_async_copy(shard[j], w.at[p.y, j, pl.ds(pl.multiple_of(p.e * packed.shape[0], 16), packed.shape[0])], loc.at[2 + j]) for j in range(NK)]
    for cp in keep:
        cp.start()
    bias[p.y] = b_qv[...]
    bias_up[p.y] = vec[...]
    sm[...] = jnp.zeros_like(sm)

    def norm_one(name, base, src, lo):
        def one(i):
            v = src[rows(lo, i, 128)].astype(f32)
            n, _ = norm_parts(v)
            f = n * vec[3:4] + vec[4:5]
            sec[rows(base, i, 128)] = f.astype(bf16)
            ft[:, rows(base, i, 128)] = f.astype(bf16).astype(f32).T.astype(bf16)

        tiled(name, half // 128, one)

    def mask_rows(name, base, src, lo):
        def one(i):
            v = jnp.where(valid((128, d_model), base + i * 128, length), src[rows(lo, i, 128)].astype(f32), 0.0)
            dr[rows(base, i, 128)] = v.astype(bf16)
            t1[:, rows(base, i, 128)] = v.T.astype(bf16)

        tiled(name, half // 128, one)

    load_t.wait()
    norm_one(AT_NORM_A, own0, tok, 0)
    send_x.wait_recv()
    norm_one(AT_NORM_B, sib0, x_all, sib0)
    load_g.wait()
    mask_rows(AT_MASK_A, own0, og, 0)
    send_dr.wait_recv()
    mask_rows(AT_MASK_B, sib0, dr, sib0)
    for cp in keep:
        cp.wait()
    mark(AT_WAIT_0)
    g.final(0)

    def collect(i):
        r = rows(0, i)
        for q in range(hw // 128):
            a = [w[yq, 0, r, q * 256 : q * 256 + 128] for yq in (0, 1)]
            b = [w[yq, 0, r, q * 256 + 128 : q * 256 + 256] for yq in (0, 1)]
            for group, v in enumerate((pick(a[0], a[1]), pick(b[0], b[1]), pick(a[1], a[0]), pick(b[1], b[0]))):
                wc[r, group * hw + q * 128 : group * hw + q * 128 + 128] = v.astype(bf16)
                if group == 3:
                    wo[q * 128 : q * 128 + 128, r] = v.T.astype(bf16)

    tiled(AT_COLLECT, d_model // TR, collect)
    send_b.wait_recv()
    send_u.wait_recv()

    def head_bias(row, first, second):
        s = [slice(HEAD_DIM * h, HEAD_DIM * (h + 1)) for h in range(hw // 128)]
        return jnp.concatenate([bias[j, row : row + 1, c] for c in s for j in (first, second)], axis=1)

    bq, bv = head_bias(0, 0, 1), head_bias(1, 1, 0)

    def project(i):
        h = sec[rows(0, i)]
        qkv[rows(0, i), 0:hw] = ((dot_nn(h, wc[:, 0:hw]) + bq).astype(bf16).astype(f32) * 0.125).astype(bf16)
        qkv[rows(0, i), hw : 2 * hw] = dot_nn(h, wc[:, hw : 2 * hw]).astype(bf16)
        qkv[rows(0, i), 2 * hw : 3 * hw] = (dot_nn(h, wc[:, 2 * hw : 3 * hw]) + bv).astype(bf16)

    tiled(AT_PROJECT, seq // TR, project)
    pairs, blocks = hw // 128, seq // BQ

    def attend(i):
        attn_fwd_pair(i, hw, length, qkv, mixed, lse, lambda b: at(i, [steps(AT_ATTEND, j * blocks + b) for j in range(pairs)]))

    loop(pairs, attend)

    def out_sib(i):
        s1[rows(0, i)] = dot_nn(mixed[rows(sib0, i)], wo[...]).astype(bf16)

    tiled(AT_OUT_SIB, nt, out_sib)
    send_h = sib(2, s1, r1)
    send_h.start()

    def out_own(i):
        result[rows(0, i)] = tok[rows(0, i)].astype(f32) + dot_nn(mixed[rows(own0, i)], wo[...]) + vec[1:2]

    tiled(AT_OUT_OWN, nt, out_own)
    send_h.wait_recv()

    def norm_two(i):
        h = result[rows(0, i, 128)] + r1[rows(0, i, 128)].astype(f32)
        result[rows(0, i, 128)] = h
        n, _ = norm_parts(h)
        sec[rows(own0, i, 128)] = (n * vec[5:6] + vec[6:7]).astype(bf16)

    tiled(AT_NORM_TWO, half // 128, norm_two)
    send_s = sib(3, sec.at[rows(own0, 0, half)], sec.at[rows(own0, 0, half)])
    send_s.start()
    mark(AT_WAIT_1)
    g.final(1)

    def up(name, base):
        def one(i):
            r = rows(base, i)
            h = sec[r]
            t2[:, r] = h.astype(f32).T.astype(bf16)
            for yq in (0, 1):
                u = dot_nn(h, w[yq, 1]) + bias_up[yq, 0:1]
                a, s = gelu_both(u)
                act[r, yq * ffq : (yq + 1) * ffq] = a.astype(bf16)
                gp[r, yq * ffq : (yq + 1) * ffq] = s.astype(bf16)

        tiled(name, nt, one)

    up(AT_UP_A, own0)
    send_s.wait_recv()
    up(AT_UP_B, sib0)
    ZR = d_model // nz

    def down_grad(i):
        r = rows(0, i, ZR)
        for yq in (0, 1):
            grf[yq, DOWN, r] = dot_nn(t1[r], act[:, yq * ffq : (yq + 1) * ffq]).astype(bf16)

    tiled(AT_DOWN_GRAD, nz, down_grad)
    mark(AT_WAIT_2)
    gd.final(2)
    gp2.final()

    def pre_grad(i):
        r = rows(0, i)
        for yq in (0, 1):
            cols = slice(yq * ffq, (yq + 1) * ffq)
            v = (dot_nn(dr[r], w[yq, 2]) * gp[r, cols].astype(f32)).astype(bf16)
            gp[r, cols] = v
            sm[ROW_B_UP + yq : ROW_B_UP + yq + 1] += jnp.sum(v.astype(f32), axis=0, keepdims=True)

    tiled(AT_PRE_GRAD, seq // TR, pre_grad)

    def up_back(i, base):
        return dot_nt(gp[rows(base, i), 0:ffq], w[0, 1]) + dot_nt(gp[rows(base, i), ffq : 2 * ffq], w[1, 1])

    send_h.wait_send()

    def second_sib(i):
        s1[rows(0, i)] = up_back(i, sib0).astype(bf16)

    tiled(AT_SECOND_SIB, nt, second_sib)
    send_d = sib(4, s1, r3)
    send_d.start()

    def second_own(i):
        part[rows(0, i)] = up_back(i, own0)

    tiled(AT_SECOND_OWN, nt, second_own)

    def up_grad(i):
        r = rows(0, i, ZR)
        for yq in (0, 1):
            grf[yq, UP, r] = dot_nn(t2[r], gp[:, yq * ffq : (yq + 1) * ffq]).astype(bf16)
        ru.first(UP, i)

    tiled(AT_UP_GRAD, nz, up_grad)
    send_d.wait_recv()

    def back_two(i):
        r = rows(0, i, 128)
        n, rr = norm_parts(result[r])
        ds = part[r] + r3[r].astype(f32)
        dres = jnp.where(valid((128, d_model), own0 + i * 128, length), og[r].astype(f32), 0.0)
        dh = dres + norm_back(n, rr, ds, vec[5:6])
        tgrad[r] = dh
        x_all[rows(own0, i, 128)] = dh.astype(bf16)
        for row, v in ((ROW_B_OUT, dh), (ROW_B_DOWN, dres), (ROW_G_TWO, ds * n), (ROW_C_TWO, ds)):
            sm[row : row + 1] += jnp.sum(v, axis=0, keepdims=True)

    tiled(AT_BACK_TWO, half // 128, back_two)
    send_dh = sib(5, x_own, x_own)
    send_dh.start()
    send_dh.wait_recv()

    def mixed_grad(i):
        r = rows(0, i)
        h = x_all[r]
        t1[:, r] = h.astype(f32).T.astype(bf16)
        dmx[r] = dot_nn(h, wc[:, 3 * hw : 4 * hw]).astype(bf16)

    tiled(AT_MIXED_GRAD, seq // TR, mixed_grad)

    def out_grad_w(i):
        go[rows(0, i)] = dot_nn(t1[rows(0, i)], mixed[...]).astype(bf16)

    tiled(AT_OUT_GRAD_W, d_model // TR, out_grad_w)

    def attend_back(i):
        attn_bwd_pair(
            i, hw, length, qkv, mixed, lse, dmx, dk_acc, dv_acc, lambda b: at(i, [steps(AT_ATTEND_BACK, j * blocks + b) for j in range(pairs)])
        )
        cq, ck, cv = [pair_cols(i, group, hw) for group in range(3)]

        def grads(t):
            r = rows(0, t, ZR)
            gq, gk, gv = [dot_nn(ft[r], qkv[:, cc]) for cc in (cq, ck, cv)]
            o = go[r, cq].astype(f32)
            grp[0, i, r, 0:128] = pick(gq, gv).astype(bf16)
            grp[0, i, r, 128:256] = pick(gk, o).astype(bf16)
            grp[1, i, r, 0:128] = pick(gv, gq).astype(bf16)
            grp[1, i, r, 128:256] = pick(o, gk).astype(bf16)
            rp.first(i, t)

        loop(nz, grads)
        at(i, [steps(AT_GRADS, j) for j in range(pairs)])
        for cc, lo in ((cq, 0), (cv, hw)):
            to = pl.ds(pl.multiple_of(lo + i * 128, 128), 128)
            sm[ROW_B_QV : ROW_B_QV + 1, to] = jnp.sum(qkv[:, cc].astype(f32), axis=0, keepdims=True)

    loop(pairs, attend_back)

    def first_back(i, base):
        return dot_nt(qkv[rows(base, i)], wc[:, 0 : 3 * hw])

    def first_sib(i):
        s2[rows(0, i)] = first_back(i, sib0).astype(bf16)

    tiled(AT_FIRST_SIB, nt, first_sib)
    send_f = sib(6, s2, r4)
    send_f.start()

    def first_own(i):
        part[rows(0, i)] = first_back(i, own0)

    tiled(AT_FIRST_OWN, nt, first_own)
    send_f.wait_recv()

    def back_one(i):
        r = rows(0, i, 128)
        n, rr = norm_parts(tok[r].astype(f32))
        df = part[r] + r4[r].astype(f32)
        tgrad[r] = tgrad[r] + norm_back(n, rr, df, vec[3:4])
        for row, v in ((ROW_G_ONE, df * n), (ROW_C_ONE, df)):
            sm[row : row + 1] += jnp.sum(v, axis=0, keepdims=True)

    tiled(AT_BACK_ONE, half // 128, back_one)
    store_t = pltpu.make_async_copy(tgrad, tgrad_hbm, loc.at[0])
    store_t.start()

    def down(i, base):
        return dot_nt(act[rows(base, i), 0:ffq], w[0, 2]) + dot_nt(act[rows(base, i), ffq : 2 * ffq], w[1, 2])

    send_d.wait_send()

    def down_sib(i):
        s1[rows(0, i)] = down(i, sib0).astype(bf16)

    tiled(AT_DOWN_SIB, nt, down_sib)
    send_r = sib(7, s1, r2)
    send_r.start()
    def down_own(i):
        part[rows(0, i)] = down(i, own0)

    tiled(AT_DOWN_OWN, nt, down_own)
    send_r.wait_recv()

    def finish(i):
        r = rows(0, i, 128)
        v = result[r] + part[r] + r2[r].astype(f32) + vec[2:3]
        result[r] = jnp.where(valid((128, d_model), own0 + i * 128, length), v, 0.0)

    tiled(AT_FINISH, half // 128, finish)
    store_r = pltpu.make_async_copy(result, result_hbm, loc.at[1])
    store_r.start()
    mark(AT_END)

    for k in range(2):
        g.drain(k)
    gd.drain(2)
    gp2.drain()
    ar.drain(0)
    ar.drain(1)
    rd.drain(DOWN)
    rq.drain()
    ru.drain(UP)
    for k in range(3):
        rp.drain(k)
    for cp in (send_x, send_b, send_u, send_dr, send_s, send_dh, send_f, send_r):
        cp.wait_send()
    store_t.wait()
    store_r.wait()


def block(lens, tokens, ograd, w_qkv, w_out, w_up, w_down, b_qv, vectors, nz):
    half, d = tokens.shape
    heads_w = w_qkv.shape[2]
    seq = 2 * half
    nk, (rows, ffq) = NK, w_up.shape
    hw = d // 2
    pw = 256
    npair = hw // 128

    def V(shape, t=bf16):
        return pltpu.VMEM(shape, t)

    scratch = [
        V((half, d), f32), V((half, d), f32), V((half, d)), V((half, d)), V((rows, d)),
        V((2, nk, d, ffq)), V((d, 4 * hw)), V((hw, d)), V((seq, d)), V((seq, d)), V((seq, d)), V((d, seq)), V((d, seq)), V((d, seq)),
        V((seq, 3 * hw)), V((seq, hw)), V((2 * npair, 1, seq), f32), V((seq, 2 * ffq)), V((seq, 2 * ffq)), V((seq, hw)), V((d, hw)),
        V((half, d)), V((half, d)), V((half, d)), V((half, d)), V((half, d)), V((half, d)), V((half, d), f32),
        V((seq, 128), f32), V((seq, 128), f32), V((2, 2, heads_w), f32), V((2, 8, ffq), f32), V((8, d), f32), V((N_SUM, d), f32), V((2, 8, 8, d), f32), V((2, nz, 8, d), f32),
        V((2, 2, d, ffq)), V((2, npair, d, pw)),
        V((2, 1, nz, rows // 2, ffq - PLANE_SCATTER)), V((2, 1, nz, rows, ffq - PLANE_SCATTER)), V((1, nz - 1, rows, ffq - PLANE_SCATTER)),
        V((2, 1, nz, rows // 2, ffq)), V((2, 1, nz, rows, ffq)), V((1, nz - 1, rows, ffq)),
        V((2, npair, nz, rows // 2, pw)), V((2, npair, nz, rows, pw)), V((npair, nz - 1, rows, pw)),
        V((nz - 1, 4, rows, PLANE_SCATTER)), V((3, rows, PLANE_SCATTER)),
    ]
    dma = pltpu.SemaphoreType.DMA
    sems = [dma((5, nk, nz))] * 4 + [dma((4, nz))] * 2 + [dma((5, 1, nz))] * 4 + [dma((4, nz))] * 2 + [dma((5, npair, nz))] * 2
    sems += [dma((10,)), dma((10,)), dma((2, 8 + nz)), dma((2, 8 + nz)), dma((2 + nk,))]
    vm = pl.BlockSpec(memory_space=pltpu.VMEM)
    anywhere = pl.BlockSpec(memory_space=pl.ANY)
    return pl.pallas_call(
        block_kernel,
        out_shape=(
            jax.ShapeDtypeStruct((half, d), f32),
            jax.ShapeDtypeStruct((half, d), f32),
            jax.ShapeDtypeStruct((rows, ffq), f32),
            jax.ShapeDtypeStruct((rows, ffq), f32),
            jax.ShapeDtypeStruct((npair, rows, pw), f32),
            jax.ShapeDtypeStruct((N_SUM, d), f32),
        ),
        in_specs=[pl.BlockSpec(memory_space=pltpu.SMEM), anywhere, anywhere, vm, vm, anywhere, anywhere] + [vm] * (1 + len(vectors)),
        out_specs=(anywhere, anywhere, vm, vm, vm, vm),
        scratch_shapes=scratch + sems,
        compiler_params=pltpu.CompilerParams(collective_id=0, has_side_effects=True, vmem_limit_bytes=64 << 20),
    )(lens, tokens, ograd, w_qkv, w_out, w_up, w_down, b_qv, *vectors)


def finish_kernel(res_in, tg_in, up_in, down_in, outp, sums, res, tg, up, down, qkv, b_qv, w_out, b_up, *rest):
    rows, (held_r, held_t, held_u, held_d, sem) = rest[:-5], rest[-5:]
    moves = []
    for source, held, to, n in ((tg_in, held_t, tg, 4), (res_in, held_r, res, 4), (up_in, held_u, up, 1), (down_in, held_d, down, 1)):
        size = held.shape[0] // n
        for i in range(n):
            part, j = pl.ds(i * size, size), len(moves)
            load = pltpu.make_async_copy(source.at[part], held.at[part], sem.at[0, j])
            load.start()
            moves.append((load, pltpu.make_async_copy(held.at[part], to.at[part], sem.at[1, j])))
    for load, store in moves:
        load.wait()
        store.start()
    second = lax.axis_index("y") == 1

    def ordered(a):
        return jnp.where(second, jnp.concatenate([a[:, HEAD_DIM:], a[:, :HEAD_DIM]], axis=1), a)

    a = [ordered(outp[h, :, : 2 * HEAD_DIM]) for h in range(outp.shape[0])]
    b = [ordered(outp[h, :, 2 * HEAD_DIM :]) for h in range(outp.shape[0])]
    qkv[0] = jnp.concatenate([v[:, :HEAD_DIM] for v in a], axis=1)
    qkv[1] = jnp.concatenate([v[:, :HEAD_DIM] for v in b], axis=1)
    qkv[2] = jnp.concatenate([v[:, HEAD_DIM:] for v in a], axis=1)
    w_out[...] = jnp.concatenate([v[:, HEAD_DIM:] for v in b], axis=1).T
    half = sums.shape[1] // 2
    for j in (0, 1):
        v = [ordered(sums[ROW_B_QV : ROW_B_QV + 1, j * half + 128 * h : j * half + 128 * h + 128]) for h in range(outp.shape[0])]
        b_qv[j : j + 1] = jnp.concatenate([c[:, HEAD_DIM * j : HEAD_DIM * (j + 1)] for c in v], axis=1)
    b_up[...] = jnp.where(second, sums[ROW_B_UP + 1], sums[ROW_B_UP])
    for ref, row in zip(rows, (ROW_B_OUT, ROW_B_DOWN, ROW_G_ONE, ROW_C_ONE, ROW_G_TWO, ROW_C_TWO)):
        ref[...] = sums[row]
    for _, store in moves:
        store.wait()


def finish(res, tg, up, down, outp, sums):
    n, (rows, ffq), d = outp.shape[0], up.shape, sums.shape[1]
    vm = pl.BlockSpec(memory_space=pltpu.VMEM)
    anywhere = pl.BlockSpec(memory_space=pl.ANY)
    shapes = [res.shape, tg.shape, up.shape, down.shape, (3, rows, n * HEAD_DIM), (2, n * HEAD_DIM), (n * HEAD_DIM, rows), (ffq,)] + [(d,)] * 6
    return pl.pallas_call(
        finish_kernel,
        out_shape=[jax.ShapeDtypeStruct(s, f32) for s in shapes],
        in_specs=[anywhere] * 4 + [vm] * 2,
        out_specs=[anywhere] * 4 + [vm] * 10,
        scratch_shapes=[pltpu.VMEM(a.shape, f32) for a in (res, tg, up, down)] + [pltpu.SemaphoreType.DMA((2, 10))],
    )(res, tg, up, down, outp, sums)


def per_device(tokens, lengths, w_qkv, b_qv, w_out, b_out, w_up, b_up, w_down, b_down, g_one, c_one, g_two, c_two, out_grad, *, nz, sub):
    if sub > 1:
        w_qkv, w_up = lax.all_gather(w_qkv, "r", axis=1, tiled=True), lax.all_gather(w_up, "r", axis=0, tiled=True)
        w_out, w_down = [lax.all_gather(a, "r", axis=1, tiled=True) for a in (w_out, w_down)]
    vectors = (b_up, b_out, b_down, g_one, c_one, g_two, c_two)
    result, tokens_grad, up, down, outp, sums = block(lengths, tokens, out_grad, w_qkv, w_out, w_up, w_down.T, b_qv, vectors, nz)
    if sub > 1:
        up, down = [lax.psum_scatter(a, "r", scatter_dimension=0, tiled=True) for a in (up, down)]
        outp = lax.psum_scatter(outp, "r", scatter_dimension=1, tiled=True)
        sums = lax.psum(sums, "r")
    result, tokens_grad, up, down, qkv, b_qv, w_out, b_up, b_out, b_down, *norms = finish(result, tokens_grad, up, down, outp, sums)
    return (result, tokens_grad, qkv, b_qv, w_out, b_out, up, b_up, down.T, b_down, *norms)


def solution(mesh):
    dp, tensor = mesh.shape["dp"], mesh.shape["tensor"]
    line = 4 * NX
    nz, sub = line // NX, dp // line
    grid = Mesh(mesh.devices.reshape(line, sub, tensor // 2, 2), ("e", "r", "y", "c"))
    dpx, tx = ("e", "r"), ("y", "c")
    rows = P(dpx + tx, None)
    return jax.shard_map(
        functools.partial(per_device, nz=nz, sub=sub),
        mesh=grid,
        in_specs=(rows, P(dpx), P(None, dpx, tx), P(None, tx), P(tx, dpx), P(), P(dpx, tx), P(tx), P(tx, dpx), P(), P(), P(), P(), P(), rows),
        out_specs=(rows, rows, P(None, dpx, tx), P(None, tx), P(tx, dpx), P(), P(dpx, tx), P(tx), P(tx, dpx), P(), P(), P(), P(), P()),
        check_vma=False,
    )
```

```python
import functools
import math

import jax
import jax.numpy as jnp
from jax import lax
from jax.experimental import pallas as pl
from jax.experimental.pallas import tpu as pltpu
from jax.sharding import Mesh
from jax.sharding import PartitionSpec as P

HEAD_DIM = 64
EPSILON = 1e-05
MESH = pl.DeviceIdType.MESH
NX = 2
NK = 3

class Place:
    def __init__(self, nz):
        self.nz = nz
        self.e = lax.axis_index("e"); self.y = lax.axis_index("y")
        self.z = self.e // NX; self.x = self.e % NX
        self.xn = {"e": self.e + 1 - 2 * self.x}
        self.yn = {"y": 1 - self.y}
        self.up = {"e": self.e + NX}
        self.dn = {"e": self.e - NX}
        self.core = {"c": 1 - lax.axis_index("c")}

BQ = 256
NEG = -1e30
f32, bf16 = jnp.float32, jnp.bfloat16
def dot_nt(a, b): return lax.dot_general(a, b, (((1,), (1,)), ((), ())), preferred_element_type=f32)
def dot_nn(a, b): return lax.dot_general(a, b, (((1,), (0,)), ((), ())), preferred_element_type=f32)
def flip(a): return a.astype(f32).T.astype(bf16)

def pair_cols(p, group, width):
    return pl.ds(pl.multiple_of(group * width + p * 128, 128), 128)

def masked_keys(k, j, length):
    n = k.shape[0]
    lane = lax.broadcasted_iota(jnp.int32, (n, 128), 1)
    row = lax.broadcasted_iota(jnp.int32, (n, 128), 0)
    out = jnp.where((lane == 64 * (1 - j)) & (row >= length), NEG, 0.0)
    return jnp.where(lane // 64 == j, k.astype(f32), out).astype(bf16)

def with_one(q, j):
    lane = lax.broadcasted_iota(jnp.int32, q.shape, 1)
    return jnp.where(lane == 64 * (1 - j), 1.0, q.astype(f32)).astype(bf16)

def only(a, h):
    lane = lax.broadcasted_iota(jnp.int32, a.shape, 1)
    return jnp.where(lane // 64 == h, a.astype(f32), 0.0).astype(bf16)

def causal(s, i):
    n = s.shape[0] - BQ
    row = lax.broadcasted_iota(jnp.int32, (BQ, BQ), 0)
    col = lax.broadcasted_iota(jnp.int32, (BQ, BQ), 1)
    d = jnp.where(row <= col, s[n:], NEG)
    return d if n == 0 else jnp.concatenate([s[:n], d], axis=0)

def attn_fwd_pair(p, width, length, qkv, mixed, lse, hook):
    n = qkv.shape[0]
    k = qkv[:, pair_cols(p, 1, width)]
    vt = flip(qkv[:, pair_cols(p, 2, width)])
    kp = [masked_keys(k, j, length) for j in (0, 1)]
    for i in range(n // BQ):
        hi = (i + 1) * BQ
        q = qkv[i * BQ:hi, pair_cols(p, 0, width)]
        outs = []
        for j in (0, 1):
            s = causal(dot_nt(kp[j][:hi], with_one(q, j)), i)
            m = jnp.max(s, axis=0, keepdims=True)
            e = jnp.exp(s - m)
            l = jnp.sum(e, axis=0, keepdims=True)
            o = dot_nn(vt[64 * (1 - j):64 * (2 - j), :hi], e.astype(bf16))
            outs.append(o * (1.0 / l))
            lse[2 * p + j, :, i * BQ:hi] = m + jnp.log(l)
        mixed[i * BQ:hi, pair_cols(p, 0, width)] = jnp.concatenate(outs[::-1], axis=0).T.astype(bf16)
        hook(i)

def attn_bwd_pair(p, width, length, qkv, mixed, lse, dmixed, dk_acc, dv_acc, hook):
    n = qkv.shape[0]
    c0, c1, c2 = [pair_cols(p, g, width) for g in range(3)]
    k = qkv[:, c1]
    kt = flip(k)
    v = qkv[:, c2]
    kp = [masked_keys(k, j, length) for j in (0, 1)]
    dk_acc[...] = jnp.zeros_like(dk_acc); dv_acc[...] = jnp.zeros_like(dv_acc)
    for i in range(n // BQ):
        hi = (i + 1) * BQ
        q = qkv[i * BQ:hi, c0]
        do = dmixed[i * BQ:hi, c0]
        prod = (do.astype(f32) * mixed[i * BQ:hi, c0].astype(f32)).T
        dq = []
        for j in (0, 1):
            vh = 1 - j
            delta = jnp.sum(prod[64 * vh:64 * (vh + 1)], axis=0, keepdims=True)
            dom = only(do, vh)
            s = causal(dot_nt(kp[j][:hi], with_one(q, j)), i)
            w = jnp.exp(s - lse[2 * p + j, :, i * BQ:hi])
            dw = dot_nt(v[:hi], dom)
            ds = (w * (dw - delta)).astype(bf16)
            dv_acc[:hi] += dot_nn(w.astype(bf16), dom)
            dk_acc[:hi] += dot_nn(ds, only(q, j))
            dq.append(dot_nn(kt[64 * j:64 * (j + 1), :hi], ds))
        qkv[i * BQ:hi, c0] = (jnp.concatenate(dq, axis=0).T * 0.125).astype(bf16)
        hook(i)
    qkv[:, c1] = dk_acc[...].astype(bf16)
    qkv[:, c2] = dv_acc[...].astype(bf16)


class Pieces:
    def __init__(self, p, full, lo, width, ssem, rsem):
        self.p, self.full, self.lo, self.width, self.ssem, self.rsem = p, full, lo, width, ssem, rsem
        self.rows = full.shape[2] // (p.nz * NX)

    def piece(self, yq, k, e, half=None):
        n = self.rows if half is None else self.rows // 2
        at_row = e * self.rows + (half or 0) * n
        return self.full.at[yq, k, pl.ds(pl.multiple_of(at_row, 16), n), pl.ds(self.lo, self.width)]

    def span(self, k, n):
        return self.full.at[0, k, pl.ds(0, n * self.rows), pl.ds(self.lo, self.width)]

    def z(self, r):
        return (self.p.z + r + self.p.nz) % self.p.nz

    def home(self, k):
        return self.out[k] if isinstance(self.out, tuple) else self.out.at[k]

    def wire(self, s, t, dev, out_at, in_at):
        return remote(s, t, self.ssem.at[out_at], self.rsem.at[in_at], dev)

    def await_in(self, ref, in_at):
        remote(ref, ref, self.ssem.at[(0,) * len(self.ssem.shape)], self.rsem.at[in_at], self.p.xn).wait_recv()

    def await_out(self, ref, out_at):
        remote(ref, ref, self.ssem.at[out_at], self.rsem.at[(0,) * len(self.rsem.shape)], self.p.xn).wait_send()


class Gather(Pieces):
    def __init__(self, p, own, *rest):
        super().__init__(p, *rest)
        self.own = own

    def mine(self, k):
        return self.own[k].at[:, pl.ds(self.lo, self.width)]

    def copy(self, kind, k, r):
        p = self.p
        back = self.z(-r)
        if kind == 0:
            s, t, dev = self.mine(k), self.piece(p.y, k, p.e), {"e": self.z(r) * NX + p.x}
        elif kind in (1, 2):
            t = self.piece(p.y, k, back * NX + p.x)
            s, dev = (t if r else self.mine(k)), (p.xn, p.yn)[kind - 1]
        elif kind == 3:
            s = t = self.piece(p.y, k, back * NX + 1 - p.x, 0)
            dev = p.yn
        else:
            s = t = self.piece(1 - p.y, k, back * NX + p.x, 1)
            dev = p.xn
        group = (kind + 1) // 2
        return self.wire(s, t, dev, (group, k), ((r - 1, 3 + r, 7)[group], k))

    def own_z(self, k):
        nz = self.p.nz
        for r in [1, nz - 1] + list(range(2, nz - 1)):
            self.copy(0, k, r).start()

    def own_xy(self, k):
        self.copy(1, k, 0).start()
        self.copy(2, k, 0).start()

    def pass_on(self, k, r):
        self.await_in(self.span(k, 1), (r - 1, k))
        self.copy(1, k, r).start()
        self.copy(2, k, r).start()

    def turn(self, k, r):
        self.await_in(self.span(k, 2), (3 + r, k))
        self.copy(3, k, r).start()
        self.copy(4, k, r).start()

    def final(self, k):
        self.await_in(self.span(k, self.p.nz), (7, k))

    def drain(self, k):
        nz = self.p.nz
        for group, n in enumerate((nz - 1, 2 * nz, nz)):
            self.await_out(self.span(k, n), (group, k))


class PlaneGather(Pieces):
    def __init__(self, p, own, k, *rest):
        super().__init__(p, *rest)
        self.own, self.k = own, k

    def spot(self, q, z):
        p = self.p
        return self.piece(1 - p.y if q >= 2 else p.y, self.k, z * NX + (1 - p.x if q % 2 else p.x))

    def mine(self):
        return self.own[self.k].at[:, pl.ds(self.lo, self.width)]

    def copy(self, q, r):
        p = self.p
        if r:
            t = self.spot(q, p.z)
            return self.wire(t if q else self.mine(), t, {"e": self.z(r) * NX + p.x}, (1,), (3,))
        if q == 3:
            t = self.spot(1, p.z)
            return self.wire(t, t, p.yn, (0,), (2,))
        return self.wire(self.mine(), self.spot(0, p.z), (p.xn, p.yn)[q - 1], (0,), (q - 1,))

    def lined(self):
        half = (self.p.nz - 1) * 2
        return self.full.at[pl.ds(0, 2), self.k, pl.ds(0, half * self.rows), pl.ds(self.lo, self.width)]

    def spread(self, q):
        if q:
            self.await_in(self.span(self.k, 1), (q - 1,))
            if q == 1:
                self.copy(3, 0).start()
        else:
            self.copy(1, 0).start()
            self.copy(2, 0).start()
        for r in range(1, self.p.nz):
            self.copy(q, r).start()

    def final(self):
        self.await_in(self.lined(), (3,))

    def drain(self):
        self.await_out(self.span(self.k, 3), (0,))
        self.await_out(self.lined(), (1,))


class Scatter(Pieces):
    def __init__(self, p, bd, bxy, bz, out, *rest):
        super().__init__(p, *rest)
        self.bd, self.bxy, self.bz, self.out = bd, bxy, bz, out

    def slot(self, k):
        return k if self.bd.shape[1] > 1 else 0

    def copy(self, kind, k, d):
        p, b = self.p, self.slot(k)
        if kind == 0:
            s, t, dev = self.piece(1 - p.y, k, d * NX + 1 - p.x, 0), self.bd.at[0, b, d], p.yn
        elif kind == 1:
            s, t, dev = self.piece(1 - p.y, k, d * NX + 1 - p.x, 1), self.bd.at[1, b, d], p.xn
        elif kind == 2:
            s, t, dev = self.piece(p.y, k, d * NX + 1 - p.x), self.bxy.at[0, b, d], p.xn
        elif kind == 3:
            s, t, dev = self.piece(1 - p.y, k, d * NX + p.x), self.bxy.at[1, b, d], p.yn
        else:
            e = self.z(d) * NX + p.x
            s, t, dev = self.piece(p.y, k, e), self.bz.at[b, d - 1], {"e": e}
        group = kind // 2
        return self.wire(s, t, dev, (group, b), ((d, p.nz + d, 2 * p.nz)[group], b))

    def first(self, k, d):
        self.copy(0, k, d).start()
        self.copy(1, k, d).start()

    def second(self, k, r):
        p, b, d = self.p, self.slot(k), self.z(r)
        self.await_in(self.bd.at[pl.ds(0, 2), b, d], (d, b))
        ref = self.piece(p.y, k, d * NX + 1 - p.x, 0)
        ref[...] = (ref[...].astype(f32) + self.bd[0, b, d].astype(f32)).astype(bf16)
        self.copy(2, k, d).start()
        ref = self.piece(1 - p.y, k, d * NX + p.x, 1)
        ref[...] = (ref[...].astype(f32) + self.bd[1, b, d].astype(f32)).astype(bf16)
        self.copy(3, k, d).start()

    def third(self, k, r):
        p, b, d = self.p, self.slot(k), self.z(r)
        self.await_in(self.bxy.at[pl.ds(0, 2), b, d], (p.nz + d, b))
        ref = self.piece(p.y, k, d * NX + p.x)
        total = ref[...].astype(f32) + self.bxy[0, b, d].astype(f32) + self.bxy[1, b, d].astype(f32)
        if r == 0:
            self.home(k)[:, self.lo : self.lo + self.width] = total
        else:
            ref[...] = total.astype(bf16)
            self.copy(4, k, r).start()

    def final(self, k):
        b = self.slot(k)
        cols = slice(self.lo, self.lo + self.width)
        self.await_in(self.bz.at[b], (2 * self.p.nz, b))
        total = self.home(k)[:, cols]
        for r in range(1, self.p.nz):
            total = total + self.bz[b, r - 1].astype(f32)
        self.home(k)[:, cols] = total

    def drain(self, k):
        nz, b = self.p.nz, self.slot(k)
        for group, n in enumerate((nz, 2 * nz, nz - 1)):
            self.await_out(self.span(k, n), (group, b))


class PlaneScatter(Pieces):
    def __init__(self, p, k, bz, bq, out, *rest):
        super().__init__(p, *rest)
        self.k, self.bz, self.bq, self.out = k, bz, bq, out

    def spot(self, q, z):
        p = self.p
        return self.piece(1 - p.y if q >= 2 else p.y, self.k, z * NX + (1 - p.x if q % 2 else p.x))

    def copy(self, q, r):
        p = self.p
        if r:
            return self.wire(self.spot(q, self.z(r)), self.bz.at[q, r - 1], {"e": self.z(r) * NX + p.x}, (1,), (q,))
        return self.wire(self.spot(q, p.z), self.bq.at[q - 1], p.yn if q == 2 else p.xn, (0,), (3 + q,))

    def first(self):
        for r in range(1, self.p.nz):
            for q in (3, 2, 1, 0):
                self.copy(q, r).start()

    def plane_sum(self, q):
        self.await_in(self.bz.at[q], (q,))
        total = self.spot(q, self.p.z)[...].astype(f32)
        for r in range(1, self.p.nz):
            total = total + self.bz[q, r - 1].astype(f32)
        return total

    def second(self):
        for q in (3, 1):
            self.spot(q, self.p.z)[...] = self.plane_sum(q).astype(bf16)
            self.copy(q, 0).start()

    def third(self):
        total = self.plane_sum(2)
        self.await_in(self.bq.at[2], (6,))
        self.spot(2, self.p.z)[...] = (total + self.bq[2].astype(f32)).astype(bf16)
        self.copy(2, 0).start()

    def final(self):
        total = self.plane_sum(0)
        for q in (1, 2):
            self.await_in(self.bq.at[q - 1], (3 + q,))
            total = total + self.bq[q - 1].astype(f32)
        self.home(self.k)[:, self.lo : self.lo + self.width] = total

    def drain(self):
        half = (self.p.nz - 1) * 2
        self.await_out(self.span(self.k, 3), (0,))
        self.await_out(self.full.at[pl.ds(0, 2), self.k, pl.ds(0, half * self.rows), pl.ds(self.lo, self.width)], (1,))


class Sums:
    def __init__(self, p, own, plane_buf, line_buf, out, peers, column, ssem, rsem):
        self.p, self.own, self.plane_buf, self.line_buf, self.out = p, own, plane_buf, line_buf, out
        self.peers, self.column, self.ssem, self.rsem = peers, column, ssem, rsem

    def tile(self, ref, t):
        return ref.at[pl.ds(8 * t, 8)]

    def wire(self, s, t, stage, tile, dev):
        return remote(s, t, self.ssem.at[tile, stage], self.rsem.at[tile, stage], dev)

    def plane_all(self, t):
        ref = self.plane_buf.at[t, pl.ds(1, len(self.peers))]
        return self.wire(ref, ref, 0, t, self.p.xn)

    def plane(self, t):
        for i, dev in self.peers:
            self.wire(self.tile(self.own, t), self.plane_buf.at[t, i], 0, t, dev).start()

    def line(self, t):
        row = lax.broadcasted_iota(jnp.int32, self.plane_buf.shape[2:], 0)
        lo, hi = SPLIT_ROWS[t]
        self.plane_all(t).wait_recv()
        total = self.own[8 * t : 8 * t + 8]
        for i, dev in self.peers:
            part = self.plane_buf[t, i]
            total = total + (jnp.where((row >= lo) & (row < hi), 0.0, part) if i % 2 else part)
        self.out[8 * t : 8 * t + 8] = total
        for r, dev in self.column:
            self.wire(self.tile(self.out, t), self.line_buf.at[t, r], 1, t, dev).start()

    def done(self, t):
        ref = self.line_buf.at[t, pl.ds(1, len(self.column))]
        both = self.wire(ref, ref, 1, t, self.p.xn)
        both.wait_recv()
        both.wait_send()
        total = self.out[8 * t : 8 * t + 8]
        for r, dev in self.column:
            total = total + self.line_buf[t, r]
        self.out[8 * t : 8 * t + 8] = total

    def drain(self, t):
        self.plane_all(t).wait_send()


def remote(src, dst, ssem, rsem, dev):
    return pltpu.make_async_remote_copy(src, dst, ssem, rsem, device_id=dev, device_id_type=MESH)


def loop(n, fn, after=()):
    def body(i, carry):
        fn(i)
        at(i, after)
        return carry

    lax.fori_loop(0, n, body, 0)


def at(i, steps):
    for j, todo in enumerate(steps):
        if todo:

            @pl.when(i == j)
            def _(todo=todo):
                for f in todo:
                    f()


def pick(a, b):
    lane = lax.broadcasted_iota(jnp.int32, a.shape, 1)
    return jnp.where(lane % 128 < 64, a.astype(f32), b.astype(f32))


def norm_parts(v):
    center = v - jnp.mean(v, axis=-1, keepdims=True)
    r = lax.rsqrt(jnp.mean(center * center, axis=-1, keepdims=True) + EPSILON)
    return center * r, r


def norm_back(n, r, d, gain):
    q = d * gain
    return r * (q - jnp.mean(q, axis=-1, keepdims=True) - n * jnp.mean(q * n, axis=-1, keepdims=True))


def gelu_both(u):
    a, b = math.sqrt(2.0 / math.pi), 0.044715
    u2 = u * u
    t = jnp.tanh(a * u * (1.0 + b * u2))
    h = 0.5 + 0.5 * t
    return u * h, h + (0.5 * a) * u * (1.0 - t * t) * (1.0 + (3.0 * b) * u2)


def valid(shape, base, length):
    return base + lax.broadcasted_iota(jnp.int32, shape, 0) < length


N_SUM = 16
ROW_B_OUT, ROW_B_DOWN, ROW_G_TWO, ROW_C_TWO, ROW_B_UP, ROW_G_ONE, ROW_C_ONE, ROW_B_QV = 0, 1, 2, 3, 4, 8, 9, 10
SPLIT_ROWS = ((4, 6), (2, 3))
PLANE_GATHER, PLANE_SCATTER = 256, 256
AT_BEGIN, AT_NORM_A, AT_NORM_B, AT_MASK_A, AT_MASK_B, AT_WAIT_0, AT_COLLECT, AT_PROJECT, AT_ATTEND, AT_OUT_SIB, AT_OUT_OWN, AT_NORM_TWO, AT_WAIT_1, AT_UP_A, AT_UP_B, AT_DOWN_GRAD, AT_WAIT_2, AT_PRE_GRAD, AT_SECOND_SIB, AT_SECOND_OWN, AT_UP_GRAD, AT_BACK_TWO, AT_MIXED_GRAD, AT_OUT_GRAD_W, AT_ATTEND_BACK, AT_GRADS, AT_FIRST_SIB, AT_FIRST_OWN, AT_BACK_ONE, AT_DOWN_SIB, AT_DOWN_OWN, AT_FINISH, AT_END = range(33)
IN_G, IN_GD, IN_GP, IN_RD, IN_RQ, IN_RU, IN_RP, IN_AR = range(8)
DO_OWN_XY, DO_OWN_Z, DO_PASS_ON, DO_TURN, DO_SPREAD, DO_FIRST, DO_SECOND, DO_THIRD, DO_FINAL, DO_PLANE, DO_LINE, DO_DONE = range(12)
METHODS = (
    lambda part: part.own_xy,
    lambda part: part.own_z,
    lambda part: part.pass_on,
    lambda part: part.turn,
    lambda part: part.spread,
    lambda part: part.first,
    lambda part: part.second,
    lambda part: part.third,
    lambda part: part.final,
    lambda part: part.plane,
    lambda part: part.line,
    lambda part: part.done,
)
PLAN = {
    (AT_BEGIN, 0): ((IN_G, DO_OWN_Z, 0), (IN_GP, DO_SPREAD, 0),),
    (AT_NORM_A, 1): ((IN_G, DO_OWN_XY, 1), (IN_G, DO_OWN_Z, 1),),
    (AT_NORM_B, 0): ((IN_G, DO_OWN_XY, 0), (IN_GP, DO_SPREAD, 1),),
    (AT_NORM_B, 1): ((IN_GD, DO_OWN_Z, 2),),
    (AT_MASK_A, 2): ((IN_GP, DO_SPREAD, 2),),
    (AT_MASK_B, 1): ((IN_G, DO_TURN, 1, 0),),
    (AT_WAIT_0, 0): ((IN_G, DO_PASS_ON, 0, 3), (IN_G, DO_TURN, 0, 0), (IN_GP, DO_SPREAD, 3), (IN_G, DO_TURN, 0, 3), (IN_G, DO_PASS_ON, 0, 2), (IN_G, DO_PASS_ON, 0, 1), (IN_G, DO_TURN, 0, 2), (IN_G, DO_TURN, 0, 1),),
    (AT_COLLECT, 0): ((IN_G, DO_PASS_ON, 1, 3),),
    (AT_PROJECT, 3): ((IN_GD, DO_OWN_XY, 2),),
    (AT_ATTEND, 1): ((IN_G, DO_TURN, 1, 3),),
    (AT_ATTEND, 3): ((IN_G, DO_PASS_ON, 1, 2), (IN_GD, DO_TURN, 2, 0),),
    (AT_ATTEND, 6): ((IN_G, DO_PASS_ON, 1, 1),),
    (AT_ATTEND, 9): ((IN_G, DO_TURN, 1, 2),),
    (AT_OUT_SIB, 0): ((IN_GD, DO_PASS_ON, 2, 3),),
    (AT_OUT_OWN, 0): ((IN_G, DO_TURN, 1, 1),),
    (AT_NORM_TWO, 2): ((IN_GD, DO_PASS_ON, 2, 2),),
    (AT_UP_A, 0): ((IN_GD, DO_PASS_ON, 2, 1), (IN_GD, DO_TURN, 2, 3),),
    (AT_UP_A, 1): ((IN_GD, DO_TURN, 2, 2),),
    (AT_UP_B, 1): ((IN_GD, DO_TURN, 2, 1),),
    (AT_DOWN_GRAD, 1): ((IN_RD, DO_FIRST, 1, 1),),
    (AT_DOWN_GRAD, 2): ((IN_RD, DO_FIRST, 1, 2),),
    (AT_DOWN_GRAD, 3): ((IN_RQ, DO_FIRST), (IN_RD, DO_FIRST, 1, 3),),
    (AT_WAIT_2, 0): ((IN_RD, DO_FIRST, 1, 0),),
    (AT_PRE_GRAD, 2): ((IN_RD, DO_SECOND, 1, 0), (IN_RD, DO_SECOND, 1, 2), (IN_RD, DO_SECOND, 1, 1),),
    (AT_SECOND_SIB, 1): ((IN_RD, DO_SECOND, 1, 3),),
    (AT_SECOND_OWN, 0): ((IN_RD, DO_THIRD, 1, 0),),
    (AT_SECOND_OWN, 1): ((IN_RD, DO_THIRD, 1, 2),),
    (AT_UP_GRAD, 2): ((IN_RD, DO_THIRD, 1, 1),),
    (AT_BACK_TWO, 1): ((IN_RD, DO_THIRD, 1, 3),),
    (AT_MIXED_GRAD, 0): ((IN_AR, DO_PLANE, 0),),
    (AT_MIXED_GRAD, 2): ((IN_RU, DO_SECOND, 0, 0), (IN_RU, DO_SECOND, 0, 2), (IN_RU, DO_SECOND, 0, 1), (IN_RU, DO_SECOND, 0, 3),),
    (AT_ATTEND_BACK, 1): ((IN_AR, DO_LINE, 0),),
    (AT_ATTEND_BACK, 2): ((IN_RQ, DO_SECOND),),
    (AT_ATTEND_BACK, 3): ((IN_RU, DO_THIRD, 0, 0),),
    (AT_ATTEND_BACK, 4): ((IN_RU, DO_THIRD, 0, 2),),
    (AT_ATTEND_BACK, 7): ((IN_AR, DO_DONE, 0), (IN_RD, DO_FINAL, 1), (IN_RU, DO_THIRD, 0, 1),),
    (AT_GRADS, 1): ((IN_RQ, DO_THIRD), (IN_RU, DO_THIRD, 0, 3),),
    (AT_ATTEND_BACK, 10): ((IN_RP, DO_SECOND, 0, 3), (IN_RP, DO_SECOND, 0, 2),),
    (AT_ATTEND_BACK, 11): ((IN_RQ, DO_FINAL), (IN_RP, DO_SECOND, 0, 0), (IN_RP, DO_SECOND, 1, 3), (IN_RP, DO_SECOND, 1, 1), (IN_RP, DO_SECOND, 1, 0), (IN_RP, DO_SECOND, 0, 1), (IN_RP, DO_THIRD, 0, 3), (IN_RP, DO_THIRD, 0, 2),),
    (AT_GRADS, 2): ((IN_RP, DO_THIRD, 0, 0), (IN_RU, DO_FINAL, 0),),
    (AT_FIRST_OWN, 0): ((IN_RP, DO_SECOND, 1, 2), (IN_RP, DO_THIRD, 1, 1), (IN_RP, DO_THIRD, 1, 3),),
    (AT_FIRST_OWN, 1): ((IN_RP, DO_THIRD, 1, 0),),
    (AT_BACK_ONE, 0): ((IN_RP, DO_THIRD, 0, 1),),
    (AT_BACK_ONE, 1): ((IN_RP, DO_SECOND, 2, 3), (IN_RP, DO_SECOND, 2, 1), (IN_RP, DO_SECOND, 2, 2), (IN_RP, DO_SECOND, 2, 0),),
    (AT_BACK_ONE, 2): ((IN_RP, DO_THIRD, 1, 2),),
    (AT_BACK_ONE, 3): ((IN_RP, DO_THIRD, 2, 3), (IN_AR, DO_PLANE, 1), (IN_RP, DO_FINAL, 0),),
    (AT_DOWN_SIB, 0): ((IN_RP, DO_THIRD, 2, 1),),
    (AT_DOWN_OWN, 0): ((IN_RP, DO_THIRD, 2, 2), (IN_RP, DO_THIRD, 2, 0), (IN_RP, DO_FINAL, 1),),
    (AT_END, 0): ((IN_AR, DO_LINE, 1), (IN_RP, DO_FINAL, 2), (IN_AR, DO_DONE, 1),),
}


def block_kernel(
    lens, tokens, ograd, w_qkv, w_out, w_up, w_down, b_qv, b_up, b_out, b_down, g_one, c_one, g_two, c_two,
    result_hbm, tgrad_hbm, up_out, down_out, outp, sums,
    result, tgrad, tok, og, packed, w, wc, wo, x_all, sec, dr, t1, t2, ft, qkv, mixed, lse, act, gp, dmx, go,
    r1, r2, r3, r4, s1, s2, part, dk_acc, dv_acc, bias, bias_up, vec, sm, ar1, ar2,
    grf, grp, dd, dxy, dz, ud, uxy, uz, pd, pxy, pz, qz, qq,
    g_ss, g_rs, q_ss, q_rs, d_ss, d_rs, u_ss, u_rs, v_ss, v_rs, p_ss, p_rs, sib_ss, sib_rs, ar_ss, ar_rs, loc,
):
    nz = ar2.shape[1]
    p = Place(nz)
    c = lax.axis_index("c")
    half, d_model = tokens.shape
    seq = 2 * half
    hw = mixed.shape[1]
    TR = 256
    nt = half // TR
    length = lens[p.y]
    own0, sib0 = c * half, (1 - c) * half

    def rows(base, i, n=TR):
        return pl.ds(pl.multiple_of(base + i * n, n), n)

    load_t = pltpu.make_async_copy(tokens, tok, loc.at[0])
    load_g = pltpu.make_async_copy(ograd, og, loc.at[1])
    load_t.start()
    load_g.start()
    peers = []
    for dx in (0, 1):
        for dy in (0, 1):
            for dc in (0, 1):
                if dx + dy + dc:
                    peers.append((4 * dx + 2 * dy + dc, {"e": p.e + dx * (1 - 2 * p.x), "y": p.y + dy * (1 - 2 * p.y), "c": c + dc * (1 - 2 * c)}))
    column = [(r, {"e": ((p.z + r) % nz) * NX + p.x}) for r in range(1, nz)]
    bar = pltpu.get_barrier_semaphore()
    for _, dev in peers + column:
        pl.semaphore_signal(bar, 1, device_id=dev, device_id_type=MESH)
    for j, ref in enumerate((b_up, b_out, b_down, g_one, c_one, g_two, c_two)):
        vec[j] = ref[...]

    flip_lanes = p.y == 1
    for h in range(hw // 128):
        s = slice(HEAD_DIM * h, HEAD_DIM * (h + 1))
        q, k, v = [w_qkv[j][:, s].astype(f32) for j in range(3)]
        o = w_out[s, :].astype(f32).T
        for j, (lo, hi) in enumerate(((q, v), (k, o))):
            put = jnp.where(flip_lanes, jnp.concatenate([hi, lo], axis=1), jnp.concatenate([lo, hi], axis=1))
            packed[:, 256 * h + 128 * j : 256 * h + 128 * j + 128] = put.astype(bf16)
    pl.semaphore_wait(bar, len(peers) + len(column))

    def sib(i, src, dst):
        return remote(src, dst, sib_ss.at[i], sib_rs.at[i], p.core)

    DOWN, UP = 1, 0
    ffq = w.shape[3]
    gcut, rcut = ffq - PLANE_GATHER, ffq - PLANE_SCATTER
    shard = (packed, w_up, w_down)
    g = Gather(p, shard, w, 0, ffq, g_ss, g_rs)
    gd = Gather(p, shard, w, 0, gcut, g_ss, g_rs)
    gp2 = PlaneGather(p, shard, 2, w, gcut, ffq - gcut, q_ss, q_rs)
    outf = (up_out, down_out)
    ru = Scatter(p, ud, uxy, uz, outf, grf, 0, ffq, u_ss, u_rs)
    rd = Scatter(p, dd, dxy, dz, outf, grf, 0, rcut, d_ss, d_rs)
    rq = PlaneScatter(p, DOWN, qz, qq, outf, grf, rcut, ffq - rcut, v_ss, v_rs)
    rp = Scatter(p, pd, pxy, pz, outp, grp, 0, grp.shape[3], p_ss, p_rs)
    ar = Sums(p, sm, ar1, ar2, sums, peers, column, ar_ss, ar_rs)
    parts = (g, gd, gp2, rd, rq, ru, rp, ar)

    def steps(name, i=0):
        return [lambda t=t: METHODS[t[1]](parts[t[0]])(*t[2:]) for t in PLAN.get((name, i), ())]

    def mark(name):
        for f in steps(name):
            f()

    def tiled(name, n, fn):
        loop(n, fn, [steps(name, i) for i in range(n)])

    x_own, x_sib = x_all.at[rows(own0, 0, half)], x_all.at[rows(sib0, 0, half)]
    mark(AT_BEGIN)
    send_x = sib(0, tokens, x_own)
    send_x.start()
    send_dr = sib(1, ograd, dr.at[rows(own0, 0, half)])
    send_dr.start()
    send_b = remote(b_qv, bias.at[p.y], sib_ss.at[8], sib_rs.at[8], p.yn)
    send_u = remote(vec, bias_up.at[p.y], sib_ss.at[9], sib_rs.at[9], p.yn)
    send_b.start()
    send_u.start()
    keep = [pltpu.make_async_copy(shard[j], w.at[p.y, j, pl.ds(pl.multiple_of(p.e * packed.shape[0], 16), packed.shape[0])], loc.at[2 + j]) for j in range(NK)]
    for cp in keep:
        cp.start()
    bias[p.y] = b_qv[...]
    bias_up[p.y] = vec[...]
    sm[...] = jnp.zeros_like(sm)

    def norm_one(name, base, src, lo):
        def one(i):
            v = src[rows(lo, i, 128)].astype(f32)
            n, _ = norm_parts(v)
            f = n * vec[3:4] + vec[4:5]
            sec[rows(base, i, 128)] = f.astype(bf16)
            ft[:, rows(base, i, 128)] = f.astype(bf16).astype(f32).T.astype(bf16)

        tiled(name, half // 128, one)

    def mask_rows(name, base, src, lo):
        def one(i):
            v = jnp.where(valid((128, d_model), base + i * 128, length), src[rows(lo, i, 128)].astype(f32), 0.0)
            dr[rows(base, i, 128)] = v.astype(bf16)
            t1[:, rows(base, i, 128)] = v.T.astype(bf16)

        tiled(name, half // 128, one)

    load_t.wait()
    norm_one(AT_NORM_A, own0, tok, 0)
    send_x.wait_recv()
    norm_one(AT_NORM_B, sib0, x_all, sib0)
    load_g.wait()
    mask_rows(AT_MASK_A, own0, og, 0)
    send_dr.wait_recv()
    mask_rows(AT_MASK_B, sib0, dr, sib0)
    for cp in keep:
        cp.wait()
    mark(AT_WAIT_0)
    g.final(0)

    def collect(i):
        r = rows(0, i)
        for q in range(hw // 128):
            a = [w[yq, 0, r, q * 256 : q * 256 + 128] for yq in (0, 1)]
            b = [w[yq, 0, r, q * 256 + 128 : q * 256 + 256] for yq in (0, 1)]
            for group, v in enumerate((pick(a[0], a[1]), pick(b[0], b[1]), pick(a[1], a[0]), pick(b[1], b[0]))):
                wc[r, group * hw + q * 128 : group * hw + q * 128 + 128] = v.astype(bf16)
                if group == 3:
                    wo[q * 128 : q * 128 + 128, r] = v.T.astype(bf16)

    tiled(AT_COLLECT, d_model // TR, collect)
    send_b.wait_recv()
    send_u.wait_recv()

    def head_bias(row, first, second):
        s = [slice(HEAD_DIM * h, HEAD_DIM * (h + 1)) for h in range(hw // 128)]
        return jnp.concatenate([bias[j, row : row + 1, c] for c in s for j in (first, second)], axis=1)

    bq, bv = head_bias(0, 0, 1), head_bias(1, 1, 0)

    def project(i):
        h = sec[rows(0, i)]
        qkv[rows(0, i), 0:hw] = ((dot_nn(h, wc[:, 0:hw]) + bq).astype(bf16).astype(f32) * 0.125).astype(bf16)
        qkv[rows(0, i), hw : 2 * hw] = dot_nn(h, wc[:, hw : 2 * hw]).astype(bf16)
        qkv[rows(0, i), 2 * hw : 3 * hw] = (dot_nn(h, wc[:, 2 * hw : 3 * hw]) + bv).astype(bf16)

    tiled(AT_PROJECT, seq // TR, project)
    pairs, blocks = hw // 128, seq // BQ

    def attend(i):
        attn_fwd_pair(i, hw, length, qkv, mixed, lse, lambda b: at(i, [steps(AT_ATTEND, j * blocks + b) for j in range(pairs)]))

    loop(pairs, attend)

    def out_sib(i):
        s1[rows(0, i)] = dot_nn(mixed[rows(sib0, i)], wo[...]).astype(bf16)

    tiled(AT_OUT_SIB, nt, out_sib)
    send_h = sib(2, s1, r1)
    send_h.start()

    def out_own(i):
        result[rows(0, i)] = tok[rows(0, i)].astype(f32) + dot_nn(mixed[rows(own0, i)], wo[...]) + vec[1:2]

    tiled(AT_OUT_OWN, nt, out_own)
    send_h.wait_recv()

    def norm_two(i):
        h = result[rows(0, i, 128)] + r1[rows(0, i, 128)].astype(f32)
        result[rows(0, i, 128)] = h
        n, _ = norm_parts(h)
        sec[rows(own0, i, 128)] = (n * vec[5:6] + vec[6:7]).astype(bf16)

    tiled(AT_NORM_TWO, half // 128, norm_two)
    send_s = sib(3, sec.at[rows(own0, 0, half)], sec.at[rows(own0, 0, half)])
    send_s.start()
    mark(AT_WAIT_1)
    g.final(1)

    def up(name, base):
        def one(i):
            r = rows(base, i)
            h = sec[r]
            t2[:, r] = h.astype(f32).T.astype(bf16)
            for yq in (0, 1):
                u = dot_nn(h, w[yq, 1]) + bias_up[yq, 0:1]
                a, s = gelu_both(u)
                act[r, yq * ffq : (yq + 1) * ffq] = a.astype(bf16)
                gp[r, yq * ffq : (yq + 1) * ffq] = s.astype(bf16)

        tiled(name, nt, one)

    up(AT_UP_A, own0)
    send_s.wait_recv()
    up(AT_UP_B, sib0)
    ZR = d_model // nz

    def down_grad(i):
        r = rows(0, i, ZR)
        for yq in (0, 1):
            grf[yq, DOWN, r] = dot_nn(t1[r], act[:, yq * ffq : (yq + 1) * ffq]).astype(bf16)

    tiled(AT_DOWN_GRAD, nz, down_grad)
    mark(AT_WAIT_2)
    gd.final(2)
    gp2.final()

    def pre_grad(i):
        r = rows(0, i)
        for yq in (0, 1):
            cols = slice(yq * ffq, (yq + 1) * ffq)
            v = (dot_nn(dr[r], w[yq, 2]) * gp[r, cols].astype(f32)).astype(bf16)
            gp[r, cols] = v
            sm[ROW_B_UP + yq : ROW_B_UP + yq + 1] += jnp.sum(v.astype(f32), axis=0, keepdims=True)

    tiled(AT_PRE_GRAD, seq // TR, pre_grad)

    def up_back(i, base):
        return dot_nt(gp[rows(base, i), 0:ffq], w[0, 1]) + dot_nt(gp[rows(base, i), ffq : 2 * ffq], w[1, 1])

    send_h.wait_send()

    def second_sib(i):
        s1[rows(0, i)] = up_back(i, sib0).astype(bf16)

    tiled(AT_SECOND_SIB, nt, second_sib)
    send_d = sib(4, s1, r3)
    send_d.start()

    def second_own(i):
        part[rows(0, i)] = up_back(i, own0)

    tiled(AT_SECOND_OWN, nt, second_own)

    def up_grad(i):
        r = rows(0, i, ZR)
        for yq in (0, 1):
            grf[yq, UP, r] = dot_nn(t2[r], gp[:, yq * ffq : (yq + 1) * ffq]).astype(bf16)
        ru.first(UP, i)

    tiled(AT_UP_GRAD, nz, up_grad)
    send_d.wait_recv()

    def back_two(i):
        r = rows(0, i, 128)
        n, rr = norm_parts(result[r])
        ds = part[r] + r3[r].astype(f32)
        dres = jnp.where(valid((128, d_model), own0 + i * 128, length), og[r].astype(f32), 0.0)
        dh = dres + norm_back(n, rr, ds, vec[5:6])
        tgrad[r] = dh
        x_all[rows(own0, i, 128)] = dh.astype(bf16)
        for row, v in ((ROW_B_OUT, dh), (ROW_B_DOWN, dres), (ROW_G_TWO, ds * n), (ROW_C_TWO, ds)):
            sm[row : row + 1] += jnp.sum(v, axis=0, keepdims=True)

    tiled(AT_BACK_TWO, half // 128, back_two)
    send_dh = sib(5, x_own, x_own)
    send_dh.start()
    send_dh.wait_recv()

    def mixed_grad(i):
        r = rows(0, i)
        h = x_all[r]
        t1[:, r] = h.astype(f32).T.astype(bf16)
        dmx[r] = dot_nn(h, wc[:, 3 * hw : 4 * hw]).astype(bf16)

    tiled(AT_MIXED_GRAD, seq // TR, mixed_grad)

    def out_grad_w(i):
        go[rows(0, i)] = dot_nn(t1[rows(0, i)], mixed[...]).astype(bf16)

    tiled(AT_OUT_GRAD_W, d_model // TR, out_grad_w)

    def attend_back(i):
        attn_bwd_pair(
            i, hw, length, qkv, mixed, lse, dmx, dk_acc, dv_acc, lambda b: at(i, [steps(AT_ATTEND_BACK, j * blocks + b) for j in range(pairs)])
        )
        cq, ck, cv = [pair_cols(i, group, hw) for group in range(3)]

        def grads(t):
            r = rows(0, t, ZR)
            gq, gk, gv = [dot_nn(ft[r], qkv[:, cc]) for cc in (cq, ck, cv)]
            o = go[r, cq].astype(f32)
            grp[0, i, r, 0:128] = pick(gq, gv).astype(bf16)
            grp[0, i, r, 128:256] = pick(gk, o).astype(bf16)
            grp[1, i, r, 0:128] = pick(gv, gq).astype(bf16)
            grp[1, i, r, 128:256] = pick(o, gk).astype(bf16)
            rp.first(i, t)

        loop(nz, grads)
        at(i, [steps(AT_GRADS, j) for j in range(pairs)])
        for cc, lo in ((cq, 0), (cv, hw)):
            to = pl.ds(pl.multiple_of(lo + i * 128, 128), 128)
            sm[ROW_B_QV : ROW_B_QV + 1, to] = jnp.sum(qkv[:, cc].astype(f32), axis=0, keepdims=True)

    loop(pairs, attend_back)

    def first_back(i, base):
        return dot_nt(qkv[rows(base, i)], wc[:, 0 : 3 * hw])

    def first_sib(i):
        s2[rows(0, i)] = first_back(i, sib0).astype(bf16)

    tiled(AT_FIRST_SIB, nt, first_sib)
    send_f = sib(6, s2, r4)
    send_f.start()

    def first_own(i):
        part[rows(0, i)] = first_back(i, own0)

    tiled(AT_FIRST_OWN, nt, first_own)
    send_f.wait_recv()

    def back_one(i):
        r = rows(0, i, 128)
        n, rr = norm_parts(tok[r].astype(f32))
        df = part[r] + r4[r].astype(f32)
        tgrad[r] = tgrad[r] + norm_back(n, rr, df, vec[3:4])
        for row, v in ((ROW_G_ONE, df * n), (ROW_C_ONE, df)):
            sm[row : row + 1] += jnp.sum(v, axis=0, keepdims=True)

    tiled(AT_BACK_ONE, half // 128, back_one)
    store_t = pltpu.make_async_copy(tgrad, tgrad_hbm, loc.at[0])
    store_t.start()

    def down(i, base):
        return dot_nt(act[rows(base, i), 0:ffq], w[0, 2]) + dot_nt(act[rows(base, i), ffq : 2 * ffq], w[1, 2])

    send_d.wait_send()

    def down_sib(i):
        s1[rows(0, i)] = down(i, sib0).astype(bf16)

    tiled(AT_DOWN_SIB, nt, down_sib)
    send_r = sib(7, s1, r2)
    send_r.start()
    def down_own(i):
        part[rows(0, i)] = down(i, own0)

    tiled(AT_DOWN_OWN, nt, down_own)
    send_r.wait_recv()

    def finish(i):
        r = rows(0, i, 128)
        v = result[r] + part[r] + r2[r].astype(f32) + vec[2:3]
        result[r] = jnp.where(valid((128, d_model), own0 + i * 128, length), v, 0.0)

    tiled(AT_FINISH, half // 128, finish)
    store_r = pltpu.make_async_copy(result, result_hbm, loc.at[1])
    store_r.start()
    mark(AT_END)

    for k in range(2):
        g.drain(k)
    gd.drain(2)
    gp2.drain()
    ar.drain(0)
    ar.drain(1)
    rd.drain(DOWN)
    rq.drain()
    ru.drain(UP)
    for k in range(3):
        rp.drain(k)
    for cp in (send_x, send_b, send_u, send_dr, send_s, send_dh, send_f, send_r):
        cp.wait_send()
    store_t.wait()
    store_r.wait()


def block(lens, tokens, ograd, w_qkv, w_out, w_up, w_down, b_qv, vectors, nz):
    half, d = tokens.shape
    heads_w = w_qkv.shape[2]
    seq = 2 * half
    nk, (rows, ffq) = NK, w_up.shape
    hw = d // 2
    pw = 256
    npair = hw // 128

    def V(shape, t=bf16):
        return pltpu.VMEM(shape, t)

    scratch = [
        V((half, d), f32), V((half, d), f32), V((half, d)), V((half, d)), V((rows, d)),
        V((2, nk, d, ffq)), V((d, 4 * hw)), V((hw, d)), V((seq, d)), V((seq, d)), V((seq, d)), V((d, seq)), V((d, seq)), V((d, seq)),
        V((seq, 3 * hw)), V((seq, hw)), V((2 * npair, 1, seq), f32), V((seq, 2 * ffq)), V((seq, 2 * ffq)), V((seq, hw)), V((d, hw)),
        V((half, d)), V((half, d)), V((half, d)), V((half, d)), V((half, d)), V((half, d)), V((half, d), f32),
        V((seq, 128), f32), V((seq, 128), f32), V((2, 2, heads_w), f32), V((2, 8, ffq), f32), V((8, d), f32), V((N_SUM, d), f32), V((2, 8, 8, d), f32), V((2, nz, 8, d), f32),
        V((2, 2, d, ffq)), V((2, npair, d, pw)),
        V((2, 1, nz, rows // 2, ffq - PLANE_SCATTER)), V((2, 1, nz, rows, ffq - PLANE_SCATTER)), V((1, nz - 1, rows, ffq - PLANE_SCATTER)),
        V((2, 1, nz, rows // 2, ffq)), V((2, 1, nz, rows, ffq)), V((1, nz - 1, rows, ffq)),
        V((2, npair, nz, rows // 2, pw)), V((2, npair, nz, rows, pw)), V((npair, nz - 1, rows, pw)),
        V((4, nz - 1, rows, PLANE_SCATTER)), V((3, rows, PLANE_SCATTER)),
    ]
    dma = pltpu.SemaphoreType.DMA
    sems = [dma((3, nk)), dma((8, nk)), dma((2,)), dma((4,)), dma((3, 1)), dma((9, 1)), dma((3, 1)), dma((9, 1)), dma((2,)), dma((7,)), dma((3, npair)), dma((9, npair))]
    sems += [dma((10,)), dma((10,)), dma((2, 2)), dma((2, 2)), dma((2 + nk,))]
    vm = pl.BlockSpec(memory_space=pltpu.VMEM)
    anywhere = pl.BlockSpec(memory_space=pl.ANY)
    return pl.pallas_call(
        block_kernel,
        out_shape=(
            jax.ShapeDtypeStruct((half, d), f32),
            jax.ShapeDtypeStruct((half, d), f32),
            jax.ShapeDtypeStruct((rows, ffq), f32),
            jax.ShapeDtypeStruct((rows, ffq), f32),
            jax.ShapeDtypeStruct((npair, rows, pw), f32),
            jax.ShapeDtypeStruct((N_SUM, d), f32),
        ),
        in_specs=[pl.BlockSpec(memory_space=pltpu.SMEM), anywhere, anywhere, vm, vm, anywhere, anywhere] + [vm] * (1 + len(vectors)),
        out_specs=(anywhere, anywhere, vm, vm, vm, vm),
        scratch_shapes=scratch + sems,
        compiler_params=pltpu.CompilerParams(collective_id=0, has_side_effects=True, vmem_limit_bytes=64 << 20),
    )(lens, tokens, ograd, w_qkv, w_out, w_up, w_down, b_qv, *vectors)


def finish_kernel(res_in, tg_in, up_in, down_in, outp, sums, res, tg, up, down, qkv, b_qv, w_out, b_up, *rest):
    rows, (held_r, held_t, held_u, held_d, sem) = rest[:-5], rest[-5:]
    moves = []
    for source, held, to, n in ((tg_in, held_t, tg, 4), (res_in, held_r, res, 4), (up_in, held_u, up, 1), (down_in, held_d, down, 1)):
        size = held.shape[0] // n
        for i in range(n):
            part, j = pl.ds(i * size, size), len(moves)
            load = pltpu.make_async_copy(source.at[part], held.at[part], sem.at[0, j])
            load.start()
            moves.append((load, pltpu.make_async_copy(held.at[part], to.at[part], sem.at[1, j])))
    for load, store in moves:
        load.wait()
        store.start()
    second = lax.axis_index("y") == 1

    def ordered(a):
        return jnp.where(second, jnp.concatenate([a[:, HEAD_DIM:], a[:, :HEAD_DIM]], axis=1), a)

    a = [ordered(outp[h, :, : 2 * HEAD_DIM]) for h in range(outp.shape[0])]
    b = [ordered(outp[h, :, 2 * HEAD_DIM :]) for h in range(outp.shape[0])]
    qkv[0] = jnp.concatenate([v[:, :HEAD_DIM] for v in a], axis=1)
    qkv[1] = jnp.concatenate([v[:, :HEAD_DIM] for v in b], axis=1)
    qkv[2] = jnp.concatenate([v[:, HEAD_DIM:] for v in a], axis=1)
    w_out[...] = jnp.concatenate([v[:, HEAD_DIM:] for v in b], axis=1).T
    half = sums.shape[1] // 2
    for j in (0, 1):
        v = [ordered(sums[ROW_B_QV : ROW_B_QV + 1, j * half + 128 * h : j * half + 128 * h + 128]) for h in range(outp.shape[0])]
        b_qv[j : j + 1] = jnp.concatenate([c[:, HEAD_DIM * j : HEAD_DIM * (j + 1)] for c in v], axis=1)
    b_up[...] = jnp.where(second, sums[ROW_B_UP + 1], sums[ROW_B_UP])
    for ref, row in zip(rows, (ROW_B_OUT, ROW_B_DOWN, ROW_G_ONE, ROW_C_ONE, ROW_G_TWO, ROW_C_TWO)):
        ref[...] = sums[row]
    for _, store in moves:
        store.wait()


def finish(res, tg, up, down, outp, sums):
    n, (rows, ffq), d = outp.shape[0], up.shape, sums.shape[1]
    vm = pl.BlockSpec(memory_space=pltpu.VMEM)
    anywhere = pl.BlockSpec(memory_space=pl.ANY)
    shapes = [res.shape, tg.shape, up.shape, down.shape, (3, rows, n * HEAD_DIM), (2, n * HEAD_DIM), (n * HEAD_DIM, rows), (ffq,)] + [(d,)] * 6
    return pl.pallas_call(
        finish_kernel,
        out_shape=[jax.ShapeDtypeStruct(s, f32) for s in shapes],
        in_specs=[anywhere] * 4 + [vm] * 2,
        out_specs=[anywhere] * 4 + [vm] * 10,
        scratch_shapes=[pltpu.VMEM(a.shape, f32) for a in (res, tg, up, down)] + [pltpu.SemaphoreType.DMA((2, 10))],
    )(res, tg, up, down, outp, sums)


def per_device(tokens, lengths, w_qkv, b_qv, w_out, b_out, w_up, b_up, w_down, b_down, g_one, c_one, g_two, c_two, out_grad, *, nz, sub):
    if sub > 1:
        w_qkv, w_up = lax.all_gather(w_qkv, "r", axis=1, tiled=True), lax.all_gather(w_up, "r", axis=0, tiled=True)
        w_out, w_down = [lax.all_gather(a, "r", axis=1, tiled=True) for a in (w_out, w_down)]
    vectors = (b_up, b_out, b_down, g_one, c_one, g_two, c_two)
    result, tokens_grad, up, down, outp, sums = block(lengths, tokens, out_grad, w_qkv, w_out, w_up, w_down.T, b_qv, vectors, nz)
    if sub > 1:
        up, down = [lax.psum_scatter(a, "r", scatter_dimension=0, tiled=True) for a in (up, down)]
        outp = lax.psum_scatter(outp, "r", scatter_dimension=1, tiled=True)
        sums = lax.psum(sums, "r")
    result, tokens_grad, up, down, qkv, b_qv, w_out, b_up, b_out, b_down, *norms = finish(result, tokens_grad, up, down, outp, sums)
    return (result, tokens_grad, qkv, b_qv, w_out, b_out, up, b_up, down.T, b_down, *norms)


def solution(mesh):
    dp, tensor = mesh.shape["dp"], mesh.shape["tensor"]
    line = 4 * NX
    nz, sub = line // NX, dp // line
    grid = Mesh(mesh.devices.reshape(line, sub, tensor // 2, 2), ("e", "r", "y", "c"))
    dpx, tx = ("e", "r"), ("y", "c")
    rows = P(dpx + tx, None)
    return jax.shard_map(
        functools.partial(per_device, nz=nz, sub=sub),
        mesh=grid,
        in_specs=(rows, P(dpx), P(None, dpx, tx), P(None, tx), P(tx, dpx), P(), P(dpx, tx), P(tx), P(tx, dpx), P(), P(), P(), P(), P(), rows),
        out_specs=(rows, rows, P(None, dpx, tx), P(None, tx), P(tx, dpx), P(), P(dpx, tx), P(tx), P(tx, dpx), P(), P(), P(), P(), P()),
        check_vma=False,
    )
```

```python
import functools
import math

import jax
import jax.numpy as jnp
from jax import lax
from jax.experimental import pallas as pl
from jax.experimental.pallas import tpu as pltpu
from jax.sharding import Mesh
from jax.sharding import PartitionSpec as P

HEAD_DIM = 64
EPSILON = 1e-05
MESH = pl.DeviceIdType.MESH
NX = 2
NK = 3

class Place:
    def __init__(self, nz):
        self.nz = nz
        self.e = lax.axis_index("e"); self.y = lax.axis_index("y")
        self.z = self.e // NX; self.x = self.e % NX
        self.xn = {"e": self.e + 1 - 2 * self.x}
        self.yn = {"y": 1 - self.y}
        self.up = {"e": self.e + NX}
        self.dn = {"e": self.e - NX}
        self.core = {"c": 1 - lax.axis_index("c")}

BQ = 256
NEG = -1e30
f32, bf16 = jnp.float32, jnp.bfloat16
def dot_nt(a, b): return lax.dot_general(a, b, (((1,), (1,)), ((), ())), preferred_element_type=f32)
def dot_nn(a, b): return lax.dot_general(a, b, (((1,), (0,)), ((), ())), preferred_element_type=f32)
def flip(a): return a.astype(f32).T.astype(bf16)

def pair_cols(p, group, width):
    return pl.ds(pl.multiple_of(group * width + p * 128, 128), 128)

def masked_keys(k, j, length):
    n = k.shape[0]
    lane = lax.broadcasted_iota(jnp.int32, (n, 128), 1)
    row = lax.broadcasted_iota(jnp.int32, (n, 128), 0)
    out = jnp.where((lane == 64 * (1 - j)) & (row >= length), NEG, 0.0)
    return jnp.where(lane // 64 == j, k.astype(f32), out).astype(bf16)

def with_one(q, j):
    lane = lax.broadcasted_iota(jnp.int32, q.shape, 1)
    return jnp.where(lane == 64 * (1 - j), 1.0, q.astype(f32)).astype(bf16)

def only(a, h):
    lane = lax.broadcasted_iota(jnp.int32, a.shape, 1)
    return jnp.where(lane // 64 == h, a.astype(f32), 0.0).astype(bf16)

def causal(s, i):
    n = s.shape[0] - BQ
    row = lax.broadcasted_iota(jnp.int32, (BQ, BQ), 0)
    col = lax.broadcasted_iota(jnp.int32, (BQ, BQ), 1)
    d = jnp.where(row <= col, s[n:], NEG)
    return d if n == 0 else jnp.concatenate([s[:n], d], axis=0)

def attn_fwd_pair(p, width, length, qkv, mixed, lse, hook):
    n = qkv.shape[0]
    k = qkv[:, pair_cols(p, 1, width)]
    vt = flip(qkv[:, pair_cols(p, 2, width)])
    kp = [masked_keys(k, j, length) for j in (0, 1)]
    for i in range(n // BQ):
        hi = (i + 1) * BQ
        q = qkv[i * BQ:hi, pair_cols(p, 0, width)]
        outs = []
        for j in (0, 1):
            s = causal(dot_nt(kp[j][:hi], with_one(q, j)), i)
            m = jnp.max(s, axis=0, keepdims=True)
            e = jnp.exp(s - m)
            l = jnp.sum(e, axis=0, keepdims=True)
            o = dot_nn(vt[64 * (1 - j):64 * (2 - j), :hi], e.astype(bf16))
            outs.append(o * (1.0 / l))
            lse[2 * p + j, :, i * BQ:hi] = m + jnp.log(l)
        mixed[i * BQ:hi, pair_cols(p, 0, width)] = jnp.concatenate(outs[::-1], axis=0).T.astype(bf16)
        hook(i)

def attn_bwd_pair(p, width, length, qkv, mixed, lse, dmixed, dk_acc, dv_acc, hook):
    n = qkv.shape[0]
    c0, c1, c2 = [pair_cols(p, g, width) for g in range(3)]
    k = qkv[:, c1]
    kt = flip(k)
    v = qkv[:, c2]
    kp = [masked_keys(k, j, length) for j in (0, 1)]
    dk_acc[...] = jnp.zeros_like(dk_acc); dv_acc[...] = jnp.zeros_like(dv_acc)
    for i in range(n // BQ):
        hi = (i + 1) * BQ
        q = qkv[i * BQ:hi, c0]
        do = dmixed[i * BQ:hi, c0]
        prod = (do.astype(f32) * mixed[i * BQ:hi, c0].astype(f32)).T
        dq = []
        for j in (0, 1):
            vh = 1 - j
            delta = jnp.sum(prod[64 * vh:64 * (vh + 1)], axis=0, keepdims=True)
            dom = only(do, vh)
            s = causal(dot_nt(kp[j][:hi], with_one(q, j)), i)
            w = jnp.exp(s - lse[2 * p + j, :, i * BQ:hi])
            dw = dot_nt(v[:hi], dom)
            ds = (w * (dw - delta)).astype(bf16)
            dv_acc[:hi] += dot_nn(w.astype(bf16), dom)
            dk_acc[:hi] += dot_nn(ds, only(q, j))
            dq.append(dot_nn(kt[64 * j:64 * (j + 1), :hi], ds))
        qkv[i * BQ:hi, c0] = (jnp.concatenate(dq, axis=0).T * 0.125).astype(bf16)
        hook(i)
    qkv[:, c1] = dk_acc[...].astype(bf16)
    qkv[:, c2] = dv_acc[...].astype(bf16)


class Pieces:
    def __init__(self, p, full, lo, width, ssem, rsem):
        self.p, self.full, self.lo, self.width, self.ssem, self.rsem = p, full, lo, width, ssem, rsem
        self.rows = full.shape[2] // (p.nz * NX)

    def piece(self, yq, k, e, half=None):
        n = self.rows if half is None else self.rows // 2
        at_row = e * self.rows + (half or 0) * n
        return self.full.at[yq, k, pl.ds(pl.multiple_of(at_row, 16), n), pl.ds(self.lo, self.width)]

    def span(self, k, n):
        return self.full.at[0, k, pl.ds(0, n * self.rows), pl.ds(self.lo, self.width)]

    def z(self, r):
        return (self.p.z + r + self.p.nz) % self.p.nz

    def home(self, k):
        return self.out[k] if isinstance(self.out, tuple) else self.out.at[k]

    def wire(self, s, t, dev, out_at, in_at):
        return remote(s, t, self.ssem.at[out_at], self.rsem.at[in_at], dev)

    def await_in(self, ref, in_at):
        remote(ref, ref, self.ssem.at[(0,) * len(self.ssem.shape)], self.rsem.at[in_at], self.p.xn).wait_recv()

    def await_out(self, ref, out_at):
        remote(ref, ref, self.ssem.at[out_at], self.rsem.at[(0,) * len(self.rsem.shape)], self.p.xn).wait_send()


class Gather(Pieces):
    def __init__(self, p, own, *rest):
        super().__init__(p, *rest)
        self.own = own

    def mine(self, k):
        return self.own[k].at[:, pl.ds(self.lo, self.width)]

    def copy(self, kind, k, r):
        p = self.p
        back = self.z(-r)
        if kind == 0:
            s, t, dev = self.mine(k), self.piece(p.y, k, p.e), {"e": self.z(r) * NX + p.x}
        elif kind in (1, 2):
            t = self.piece(p.y, k, back * NX + p.x)
            s, dev = (t if r else self.mine(k)), (p.xn, p.yn)[kind - 1]
        elif kind == 3:
            s = t = self.piece(p.y, k, back * NX + 1 - p.x, 0)
            dev = p.yn
        else:
            s = t = self.piece(1 - p.y, k, back * NX + p.x, 1)
            dev = p.xn
        group = (kind + 1) // 2
        return self.wire(s, t, dev, (group, k), ((r - 1, 3 + r, 7)[group], k))

    def own_z(self, k):
        nz = self.p.nz
        for r in [1, nz - 1] + list(range(2, nz - 1)):
            self.copy(0, k, r).start()

    def own_xy(self, k):
        self.copy(1, k, 0).start()
        self.copy(2, k, 0).start()

    def pass_on(self, k, r):
        self.await_in(self.span(k, 1), (r - 1, k))
        self.copy(1, k, r).start()
        self.copy(2, k, r).start()

    def turn(self, k, r):
        self.await_in(self.span(k, 2), (3 + r, k))
        self.copy(3, k, r).start()
        self.copy(4, k, r).start()

    def final(self, k):
        self.await_in(self.span(k, self.p.nz), (7, k))

    def drain(self, k):
        nz = self.p.nz
        for group, n in enumerate((nz - 1, 2 * nz, nz)):
            self.await_out(self.span(k, n), (group, k))


class PlaneGather(Pieces):
    def __init__(self, p, own, k, *rest):
        super().__init__(p, *rest)
        self.own, self.k = own, k

    def spot(self, q, z):
        p = self.p
        return self.piece(1 - p.y if q >= 2 else p.y, self.k, z * NX + (1 - p.x if q % 2 else p.x))

    def mine(self):
        return self.own[self.k].at[:, pl.ds(self.lo, self.width)]

    def copy(self, q, r):
        p = self.p
        if r:
            t = self.spot(q, p.z)
            return self.wire(t if q else self.mine(), t, {"e": self.z(r) * NX + p.x}, (1,), (3,))
        if q == 3:
            t = self.spot(1, p.z)
            return self.wire(t, t, p.yn, (0,), (2,))
        return self.wire(self.mine(), self.spot(0, p.z), (p.xn, p.yn)[q - 1], (0,), (q - 1,))

    def lined(self):
        half = (self.p.nz - 1) * 2
        return self.full.at[pl.ds(0, 2), self.k, pl.ds(0, half * self.rows), pl.ds(self.lo, self.width)]

    def spread(self, q):
        if q:
            self.await_in(self.span(self.k, 1), (q - 1,))
            if q == 1:
                self.copy(3, 0).start()
        else:
            self.copy(1, 0).start()
            self.copy(2, 0).start()
        for r in range(1, self.p.nz):
            self.copy(q, r).start()

    def final(self):
        self.await_in(self.lined(), (3,))

    def drain(self):
        self.await_out(self.span(self.k, 3), (0,))
        self.await_out(self.lined(), (1,))


class Scatter(Pieces):
    def __init__(self, p, bd, bxy, bz, out, *rest):
        super().__init__(p, *rest)
        self.bd, self.bxy, self.bz, self.out = bd, bxy, bz, out

    def slot(self, k):
        return k if self.bd.shape[1] > 1 else 0

    def copy(self, kind, k, d):
        p, b = self.p, self.slot(k)
        if kind == 0:
            s, t, dev = self.piece(1 - p.y, k, d * NX + 1 - p.x, 0), self.bd.at[0, b, d], p.yn
        elif kind == 1:
            s, t, dev = self.piece(1 - p.y, k, d * NX + 1 - p.x, 1), self.bd.at[1, b, d], p.xn
        elif kind == 2:
            s, t, dev = self.piece(p.y, k, d * NX + 1 - p.x), self.bxy.at[0, b, d], p.xn
        elif kind == 3:
            s, t, dev = self.piece(1 - p.y, k, d * NX + p.x), self.bxy.at[1, b, d], p.yn
        else:
            e = self.z(d) * NX + p.x
            s, t, dev = self.piece(p.y, k, e), self.bz.at[b, d - 1], {"e": e}
        group = kind // 2
        return self.wire(s, t, dev, (group, b), ((d, p.nz + d, 2 * p.nz)[group], b))

    def first(self, k, d):
        self.copy(0, k, d).start()
        self.copy(1, k, d).start()

    def second(self, k, r):
        p, b, d = self.p, self.slot(k), self.z(r)
        self.await_in(self.bd.at[pl.ds(0, 2), b, d], (d, b))
        ref = self.piece(p.y, k, d * NX + 1 - p.x, 0)
        ref[...] = (ref[...].astype(f32) + self.bd[0, b, d].astype(f32)).astype(bf16)
        self.copy(2, k, d).start()
        ref = self.piece(1 - p.y, k, d * NX + p.x, 1)
        ref[...] = (ref[...].astype(f32) + self.bd[1, b, d].astype(f32)).astype(bf16)
        self.copy(3, k, d).start()

    def third(self, k, r):
        p, b, d = self.p, self.slot(k), self.z(r)
        self.await_in(self.bxy.at[pl.ds(0, 2), b, d], (p.nz + d, b))
        ref = self.piece(p.y, k, d * NX + p.x)
        total = ref[...].astype(f32) + self.bxy[0, b, d].astype(f32) + self.bxy[1, b, d].astype(f32)
        if r == 0:
            self.home(k)[:, self.lo : self.lo + self.width] = total
        else:
            ref[...] = total.astype(bf16)
            self.copy(4, k, r).start()

    def final(self, k):
        b = self.slot(k)
        cols = slice(self.lo, self.lo + self.width)
        self.await_in(self.bz.at[b], (2 * self.p.nz, b))
        total = self.home(k)[:, cols]
        for r in range(1, self.p.nz):
            total = total + self.bz[b, r - 1].astype(f32)
        self.home(k)[:, cols] = total

    def drain(self, k):
        nz, b = self.p.nz, self.slot(k)
        for group, n in enumerate((nz, 2 * nz, nz - 1)):
            self.await_out(self.span(k, n), (group, b))


class PlaneScatter(Pieces):
    def __init__(self, p, k, bz, bq, out, *rest):
        super().__init__(p, *rest)
        self.k, self.bz, self.bq, self.out = k, bz, bq, out

    def spot(self, q, z):
        p = self.p
        return self.piece(1 - p.y if q >= 2 else p.y, self.k, z * NX + (1 - p.x if q % 2 else p.x))

    def copy(self, q, r):
        p = self.p
        if r:
            return self.wire(self.spot(q, self.z(r)), self.bz.at[q, r - 1], {"e": self.z(r) * NX + p.x}, (1,), (q,))
        return self.wire(self.spot(q, p.z), self.bq.at[q - 1], p.yn if q == 2 else p.xn, (0,), (3 + q,))

    def first(self):
        for r in range(1, self.p.nz):
            for q in (3, 2, 1, 0):
                self.copy(q, r).start()

    def plane_sum(self, q):
        self.await_in(self.bz.at[q], (q,))
        total = self.spot(q, self.p.z)[...].astype(f32)
        for r in range(1, self.p.nz):
            total = total + self.bz[q, r - 1].astype(f32)
        return total

    def second(self):
        for q in (3, 1):
            self.spot(q, self.p.z)[...] = self.plane_sum(q).astype(bf16)
            self.copy(q, 0).start()

    def third(self):
        total = self.plane_sum(2)
        self.await_in(self.bq.at[2], (6,))
        self.spot(2, self.p.z)[...] = (total + self.bq[2].astype(f32)).astype(bf16)
        self.copy(2, 0).start()

    def final(self):
        total = self.plane_sum(0)
        for q in (1, 2):
            self.await_in(self.bq.at[q - 1], (3 + q,))
            total = total + self.bq[q - 1].astype(f32)
        self.home(self.k)[:, self.lo : self.lo + self.width] = total

    def drain(self):
        half = (self.p.nz - 1) * 2
        self.await_out(self.span(self.k, 3), (0,))
        self.await_out(self.full.at[pl.ds(0, 2), self.k, pl.ds(0, half * self.rows), pl.ds(self.lo, self.width)], (1,))


class Sums:
    def __init__(self, p, own, plane_buf, line_buf, out, peers, column, ssem, rsem):
        self.p, self.own, self.plane_buf, self.line_buf, self.out = p, own, plane_buf, line_buf, out
        self.peers, self.column, self.ssem, self.rsem = peers, column, ssem, rsem

    def tile(self, ref, t):
        return ref.at[pl.ds(8 * t, 8)]

    def wire(self, s, t, stage, tile, dev):
        return remote(s, t, self.ssem.at[tile, stage], self.rsem.at[tile, stage], dev)

    def plane_all(self, t):
        ref = self.plane_buf.at[t, pl.ds(1, len(self.peers))]
        return self.wire(ref, ref, 0, t, self.p.xn)

    def plane(self, t):
        for i, dev in self.peers:
            self.wire(self.tile(self.own, t), self.plane_buf.at[t, i], 0, t, dev).start()

    def line(self, t):
        row = lax.broadcasted_iota(jnp.int32, self.plane_buf.shape[2:], 0)
        lo, hi = SPLIT_ROWS[t]
        self.plane_all(t).wait_recv()
        total = self.own[8 * t : 8 * t + 8]
        for i, dev in self.peers:
            part = self.plane_buf[t, i]
            total = total + (jnp.where((row >= lo) & (row < hi), 0.0, part) if i % 2 else part)
        self.out[8 * t : 8 * t + 8] = total
        for r, dev in self.column:
            self.wire(self.tile(self.out, t), self.line_buf.at[t, r], 1, t, dev).start()

    def done(self, t):
        ref = self.line_buf.at[t, pl.ds(1, len(self.column))]
        both = self.wire(ref, ref, 1, t, self.p.xn)
        both.wait_recv()
        both.wait_send()
        total = self.out[8 * t : 8 * t + 8]
        for r, dev in self.column:
            total = total + self.line_buf[t, r]
        self.out[8 * t : 8 * t + 8] = total

    def drain(self, t):
        self.plane_all(t).wait_send()


def remote(src, dst, ssem, rsem, dev):
    return pltpu.make_async_remote_copy(src, dst, ssem, rsem, device_id=dev, device_id_type=MESH)


def loop(n, fn, after=()):
    def body(i, carry):
        fn(i)
        at(i, after)
        return carry

    lax.fori_loop(0, n, body, 0)


def at(i, steps):
    for j, todo in enumerate(steps):
        if todo:

            @pl.when(i == j)
            def _(todo=todo):
                for f in todo:
                    f()


def pick(a, b):
    lane = lax.broadcasted_iota(jnp.int32, a.shape, 1)
    return jnp.where(lane % 128 < 64, a.astype(f32), b.astype(f32))


def norm_parts(v):
    center = v - jnp.mean(v, axis=-1, keepdims=True)
    r = lax.rsqrt(jnp.mean(center * center, axis=-1, keepdims=True) + EPSILON)
    return center * r, r


def norm_back(n, r, d, gain):
    q = d * gain
    return r * (q - jnp.mean(q, axis=-1, keepdims=True) - n * jnp.mean(q * n, axis=-1, keepdims=True))


def gelu_both(u):
    a, b = math.sqrt(2.0 / math.pi), 0.044715
    u2 = u * u
    t = jnp.tanh(a * u * (1.0 + b * u2))
    h = 0.5 + 0.5 * t
    return u * h, h + (0.5 * a) * u * (1.0 - t * t) * (1.0 + (3.0 * b) * u2)


def valid(shape, base, length):
    return base + lax.broadcasted_iota(jnp.int32, shape, 0) < length


N_SUM = 16
ROW_B_OUT, ROW_B_DOWN, ROW_G_TWO, ROW_C_TWO, ROW_B_UP, ROW_G_ONE, ROW_C_ONE, ROW_B_QV = 0, 1, 2, 3, 4, 8, 9, 10
SPLIT_ROWS = ((4, 6), (2, 3))
PLANE_GATHER, PLANE_SCATTER = 256, 256
AT_BEGIN, AT_NORM_A, AT_NORM_B, AT_MASK_A, AT_MASK_B, AT_WAIT_0, AT_COLLECT, AT_PROJECT, AT_ATTEND, AT_OUT_SIB, AT_OUT_OWN, AT_NORM_TWO, AT_WAIT_1, AT_UP_A, AT_UP_B, AT_DOWN_GRAD, AT_WAIT_2, AT_PRE_GRAD, AT_SECOND_SIB, AT_SECOND_OWN, AT_UP_GRAD, AT_BACK_TWO, AT_MIXED_GRAD, AT_OUT_GRAD_W, AT_ATTEND_BACK, AT_GRADS, AT_FIRST_SIB, AT_FIRST_OWN, AT_BACK_ONE, AT_DOWN_SIB, AT_DOWN_OWN, AT_FINISH, AT_END = range(33)
IN_G, IN_GD, IN_GP, IN_RD, IN_RQ, IN_RU, IN_RP, IN_AR = range(8)
DO_OWN_XY, DO_OWN_Z, DO_PASS_ON, DO_TURN, DO_SPREAD, DO_FIRST, DO_SECOND, DO_THIRD, DO_FINAL, DO_PLANE, DO_LINE, DO_DONE = range(12)
METHODS = (
    lambda part: part.own_xy,
    lambda part: part.own_z,
    lambda part: part.pass_on,
    lambda part: part.turn,
    lambda part: part.spread,
    lambda part: part.first,
    lambda part: part.second,
    lambda part: part.third,
    lambda part: part.final,
    lambda part: part.plane,
    lambda part: part.line,
    lambda part: part.done,
)
PLAN = {
    (AT_BEGIN, 0): ((IN_G, DO_OWN_Z, 0), (IN_GP, DO_SPREAD, 0),),
    (AT_NORM_A, 1): ((IN_G, DO_OWN_XY, 1), (IN_G, DO_OWN_Z, 1),),
    (AT_NORM_B, 0): ((IN_G, DO_OWN_XY, 0), (IN_GP, DO_SPREAD, 1),),
    (AT_NORM_B, 1): ((IN_GD, DO_OWN_Z, 2),),
    (AT_MASK_A, 2): ((IN_GP, DO_SPREAD, 2),),
    (AT_MASK_B, 1): ((IN_G, DO_TURN, 1, 0),),
    (AT_WAIT_0, 0): ((IN_G, DO_PASS_ON, 0, 3), (IN_G, DO_TURN, 0, 0), (IN_GP, DO_SPREAD, 3), (IN_G, DO_TURN, 0, 3), (IN_G, DO_PASS_ON, 0, 2), (IN_G, DO_PASS_ON, 0, 1), (IN_G, DO_TURN, 0, 2), (IN_G, DO_TURN, 0, 1),),
    (AT_COLLECT, 0): ((IN_G, DO_PASS_ON, 1, 3),),
    (AT_PROJECT, 3): ((IN_GD, DO_OWN_XY, 2),),
    (AT_ATTEND, 1): ((IN_G, DO_TURN, 1, 3),),
    (AT_ATTEND, 3): ((IN_G, DO_PASS_ON, 1, 2), (IN_GD, DO_TURN, 2, 0),),
    (AT_ATTEND, 6): ((IN_G, DO_PASS_ON, 1, 1),),
    (AT_ATTEND, 9): ((IN_G, DO_TURN, 1, 2),),
    (AT_OUT_SIB, 0): ((IN_GD, DO_PASS_ON, 2, 3),),
    (AT_OUT_OWN, 0): ((IN_G, DO_TURN, 1, 1),),
    (AT_NORM_TWO, 2): ((IN_GD, DO_PASS_ON, 2, 2),),
    (AT_UP_A, 0): ((IN_GD, DO_PASS_ON, 2, 1), (IN_GD, DO_TURN, 2, 3),),
    (AT_UP_A, 1): ((IN_GD, DO_TURN, 2, 2),),
    (AT_UP_B, 1): ((IN_GD, DO_TURN, 2, 1),),
    (AT_DOWN_GRAD, 1): ((IN_RD, DO_FIRST, 1, 1),),
    (AT_DOWN_GRAD, 2): ((IN_RD, DO_FIRST, 1, 2),),
    (AT_DOWN_GRAD, 3): ((IN_RQ, DO_FIRST), (IN_RD, DO_FIRST, 1, 3),),
    (AT_WAIT_2, 0): ((IN_RD, DO_FIRST, 1, 0),),
    (AT_PRE_GRAD, 2): ((IN_RD, DO_SECOND, 1, 0), (IN_RD, DO_SECOND, 1, 2), (IN_RD, DO_SECOND, 1, 1),),
    (AT_SECOND_SIB, 1): ((IN_RD, DO_SECOND, 1, 3),),
    (AT_SECOND_OWN, 0): ((IN_RD, DO_THIRD, 1, 0),),
    (AT_SECOND_OWN, 1): ((IN_RD, DO_THIRD, 1, 2),),
    (AT_UP_GRAD, 2): ((IN_RD, DO_THIRD, 1, 1),),
    (AT_BACK_TWO, 1): ((IN_RD, DO_THIRD, 1, 3),),
    (AT_MIXED_GRAD, 0): ((IN_AR, DO_PLANE, 0),),
    (AT_MIXED_GRAD, 2): ((IN_RU, DO_SECOND, 0, 0), (IN_RU, DO_SECOND, 0, 2), (IN_RU, DO_SECOND, 0, 1), (IN_RU, DO_SECOND, 0, 3),),
    (AT_ATTEND_BACK, 1): ((IN_AR, DO_LINE, 0),),
    (AT_ATTEND_BACK, 2): ((IN_RQ, DO_SECOND),),
    (AT_ATTEND_BACK, 3): ((IN_RU, DO_THIRD, 0, 0),),
    (AT_ATTEND_BACK, 4): ((IN_RU, DO_THIRD, 0, 2),),
    (AT_ATTEND_BACK, 7): ((IN_AR, DO_DONE, 0), (IN_RD, DO_FINAL, 1), (IN_RU, DO_THIRD, 0, 1),),
    (AT_GRADS, 1): ((IN_RQ, DO_THIRD), (IN_RU, DO_THIRD, 0, 3),),
    (AT_ATTEND_BACK, 10): ((IN_RP, DO_SECOND, 0, 3), (IN_RP, DO_SECOND, 0, 2),),
    (AT_ATTEND_BACK, 11): ((IN_RQ, DO_FINAL), (IN_RP, DO_SECOND, 0, 0), (IN_RP, DO_SECOND, 1, 3), (IN_RP, DO_SECOND, 1, 1), (IN_RP, DO_SECOND, 1, 0), (IN_RP, DO_SECOND, 0, 1), (IN_RP, DO_THIRD, 0, 3), (IN_RP, DO_THIRD, 0, 2),),
    (AT_GRADS, 2): ((IN_RP, DO_THIRD, 0, 0), (IN_RU, DO_FINAL, 0),),
    (AT_FIRST_OWN, 0): ((IN_RP, DO_SECOND, 1, 2), (IN_RP, DO_THIRD, 1, 1), (IN_RP, DO_THIRD, 1, 3),),
    (AT_FIRST_OWN, 1): ((IN_RP, DO_THIRD, 1, 0),),
    (AT_BACK_ONE, 0): ((IN_RP, DO_THIRD, 0, 1),),
    (AT_BACK_ONE, 1): ((IN_RP, DO_SECOND, 2, 3), (IN_RP, DO_SECOND, 2, 1), (IN_RP, DO_SECOND, 2, 2), (IN_RP, DO_SECOND, 2, 0),),
    (AT_BACK_ONE, 2): ((IN_RP, DO_THIRD, 1, 2),),
    (AT_BACK_ONE, 3): ((IN_RP, DO_THIRD, 2, 3), (IN_AR, DO_PLANE, 1), (IN_RP, DO_FINAL, 0),),
    (AT_DOWN_SIB, 0): ((IN_RP, DO_THIRD, 2, 1),),
    (AT_DOWN_OWN, 0): ((IN_RP, DO_THIRD, 2, 2), (IN_RP, DO_THIRD, 2, 0), (IN_RP, DO_FINAL, 1),),
    (AT_END, 0): ((IN_AR, DO_LINE, 1), (IN_RP, DO_FINAL, 2), (IN_AR, DO_DONE, 1),),
}


def block_kernel(
    lens, tokens, ograd, w_qkv, w_out, w_up, w_down, b_qv, b_up, b_out, b_down, g_one, c_one, g_two, c_two,
    result_hbm, tgrad_hbm, up_out, down_out, outp, sums,
    result, tgrad, tok, og, packed, w, wc, wo, x_all, sec, dr, t1, t2, ft, qkv, mixed, lse, act, gp, dmx, go,
    r1, r2, r3, r4, s1, s2, part, dk_acc, dv_acc, bias, bias_up, vec, sm, ar1, ar2,
    grf, grp, dd, dxy, dz, ud, uxy, uz, pd, pxy, pz, qz, qq,
    g_ss, g_rs, q_ss, q_rs, d_ss, d_rs, u_ss, u_rs, v_ss, v_rs, p_ss, p_rs, sib_ss, sib_rs, ar_ss, ar_rs, loc,
):
    nz = ar2.shape[1]
    p = Place(nz)
    c = lax.axis_index("c")
    half, d_model = tokens.shape
    seq = 2 * half
    hw = mixed.shape[1]
    TR = 256
    nt = half // TR
    length = lens[p.y]
    own0, sib0 = c * half, (1 - c) * half

    def rows(base, i, n=TR):
        return pl.ds(pl.multiple_of(base + i * n, n), n)

    load_t = pltpu.make_async_copy(tokens, tok, loc.at[0])
    load_g = pltpu.make_async_copy(ograd, og, loc.at[1])
    load_t.start()
    load_g.start()
    peers = []
    for dx in (0, 1):
        for dy in (0, 1):
            for dc in (0, 1):
                if dx + dy + dc:
                    peers.append((4 * dx + 2 * dy + dc, {"e": p.e + dx * (1 - 2 * p.x), "y": p.y + dy * (1 - 2 * p.y), "c": c + dc * (1 - 2 * c)}))
    column = [(r, {"e": ((p.z + r) % nz) * NX + p.x}) for r in range(1, nz)]
    bar = pltpu.get_barrier_semaphore()
    for _, dev in peers + column:
        pl.semaphore_signal(bar, 1, device_id=dev, device_id_type=MESH)
    for j, ref in enumerate((b_up, b_out, b_down, g_one, c_one, g_two, c_two)):
        vec[j] = ref[...]

    flip_lanes = p.y == 1
    for h in range(hw // 128):
        s = slice(HEAD_DIM * h, HEAD_DIM * (h + 1))
        q, k, v = [w_qkv[j][:, s].astype(f32) for j in range(3)]
        o = w_out[s, :].astype(f32).T
        for j, (lo, hi) in enumerate(((q, v), (k, o))):
            put = jnp.where(flip_lanes, jnp.concatenate([hi, lo], axis=1), jnp.concatenate([lo, hi], axis=1))
            packed[:, 256 * h + 128 * j : 256 * h + 128 * j + 128] = put.astype(bf16)
    pl.semaphore_wait(bar, len(peers) + len(column))

    def sib(i, src, dst):
        return remote(src, dst, sib_ss.at[i], sib_rs.at[i], p.core)

    DOWN, UP = 1, 0
    ffq = w.shape[3]
    gcut, rcut = ffq - PLANE_GATHER, ffq - PLANE_SCATTER
    shard = (packed, w_up, w_down)
    g = Gather(p, shard, w, 0, ffq, g_ss, g_rs)
    gd = Gather(p, shard, w, 0, gcut, g_ss, g_rs)
    gp2 = PlaneGather(p, shard, 2, w, gcut, ffq - gcut, q_ss, q_rs)
    outf = (up_out, down_out)
    ru = Scatter(p, ud, uxy, uz, outf, grf, 0, ffq, u_ss, u_rs)
    rd = Scatter(p, dd, dxy, dz, outf, grf, 0, rcut, d_ss, d_rs)
    rq = PlaneScatter(p, DOWN, qz, qq, outf, grf, rcut, ffq - rcut, v_ss, v_rs)
    rp = Scatter(p, pd, pxy, pz, outp, grp, 0, grp.shape[3], p_ss, p_rs)
    ar = Sums(p, sm, ar1, ar2, sums, peers, column, ar_ss, ar_rs)
    parts = (g, gd, gp2, rd, rq, ru, rp, ar)

    def steps(name, i=0):
        return [lambda t=t: METHODS[t[1]](parts[t[0]])(*t[2:]) for t in PLAN.get((name, i), ())]

    def mark(name):
        for f in steps(name):
            f()

    def tiled(name, n, fn):
        loop(n, fn, [steps(name, i) for i in range(n)])

    x_own, x_sib = x_all.at[rows(own0, 0, half)], x_all.at[rows(sib0, 0, half)]
    mark(AT_BEGIN)
    send_x = sib(0, tokens, x_own)
    send_x.start()
    send_dr = sib(1, ograd, dr.at[rows(own0, 0, half)])
    send_dr.start()
    send_b = remote(b_qv, bias.at[p.y], sib_ss.at[8], sib_rs.at[8], p.yn)
    send_u = remote(vec, bias_up.at[p.y], sib_ss.at[9], sib_rs.at[9], p.yn)
    send_b.start()
    send_u.start()
    keep = [pltpu.make_async_copy(shard[j], w.at[p.y, j, pl.ds(pl.multiple_of(p.e * packed.shape[0], 16), packed.shape[0])], loc.at[2 + j]) for j in range(NK)]
    for cp in keep:
        cp.start()
    bias[p.y] = b_qv[...]
    bias_up[p.y] = vec[...]
    sm[...] = jnp.zeros_like(sm)

    def norm_one(name, base, src, lo):
        def one(i):
            v = src[rows(lo, i, 128)].astype(f32)
            n, _ = norm_parts(v)
            f = n * vec[3:4] + vec[4:5]
            sec[rows(base, i, 128)] = f.astype(bf16)
            ft[:, rows(base, i, 128)] = f.astype(bf16).astype(f32).T.astype(bf16)

        tiled(name, half // 128, one)

    def mask_rows(name, base, src, lo):
        def one(i):
            v = jnp.where(valid((128, d_model), base + i * 128, length), src[rows(lo, i, 128)].astype(f32), 0.0)
            dr[rows(base, i, 128)] = v.astype(bf16)
            t1[:, rows(base, i, 128)] = v.T.astype(bf16)

        tiled(name, half // 128, one)

    load_t.wait()
    norm_one(AT_NORM_A, own0, tok, 0)
    send_x.wait_recv()
    norm_one(AT_NORM_B, sib0, x_all, sib0)
    load_g.wait()
    mask_rows(AT_MASK_A, own0, og, 0)
    send_dr.wait_recv()
    mask_rows(AT_MASK_B, sib0, dr, sib0)
    for cp in keep:
        cp.wait()
    mark(AT_WAIT_0)
    g.final(0)

    def collect(i):
        r = rows(0, i)
        for q in range(hw // 128):
            a = [w[yq, 0, r, q * 256 : q * 256 + 128] for yq in (0, 1)]
            b = [w[yq, 0, r, q * 256 + 128 : q * 256 + 256] for yq in (0, 1)]
            for group, v in enumerate((pick(a[0], a[1]), pick(b[0], b[1]), pick(a[1], a[0]), pick(b[1], b[0]))):
                wc[r, group * hw + q * 128 : group * hw + q * 128 + 128] = v.astype(bf16)
                if group == 3:
                    wo[q * 128 : q * 128 + 128, r] = v.T.astype(bf16)

    tiled(AT_COLLECT, d_model // TR, collect)
    send_b.wait_recv()
    send_u.wait_recv()

    def head_bias(row, first, second):
        s = [slice(HEAD_DIM * h, HEAD_DIM * (h + 1)) for h in range(hw // 128)]
        return jnp.concatenate([bias[j, row : row + 1, c] for c in s for j in (first, second)], axis=1)

    bq, bv = head_bias(0, 0, 1), head_bias(1, 1, 0)

    def project(i):
        h = sec[rows(0, i)]
        qkv[rows(0, i), 0:hw] = ((dot_nn(h, wc[:, 0:hw]) + bq).astype(bf16).astype(f32) * 0.125).astype(bf16)
        qkv[rows(0, i), hw : 2 * hw] = dot_nn(h, wc[:, hw : 2 * hw]).astype(bf16)
        qkv[rows(0, i), 2 * hw : 3 * hw] = (dot_nn(h, wc[:, 2 * hw : 3 * hw]) + bv).astype(bf16)

    tiled(AT_PROJECT, seq // TR, project)
    pairs, blocks = hw // 128, seq // BQ

    def attend(i):
        attn_fwd_pair(i, hw, length, qkv, mixed, lse, lambda b: at(i, [steps(AT_ATTEND, j * blocks + b) for j in range(pairs)]))

    loop(pairs, attend)

    def out_sib(i):
        s1[rows(0, i)] = dot_nn(mixed[rows(sib0, i)], wo[...]).astype(bf16)

    tiled(AT_OUT_SIB, nt, out_sib)
    send_h = sib(2, s1, r1)
    send_h.start()

    def out_own(i):
        result[rows(0, i)] = tok[rows(0, i)].astype(f32) + dot_nn(mixed[rows(own0, i)], wo[...]) + vec[1:2]

    tiled(AT_OUT_OWN, nt, out_own)
    send_h.wait_recv()

    def norm_two(i):
        h = result[rows(0, i, 128)] + r1[rows(0, i, 128)].astype(f32)
        result[rows(0, i, 128)] = h
        n, _ = norm_parts(h)
        sec[rows(own0, i, 128)] = (n * vec[5:6] + vec[6:7]).astype(bf16)

    tiled(AT_NORM_TWO, half // 128, norm_two)
    send_s = sib(3, sec.at[rows(own0, 0, half)], sec.at[rows(own0, 0, half)])
    send_s.start()
    mark(AT_WAIT_1)
    g.final(1)

    def up(name, base):
        def one(i):
            r = rows(base, i)
            h = sec[r]
            t2[:, r] = h.astype(f32).T.astype(bf16)
            for yq in (0, 1):
                u = dot_nn(h, w[yq, 1]) + bias_up[yq, 0:1]
                a, s = gelu_both(u)
                act[r, yq * ffq : (yq + 1) * ffq] = a.astype(bf16)
                gp[r, yq * ffq : (yq + 1) * ffq] = s.astype(bf16)

        tiled(name, nt, one)

    up(AT_UP_A, own0)
    send_s.wait_recv()
    up(AT_UP_B, sib0)
    ZR = d_model // nz

    def down_grad(i):
        r = rows(0, i, ZR)
        for yq in (0, 1):
            grf[yq, DOWN, r] = dot_nn(t1[r], act[:, yq * ffq : (yq + 1) * ffq]).astype(bf16)

    tiled(AT_DOWN_GRAD, nz, down_grad)
    mark(AT_WAIT_2)
    gd.final(2)
    gp2.final()

    def pre_grad(i):
        r = rows(0, i)
        for yq in (0, 1):
            cols = slice(yq * ffq, (yq + 1) * ffq)
            v = (dot_nn(dr[r], w[yq, 2]) * gp[r, cols].astype(f32)).astype(bf16)
            gp[r, cols] = v
            sm[ROW_B_UP + yq : ROW_B_UP + yq + 1] += jnp.sum(v.astype(f32), axis=0, keepdims=True)

    tiled(AT_PRE_GRAD, seq // TR, pre_grad)

    def up_back(i, base):
        return dot_nt(gp[rows(base, i), 0:ffq], w[0, 1]) + dot_nt(gp[rows(base, i), ffq : 2 * ffq], w[1, 1])

    send_h.wait_send()

    def second_sib(i):
        s1[rows(0, i)] = up_back(i, sib0).astype(bf16)

    tiled(AT_SECOND_SIB, nt, second_sib)
    send_d = sib(4, s1, r3)
    send_d.start()

    def second_own(i):
        part[rows(0, i)] = up_back(i, own0)

    tiled(AT_SECOND_OWN, nt, second_own)

    def up_grad(i):
        r = rows(0, i, ZR)
        for yq in (0, 1):
            grf[yq, UP, r] = dot_nn(t2[r], gp[:, yq * ffq : (yq + 1) * ffq]).astype(bf16)
        ru.first(UP, i)

    tiled(AT_UP_GRAD, nz, up_grad)
    send_d.wait_recv()

    def back_two(i):
        r = rows(0, i, 128)
        n, rr = norm_parts(result[r])
        ds = part[r] + r3[r].astype(f32)
        dres = jnp.where(valid((128, d_model), own0 + i * 128, length), og[r].astype(f32), 0.0)
        dh = dres + norm_back(n, rr, ds, vec[5:6])
        tgrad[r] = dh
        x_all[rows(own0, i, 128)] = dh.astype(bf16)
        for row, v in ((ROW_B_OUT, dh), (ROW_B_DOWN, dres), (ROW_G_TWO, ds * n), (ROW_C_TWO, ds)):
            sm[row : row + 1] += jnp.sum(v, axis=0, keepdims=True)

    tiled(AT_BACK_TWO, half // 128, back_two)
    send_dh = sib(5, x_own, x_own)
    send_dh.start()
    send_dh.wait_recv()

    def mixed_grad(i):
        r = rows(0, i)
        h = x_all[r]
        t1[:, r] = h.astype(f32).T.astype(bf16)
        dmx[r] = dot_nn(h, wc[:, 3 * hw : 4 * hw]).astype(bf16)

    tiled(AT_MIXED_GRAD, seq // TR, mixed_grad)

    def out_grad_w(i):
        go[rows(0, i)] = dot_nn(t1[rows(0, i)], mixed[...]).astype(bf16)

    tiled(AT_OUT_GRAD_W, d_model // TR, out_grad_w)

    def attend_back(i):
        attn_bwd_pair(
            i, hw, length, qkv, mixed, lse, dmx, dk_acc, dv_acc, lambda b: at(i, [steps(AT_ATTEND_BACK, j * blocks + b) for j in range(pairs)])
        )
        cq, ck, cv = [pair_cols(i, group, hw) for group in range(3)]

        def grads(t):
            r = rows(0, t, ZR)
            gq, gk, gv = [dot_nn(ft[r], qkv[:, cc]) for cc in (cq, ck, cv)]
            o = go[r, cq].astype(f32)
            grp[0, i, r, 0:128] = pick(gq, gv).astype(bf16)
            grp[0, i, r, 128:256] = pick(gk, o).astype(bf16)
            grp[1, i, r, 0:128] = pick(gv, gq).astype(bf16)
            grp[1, i, r, 128:256] = pick(o, gk).astype(bf16)
            rp.first(i, t)

        loop(nz, grads)
        at(i, [steps(AT_GRADS, j) for j in range(pairs)])
        for cc, lo in ((cq, 0), (cv, hw)):
            to = pl.ds(pl.multiple_of(lo + i * 128, 128), 128)
            sm[ROW_B_QV : ROW_B_QV + 1, to] = jnp.sum(qkv[:, cc].astype(f32), axis=0, keepdims=True)

    loop(pairs, attend_back)

    def first_back(i, base):
        return dot_nt(qkv[rows(base, i)], wc[:, 0 : 3 * hw])

    def first_sib(i):
        s2[rows(0, i)] = first_back(i, sib0).astype(bf16)

    tiled(AT_FIRST_SIB, nt, first_sib)
    send_f = sib(6, s2, r4)
    send_f.start()

    def first_own(i):
        part[rows(0, i)] = first_back(i, own0)

    tiled(AT_FIRST_OWN, nt, first_own)
    send_f.wait_recv()

    def back_one(i):
        r = rows(0, i, 128)
        n, rr = norm_parts(tok[r].astype(f32))
        df = part[r] + r4[r].astype(f32)
        tgrad[r] = tgrad[r] + norm_back(n, rr, df, vec[3:4])
        for row, v in ((ROW_G_ONE, df * n), (ROW_C_ONE, df)):
            sm[row : row + 1] += jnp.sum(v, axis=0, keepdims=True)

    tiled(AT_BACK_ONE, half // 128, back_one)
    store_t = pltpu.make_async_copy(tgrad, tgrad_hbm, loc.at[0])
    store_t.start()

    def down(i, base):
        return dot_nt(act[rows(base, i), 0:ffq], w[0, 2]) + dot_nt(act[rows(base, i), ffq : 2 * ffq], w[1, 2])

    send_d.wait_send()

    def down_sib(i):
        s1[rows(0, i)] = down(i, sib0).astype(bf16)

    tiled(AT_DOWN_SIB, nt, down_sib)
    send_r = sib(7, s1, r2)
    send_r.start()
    def down_own(i):
        part[rows(0, i)] = down(i, own0)

    tiled(AT_DOWN_OWN, nt, down_own)
    send_r.wait_recv()

    def finish(i):
        r = rows(0, i, 128)
        v = result[r] + part[r] + r2[r].astype(f32) + vec[2:3]
        result[r] = jnp.where(valid((128, d_model), own0 + i * 128, length), v, 0.0)

    tiled(AT_FINISH, half // 128, finish)
    store_r = pltpu.make_async_copy(result, result_hbm, loc.at[1])
    store_r.start()
    mark(AT_END)

    for k in range(2):
        g.drain(k)
    gd.drain(2)
    gp2.drain()
    ar.drain(0)
    ar.drain(1)
    rd.drain(DOWN)
    rq.drain()
    ru.drain(UP)
    for k in range(3):
        rp.drain(k)
    for cp in (send_x, send_b, send_u, send_dr, send_s, send_dh, send_f, send_r):
        cp.wait_send()
    store_t.wait()
    store_r.wait()


def block(lens, tokens, ograd, w_qkv, w_out, w_up, w_down, b_qv, vectors, nz):
    half, d = tokens.shape
    heads_w = w_qkv.shape[2]
    seq = 2 * half
    nk, (rows, ffq) = NK, w_up.shape
    hw = d // 2
    pw = 256
    npair = hw // 128

    def V(shape, t=bf16):
        return pltpu.VMEM(shape, t)

    scratch = [
        V((half, d), f32), V((half, d), f32), V((half, d)), V((half, d)), V((rows, d)),
        V((2, nk, d, ffq)), V((d, 4 * hw)), V((hw, d)), V((seq, d)), V((seq, d)), V((seq, d)), V((d, seq)), V((d, seq)), V((d, seq)),
        V((seq, 3 * hw)), V((seq, hw)), V((2 * npair, 1, seq), f32), V((seq, 2 * ffq)), V((seq, 2 * ffq)), V((seq, hw)), V((d, hw)),
        V((half, d)), V((half, d)), V((half, d)), V((half, d)), V((half, d)), V((half, d)), V((half, d), f32),
        V((seq, 128), f32), V((seq, 128), f32), V((2, 2, heads_w), f32), V((2, 8, ffq), f32), V((8, d), f32), V((N_SUM, d), f32), V((2, 8, 8, d), f32), V((2, nz, 8, d), f32),
        V((2, 2, d, ffq)), V((2, npair, d, pw)),
        V((2, 1, nz, rows // 2, ffq - PLANE_SCATTER)), V((2, 1, nz, rows, ffq - PLANE_SCATTER)), V((1, nz - 1, rows, ffq - PLANE_SCATTER)),
        V((2, 1, nz, rows // 2, ffq)), V((2, 1, nz, rows, ffq)), V((1, nz - 1, rows, ffq)),
        V((2, npair, nz, rows // 2, pw)), V((2, npair, nz, rows, pw)), V((npair, nz - 1, rows, pw)),
        V((4, nz - 1, rows, PLANE_SCATTER)), V((3, rows, PLANE_SCATTER)),
    ]
    dma = pltpu.SemaphoreType.DMA
    sems = [dma((3, nk)), dma((8, nk)), dma((2,)), dma((4,)), dma((3, 1)), dma((9, 1)), dma((3, 1)), dma((9, 1)), dma((2,)), dma((7,)), dma((3, npair)), dma((9, npair))]
    sems += [dma((10,)), dma((10,)), dma((2, 2)), dma((2, 2)), dma((2 + nk,))]
    vm = pl.BlockSpec(memory_space=pltpu.VMEM)
    anywhere = pl.BlockSpec(memory_space=pl.ANY)
    return pl.pallas_call(
        block_kernel,
        out_shape=(
            jax.ShapeDtypeStruct((half, d), f32),
            jax.ShapeDtypeStruct((half, d), f32),
            jax.ShapeDtypeStruct((rows, ffq), f32),
            jax.ShapeDtypeStruct((rows, ffq), f32),
            jax.ShapeDtypeStruct((npair, rows, pw), f32),
            jax.ShapeDtypeStruct((N_SUM, d), f32),
        ),
        in_specs=[pl.BlockSpec(memory_space=pltpu.SMEM), anywhere, anywhere, vm, vm, anywhere, anywhere] + [vm] * (1 + len(vectors)),
        out_specs=(anywhere, anywhere, vm, vm, vm, vm),
        scratch_shapes=scratch + sems,
        compiler_params=pltpu.CompilerParams(collective_id=0, has_side_effects=True, vmem_limit_bytes=64 << 20),
    )(lens, tokens, ograd, w_qkv, w_out, w_up, w_down, b_qv, *vectors)


def finish_kernel(res_in, tg_in, up_in, down_in, outp_in, sums_in, *rest):
    outs, (held_r, held_t, held_u, held_d, outp, sums), made, (load_sem, store_sem) = rest[:14], rest[14:20], rest[20:30], rest[30:]
    res, tg, up, down = outs[:4]
    qkv, b_qv, w_out, b_up, *rows = made
    first = [pltpu.make_async_copy(a, b, load_sem.at[i]) for i, (a, b) in enumerate(((outp_in, outp), (sums_in, sums)))]
    for cp in first:
        cp.start()
    moves = []
    for source, held, to, n in ((tg_in, held_t, tg, 4), (res_in, held_r, res, 4), (up_in, held_u, up, 1), (down_in, held_d, down, 1)):
        size = held.shape[0] // n
        for i in range(n):
            part, j = pl.ds(i * size, size), len(moves)
            load = pltpu.make_async_copy(source.at[part], held.at[part], load_sem.at[2 + j])
            load.start()
            moves.append((load, pltpu.make_async_copy(held.at[part], to.at[part], store_sem.at[j])))
    for cp in first:
        cp.wait()
    second = lax.axis_index("y") == 1

    def ordered(a):
        return jnp.where(second, jnp.concatenate([a[:, HEAD_DIM:], a[:, :HEAD_DIM]], axis=1), a)

    a = [ordered(outp[h, :, : 2 * HEAD_DIM]) for h in range(outp.shape[0])]
    b = [ordered(outp[h, :, 2 * HEAD_DIM :]) for h in range(outp.shape[0])]
    qkv[0] = jnp.concatenate([v[:, :HEAD_DIM] for v in a], axis=1)
    qkv[1] = jnp.concatenate([v[:, :HEAD_DIM] for v in b], axis=1)
    qkv[2] = jnp.concatenate([v[:, HEAD_DIM:] for v in a], axis=1)
    w_out[...] = jnp.concatenate([v[:, HEAD_DIM:] for v in b], axis=1).T
    half = sums.shape[1] // 2
    for j in (0, 1):
        v = [ordered(sums[ROW_B_QV : ROW_B_QV + 1, j * half + 128 * h : j * half + 128 * h + 128]) for h in range(outp.shape[0])]
        b_qv[j : j + 1] = jnp.concatenate([c[:, HEAD_DIM * j : HEAD_DIM * (j + 1)] for c in v], axis=1)
    b_up[...] = jnp.where(second, sums[ROW_B_UP + 1], sums[ROW_B_UP])
    for ref, row in zip(rows, (ROW_B_OUT, ROW_B_DOWN, ROW_G_ONE, ROW_C_ONE, ROW_G_TWO, ROW_C_TWO)):
        ref[...] = sums[row]
    last = [pltpu.make_async_copy(src, dst, store_sem.at[len(moves) + i]) for i, (src, dst) in enumerate(zip(made, outs[4:]))]
    for cp in last:
        cp.start()
    for load, store in moves:
        load.wait()
        store.start()
    for cp in last + [store for _, store in moves]:
        cp.wait()


def finish(res, tg, up, down, outp, sums):
    n, (rows, ffq), d = outp.shape[0], up.shape, sums.shape[1]
    anywhere = pl.BlockSpec(memory_space=pl.ANY)
    big = [res.shape, tg.shape, up.shape, down.shape]
    made = [(3, rows, n * HEAD_DIM), (2, n * HEAD_DIM), (n * HEAD_DIM, rows), (ffq,)] + [(d,)] * 6
    return pl.pallas_call(
        finish_kernel,
        out_shape=[jax.ShapeDtypeStruct(s, f32) for s in big + made],
        in_specs=[anywhere] * 6,
        out_specs=[anywhere] * 14,
        scratch_shapes=[pltpu.VMEM(s, f32) for s in big + [outp.shape, sums.shape] + made] + [pltpu.SemaphoreType.DMA((12,)), pltpu.SemaphoreType.DMA((20,))],
    )(res, tg, up, down, outp, sums)


def per_device(tokens, lengths, w_qkv, b_qv, w_out, b_out, w_up, b_up, w_down, b_down, g_one, c_one, g_two, c_two, out_grad, *, nz, sub):
    if sub > 1:
        w_qkv, w_up = lax.all_gather(w_qkv, "r", axis=1, tiled=True), lax.all_gather(w_up, "r", axis=0, tiled=True)
        w_out, w_down = [lax.all_gather(a, "r", axis=1, tiled=True) for a in (w_out, w_down)]
    vectors = (b_up, b_out, b_down, g_one, c_one, g_two, c_two)
    result, tokens_grad, up, down, outp, sums = block(lengths, tokens, out_grad, w_qkv, w_out, w_up, w_down.T, b_qv, vectors, nz)
    if sub > 1:
        up, down = [lax.psum_scatter(a, "r", scatter_dimension=0, tiled=True) for a in (up, down)]
        outp = lax.psum_scatter(outp, "r", scatter_dimension=1, tiled=True)
        sums = lax.psum(sums, "r")
    result, tokens_grad, up, down, qkv, b_qv, w_out, b_up, b_out, b_down, *norms = finish(result, tokens_grad, up, down, outp, sums)
    return (result, tokens_grad, qkv, b_qv, w_out, b_out, up, b_up, down.T, b_down, *norms)


def solution(mesh):
    dp, tensor = mesh.shape["dp"], mesh.shape["tensor"]
    line = 4 * NX
    nz, sub = line // NX, dp // line
    grid = Mesh(mesh.devices.reshape(line, sub, tensor // 2, 2), ("e", "r", "y", "c"))
    dpx, tx = ("e", "r"), ("y", "c")
    rows = P(dpx + tx, None)
    return jax.shard_map(
        functools.partial(per_device, nz=nz, sub=sub),
        mesh=grid,
        in_specs=(rows, P(dpx), P(None, dpx, tx), P(None, tx), P(tx, dpx), P(), P(dpx, tx), P(tx), P(tx, dpx), P(), P(), P(), P(), P(), rows),
        out_specs=(rows, rows, P(None, dpx, tx), P(None, tx), P(tx, dpx), P(), P(dpx, tx), P(tx), P(tx, dpx), P(), P(), P(), P(), P()),
        check_vma=False,
    )
```

```python
import functools
import math

import jax
import jax.numpy as jnp
from jax import lax
from jax.experimental import pallas as pl
from jax.experimental.pallas import tpu as pltpu
from jax.sharding import Mesh
from jax.sharding import PartitionSpec as P

HEAD_DIM = 64
EPSILON = 1e-05
MESH = pl.DeviceIdType.MESH
NX = 2
NK = 3

class Place:
    def __init__(self, nz):
        self.nz = nz
        self.e = lax.axis_index("e"); self.y = lax.axis_index("y")
        self.z = self.e // NX; self.x = self.e % NX
        self.xn = {"e": self.e + 1 - 2 * self.x}
        self.yn = {"y": 1 - self.y}
        self.up = {"e": self.e + NX}
        self.dn = {"e": self.e - NX}
        self.core = {"c": 1 - lax.axis_index("c")}

BQ = 256
NEG = -1e30
f32, bf16 = jnp.float32, jnp.bfloat16
def dot_nt(a, b): return lax.dot_general(a, b, (((1,), (1,)), ((), ())), preferred_element_type=f32)
def dot_nn(a, b): return lax.dot_general(a, b, (((1,), (0,)), ((), ())), preferred_element_type=f32)
def flip(a): return a.astype(f32).T.astype(bf16)

def pair_cols(p, group, width):
    return pl.ds(pl.multiple_of(group * width + p * 128, 128), 128)

def masked_keys(k, j, length):
    n = k.shape[0]
    lane = lax.broadcasted_iota(jnp.int32, (n, 128), 1)
    row = lax.broadcasted_iota(jnp.int32, (n, 128), 0)
    out = jnp.where((lane == 64 * (1 - j)) & (row >= length), NEG, 0.0)
    return jnp.where(lane // 64 == j, k.astype(f32), out).astype(bf16)

def with_one(q, j):
    lane = lax.broadcasted_iota(jnp.int32, q.shape, 1)
    return jnp.where(lane == 64 * (1 - j), 1.0, q.astype(f32)).astype(bf16)

def only(a, h):
    lane = lax.broadcasted_iota(jnp.int32, a.shape, 1)
    return jnp.where(lane // 64 == h, a.astype(f32), 0.0).astype(bf16)

def causal(s, i):
    n = s.shape[0] - BQ
    row = lax.broadcasted_iota(jnp.int32, (BQ, BQ), 0)
    col = lax.broadcasted_iota(jnp.int32, (BQ, BQ), 1)
    d = jnp.where(row <= col, s[n:], NEG)
    return d if n == 0 else jnp.concatenate([s[:n], d], axis=0)

def attn_fwd_pair(p, width, length, qkv, mixed, lse, hook):
    n = qkv.shape[0]
    k = qkv[:, pair_cols(p, 1, width)]
    vt = flip(qkv[:, pair_cols(p, 2, width)])
    kp = [masked_keys(k, j, length) for j in (0, 1)]
    for i in range(n // BQ):
        hi = (i + 1) * BQ
        q = qkv[i * BQ:hi, pair_cols(p, 0, width)]
        outs = []
        for j in (0, 1):
            s = causal(dot_nt(kp[j][:hi], with_one(q, j)), i)
            m = jnp.max(s, axis=0, keepdims=True)
            e = jnp.exp(s - m)
            l = jnp.sum(e, axis=0, keepdims=True)
            o = dot_nn(vt[64 * (1 - j):64 * (2 - j), :hi], e.astype(bf16))
            outs.append(o * (1.0 / l))
            lse[2 * p + j, :, i * BQ:hi] = m + jnp.log(l)
        mixed[i * BQ:hi, pair_cols(p, 0, width)] = jnp.concatenate(outs[::-1], axis=0).T.astype(bf16)
        hook(i)

def attn_bwd_pair(p, width, length, qkv, mixed, lse, dmixed, dk_acc, dv_acc, hook):
    n = qkv.shape[0]
    c0, c1, c2 = [pair_cols(p, g, width) for g in range(3)]
    k = qkv[:, c1]
    kt = flip(k)
    v = qkv[:, c2]
    kp = [masked_keys(k, j, length) for j in (0, 1)]
    dk_acc[...] = jnp.zeros_like(dk_acc); dv_acc[...] = jnp.zeros_like(dv_acc)
    for i in range(n // BQ):
        hi = (i + 1) * BQ
        q = qkv[i * BQ:hi, c0]
        do = dmixed[i * BQ:hi, c0]
        prod = (do.astype(f32) * mixed[i * BQ:hi, c0].astype(f32)).T
        dq = []
        for j in (0, 1):
            vh = 1 - j
            delta = jnp.sum(prod[64 * vh:64 * (vh + 1)], axis=0, keepdims=True)
            dom = only(do, vh)
            s = causal(dot_nt(kp[j][:hi], with_one(q, j)), i)
            w = jnp.exp(s - lse[2 * p + j, :, i * BQ:hi])
            dw = dot_nt(v[:hi], dom)
            ds = (w * (dw - delta)).astype(bf16)
            dv_acc[:hi] += dot_nn(w.astype(bf16), dom)
            dk_acc[:hi] += dot_nn(ds, only(q, j))
            dq.append(dot_nn(kt[64 * j:64 * (j + 1), :hi], ds))
        qkv[i * BQ:hi, c0] = (jnp.concatenate(dq, axis=0).T * 0.125).astype(bf16)
        hook(i)
    qkv[:, c1] = dk_acc[...].astype(bf16)
    qkv[:, c2] = dv_acc[...].astype(bf16)


class Pieces:
    def __init__(self, p, full, lo, width, ssem, rsem):
        self.p, self.full, self.lo, self.width, self.ssem, self.rsem = p, full, lo, width, ssem, rsem
        self.rows = full.shape[2] // (p.nz * NX)

    def piece(self, yq, k, e, half=None):
        n = self.rows if half is None else self.rows // 2
        at_row = e * self.rows + (half or 0) * n
        return self.full.at[yq, k, pl.ds(pl.multiple_of(at_row, 16), n), pl.ds(self.lo, self.width)]

    def span(self, k, n):
        return self.full.at[0, k, pl.ds(0, n * self.rows), pl.ds(self.lo, self.width)]

    def z(self, r):
        return (self.p.z + r + self.p.nz) % self.p.nz

    def home(self, k):
        return self.out[k] if isinstance(self.out, tuple) else self.out.at[k]

    def wire(self, s, t, dev, out_at, in_at):
        return remote(s, t, self.ssem.at[out_at], self.rsem.at[in_at], dev)

    def await_in(self, ref, in_at):
        remote(ref, ref, self.ssem.at[(0,) * len(self.ssem.shape)], self.rsem.at[in_at], self.p.xn).wait_recv()

    def await_out(self, ref, out_at):
        remote(ref, ref, self.ssem.at[out_at], self.rsem.at[(0,) * len(self.rsem.shape)], self.p.xn).wait_send()


class Gather(Pieces):
    def __init__(self, p, own, *rest):
        super().__init__(p, *rest)
        self.own = own

    def mine(self, k):
        return self.own[k].at[:, pl.ds(self.lo, self.width)]

    def copy(self, kind, k, r):
        p = self.p
        back = self.z(-r)
        if kind == 0:
            s, t, dev = self.mine(k), self.piece(p.y, k, p.e), {"e": self.z(r) * NX + p.x}
        elif kind in (1, 2):
            t = self.piece(p.y, k, back * NX + p.x)
            s, dev = (t if r else self.mine(k)), (p.xn, p.yn)[kind - 1]
        elif kind == 3:
            s = t = self.piece(p.y, k, back * NX + 1 - p.x, 0)
            dev = p.yn
        else:
            s = t = self.piece(1 - p.y, k, back * NX + p.x, 1)
            dev = p.xn
        group = (kind + 1) // 2
        return self.wire(s, t, dev, (group, k), ((r - 1, 3 + r, 7)[group], k))

    def own_z(self, k):
        nz = self.p.nz
        for r in [1, nz - 1] + list(range(2, nz - 1)):
            self.copy(0, k, r).start()

    def own_xy(self, k):
        self.copy(1, k, 0).start()
        self.copy(2, k, 0).start()

    def pass_on(self, k, r):
        self.await_in(self.span(k, 1), (r - 1, k))
        self.copy(1, k, r).start()
        self.copy(2, k, r).start()

    def turn(self, k, r):
        self.await_in(self.span(k, 2), (3 + r, k))
        self.copy(3, k, r).start()
        self.copy(4, k, r).start()

    def final(self, k):
        self.await_in(self.span(k, self.p.nz), (7, k))

    def drain(self, k):
        nz = self.p.nz
        for group, n in enumerate((nz - 1, 2 * nz, nz)):
            self.await_out(self.span(k, n), (group, k))


class PlaneGather(Pieces):
    def __init__(self, p, own, k, *rest):
        super().__init__(p, *rest)
        self.own, self.k = own, k

    def spot(self, q, z):
        p = self.p
        return self.piece(1 - p.y if q >= 2 else p.y, self.k, z * NX + (1 - p.x if q % 2 else p.x))

    def mine(self):
        return self.own[self.k].at[:, pl.ds(self.lo, self.width)]

    def copy(self, q, r):
        p = self.p
        if r:
            t = self.spot(q, p.z)
            return self.wire(t if q else self.mine(), t, {"e": self.z(r) * NX + p.x}, (1,), (3,))
        if q == 3:
            t = self.spot(1, p.z)
            return self.wire(t, t, p.yn, (0,), (2,))
        return self.wire(self.mine(), self.spot(0, p.z), (p.xn, p.yn)[q - 1], (0,), (q - 1,))

    def lined(self):
        half = (self.p.nz - 1) * 2
        return self.full.at[pl.ds(0, 2), self.k, pl.ds(0, half * self.rows), pl.ds(self.lo, self.width)]

    def spread(self, q):
        if q:
            self.await_in(self.span(self.k, 1), (q - 1,))
            if q == 1:
                self.copy(3, 0).start()
        else:
            self.copy(1, 0).start()
            self.copy(2, 0).start()
        for r in range(1, self.p.nz):
            self.copy(q, r).start()

    def final(self):
        self.await_in(self.lined(), (3,))

    def drain(self):
        self.await_out(self.span(self.k, 3), (0,))
        self.await_out(self.lined(), (1,))


class Scatter(Pieces):
    def __init__(self, p, bd, bxy, bz, out, *rest):
        super().__init__(p, *rest)
        self.bd, self.bxy, self.bz, self.out = bd, bxy, bz, out

    def slot(self, k):
        return k if self.bd.shape[1] > 1 else 0

    def copy(self, kind, k, d):
        p, b = self.p, self.slot(k)
        if kind == 0:
            s, t, dev = self.piece(1 - p.y, k, d * NX + 1 - p.x, 0), self.bd.at[0, b, d], p.yn
        elif kind == 1:
            s, t, dev = self.piece(1 - p.y, k, d * NX + 1 - p.x, 1), self.bd.at[1, b, d], p.xn
        elif kind == 2:
            s, t, dev = self.piece(p.y, k, d * NX + 1 - p.x), self.bxy.at[0, b, d], p.xn
        elif kind == 3:
            s, t, dev = self.piece(1 - p.y, k, d * NX + p.x), self.bxy.at[1, b, d], p.yn
        else:
            e = self.z(d) * NX + p.x
            s, t, dev = self.piece(p.y, k, e), self.bz.at[b, d - 1], {"e": e}
        group = kind // 2
        return self.wire(s, t, dev, (group, b), ((d, p.nz + d, 2 * p.nz)[group], b))

    def first(self, k, d):
        self.copy(0, k, d).start()
        self.copy(1, k, d).start()

    def second(self, k, r):
        p, b, d = self.p, self.slot(k), self.z(r)
        self.await_in(self.bd.at[pl.ds(0, 2), b, d], (d, b))
        ref = self.piece(p.y, k, d * NX + 1 - p.x, 0)
        ref[...] = (ref[...].astype(f32) + self.bd[0, b, d].astype(f32)).astype(bf16)
        self.copy(2, k, d).start()
        ref = self.piece(1 - p.y, k, d * NX + p.x, 1)
        ref[...] = (ref[...].astype(f32) + self.bd[1, b, d].astype(f32)).astype(bf16)
        self.copy(3, k, d).start()

    def third(self, k, r):
        p, b, d = self.p, self.slot(k), self.z(r)
        self.await_in(self.bxy.at[pl.ds(0, 2), b, d], (p.nz + d, b))
        ref = self.piece(p.y, k, d * NX + p.x)
        total = ref[...].astype(f32) + self.bxy[0, b, d].astype(f32) + self.bxy[1, b, d].astype(f32)
        if r == 0:
            self.home(k)[:, self.lo : self.lo + self.width] = total
        else:
            ref[...] = total.astype(bf16)
            self.copy(4, k, r).start()

    def final(self, k):
        b = self.slot(k)
        cols = slice(self.lo, self.lo + self.width)
        self.await_in(self.bz.at[b], (2 * self.p.nz, b))
        total = self.home(k)[:, cols]
        for r in range(1, self.p.nz):
            total = total + self.bz[b, r - 1].astype(f32)
        self.home(k)[:, cols] = total

    def drain(self, k):
        nz, b = self.p.nz, self.slot(k)
        for group, n in enumerate((nz, 2 * nz, nz - 1)):
            self.await_out(self.span(k, n), (group, b))


class PlaneScatter(Pieces):
    def __init__(self, p, k, bz, bq, out, *rest):
        super().__init__(p, *rest)
        self.k, self.bz, self.bq, self.out = k, bz, bq, out

    def spot(self, q, z):
        p = self.p
        return self.piece(1 - p.y if q >= 2 else p.y, self.k, z * NX + (1 - p.x if q % 2 else p.x))

    def copy(self, q, r):
        p = self.p
        if r:
            return self.wire(self.spot(q, self.z(r)), self.bz.at[q, r - 1], {"e": self.z(r) * NX + p.x}, (1,), (q,))
        return self.wire(self.spot(q, p.z), self.bq.at[q - 1], p.yn if q == 2 else p.xn, (0,), (3 + q,))

    def first(self):
        for r in range(1, self.p.nz):
            for q in (3, 2, 1, 0):
                self.copy(q, r).start()

    def plane_sum(self, q):
        self.await_in(self.bz.at[q], (q,))
        total = self.spot(q, self.p.z)[...].astype(f32)
        for r in range(1, self.p.nz):
            total = total + self.bz[q, r - 1].astype(f32)
        return total

    def second(self):
        for q in (3, 1):
            self.spot(q, self.p.z)[...] = self.plane_sum(q).astype(bf16)
            self.copy(q, 0).start()

    def third(self):
        total = self.plane_sum(2)
        self.await_in(self.bq.at[2], (6,))
        self.spot(2, self.p.z)[...] = (total + self.bq[2].astype(f32)).astype(bf16)
        self.copy(2, 0).start()

    def final(self):
        total = self.plane_sum(0)
        for q in (1, 2):
            self.await_in(self.bq.at[q - 1], (3 + q,))
            total = total + self.bq[q - 1].astype(f32)
        self.home(self.k)[:, self.lo : self.lo + self.width] = total

    def drain(self):
        half = (self.p.nz - 1) * 2
        self.await_out(self.span(self.k, 3), (0,))
        self.await_out(self.full.at[pl.ds(0, 2), self.k, pl.ds(0, half * self.rows), pl.ds(self.lo, self.width)], (1,))


class Sums:
    def __init__(self, p, own, plane_buf, line_buf, out, peers, column, ssem, rsem):
        self.p, self.own, self.plane_buf, self.line_buf, self.out = p, own, plane_buf, line_buf, out
        self.peers, self.column, self.ssem, self.rsem = peers, column, ssem, rsem

    def tile(self, ref, t):
        return ref.at[pl.ds(8 * t, 8)]

    def wire(self, s, t, stage, tile, dev):
        return remote(s, t, self.ssem.at[tile, stage], self.rsem.at[tile, stage], dev)

    def plane_all(self, t):
        ref = self.plane_buf.at[t, pl.ds(1, len(self.peers))]
        return self.wire(ref, ref, 0, t, self.p.xn)

    def plane(self, t):
        for i, dev in self.peers:
            self.wire(self.tile(self.own, t), self.plane_buf.at[t, i], 0, t, dev).start()

    def line(self, t):
        row = lax.broadcasted_iota(jnp.int32, self.plane_buf.shape[2:], 0)
        lo, hi = SPLIT_ROWS[t]
        self.plane_all(t).wait_recv()
        total = self.own[8 * t : 8 * t + 8]
        for i, dev in self.peers:
            part = self.plane_buf[t, i]
            total = total + (jnp.where((row >= lo) & (row < hi), 0.0, part) if i % 2 else part)
        self.out[8 * t : 8 * t + 8] = total
        for r, dev in self.column:
            self.wire(self.tile(self.out, t), self.line_buf.at[t, r], 1, t, dev).start()

    def done(self, t):
        ref = self.line_buf.at[t, pl.ds(1, len(self.column))]
        both = self.wire(ref, ref, 1, t, self.p.xn)
        both.wait_recv()
        both.wait_send()
        total = self.out[8 * t : 8 * t + 8]
        for r, dev in self.column:
            total = total + self.line_buf[t, r]
        self.out[8 * t : 8 * t + 8] = total

    def drain(self, t):
        self.plane_all(t).wait_send()


def remote(src, dst, ssem, rsem, dev):
    return pltpu.make_async_remote_copy(src, dst, ssem, rsem, device_id=dev, device_id_type=MESH)


def loop(n, fn, after=()):
    def body(i, carry):
        fn(i)
        at(i, after)
        return carry

    lax.fori_loop(0, n, body, 0)


def at(i, steps):
    for j, todo in enumerate(steps):
        if todo:

            @pl.when(i == j)
            def _(todo=todo):
                for f in todo:
                    f()


def pick(a, b):
    lane = lax.broadcasted_iota(jnp.int32, a.shape, 1)
    return jnp.where(lane % 128 < 64, a.astype(f32), b.astype(f32))


def norm_parts(v):
    center = v - jnp.mean(v, axis=-1, keepdims=True)
    r = lax.rsqrt(jnp.mean(center * center, axis=-1, keepdims=True) + EPSILON)
    return center * r, r


def norm_back(n, r, d, gain):
    q = d * gain
    return r * (q - jnp.mean(q, axis=-1, keepdims=True) - n * jnp.mean(q * n, axis=-1, keepdims=True))


def gelu_both(u):
    a, b = math.sqrt(2.0 / math.pi), 0.044715
    u2 = u * u
    t = jnp.tanh(a * u * (1.0 + b * u2))
    h = 0.5 + 0.5 * t
    return u * h, h + (0.5 * a) * u * (1.0 - t * t) * (1.0 + (3.0 * b) * u2)


def valid(shape, base, length):
    return base + lax.broadcasted_iota(jnp.int32, shape, 0) < length


N_SUM = 16
ROW_B_OUT, ROW_B_DOWN, ROW_G_TWO, ROW_C_TWO, ROW_B_UP, ROW_G_ONE, ROW_C_ONE, ROW_B_QV = 0, 1, 2, 3, 4, 8, 9, 10
SPLIT_ROWS = ((4, 6), (2, 3))
PLANE_GATHER, PLANE_SCATTER = 128, 256
AT_BEGIN, AT_NORM_A, AT_NORM_B, AT_MASK_A, AT_MASK_B, AT_WAIT_0, AT_COLLECT, AT_PROJECT, AT_ATTEND, AT_OUT_SIB, AT_OUT_OWN, AT_NORM_TWO, AT_WAIT_1, AT_UP_A, AT_UP_B, AT_DOWN_GRAD, AT_WAIT_2, AT_PRE_GRAD, AT_SECOND_SIB, AT_SECOND_OWN, AT_UP_GRAD, AT_BACK_TWO, AT_MIXED_GRAD, AT_OUT_GRAD_W, AT_ATTEND_BACK, AT_GRADS, AT_FIRST_SIB, AT_FIRST_OWN, AT_BACK_ONE, AT_DOWN_SIB, AT_DOWN_OWN, AT_FINISH, AT_END = range(33)
IN_G, IN_GD, IN_GP, IN_RD, IN_RQ, IN_RU, IN_RP, IN_AR = range(8)
DO_OWN_XY, DO_OWN_Z, DO_PASS_ON, DO_TURN, DO_SPREAD, DO_FIRST, DO_SECOND, DO_THIRD, DO_FINAL, DO_PLANE, DO_LINE, DO_DONE = range(12)
METHODS = (
    lambda part: part.own_xy,
    lambda part: part.own_z,
    lambda part: part.pass_on,
    lambda part: part.turn,
    lambda part: part.spread,
    lambda part: part.first,
    lambda part: part.second,
    lambda part: part.third,
    lambda part: part.final,
    lambda part: part.plane,
    lambda part: part.line,
    lambda part: part.done,
)
PLAN = {
    (AT_BEGIN, 0): ((IN_G, DO_OWN_Z, 0), (IN_GP, DO_SPREAD, 0),),
    (AT_NORM_A, 1): ((IN_G, DO_OWN_XY, 1), (IN_G, DO_OWN_Z, 1),),
    (AT_NORM_B, 0): ((IN_G, DO_OWN_XY, 0), (IN_GP, DO_SPREAD, 1),),
    (AT_NORM_B, 1): ((IN_GD, DO_OWN_Z, 2),),
    (AT_MASK_A, 2): ((IN_GP, DO_SPREAD, 2),),
    (AT_MASK_B, 1): ((IN_G, DO_TURN, 1, 0),),
    (AT_WAIT_0, 0): ((IN_G, DO_PASS_ON, 0, 3), (IN_G, DO_TURN, 0, 0), (IN_GP, DO_SPREAD, 3), (IN_G, DO_TURN, 0, 3), (IN_G, DO_PASS_ON, 0, 2), (IN_G, DO_PASS_ON, 0, 1), (IN_G, DO_TURN, 0, 2), (IN_G, DO_TURN, 0, 1),),
    (AT_COLLECT, 0): ((IN_G, DO_PASS_ON, 1, 3),),
    (AT_PROJECT, 3): ((IN_GD, DO_OWN_XY, 2),),
    (AT_ATTEND, 1): ((IN_G, DO_TURN, 1, 3),),
    (AT_ATTEND, 3): ((IN_G, DO_PASS_ON, 1, 2), (IN_GD, DO_TURN, 2, 0),),
    (AT_ATTEND, 6): ((IN_G, DO_PASS_ON, 1, 1),),
    (AT_ATTEND, 9): ((IN_G, DO_TURN, 1, 2),),
    (AT_OUT_SIB, 0): ((IN_GD, DO_PASS_ON, 2, 3),),
    (AT_OUT_OWN, 0): ((IN_G, DO_TURN, 1, 1),),
    (AT_NORM_TWO, 2): ((IN_GD, DO_PASS_ON, 2, 2),),
    (AT_UP_A, 0): ((IN_GD, DO_PASS_ON, 2, 1), (IN_GD, DO_TURN, 2, 3),),
    (AT_UP_A, 1): ((IN_GD, DO_TURN, 2, 2),),
    (AT_UP_B, 1): ((IN_GD, DO_TURN, 2, 1),),
    (AT_DOWN_GRAD, 1): ((IN_RD, DO_FIRST, 1, 1),),
    (AT_DOWN_GRAD, 2): ((IN_RD, DO_FIRST, 1, 2),),
    (AT_DOWN_GRAD, 3): ((IN_RQ, DO_FIRST), (IN_RD, DO_FIRST, 1, 3),),
    (AT_WAIT_2, 0): ((IN_RD, DO_FIRST, 1, 0),),
    (AT_PRE_GRAD, 2): ((IN_RD, DO_SECOND, 1, 0), (IN_RD, DO_SECOND, 1, 2), (IN_RD, DO_SECOND, 1, 1),),
    (AT_SECOND_SIB, 1): ((IN_RD, DO_SECOND, 1, 3),),
    (AT_SECOND_OWN, 0): ((IN_RD, DO_THIRD, 1, 0),),
    (AT_SECOND_OWN, 1): ((IN_RD, DO_THIRD, 1, 2),),
    (AT_UP_GRAD, 2): ((IN_RD, DO_THIRD, 1, 1),),
    (AT_BACK_TWO, 1): ((IN_RD, DO_THIRD, 1, 3),),
    (AT_MIXED_GRAD, 0): ((IN_AR, DO_PLANE, 0),),
    (AT_MIXED_GRAD, 2): ((IN_RU, DO_SECOND, 0, 0), (IN_RU, DO_SECOND, 0, 2), (IN_RU, DO_SECOND, 0, 1), (IN_RU, DO_SECOND, 0, 3),),
    (AT_ATTEND_BACK, 1): ((IN_AR, DO_LINE, 0),),
    (AT_ATTEND_BACK, 2): ((IN_RQ, DO_SECOND),),
    (AT_ATTEND_BACK, 3): ((IN_RU, DO_THIRD, 0, 0),),
    (AT_ATTEND_BACK, 4): ((IN_RU, DO_THIRD, 0, 2),),
    (AT_ATTEND_BACK, 7): ((IN_AR, DO_DONE, 0), (IN_RD, DO_FINAL, 1), (IN_RU, DO_THIRD, 0, 1),),
    (AT_GRADS, 1): ((IN_RQ, DO_THIRD), (IN_RU, DO_THIRD, 0, 3),),
    (AT_ATTEND_BACK, 10): ((IN_RP, DO_SECOND, 0, 3), (IN_RP, DO_SECOND, 0, 2),),
    (AT_ATTEND_BACK, 11): ((IN_RQ, DO_FINAL), (IN_RP, DO_SECOND, 0, 0), (IN_RP, DO_SECOND, 1, 3), (IN_RP, DO_SECOND, 1, 1), (IN_RP, DO_SECOND, 1, 0), (IN_RP, DO_SECOND, 0, 1), (IN_RP, DO_THIRD, 0, 3), (IN_RP, DO_THIRD, 0, 2),),
    (AT_GRADS, 2): ((IN_RP, DO_THIRD, 0, 0), (IN_RU, DO_FINAL, 0),),
    (AT_FIRST_OWN, 0): ((IN_RP, DO_SECOND, 1, 2), (IN_RP, DO_THIRD, 1, 1), (IN_RP, DO_THIRD, 1, 3),),
    (AT_FIRST_OWN, 1): ((IN_RP, DO_THIRD, 1, 0),),
    (AT_BACK_ONE, 0): ((IN_RP, DO_THIRD, 0, 1),),
    (AT_BACK_ONE, 1): ((IN_RP, DO_SECOND, 2, 3), (IN_RP, DO_SECOND, 2, 1), (IN_RP, DO_SECOND, 2, 2), (IN_RP, DO_SECOND, 2, 0),),
    (AT_BACK_ONE, 2): ((IN_RP, DO_THIRD, 1, 2),),
    (AT_BACK_ONE, 3): ((IN_RP, DO_THIRD, 2, 3), (IN_AR, DO_PLANE, 1), (IN_RP, DO_FINAL, 0),),
    (AT_DOWN_SIB, 0): ((IN_RP, DO_THIRD, 2, 1),),
    (AT_DOWN_OWN, 0): ((IN_RP, DO_THIRD, 2, 2), (IN_RP, DO_THIRD, 2, 0), (IN_RP, DO_FINAL, 1),),
    (AT_END, 0): ((IN_AR, DO_LINE, 1), (IN_RP, DO_FINAL, 2), (IN_AR, DO_DONE, 1),),
}


def block_kernel(
    lens, tokens, ograd, w_qkv, w_out, w_up, w_down, b_qv, b_up, b_out, b_down, g_one, c_one, g_two, c_two,
    result_hbm, tgrad_hbm, up_out, down_out, outp, sums,
    result, tgrad, tok, og, packed, w, wc, wo, x_all, sec, dr, t1, t2, ft, qkv, mixed, lse, act, gp, dmx, go,
    r1, r2, r3, r4, s1, s2, part, dk_acc, dv_acc, bias, bias_up, vec, sm, ar1, ar2,
    grf, grp, dd, dxy, dz, ud, uxy, uz, pd, pxy, pz, qz, qq,
    g_ss, g_rs, q_ss, q_rs, d_ss, d_rs, u_ss, u_rs, v_ss, v_rs, p_ss, p_rs, sib_ss, sib_rs, ar_ss, ar_rs, loc,
):
    nz = ar2.shape[1]
    p = Place(nz)
    c = lax.axis_index("c")
    half, d_model = tokens.shape
    seq = 2 * half
    hw = mixed.shape[1]
    TR = 256
    nt = half // TR
    length = lens[p.y]
    own0, sib0 = c * half, (1 - c) * half

    def rows(base, i, n=TR):
        return pl.ds(pl.multiple_of(base + i * n, n), n)

    load_t = pltpu.make_async_copy(tokens, tok, loc.at[0])
    load_g = pltpu.make_async_copy(ograd, og, loc.at[1])
    load_t.start()
    load_g.start()
    peers = []
    for dx in (0, 1):
        for dy in (0, 1):
            for dc in (0, 1):
                if dx + dy + dc:
                    peers.append((4 * dx + 2 * dy + dc, {"e": p.e + dx * (1 - 2 * p.x), "y": p.y + dy * (1 - 2 * p.y), "c": c + dc * (1 - 2 * c)}))
    column = [(r, {"e": ((p.z + r) % nz) * NX + p.x}) for r in range(1, nz)]
    bar = pltpu.get_barrier_semaphore()
    for _, dev in peers + column:
        pl.semaphore_signal(bar, 1, device_id=dev, device_id_type=MESH)
    for j, ref in enumerate((b_up, b_out, b_down, g_one, c_one, g_two, c_two)):
        vec[j] = ref[...]

    flip_lanes = p.y == 1
    for h in range(hw // 128):
        s = slice(HEAD_DIM * h, HEAD_DIM * (h + 1))
        q, k, v = [w_qkv[j][:, s].astype(f32) for j in range(3)]
        o = w_out[s, :].astype(f32).T
        for j, (lo, hi) in enumerate(((q, v), (k, o))):
            put = jnp.where(flip_lanes, jnp.concatenate([hi, lo], axis=1), jnp.concatenate([lo, hi], axis=1))
            packed[:, 256 * h + 128 * j : 256 * h + 128 * j + 128] = put.astype(bf16)
    pl.semaphore_wait(bar, len(peers) + len(column))

    def sib(i, src, dst):
        return remote(src, dst, sib_ss.at[i], sib_rs.at[i], p.core)

    DOWN, UP = 1, 0
    ffq = w.shape[3]
    gcut, rcut = ffq - PLANE_GATHER, ffq - PLANE_SCATTER
    shard = (packed, w_up, w_down)
    g = Gather(p, shard, w, 0, ffq, g_ss, g_rs)
    gd = Gather(p, shard, w, 0, gcut, g_ss, g_rs)
    gp2 = PlaneGather(p, shard, 2, w, gcut, ffq - gcut, q_ss, q_rs)
    outf = (up_out, down_out)
    ru = Scatter(p, ud, uxy, uz, outf, grf, 0, ffq, u_ss, u_rs)
    rd = Scatter(p, dd, dxy, dz, outf, grf, 0, rcut, d_ss, d_rs)
    rq = PlaneScatter(p, DOWN, qz, qq, outf, grf, rcut, ffq - rcut, v_ss, v_rs)
    rp = Scatter(p, pd, pxy, pz, outp, grp, 0, grp.shape[3], p_ss, p_rs)
    ar = Sums(p, sm, ar1, ar2, sums, peers, column, ar_ss, ar_rs)
    parts = (g, gd, gp2, rd, rq, ru, rp, ar)

    def steps(name, i=0):
        return [lambda t=t: METHODS[t[1]](parts[t[0]])(*t[2:]) for t in PLAN.get((name, i), ())]

    def mark(name):
        for f in steps(name):
            f()

    def tiled(name, n, fn):
        loop(n, fn, [steps(name, i) for i in range(n)])

    x_own, x_sib = x_all.at[rows(own0, 0, half)], x_all.at[rows(sib0, 0, half)]
    mark(AT_BEGIN)
    send_x = sib(0, tokens, x_own)
    send_x.start()
    send_dr = sib(1, ograd, dr.at[rows(own0, 0, half)])
    send_dr.start()
    send_b = remote(b_qv, bias.at[p.y], sib_ss.at[8], sib_rs.at[8], p.yn)
    send_u = remote(vec, bias_up.at[p.y], sib_ss.at[9], sib_rs.at[9], p.yn)
    send_b.start()
    send_u.start()
    keep = [pltpu.make_async_copy(shard[j], w.at[p.y, j, pl.ds(pl.multiple_of(p.e * packed.shape[0], 16), packed.shape[0])], loc.at[2 + j]) for j in range(NK)]
    for cp in keep:
        cp.start()
    bias[p.y] = b_qv[...]
    bias_up[p.y] = vec[...]
    sm[...] = jnp.zeros_like(sm)

    def norm_one(name, base, src, lo):
        def one(i):
            v = src[rows(lo, i, 128)].astype(f32)
            n, _ = norm_parts(v)
            f = n * vec[3:4] + vec[4:5]
            sec[rows(base, i, 128)] = f.astype(bf16)
            ft[:, rows(base, i, 128)] = f.astype(bf16).astype(f32).T.astype(bf16)

        tiled(name, half // 128, one)

    def mask_rows(name, base, src, lo):
        def one(i):
            v = jnp.where(valid((128, d_model), base + i * 128, length), src[rows(lo, i, 128)].astype(f32), 0.0)
            dr[rows(base, i, 128)] = v.astype(bf16)
            t1[:, rows(base, i, 128)] = v.T.astype(bf16)

        tiled(name, half // 128, one)

    load_t.wait()
    norm_one(AT_NORM_A, own0, tok, 0)
    send_x.wait_recv()
    norm_one(AT_NORM_B, sib0, x_all, sib0)
    load_g.wait()
    mask_rows(AT_MASK_A, own0, og, 0)
    send_dr.wait_recv()
    mask_rows(AT_MASK_B, sib0, dr, sib0)
    for cp in keep:
        cp.wait()
    mark(AT_WAIT_0)
    g.final(0)

    def collect(i):
        r = rows(0, i)
        for q in range(hw // 128):
            a = [w[yq, 0, r, q * 256 : q * 256 + 128] for yq in (0, 1)]
            b = [w[yq, 0, r, q * 256 + 128 : q * 256 + 256] for yq in (0, 1)]
            for group, v in enumerate((pick(a[0], a[1]), pick(b[0], b[1]), pick(a[1], a[0]), pick(b[1], b[0]))):
                wc[r, group * hw + q * 128 : group * hw + q * 128 + 128] = v.astype(bf16)
                if group == 3:
                    wo[q * 128 : q * 128 + 128, r] = v.T.astype(bf16)

    tiled(AT_COLLECT, d_model // TR, collect)
    send_b.wait_recv()
    send_u.wait_recv()

    def head_bias(row, first, second):
        s = [slice(HEAD_DIM * h, HEAD_DIM * (h + 1)) for h in range(hw // 128)]
        return jnp.concatenate([bias[j, row : row + 1, c] for c in s for j in (first, second)], axis=1)

    bq, bv = head_bias(0, 0, 1), head_bias(1, 1, 0)

    def project(i):
        h = sec[rows(0, i)]
        qkv[rows(0, i), 0:hw] = ((dot_nn(h, wc[:, 0:hw]) + bq).astype(bf16).astype(f32) * 0.125).astype(bf16)
        qkv[rows(0, i), hw : 2 * hw] = dot_nn(h, wc[:, hw : 2 * hw]).astype(bf16)
        qkv[rows(0, i), 2 * hw : 3 * hw] = (dot_nn(h, wc[:, 2 * hw : 3 * hw]) + bv).astype(bf16)

    tiled(AT_PROJECT, seq // TR, project)
    pairs, blocks = hw // 128, seq // BQ

    def attend(i):
        attn_fwd_pair(i, hw, length, qkv, mixed, lse, lambda b: at(i, [steps(AT_ATTEND, j * blocks + b) for j in range(pairs)]))

    loop(pairs, attend)

    def out_sib(i):
        s1[rows(0, i)] = dot_nn(mixed[rows(sib0, i)], wo[...]).astype(bf16)

    tiled(AT_OUT_SIB, nt, out_sib)
    send_h = sib(2, s1, r1)
    send_h.start()

    def out_own(i):
        result[rows(0, i)] = tok[rows(0, i)].astype(f32) + dot_nn(mixed[rows(own0, i)], wo[...]) + vec[1:2]

    tiled(AT_OUT_OWN, nt, out_own)
    send_h.wait_recv()

    def norm_two(i):
        h = result[rows(0, i, 128)] + r1[rows(0, i, 128)].astype(f32)
        result[rows(0, i, 128)] = h
        n, _ = norm_parts(h)
        sec[rows(own0, i, 128)] = (n * vec[5:6] + vec[6:7]).astype(bf16)

    tiled(AT_NORM_TWO, half // 128, norm_two)
    send_s = sib(3, sec.at[rows(own0, 0, half)], sec.at[rows(own0, 0, half)])
    send_s.start()
    mark(AT_WAIT_1)
    g.final(1)

    def up(name, base):
        def one(i):
            r = rows(base, i)
            h = sec[r]
            t2[:, r] = h.astype(f32).T.astype(bf16)
            for yq in (0, 1):
                u = dot_nn(h, w[yq, 1]) + bias_up[yq, 0:1]
                a, s = gelu_both(u)
                act[r, yq * ffq : (yq + 1) * ffq] = a.astype(bf16)
                gp[r, yq * ffq : (yq + 1) * ffq] = s.astype(bf16)

        tiled(name, nt, one)

    up(AT_UP_A, own0)
    send_s.wait_recv()
    up(AT_UP_B, sib0)
    ZR = d_model // nz

    def down_grad(i):
        r = rows(0, i, ZR)
        for yq in (0, 1):
            grf[yq, DOWN, r] = dot_nn(t1[r], act[:, yq * ffq : (yq + 1) * ffq]).astype(bf16)

    tiled(AT_DOWN_GRAD, nz, down_grad)
    mark(AT_WAIT_2)
    gd.final(2)
    gp2.final()

    def pre_grad(i):
        r = rows(0, i)
        for yq in (0, 1):
            cols = slice(yq * ffq, (yq + 1) * ffq)
            v = (dot_nn(dr[r], w[yq, 2]) * gp[r, cols].astype(f32)).astype(bf16)
            gp[r, cols] = v
            sm[ROW_B_UP + yq : ROW_B_UP + yq + 1] += jnp.sum(v.astype(f32), axis=0, keepdims=True)

    tiled(AT_PRE_GRAD, seq // TR, pre_grad)

    def up_back(i, base):
        return dot_nt(gp[rows(base, i), 0:ffq], w[0, 1]) + dot_nt(gp[rows(base, i), ffq : 2 * ffq], w[1, 1])

    send_h.wait_send()

    def second_sib(i):
        s1[rows(0, i)] = up_back(i, sib0).astype(bf16)

    tiled(AT_SECOND_SIB, nt, second_sib)
    send_d = sib(4, s1, r3)
    send_d.start()

    def second_own(i):
        part[rows(0, i)] = up_back(i, own0)

    tiled(AT_SECOND_OWN, nt, second_own)

    def up_grad(i):
        r = rows(0, i, ZR)
        for yq in (0, 1):
            grf[yq, UP, r] = dot_nn(t2[r], gp[:, yq * ffq : (yq + 1) * ffq]).astype(bf16)
        ru.first(UP, i)

    tiled(AT_UP_GRAD, nz, up_grad)
    send_d.wait_recv()

    def back_two(i):
        r = rows(0, i, 128)
        n, rr = norm_parts(result[r])
        ds = part[r] + r3[r].astype(f32)
        dres = jnp.where(valid((128, d_model), own0 + i * 128, length), og[r].astype(f32), 0.0)
        dh = dres + norm_back(n, rr, ds, vec[5:6])
        tgrad[r] = dh
        x_all[rows(own0, i, 128)] = dh.astype(bf16)
        for row, v in ((ROW_B_OUT, dh), (ROW_B_DOWN, dres), (ROW_G_TWO, ds * n), (ROW_C_TWO, ds)):
            sm[row : row + 1] += jnp.sum(v, axis=0, keepdims=True)

    tiled(AT_BACK_TWO, half // 128, back_two)
    send_dh = sib(5, x_own, x_own)
    send_dh.start()
    send_dh.wait_recv()

    def mixed_grad(i):
        r = rows(0, i)
        h = x_all[r]
        t1[:, r] = h.astype(f32).T.astype(bf16)
        dmx[r] = dot_nn(h, wc[:, 3 * hw : 4 * hw]).astype(bf16)

    tiled(AT_MIXED_GRAD, seq // TR, mixed_grad)

    def out_grad_w(i):
        go[rows(0, i)] = dot_nn(t1[rows(0, i)], mixed[...]).astype(bf16)

    tiled(AT_OUT_GRAD_W, d_model // TR, out_grad_w)

    def attend_back(i):
        attn_bwd_pair(
            i, hw, length, qkv, mixed, lse, dmx, dk_acc, dv_acc, lambda b: at(i, [steps(AT_ATTEND_BACK, j * blocks + b) for j in range(pairs)])
        )
        cq, ck, cv = [pair_cols(i, group, hw) for group in range(3)]

        def grads(t):
            r = rows(0, t, ZR)
            gq, gk, gv = [dot_nn(ft[r], qkv[:, cc]) for cc in (cq, ck, cv)]
            o = go[r, cq].astype(f32)
            grp[0, i, r, 0:128] = pick(gq, gv).astype(bf16)
            grp[0, i, r, 128:256] = pick(gk, o).astype(bf16)
            grp[1, i, r, 0:128] = pick(gv, gq).astype(bf16)
            grp[1, i, r, 128:256] = pick(o, gk).astype(bf16)
            rp.first(i, t)

        loop(nz, grads)
        at(i, [steps(AT_GRADS, j) for j in range(pairs)])
        for cc, lo in ((cq, 0), (cv, hw)):
            to = pl.ds(pl.multiple_of(lo + i * 128, 128), 128)
            sm[ROW_B_QV : ROW_B_QV + 1, to] = jnp.sum(qkv[:, cc].astype(f32), axis=0, keepdims=True)

    loop(pairs, attend_back)

    def first_back(i, base):
        return dot_nt(qkv[rows(base, i)], wc[:, 0 : 3 * hw])

    def first_sib(i):
        s2[rows(0, i)] = first_back(i, sib0).astype(bf16)

    tiled(AT_FIRST_SIB, nt, first_sib)
    send_f = sib(6, s2, r4)
    send_f.start()

    def first_own(i):
        part[rows(0, i)] = first_back(i, own0)

    tiled(AT_FIRST_OWN, nt, first_own)
    send_f.wait_recv()

    def back_one(i):
        r = rows(0, i, 128)
        n, rr = norm_parts(tok[r].astype(f32))
        df = part[r] + r4[r].astype(f32)
        tgrad[r] = tgrad[r] + norm_back(n, rr, df, vec[3:4])
        for row, v in ((ROW_G_ONE, df * n), (ROW_C_ONE, df)):
            sm[row : row + 1] += jnp.sum(v, axis=0, keepdims=True)

    tiled(AT_BACK_ONE, half // 128, back_one)
    store_t = pltpu.make_async_copy(tgrad, tgrad_hbm, loc.at[0])
    store_t.start()

    def down(i, base):
        return dot_nt(act[rows(base, i), 0:ffq], w[0, 2]) + dot_nt(act[rows(base, i), ffq : 2 * ffq], w[1, 2])

    send_d.wait_send()

    def down_sib(i):
        s1[rows(0, i)] = down(i, sib0).astype(bf16)

    tiled(AT_DOWN_SIB, nt, down_sib)
    send_r = sib(7, s1, r2)
    send_r.start()
    def down_own(i):
        part[rows(0, i)] = down(i, own0)

    tiled(AT_DOWN_OWN, nt, down_own)
    send_r.wait_recv()

    def finish(i):
        r = rows(0, i, 128)
        v = result[r] + part[r] + r2[r].astype(f32) + vec[2:3]
        result[r] = jnp.where(valid((128, d_model), own0 + i * 128, length), v, 0.0)

    tiled(AT_FINISH, half // 128, finish)
    store_r = pltpu.make_async_copy(result, result_hbm, loc.at[1])
    store_r.start()
    mark(AT_END)

    for k in range(2):
        g.drain(k)
    gd.drain(2)
    gp2.drain()
    ar.drain(0)
    ar.drain(1)
    rd.drain(DOWN)
    rq.drain()
    ru.drain(UP)
    for k in range(3):
        rp.drain(k)
    for cp in (send_x, send_b, send_u, send_dr, send_s, send_dh, send_f, send_r):
        cp.wait_send()
    store_t.wait()
    store_r.wait()


def block(lens, tokens, ograd, w_qkv, w_out, w_up, w_down, b_qv, vectors, nz):
    half, d = tokens.shape
    heads_w = w_qkv.shape[2]
    seq = 2 * half
    nk, (rows, ffq) = NK, w_up.shape
    hw = d // 2
    pw = 256
    npair = hw // 128

    def V(shape, t=bf16):
        return pltpu.VMEM(shape, t)

    scratch = [
        V((half, d), f32), V((half, d), f32), V((half, d)), V((half, d)), V((rows, d)),
        V((2, nk, d, ffq)), V((d, 4 * hw)), V((hw, d)), V((seq, d)), V((seq, d)), V((seq, d)), V((d, seq)), V((d, seq)), V((d, seq)),
        V((seq, 3 * hw)), V((seq, hw)), V((2 * npair, 1, seq), f32), V((seq, 2 * ffq)), V((seq, 2 * ffq)), V((seq, hw)), V((d, hw)),
        V((half, d)), V((half, d)), V((half, d)), V((half, d)), V((half, d)), V((half, d)), V((half, d), f32),
        V((seq, 128), f32), V((seq, 128), f32), V((2, 2, heads_w), f32), V((2, 8, ffq), f32), V((8, d), f32), V((N_SUM, d), f32), V((2, 8, 8, d), f32), V((2, nz, 8, d), f32),
        V((2, 2, d, ffq)), V((2, npair, d, pw)),
        V((2, 1, nz, rows // 2, ffq - PLANE_SCATTER)), V((2, 1, nz, rows, ffq - PLANE_SCATTER)), V((1, nz - 1, rows, ffq - PLANE_SCATTER)),
        V((2, 1, nz, rows // 2, ffq)), V((2, 1, nz, rows, ffq)), V((1, nz - 1, rows, ffq)),
        V((2, npair, nz, rows // 2, pw)), V((2, npair, nz, rows, pw)), V((npair, nz - 1, rows, pw)),
        V((4, nz - 1, rows, PLANE_SCATTER)), V((3, rows, PLANE_SCATTER)),
    ]
    dma = pltpu.SemaphoreType.DMA
    sems = [dma((3, nk)), dma((8, nk)), dma((2,)), dma((4,)), dma((3, 1)), dma((9, 1)), dma((3, 1)), dma((9, 1)), dma((2,)), dma((7,)), dma((3, npair)), dma((9, npair))]
    sems += [dma((10,)), dma((10,)), dma((2, 2)), dma((2, 2)), dma((2 + nk,))]
    vm = pl.BlockSpec(memory_space=pltpu.VMEM)
    anywhere = pl.BlockSpec(memory_space=pl.ANY)
    return pl.pallas_call(
        block_kernel,
        out_shape=(
            jax.ShapeDtypeStruct((half, d), f32),
            jax.ShapeDtypeStruct((half, d), f32),
            jax.ShapeDtypeStruct((rows, ffq), f32),
            jax.ShapeDtypeStruct((rows, ffq), f32),
            jax.ShapeDtypeStruct((npair, rows, pw), f32),
            jax.ShapeDtypeStruct((N_SUM, d), f32),
        ),
        in_specs=[pl.BlockSpec(memory_space=pltpu.SMEM), anywhere, anywhere, vm, vm, anywhere, anywhere] + [vm] * (1 + len(vectors)),
        out_specs=(anywhere, anywhere, vm, vm, vm, vm),
        scratch_shapes=scratch + sems,
        compiler_params=pltpu.CompilerParams(collective_id=0, has_side_effects=True, vmem_limit_bytes=64 << 20),
    )(lens, tokens, ograd, w_qkv, w_out, w_up, w_down, b_qv, *vectors)


def finish_kernel(res_in, tg_in, up_in, down_in, outp_in, sums_in, *rest):
    outs, (held_r, held_t, held_u, held_d, outp, sums), made, (load_sem, store_sem) = rest[:14], rest[14:20], rest[20:30], rest[30:]
    res, tg, up, down = outs[:4]
    qkv, b_qv, w_out, b_up, *rows = made
    first = [pltpu.make_async_copy(a, b, load_sem.at[i]) for i, (a, b) in enumerate(((outp_in, outp), (sums_in, sums)))]
    for cp in first:
        cp.start()
    moves = []
    for source, held, to, n in ((tg_in, held_t, tg, 4), (res_in, held_r, res, 4), (up_in, held_u, up, 1), (down_in, held_d, down, 1)):
        size = held.shape[0] // n
        for i in range(n):
            part, j = pl.ds(i * size, size), len(moves)
            load = pltpu.make_async_copy(source.at[part], held.at[part], load_sem.at[2 + j])
            load.start()
            moves.append((load, pltpu.make_async_copy(held.at[part], to.at[part], store_sem.at[j])))
    for cp in first:
        cp.wait()
    second = lax.axis_index("y") == 1

    def ordered(a):
        return jnp.where(second, jnp.concatenate([a[:, HEAD_DIM:], a[:, :HEAD_DIM]], axis=1), a)

    a = [ordered(outp[h, :, : 2 * HEAD_DIM]) for h in range(outp.shape[0])]
    b = [ordered(outp[h, :, 2 * HEAD_DIM :]) for h in range(outp.shape[0])]
    qkv[0] = jnp.concatenate([v[:, :HEAD_DIM] for v in a], axis=1)
    qkv[1] = jnp.concatenate([v[:, :HEAD_DIM] for v in b], axis=1)
    qkv[2] = jnp.concatenate([v[:, HEAD_DIM:] for v in a], axis=1)
    w_out[...] = jnp.concatenate([v[:, HEAD_DIM:] for v in b], axis=1).T
    half = sums.shape[1] // 2
    for j in (0, 1):
        v = [ordered(sums[ROW_B_QV : ROW_B_QV + 1, j * half + 128 * h : j * half + 128 * h + 128]) for h in range(outp.shape[0])]
        b_qv[j : j + 1] = jnp.concatenate([c[:, HEAD_DIM * j : HEAD_DIM * (j + 1)] for c in v], axis=1)
    b_up[...] = jnp.where(second, sums[ROW_B_UP + 1], sums[ROW_B_UP])
    for ref, row in zip(rows, (ROW_B_OUT, ROW_B_DOWN, ROW_G_ONE, ROW_C_ONE, ROW_G_TWO, ROW_C_TWO)):
        ref[...] = sums[row]
    last = [pltpu.make_async_copy(src, dst, store_sem.at[len(moves) + i]) for i, (src, dst) in enumerate(zip(made, outs[4:]))]
    for cp in last:
        cp.start()
    for load, store in moves:
        load.wait()
        store.start()
    for cp in last + [store for _, store in moves]:
        cp.wait()


def finish(res, tg, up, down, outp, sums):
    n, (rows, ffq), d = outp.shape[0], up.shape, sums.shape[1]
    anywhere = pl.BlockSpec(memory_space=pl.ANY)
    big = [res.shape, tg.shape, up.shape, down.shape]
    made = [(3, rows, n * HEAD_DIM), (2, n * HEAD_DIM), (n * HEAD_DIM, rows), (ffq,)] + [(d,)] * 6
    return pl.pallas_call(
        finish_kernel,
        out_shape=[jax.ShapeDtypeStruct(s, f32) for s in big + made],
        in_specs=[anywhere] * 6,
        out_specs=[anywhere] * 14,
        scratch_shapes=[pltpu.VMEM(s, f32) for s in big + [outp.shape, sums.shape] + made] + [pltpu.SemaphoreType.DMA((12,)), pltpu.SemaphoreType.DMA((20,))],
    )(res, tg, up, down, outp, sums)


def per_device(tokens, lengths, w_qkv, b_qv, w_out, b_out, w_up, b_up, w_down, b_down, g_one, c_one, g_two, c_two, out_grad, *, nz, sub):
    if sub > 1:
        w_qkv, w_up = lax.all_gather(w_qkv, "r", axis=1, tiled=True), lax.all_gather(w_up, "r", axis=0, tiled=True)
        w_out, w_down = [lax.all_gather(a, "r", axis=1, tiled=True) for a in (w_out, w_down)]
    vectors = (b_up, b_out, b_down, g_one, c_one, g_two, c_two)
    result, tokens_grad, up, down, outp, sums = block(lengths, tokens, out_grad, w_qkv, w_out, w_up, w_down.T, b_qv, vectors, nz)
    if sub > 1:
        up, down = [lax.psum_scatter(a, "r", scatter_dimension=0, tiled=True) for a in (up, down)]
        outp = lax.psum_scatter(outp, "r", scatter_dimension=1, tiled=True)
        sums = lax.psum(sums, "r")
    result, tokens_grad, up, down, qkv, b_qv, w_out, b_up, b_out, b_down, *norms = finish(result, tokens_grad, up, down, outp, sums)
    return (result, tokens_grad, qkv, b_qv, w_out, b_out, up, b_up, down.T, b_down, *norms)


def solution(mesh):
    dp, tensor = mesh.shape["dp"], mesh.shape["tensor"]
    line = 4 * NX
    nz, sub = line // NX, dp // line
    grid = Mesh(mesh.devices.reshape(line, sub, tensor // 2, 2), ("e", "r", "y", "c"))
    dpx, tx = ("e", "r"), ("y", "c")
    rows = P(dpx + tx, None)
    return jax.shard_map(
        functools.partial(per_device, nz=nz, sub=sub),
        mesh=grid,
        in_specs=(rows, P(dpx), P(None, dpx, tx), P(None, tx), P(tx, dpx), P(), P(dpx, tx), P(tx), P(tx, dpx), P(), P(), P(), P(), P(), rows),
        out_specs=(rows, rows, P(None, dpx, tx), P(None, tx), P(tx, dpx), P(), P(dpx, tx), P(tx), P(tx, dpx), P(), P(), P(), P(), P()),
        check_vma=False,
    )
```

```python
import functools
import math

import jax
import jax.numpy as jnp
from jax import lax
from jax.experimental import pallas as pl
from jax.experimental.pallas import tpu as pltpu
from jax.sharding import Mesh
from jax.sharding import PartitionSpec as P

HEAD_DIM = 64
EPSILON = 1e-05
MESH = pl.DeviceIdType.MESH
NX = 2
NK = 3

class Place:
    def __init__(self, nz):
        self.nz = nz
        self.e = lax.axis_index("e"); self.y = lax.axis_index("y")
        self.z = self.e // NX; self.x = self.e % NX
        self.xn = {"e": self.e + 1 - 2 * self.x}
        self.yn = {"y": 1 - self.y}
        self.up = {"e": self.e + NX}
        self.dn = {"e": self.e - NX}
        self.core = {"c": 1 - lax.axis_index("c")}

BQ = 256
NEG = -1e30
f32, bf16 = jnp.float32, jnp.bfloat16
def dot_nt(a, b): return lax.dot_general(a, b, (((1,), (1,)), ((), ())), preferred_element_type=f32)
def dot_nn(a, b): return lax.dot_general(a, b, (((1,), (0,)), ((), ())), preferred_element_type=f32)
def flip(a): return a.astype(f32).T.astype(bf16)

def pair_cols(p, group, width):
    return pl.ds(pl.multiple_of(group * width + p * 128, 128), 128)

def masked_keys(k, j, length):
    n = k.shape[0]
    lane = lax.broadcasted_iota(jnp.int32, (n, 128), 1)
    row = lax.broadcasted_iota(jnp.int32, (n, 128), 0)
    out = jnp.where((lane == 64 * (1 - j)) & (row >= length), NEG, 0.0)
    return jnp.where(lane // 64 == j, k.astype(f32), out).astype(bf16)

def with_one(q, j):
    lane = lax.broadcasted_iota(jnp.int32, q.shape, 1)
    return jnp.where(lane == 64 * (1 - j), 1.0, q.astype(f32)).astype(bf16)

def only(a, h):
    lane = lax.broadcasted_iota(jnp.int32, a.shape, 1)
    return jnp.where(lane // 64 == h, a.astype(f32), 0.0).astype(bf16)

def causal(s, i):
    n = s.shape[0] - BQ
    row = lax.broadcasted_iota(jnp.int32, (BQ, BQ), 0)
    col = lax.broadcasted_iota(jnp.int32, (BQ, BQ), 1)
    d = jnp.where(row <= col, s[n:], NEG)
    return d if n == 0 else jnp.concatenate([s[:n], d], axis=0)

def attn_fwd_pair(p, width, length, qkv, mixed, lse, hook):
    n = qkv.shape[0]
    k = qkv[:, pair_cols(p, 1, width)]
    vt = flip(qkv[:, pair_cols(p, 2, width)])
    kp = [masked_keys(k, j, length) for j in (0, 1)]
    for i in range(n // BQ):
        hi = (i + 1) * BQ
        q = qkv[i * BQ:hi, pair_cols(p, 0, width)]
        outs = []
        for j in (0, 1):
            s = causal(dot_nt(kp[j][:hi], with_one(q, j)), i)
            m = jnp.max(s, axis=0, keepdims=True)
            e = jnp.exp(s - m)
            l = jnp.sum(e, axis=0, keepdims=True)
            o = dot_nn(vt[64 * (1 - j):64 * (2 - j), :hi], e.astype(bf16))
            outs.append(o * (1.0 / l))
            lse[2 * p + j, :, i * BQ:hi] = m + jnp.log(l)
        mixed[i * BQ:hi, pair_cols(p, 0, width)] = jnp.concatenate(outs[::-1], axis=0).T.astype(bf16)
        hook(i)

def attn_bwd_pair(p, width, length, qkv, mixed, lse, dmixed, dk_acc, dv_acc, hook):
    n = qkv.shape[0]
    c0, c1, c2 = [pair_cols(p, g, width) for g in range(3)]
    k = qkv[:, c1]
    kt = flip(k)
    v = qkv[:, c2]
    kp = [masked_keys(k, j, length) for j in (0, 1)]
    dk_acc[...] = jnp.zeros_like(dk_acc); dv_acc[...] = jnp.zeros_like(dv_acc)
    for i in range(n // BQ):
        hi = (i + 1) * BQ
        q = qkv[i * BQ:hi, c0]
        do = dmixed[i * BQ:hi, c0]
        prod = (do.astype(f32) * mixed[i * BQ:hi, c0].astype(f32)).T
        dq = []
        for j in (0, 1):
            vh = 1 - j
            delta = jnp.sum(prod[64 * vh:64 * (vh + 1)], axis=0, keepdims=True)
            dom = only(do, vh)
            s = causal(dot_nt(kp[j][:hi], with_one(q, j)), i)
            w = jnp.exp(s - lse[2 * p + j, :, i * BQ:hi])
            dw = dot_nt(v[:hi], dom)
            ds = (w * (dw - delta)).astype(bf16)
            dv_acc[:hi] += dot_nn(w.astype(bf16), dom)
            dk_acc[:hi] += dot_nn(ds, only(q, j))
            dq.append(dot_nn(kt[64 * j:64 * (j + 1), :hi], ds))
        qkv[i * BQ:hi, c0] = (jnp.concatenate(dq, axis=0).T * 0.125).astype(bf16)
        hook(i)
    qkv[:, c1] = dk_acc[...].astype(bf16)
    qkv[:, c2] = dv_acc[...].astype(bf16)


class Pieces:
    def __init__(self, p, full, lo, width, ssem, rsem):
        self.p, self.full, self.lo, self.width, self.ssem, self.rsem = p, full, lo, width, ssem, rsem
        self.rows = full.shape[2] // (p.nz * NX)

    def piece(self, yq, k, e, half=None):
        n = self.rows if half is None else self.rows // 2
        at_row = e * self.rows + (half or 0) * n
        return self.full.at[yq, k, pl.ds(pl.multiple_of(at_row, 16), n), pl.ds(self.lo, self.width)]

    def span(self, k, n):
        return self.full.at[0, k, pl.ds(0, n * self.rows), pl.ds(self.lo, self.width)]

    def z(self, r):
        return (self.p.z + r + self.p.nz) % self.p.nz

    def home(self, k):
        return self.out[k] if isinstance(self.out, tuple) else self.out.at[k]

    def wire(self, s, t, dev, out_at, in_at):
        return remote(s, t, self.ssem.at[out_at], self.rsem.at[in_at], dev)

    def await_in(self, ref, in_at):
        remote(ref, ref, self.ssem.at[(0,) * len(self.ssem.shape)], self.rsem.at[in_at], self.p.xn).wait_recv()

    def await_out(self, ref, out_at):
        remote(ref, ref, self.ssem.at[out_at], self.rsem.at[(0,) * len(self.rsem.shape)], self.p.xn).wait_send()


class Gather(Pieces):
    def __init__(self, p, own, *rest):
        super().__init__(p, *rest)
        self.own = own

    def mine(self, k):
        return self.own[k].at[:, pl.ds(self.lo, self.width)]

    def copy(self, kind, k, r):
        p = self.p
        back = self.z(-r)
        if kind == 0:
            s, t, dev = self.mine(k), self.piece(p.y, k, p.e), {"e": self.z(r) * NX + p.x}
        elif kind in (1, 2):
            t = self.piece(p.y, k, back * NX + p.x)
            s, dev = (t if r else self.mine(k)), (p.xn, p.yn)[kind - 1]
        elif kind == 3:
            s = t = self.piece(p.y, k, back * NX + 1 - p.x, 0)
            dev = p.yn
        else:
            s = t = self.piece(1 - p.y, k, back * NX + p.x, 1)
            dev = p.xn
        group = (kind + 1) // 2
        return self.wire(s, t, dev, (group, k), ((r - 1, 3 + r, 7)[group], k))

    def own_z(self, k):
        nz = self.p.nz
        for r in [1, nz - 1] + list(range(2, nz - 1)):
            self.copy(0, k, r).start()

    def own_xy(self, k):
        self.copy(1, k, 0).start()
        self.copy(2, k, 0).start()

    def pass_on(self, k, r):
        self.await_in(self.span(k, 1), (r - 1, k))
        self.copy(1, k, r).start()
        self.copy(2, k, r).start()

    def turn(self, k, r):
        self.await_in(self.span(k, 2), (3 + r, k))
        self.copy(3, k, r).start()
        self.copy(4, k, r).start()

    def final(self, k):
        self.await_in(self.span(k, self.p.nz), (7, k))

    def drain(self, k):
        nz = self.p.nz
        for group, n in enumerate((nz - 1, 2 * nz, nz)):
            self.await_out(self.span(k, n), (group, k))


class PlaneGather(Pieces):
    def __init__(self, p, own, k, *rest):
        super().__init__(p, *rest)
        self.own, self.k = own, k

    def spot(self, q, z):
        p = self.p
        return self.piece(1 - p.y if q >= 2 else p.y, self.k, z * NX + (1 - p.x if q % 2 else p.x))

    def mine(self):
        return self.own[self.k].at[:, pl.ds(self.lo, self.width)]

    def copy(self, q, r):
        p = self.p
        if r:
            t = self.spot(q, p.z)
            return self.wire(t if q else self.mine(), t, {"e": self.z(r) * NX + p.x}, (1,), (3,))
        if q == 3:
            t = self.spot(1, p.z)
            return self.wire(t, t, p.yn, (0,), (2,))
        return self.wire(self.mine(), self.spot(0, p.z), (p.xn, p.yn)[q - 1], (0,), (q - 1,))

    def lined(self):
        half = (self.p.nz - 1) * 2
        return self.full.at[pl.ds(0, 2), self.k, pl.ds(0, half * self.rows), pl.ds(self.lo, self.width)]

    def spread(self, q):
        if q:
            self.await_in(self.span(self.k, 1), (q - 1,))
            if q == 1:
                self.copy(3, 0).start()
        else:
            self.copy(1, 0).start()
            self.copy(2, 0).start()
        for r in range(1, self.p.nz):
            self.copy(q, r).start()

    def final(self):
        self.await_in(self.lined(), (3,))

    def drain(self):
        self.await_out(self.span(self.k, 3), (0,))
        self.await_out(self.lined(), (1,))


class Scatter(Pieces):
    def __init__(self, p, bd, bxy, bz, out, *rest):
        super().__init__(p, *rest)
        self.bd, self.bxy, self.bz, self.out = bd, bxy, bz, out

    def slot(self, k):
        return k if self.bd.shape[1] > 1 else 0

    def copy(self, kind, k, d):
        p, b = self.p, self.slot(k)
        if kind == 0:
            s, t, dev = self.piece(1 - p.y, k, d * NX + 1 - p.x, 0), self.bd.at[0, b, d], p.yn
        elif kind == 1:
            s, t, dev = self.piece(1 - p.y, k, d * NX + 1 - p.x, 1), self.bd.at[1, b, d], p.xn
        elif kind == 2:
            s, t, dev = self.piece(p.y, k, d * NX + 1 - p.x), self.bxy.at[0, b, d], p.xn
        elif kind == 3:
            s, t, dev = self.piece(1 - p.y, k, d * NX + p.x), self.bxy.at[1, b, d], p.yn
        else:
            e = self.z(d) * NX + p.x
            s, t, dev = self.piece(p.y, k, e), self.bz.at[b, d - 1], {"e": e}
        group = kind // 2
        return self.wire(s, t, dev, (group, b), ((d, p.nz + d, 2 * p.nz)[group], b))

    def first(self, k, d):
        self.copy(0, k, d).start()
        self.copy(1, k, d).start()

    def second(self, k, r):
        p, b, d = self.p, self.slot(k), self.z(r)
        self.await_in(self.bd.at[pl.ds(0, 2), b, d], (d, b))
        ref = self.piece(p.y, k, d * NX + 1 - p.x, 0)
        ref[...] = (ref[...].astype(f32) + self.bd[0, b, d].astype(f32)).astype(bf16)
        self.copy(2, k, d).start()
        ref = self.piece(1 - p.y, k, d * NX + p.x, 1)
        ref[...] = (ref[...].astype(f32) + self.bd[1, b, d].astype(f32)).astype(bf16)
        self.copy(3, k, d).start()

    def third(self, k, r):
        p, b, d = self.p, self.slot(k), self.z(r)
        self.await_in(self.bxy.at[pl.ds(0, 2), b, d], (p.nz + d, b))
        ref = self.piece(p.y, k, d * NX + p.x)
        total = ref[...].astype(f32) + self.bxy[0, b, d].astype(f32) + self.bxy[1, b, d].astype(f32)
        if r == 0:
            self.home(k)[:, self.lo : self.lo + self.width] = total
        else:
            ref[...] = total.astype(bf16)
            self.copy(4, k, r).start()

    def final(self, k):
        b = self.slot(k)
        cols = slice(self.lo, self.lo + self.width)
        self.await_in(self.bz.at[b], (2 * self.p.nz, b))
        total = self.home(k)[:, cols]
        for r in range(1, self.p.nz):
            total = total + self.bz[b, r - 1].astype(f32)
        self.home(k)[:, cols] = total

    def drain(self, k):
        nz, b = self.p.nz, self.slot(k)
        for group, n in enumerate((nz, 2 * nz, nz - 1)):
            self.await_out(self.span(k, n), (group, b))


class PlaneScatter(Pieces):
    def __init__(self, p, k, bz, bq, out, *rest):
        super().__init__(p, *rest)
        self.k, self.bz, self.bq, self.out = k, bz, bq, out

    def spot(self, q, z):
        p = self.p
        return self.piece(1 - p.y if q >= 2 else p.y, self.k, z * NX + (1 - p.x if q % 2 else p.x))

    def copy(self, q, r):
        p = self.p
        if r:
            return self.wire(self.spot(q, self.z(r)), self.bz.at[q, r - 1], {"e": self.z(r) * NX + p.x}, (1,), (q,))
        return self.wire(self.spot(q, p.z), self.bq.at[q - 1], p.yn if q == 2 else p.xn, (0,), (3 + q,))

    def first(self):
        for r in range(1, self.p.nz):
            for q in (3, 2, 1, 0):
                self.copy(q, r).start()

    def plane_sum(self, q):
        self.await_in(self.bz.at[q], (q,))
        total = self.spot(q, self.p.z)[...].astype(f32)
        for r in range(1, self.p.nz):
            total = total + self.bz[q, r - 1].astype(f32)
        return total

    def second(self):
        for q in (3, 1):
            self.spot(q, self.p.z)[...] = self.plane_sum(q).astype(bf16)
            self.copy(q, 0).start()

    def third(self):
        total = self.plane_sum(2)
        self.await_in(self.bq.at[2], (6,))
        self.spot(2, self.p.z)[...] = (total + self.bq[2].astype(f32)).astype(bf16)
        self.copy(2, 0).start()

    def final(self):
        total = self.plane_sum(0)
        for q in (1, 2):
            self.await_in(self.bq.at[q - 1], (3 + q,))
            total = total + self.bq[q - 1].astype(f32)
        self.home(self.k)[:, self.lo : self.lo + self.width] = total

    def drain(self):
        half = (self.p.nz - 1) * 2
        self.await_out(self.span(self.k, 3), (0,))
        self.await_out(self.full.at[pl.ds(0, 2), self.k, pl.ds(0, half * self.rows), pl.ds(self.lo, self.width)], (1,))


class Sums:
    def __init__(self, p, own, plane_buf, line_buf, out, peers, column, ssem, rsem):
        self.p, self.own, self.plane_buf, self.line_buf, self.out = p, own, plane_buf, line_buf, out
        self.peers, self.column, self.ssem, self.rsem = peers, column, ssem, rsem

    def tile(self, ref, t):
        return ref.at[pl.ds(8 * t, 8)]

    def wire(self, s, t, stage, tile, dev):
        return remote(s, t, self.ssem.at[tile, stage], self.rsem.at[tile, stage], dev)

    def plane_all(self, t):
        ref = self.plane_buf.at[t, pl.ds(1, len(self.peers))]
        return self.wire(ref, ref, 0, t, self.p.xn)

    def plane(self, t):
        for i, dev in self.peers:
            self.wire(self.tile(self.own, t), self.plane_buf.at[t, i], 0, t, dev).start()

    def line(self, t):
        row = lax.broadcasted_iota(jnp.int32, self.plane_buf.shape[2:], 0)
        lo, hi = SPLIT_ROWS[t]
        self.plane_all(t).wait_recv()
        total = self.own[8 * t : 8 * t + 8]
        for i, dev in self.peers:
            part = self.plane_buf[t, i]
            total = total + (jnp.where((row >= lo) & (row < hi), 0.0, part) if i % 2 else part)
        self.out[8 * t : 8 * t + 8] = total
        for r, dev in self.column:
            self.wire(self.tile(self.out, t), self.line_buf.at[t, r], 1, t, dev).start()

    def done(self, t):
        ref = self.line_buf.at[t, pl.ds(1, len(self.column))]
        both = self.wire(ref, ref, 1, t, self.p.xn)
        both.wait_recv()
        both.wait_send()
        total = self.out[8 * t : 8 * t + 8]
        for r, dev in self.column:
            total = total + self.line_buf[t, r]
        self.out[8 * t : 8 * t + 8] = total

    def drain(self, t):
        self.plane_all(t).wait_send()


def remote(src, dst, ssem, rsem, dev):
    return pltpu.make_async_remote_copy(src, dst, ssem, rsem, device_id=dev, device_id_type=MESH)


def loop(n, fn, after=()):
    def body(i, carry):
        fn(i)
        at(i, after)
        return carry

    lax.fori_loop(0, n, body, 0)


def at(i, steps):
    for j, todo in enumerate(steps):
        if todo:

            @pl.when(i == j)
            def _(todo=todo):
                for f in todo:
                    f()


def pick(a, b):
    lane = lax.broadcasted_iota(jnp.int32, a.shape, 1)
    return jnp.where(lane % 128 < 64, a.astype(f32), b.astype(f32))


def norm_parts(v):
    center = v - jnp.mean(v, axis=-1, keepdims=True)
    r = lax.rsqrt(jnp.mean(center * center, axis=-1, keepdims=True) + EPSILON)
    return center * r, r


def norm_back(n, r, d, gain):
    q = d * gain
    return r * (q - jnp.mean(q, axis=-1, keepdims=True) - n * jnp.mean(q * n, axis=-1, keepdims=True))


def gelu_both(u):
    a, b = math.sqrt(2.0 / math.pi), 0.044715
    u2 = u * u
    t = jnp.tanh(a * u * (1.0 + b * u2))
    h = 0.5 + 0.5 * t
    return u * h, h + (0.5 * a) * u * (1.0 - t * t) * (1.0 + (3.0 * b) * u2)


def valid(shape, base, length):
    return base + lax.broadcasted_iota(jnp.int32, shape, 0) < length


N_SUM = 16
ROW_B_OUT, ROW_B_DOWN, ROW_G_TWO, ROW_C_TWO, ROW_B_UP, ROW_G_ONE, ROW_C_ONE, ROW_B_QV = 0, 1, 2, 3, 4, 8, 9, 10
SPLIT_ROWS = ((4, 6), (2, 3))
PLANE_GATHER, PLANE_SCATTER = 128, 256
AT_BEGIN, AT_NORM_A, AT_NORM_B, AT_MASK_A, AT_MASK_B, AT_WAIT_0, AT_COLLECT, AT_PROJECT, AT_ATTEND, AT_OUT_SIB, AT_OUT_OWN, AT_NORM_TWO, AT_WAIT_1, AT_UP_A, AT_UP_B, AT_DOWN_GRAD, AT_WAIT_2, AT_PRE_GRAD, AT_SECOND_SIB, AT_SECOND_OWN, AT_UP_GRAD, AT_BACK_TWO, AT_MIXED_GRAD, AT_OUT_GRAD_W, AT_ATTEND_BACK, AT_GRADS, AT_FIRST_SIB, AT_FIRST_OWN, AT_BACK_ONE, AT_DOWN_SIB, AT_DOWN_OWN, AT_FINISH, AT_END = range(33)
IN_G, IN_GD, IN_GP, IN_RD, IN_RQ, IN_RU, IN_RP, IN_AR = range(8)
DO_OWN_XY, DO_OWN_Z, DO_PASS_ON, DO_TURN, DO_SPREAD, DO_FIRST, DO_SECOND, DO_THIRD, DO_FINAL, DO_PLANE, DO_LINE, DO_DONE = range(12)
METHODS = (
    lambda part: part.own_xy,
    lambda part: part.own_z,
    lambda part: part.pass_on,
    lambda part: part.turn,
    lambda part: part.spread,
    lambda part: part.first,
    lambda part: part.second,
    lambda part: part.third,
    lambda part: part.final,
    lambda part: part.plane,
    lambda part: part.line,
    lambda part: part.done,
)
PLAN = {
    (AT_BEGIN, 0): ((IN_G, DO_OWN_Z, 0), (IN_GP, DO_SPREAD, 0),),
    (AT_NORM_A, 1): ((IN_G, DO_OWN_XY, 1), (IN_G, DO_OWN_Z, 1),),
    (AT_NORM_B, 0): ((IN_G, DO_OWN_XY, 0), (IN_GP, DO_SPREAD, 1),),
    (AT_NORM_B, 1): ((IN_GD, DO_OWN_Z, 2),),
    (AT_MASK_A, 2): ((IN_GP, DO_SPREAD, 2),),
    (AT_MASK_B, 1): ((IN_G, DO_TURN, 1, 0),),
    (AT_WAIT_0, 0): ((IN_G, DO_PASS_ON, 0, 3), (IN_G, DO_TURN, 0, 0), (IN_GP, DO_SPREAD, 3), (IN_G, DO_TURN, 0, 3), (IN_G, DO_PASS_ON, 0, 2), (IN_G, DO_PASS_ON, 0, 1), (IN_G, DO_TURN, 0, 2), (IN_G, DO_TURN, 0, 1),),
    (AT_COLLECT, 0): ((IN_G, DO_PASS_ON, 1, 3),),
    (AT_PROJECT, 0): ((IN_GD, DO_OWN_XY, 2),),
    (AT_ATTEND, 2): ((IN_G, DO_TURN, 1, 3),),
    (AT_ATTEND, 3): ((IN_G, DO_PASS_ON, 1, 2), (IN_GD, DO_TURN, 2, 0),),
    (AT_ATTEND, 6): ((IN_G, DO_PASS_ON, 1, 1),),
    (AT_ATTEND, 10): ((IN_G, DO_TURN, 1, 2),),
    (AT_OUT_SIB, 0): ((IN_GD, DO_PASS_ON, 2, 3),),
    (AT_OUT_OWN, 0): ((IN_G, DO_TURN, 1, 1),),
    (AT_NORM_TWO, 2): ((IN_GD, DO_PASS_ON, 2, 2),),
    (AT_UP_A, 0): ((IN_GD, DO_PASS_ON, 2, 1), (IN_GD, DO_TURN, 2, 3),),
    (AT_UP_A, 1): ((IN_GD, DO_TURN, 2, 2),),
    (AT_UP_B, 1): ((IN_GD, DO_TURN, 2, 1),),
    (AT_DOWN_GRAD, 1): ((IN_RD, DO_FIRST, 1, 1),),
    (AT_DOWN_GRAD, 2): ((IN_RD, DO_FIRST, 1, 2),),
    (AT_DOWN_GRAD, 3): ((IN_RQ, DO_FIRST), (IN_RD, DO_FIRST, 1, 3),),
    (AT_WAIT_2, 0): ((IN_RD, DO_FIRST, 1, 0),),
    (AT_PRE_GRAD, 2): ((IN_RD, DO_SECOND, 1, 0), (IN_RD, DO_SECOND, 1, 2), (IN_RD, DO_SECOND, 1, 1),),
    (AT_SECOND_SIB, 1): ((IN_RD, DO_SECOND, 1, 3),),
    (AT_SECOND_OWN, 0): ((IN_RD, DO_THIRD, 1, 0),),
    (AT_SECOND_OWN, 1): ((IN_RD, DO_THIRD, 1, 2),),
    (AT_UP_GRAD, 2): ((IN_RD, DO_THIRD, 1, 1),),
    (AT_BACK_TWO, 1): ((IN_RD, DO_THIRD, 1, 3),),
    (AT_MIXED_GRAD, 0): ((IN_AR, DO_PLANE, 0),),
    (AT_MIXED_GRAD, 2): ((IN_RU, DO_SECOND, 0, 0), (IN_RU, DO_SECOND, 0, 2), (IN_RU, DO_SECOND, 0, 1), (IN_RU, DO_SECOND, 0, 3),),
    (AT_ATTEND_BACK, 1): ((IN_AR, DO_LINE, 0),),
    (AT_ATTEND_BACK, 2): ((IN_RQ, DO_SECOND),),
    (AT_ATTEND_BACK, 3): ((IN_RU, DO_THIRD, 0, 0),),
    (AT_ATTEND_BACK, 4): ((IN_RU, DO_THIRD, 0, 2),),
    (AT_ATTEND_BACK, 7): ((IN_AR, DO_DONE, 0), (IN_RD, DO_FINAL, 1), (IN_RU, DO_THIRD, 0, 1),),
    (AT_GRADS, 1): ((IN_RQ, DO_THIRD), (IN_RU, DO_THIRD, 0, 3),),
    (AT_ATTEND_BACK, 10): ((IN_RP, DO_SECOND, 0, 3), (IN_RP, DO_SECOND, 0, 2),),
    (AT_ATTEND_BACK, 11): ((IN_RQ, DO_FINAL), (IN_RP, DO_SECOND, 0, 0), (IN_RP, DO_SECOND, 1, 3), (IN_RP, DO_SECOND, 1, 1), (IN_RP, DO_SECOND, 1, 0), (IN_RP, DO_SECOND, 0, 1), (IN_RP, DO_THIRD, 0, 3), (IN_RP, DO_THIRD, 0, 2),),
    (AT_GRADS, 2): ((IN_RP, DO_THIRD, 0, 0), (IN_RU, DO_FINAL, 0),),
    (AT_FIRST_OWN, 0): ((IN_RP, DO_SECOND, 1, 2), (IN_RP, DO_THIRD, 1, 1), (IN_RP, DO_THIRD, 1, 3),),
    (AT_FIRST_OWN, 1): ((IN_RP, DO_THIRD, 1, 0),),
    (AT_BACK_ONE, 0): ((IN_RP, DO_THIRD, 0, 1),),
    (AT_BACK_ONE, 1): ((IN_RP, DO_SECOND, 2, 3), (IN_RP, DO_SECOND, 2, 1), (IN_RP, DO_SECOND, 2, 2), (IN_RP, DO_SECOND, 2, 0),),
    (AT_BACK_ONE, 2): ((IN_RP, DO_THIRD, 1, 2),),
    (AT_BACK_ONE, 3): ((IN_RP, DO_THIRD, 2, 3), (IN_AR, DO_PLANE, 1), (IN_RP, DO_FINAL, 0),),
    (AT_DOWN_SIB, 0): ((IN_RP, DO_THIRD, 2, 1),),
    (AT_DOWN_OWN, 0): ((IN_RP, DO_THIRD, 2, 2), (IN_RP, DO_THIRD, 2, 0), (IN_RP, DO_FINAL, 1),),
    (AT_END, 0): ((IN_AR, DO_LINE, 1), (IN_RP, DO_FINAL, 2), (IN_AR, DO_DONE, 1),),
}


def block_kernel(
    lens, tokens, ograd, w_qkv, w_out, w_up, w_down, b_qv, b_up, b_out, b_down, g_one, c_one, g_two, c_two,
    result_hbm, tgrad_hbm, up_out, down_out, outp, sums,
    result, tgrad, tok, og, packed, w, wc, wo, x_all, sec, dr, t1, t2, ft, qkv, mixed, lse, act, gp, dmx, go,
    r1, r2, r3, r4, s1, s2, part, dk_acc, dv_acc, bias, bias_up, vec, sm, ar1, ar2,
    grf, grp, dd, dxy, dz, ud, uxy, uz, pd, pxy, pz, qz, qq,
    g_ss, g_rs, q_ss, q_rs, d_ss, d_rs, u_ss, u_rs, v_ss, v_rs, p_ss, p_rs, sib_ss, sib_rs, ar_ss, ar_rs, loc,
):
    nz = ar2.shape[1]
    p = Place(nz)
    c = lax.axis_index("c")
    half, d_model = tokens.shape
    seq = 2 * half
    hw = mixed.shape[1]
    TR = 256
    nt = half // TR
    length = lens[p.y]
    own0, sib0 = c * half, (1 - c) * half

    def rows(base, i, n=TR):
        return pl.ds(pl.multiple_of(base + i * n, n), n)

    load_t = pltpu.make_async_copy(tokens, tok, loc.at[0])
    load_g = pltpu.make_async_copy(ograd, og, loc.at[1])
    load_t.start()
    load_g.start()
    peers = []
    for dx in (0, 1):
        for dy in (0, 1):
            for dc in (0, 1):
                if dx + dy + dc:
                    peers.append((4 * dx + 2 * dy + dc, {"e": p.e + dx * (1 - 2 * p.x), "y": p.y + dy * (1 - 2 * p.y), "c": c + dc * (1 - 2 * c)}))
    column = [(r, {"e": ((p.z + r) % nz) * NX + p.x}) for r in range(1, nz)]
    bar = pltpu.get_barrier_semaphore()
    for _, dev in peers + column:
        pl.semaphore_signal(bar, 1, device_id=dev, device_id_type=MESH)
    for j, ref in enumerate((b_up, b_out, b_down, g_one, c_one, g_two, c_two)):
        vec[j] = ref[...]

    flip_lanes = p.y == 1
    for h in range(hw // 128):
        s = slice(HEAD_DIM * h, HEAD_DIM * (h + 1))
        q, k, v = [w_qkv[j][:, s].astype(f32) for j in range(3)]
        o = w_out[s, :].astype(f32).T
        for j, (lo, hi) in enumerate(((q, v), (k, o))):
            put = jnp.where(flip_lanes, jnp.concatenate([hi, lo], axis=1), jnp.concatenate([lo, hi], axis=1))
            packed[:, 256 * h + 128 * j : 256 * h + 128 * j + 128] = put.astype(bf16)
    pl.semaphore_wait(bar, len(peers) + len(column))

    def sib(i, src, dst):
        return remote(src, dst, sib_ss.at[i], sib_rs.at[i], p.core)

    DOWN, UP = 1, 0
    ffq = w.shape[3]
    gcut, rcut = ffq - PLANE_GATHER, ffq - PLANE_SCATTER
    shard = (packed, w_up, w_down)
    g = Gather(p, shard, w, 0, ffq, g_ss, g_rs)
    gd = Gather(p, shard, w, 0, gcut, g_ss, g_rs)
    gp2 = PlaneGather(p, shard, 2, w, gcut, ffq - gcut, q_ss, q_rs)
    outf = (up_out, down_out)
    ru = Scatter(p, ud, uxy, uz, outf, grf, 0, ffq, u_ss, u_rs)
    rd = Scatter(p, dd, dxy, dz, outf, grf, 0, rcut, d_ss, d_rs)
    rq = PlaneScatter(p, DOWN, qz, qq, outf, grf, rcut, ffq - rcut, v_ss, v_rs)
    rp = Scatter(p, pd, pxy, pz, outp, grp, 0, grp.shape[3], p_ss, p_rs)
    ar = Sums(p, sm, ar1, ar2, sums, peers, column, ar_ss, ar_rs)
    parts = (g, gd, gp2, rd, rq, ru, rp, ar)

    def steps(name, i=0):
        return [lambda t=t: METHODS[t[1]](parts[t[0]])(*t[2:]) for t in PLAN.get((name, i), ())]

    def mark(name):
        for f in steps(name):
            f()

    def tiled(name, n, fn):
        loop(n, fn, [steps(name, i) for i in range(n)])

    x_own, x_sib = x_all.at[rows(own0, 0, half)], x_all.at[rows(sib0, 0, half)]
    mark(AT_BEGIN)
    send_x = sib(0, tokens, x_own)
    send_x.start()
    send_dr = sib(1, ograd, dr.at[rows(own0, 0, half)])
    send_dr.start()
    send_b = remote(b_qv, bias.at[p.y], sib_ss.at[8], sib_rs.at[8], p.yn)
    send_u = remote(vec, bias_up.at[p.y], sib_ss.at[9], sib_rs.at[9], p.yn)
    send_b.start()
    send_u.start()
    keep = [pltpu.make_async_copy(shard[j], w.at[p.y, j, pl.ds(pl.multiple_of(p.e * packed.shape[0], 16), packed.shape[0])], loc.at[2 + j]) for j in range(NK)]
    for cp in keep:
        cp.start()
    bias[p.y] = b_qv[...]
    bias_up[p.y] = vec[...]
    sm[...] = jnp.zeros_like(sm)

    def norm_one(name, base, src, lo):
        def one(i):
            v = src[rows(lo, i, 128)].astype(f32)
            n, _ = norm_parts(v)
            f = n * vec[3:4] + vec[4:5]
            sec[rows(base, i, 128)] = f.astype(bf16)
            ft[:, rows(base, i, 128)] = f.astype(bf16).astype(f32).T.astype(bf16)

        tiled(name, half // 128, one)

    def mask_rows(name, base, src, lo):
        def one(i):
            v = jnp.where(valid((128, d_model), base + i * 128, length), src[rows(lo, i, 128)].astype(f32), 0.0)
            dr[rows(base, i, 128)] = v.astype(bf16)
            t1[:, rows(base, i, 128)] = v.T.astype(bf16)

        tiled(name, half // 128, one)

    load_t.wait()
    norm_one(AT_NORM_A, own0, tok, 0)
    send_x.wait_recv()
    norm_one(AT_NORM_B, sib0, x_all, sib0)
    load_g.wait()
    mask_rows(AT_MASK_A, own0, og, 0)
    send_dr.wait_recv()
    mask_rows(AT_MASK_B, sib0, dr, sib0)
    for cp in keep:
        cp.wait()
    mark(AT_WAIT_0)
    g.final(0)

    def collect(i):
        r = rows(0, i)
        for q in range(hw // 128):
            a = [w[yq, 0, r, q * 256 : q * 256 + 128] for yq in (0, 1)]
            b = [w[yq, 0, r, q * 256 + 128 : q * 256 + 256] for yq in (0, 1)]
            for group, v in enumerate((pick(a[0], a[1]), pick(b[0], b[1]), pick(a[1], a[0]), pick(b[1], b[0]))):
                wc[r, group * hw + q * 128 : group * hw + q * 128 + 128] = v.astype(bf16)
                if group == 3:
                    wo[q * 128 : q * 128 + 128, r] = v.T.astype(bf16)

    tiled(AT_COLLECT, d_model // TR, collect)
    send_b.wait_recv()
    send_u.wait_recv()

    def head_bias(row, first, second):
        s = [slice(HEAD_DIM * h, HEAD_DIM * (h + 1)) for h in range(hw // 128)]
        return jnp.concatenate([bias[j, row : row + 1, c] for c in s for j in (first, second)], axis=1)

    bq, bv = head_bias(0, 0, 1), head_bias(1, 1, 0)

    def project(i):
        h = sec[rows(0, i)]
        qkv[rows(0, i), 0:hw] = ((dot_nn(h, wc[:, 0:hw]) + bq).astype(bf16).astype(f32) * 0.125).astype(bf16)
        qkv[rows(0, i), hw : 2 * hw] = dot_nn(h, wc[:, hw : 2 * hw]).astype(bf16)
        qkv[rows(0, i), 2 * hw : 3 * hw] = (dot_nn(h, wc[:, 2 * hw : 3 * hw]) + bv).astype(bf16)

    tiled(AT_PROJECT, seq // TR, project)
    pairs, blocks = hw // 128, seq // BQ

    def attend(i):
        attn_fwd_pair(i, hw, length, qkv, mixed, lse, lambda b: at(i, [steps(AT_ATTEND, j * blocks + b) for j in range(pairs)]))

    loop(pairs, attend)

    def out_sib(i):
        s1[rows(0, i)] = dot_nn(mixed[rows(sib0, i)], wo[...]).astype(bf16)

    tiled(AT_OUT_SIB, nt, out_sib)
    send_h = sib(2, s1, r1)
    send_h.start()

    def out_own(i):
        result[rows(0, i)] = tok[rows(0, i)].astype(f32) + dot_nn(mixed[rows(own0, i)], wo[...]) + vec[1:2]

    tiled(AT_OUT_OWN, nt, out_own)
    send_h.wait_recv()

    def norm_two(i):
        h = result[rows(0, i, 128)] + r1[rows(0, i, 128)].astype(f32)
        result[rows(0, i, 128)] = h
        n, _ = norm_parts(h)
        sec[rows(own0, i, 128)] = (n * vec[5:6] + vec[6:7]).astype(bf16)

    tiled(AT_NORM_TWO, half // 128, norm_two)
    send_s = sib(3, sec.at[rows(own0, 0, half)], sec.at[rows(own0, 0, half)])
    send_s.start()
    mark(AT_WAIT_1)
    g.final(1)

    def up(name, base):
        def one(i):
            r = rows(base, i)
            h = sec[r]
            t2[:, r] = h.astype(f32).T.astype(bf16)
            for yq in (0, 1):
                u = dot_nn(h, w[yq, 1]) + bias_up[yq, 0:1]
                a, s = gelu_both(u)
                act[r, yq * ffq : (yq + 1) * ffq] = a.astype(bf16)
                gp[r, yq * ffq : (yq + 1) * ffq] = s.astype(bf16)

        tiled(name, nt, one)

    up(AT_UP_A, own0)
    send_s.wait_recv()
    up(AT_UP_B, sib0)
    ZR = d_model // nz

    def down_grad(i):
        r = rows(0, i, ZR)
        for yq in (0, 1):
            grf[yq, DOWN, r] = dot_nn(t1[r], act[:, yq * ffq : (yq + 1) * ffq]).astype(bf16)

    tiled(AT_DOWN_GRAD, nz, down_grad)
    mark(AT_WAIT_2)
    gd.final(2)
    gp2.final()

    def pre_grad(i):
        r = rows(0, i)
        for yq in (0, 1):
            cols = slice(yq * ffq, (yq + 1) * ffq)
            v = (dot_nn(dr[r], w[yq, 2]) * gp[r, cols].astype(f32)).astype(bf16)
            gp[r, cols] = v
            sm[ROW_B_UP + yq : ROW_B_UP + yq + 1] += jnp.sum(v.astype(f32), axis=0, keepdims=True)

    tiled(AT_PRE_GRAD, seq // TR, pre_grad)

    def up_back(i, base):
        return dot_nt(gp[rows(base, i), 0:ffq], w[0, 1]) + dot_nt(gp[rows(base, i), ffq : 2 * ffq], w[1, 1])

    send_h.wait_send()

    def second_sib(i):
        s1[rows(0, i)] = up_back(i, sib0).astype(bf16)

    tiled(AT_SECOND_SIB, nt, second_sib)
    send_d = sib(4, s1, r3)
    send_d.start()

    def second_own(i):
        part[rows(0, i)] = up_back(i, own0)

    tiled(AT_SECOND_OWN, nt, second_own)

    def up_grad(i):
        r = rows(0, i, ZR)
        for yq in (0, 1):
            grf[yq, UP, r] = dot_nn(t2[r], gp[:, yq * ffq : (yq + 1) * ffq]).astype(bf16)
        ru.first(UP, i)

    tiled(AT_UP_GRAD, nz, up_grad)
    send_d.wait_recv()

    def back_two(i):
        r = rows(0, i, 128)
        n, rr = norm_parts(result[r])
        ds = part[r] + r3[r].astype(f32)
        dres = jnp.where(valid((128, d_model), own0 + i * 128, length), og[r].astype(f32), 0.0)
        dh = dres + norm_back(n, rr, ds, vec[5:6])
        tgrad[r] = dh
        x_all[rows(own0, i, 128)] = dh.astype(bf16)
        for row, v in ((ROW_B_OUT, dh), (ROW_B_DOWN, dres), (ROW_G_TWO, ds * n), (ROW_C_TWO, ds)):
            sm[row : row + 1] += jnp.sum(v, axis=0, keepdims=True)

    tiled(AT_BACK_TWO, half // 128, back_two)
    send_dh = sib(5, x_own, x_own)
    send_dh.start()
    send_dh.wait_recv()

    def mixed_grad(i):
        r = rows(0, i)
        h = x_all[r]
        t1[:, r] = h.astype(f32).T.astype(bf16)
        dmx[r] = dot_nn(h, wc[:, 3 * hw : 4 * hw]).astype(bf16)

    tiled(AT_MIXED_GRAD, seq // TR, mixed_grad)

    def out_grad_w(i):
        go[rows(0, i)] = dot_nn(t1[rows(0, i)], mixed[...]).astype(bf16)

    tiled(AT_OUT_GRAD_W, d_model // TR, out_grad_w)

    def attend_back(i):
        attn_bwd_pair(
            i, hw, length, qkv, mixed, lse, dmx, dk_acc, dv_acc, lambda b: at(i, [steps(AT_ATTEND_BACK, j * blocks + b) for j in range(pairs)])
        )
        cq, ck, cv = [pair_cols(i, group, hw) for group in range(3)]

        def grads(t):
            r = rows(0, t, ZR)
            gq, gk, gv = [dot_nn(ft[r], qkv[:, cc]) for cc in (cq, ck, cv)]
            o = go[r, cq].astype(f32)
            grp[0, i, r, 0:128] = pick(gq, gv).astype(bf16)
            grp[0, i, r, 128:256] = pick(gk, o).astype(bf16)
            grp[1, i, r, 0:128] = pick(gv, gq).astype(bf16)
            grp[1, i, r, 128:256] = pick(o, gk).astype(bf16)
            rp.first(i, t)

        loop(nz, grads)
        at(i, [steps(AT_GRADS, j) for j in range(pairs)])
        for cc, lo in ((cq, 0), (cv, hw)):
            to = pl.ds(pl.multiple_of(lo + i * 128, 128), 128)
            sm[ROW_B_QV : ROW_B_QV + 1, to] = jnp.sum(qkv[:, cc].astype(f32), axis=0, keepdims=True)

    loop(pairs, attend_back)

    def first_back(i, base):
        return dot_nt(qkv[rows(base, i)], wc[:, 0 : 3 * hw])

    def first_sib(i):
        s2[rows(0, i)] = first_back(i, sib0).astype(bf16)

    tiled(AT_FIRST_SIB, nt, first_sib)
    send_f = sib(6, s2, r4)
    send_f.start()

    def first_own(i):
        part[rows(0, i)] = first_back(i, own0)

    tiled(AT_FIRST_OWN, nt, first_own)
    send_f.wait_recv()

    def back_one(i):
        r = rows(0, i, 128)
        n, rr = norm_parts(tok[r].astype(f32))
        df = part[r] + r4[r].astype(f32)
        tgrad[r] = tgrad[r] + norm_back(n, rr, df, vec[3:4])
        for row, v in ((ROW_G_ONE, df * n), (ROW_C_ONE, df)):
            sm[row : row + 1] += jnp.sum(v, axis=0, keepdims=True)

    tiled(AT_BACK_ONE, half // 128, back_one)
    store_t = pltpu.make_async_copy(tgrad, tgrad_hbm, loc.at[0])
    store_t.start()

    def down(i, base):
        return dot_nt(act[rows(base, i), 0:ffq], w[0, 2]) + dot_nt(act[rows(base, i), ffq : 2 * ffq], w[1, 2])

    send_d.wait_send()

    def down_sib(i):
        s1[rows(0, i)] = down(i, sib0).astype(bf16)

    tiled(AT_DOWN_SIB, nt, down_sib)
    send_r = sib(7, s1, r2)
    send_r.start()
    def down_own(i):
        part[rows(0, i)] = down(i, own0)

    tiled(AT_DOWN_OWN, nt, down_own)
    send_r.wait_recv()

    def finish(i):
        r = rows(0, i, 128)
        v = result[r] + part[r] + r2[r].astype(f32) + vec[2:3]
        result[r] = jnp.where(valid((128, d_model), own0 + i * 128, length), v, 0.0)

    tiled(AT_FINISH, half // 128, finish)
    store_r = pltpu.make_async_copy(result, result_hbm, loc.at[1])
    store_r.start()
    mark(AT_END)

    for k in range(2):
        g.drain(k)
    gd.drain(2)
    gp2.drain()
    ar.drain(0)
    ar.drain(1)
    rd.drain(DOWN)
    rq.drain()
    ru.drain(UP)
    for k in range(3):
        rp.drain(k)
    for cp in (send_x, send_b, send_u, send_dr, send_s, send_dh, send_f, send_r):
        cp.wait_send()
    store_t.wait()
    store_r.wait()


def block(lens, tokens, ograd, w_qkv, w_out, w_up, w_down, b_qv, vectors, nz):
    half, d = tokens.shape
    heads_w = w_qkv.shape[2]
    seq = 2 * half
    nk, (rows, ffq) = NK, w_up.shape
    hw = d // 2
    pw = 256
    npair = hw // 128

    def V(shape, t=bf16):
        return pltpu.VMEM(shape, t)

    scratch = [
        V((half, d), f32), V((half, d), f32), V((half, d)), V((half, d)), V((rows, d)),
        V((2, nk, d, ffq)), V((d, 4 * hw)), V((hw, d)), V((seq, d)), V((seq, d)), V((seq, d)), V((d, seq)), V((d, seq)), V((d, seq)),
        V((seq, 3 * hw)), V((seq, hw)), V((2 * npair, 1, seq), f32), V((seq, 2 * ffq)), V((seq, 2 * ffq)), V((seq, hw)), V((d, hw)),
        V((half, d)), V((half, d)), V((half, d)), V((half, d)), V((half, d)), V((half, d)), V((half, d), f32),
        V((seq, 128), f32), V((seq, 128), f32), V((2, 2, heads_w), f32), V((2, 8, ffq), f32), V((8, d), f32), V((N_SUM, d), f32), V((2, 8, 8, d), f32), V((2, nz, 8, d), f32),
        V((2, 2, d, ffq)), V((2, npair, d, pw)),
        V((2, 1, nz, rows // 2, ffq - PLANE_SCATTER)), V((2, 1, nz, rows, ffq - PLANE_SCATTER)), V((1, nz - 1, rows, ffq - PLANE_SCATTER)),
        V((2, 1, nz, rows // 2, ffq)), V((2, 1, nz, rows, ffq)), V((1, nz - 1, rows, ffq)),
        V((2, npair, nz, rows // 2, pw)), V((2, npair, nz, rows, pw)), V((npair, nz - 1, rows, pw)),
        V((4, nz - 1, rows, PLANE_SCATTER)), V((3, rows, PLANE_SCATTER)),
    ]
    dma = pltpu.SemaphoreType.DMA
    sems = [dma((3, nk)), dma((8, nk)), dma((2,)), dma((4,)), dma((3, 1)), dma((9, 1)), dma((3, 1)), dma((9, 1)), dma((2,)), dma((7,)), dma((3, npair)), dma((9, npair))]
    sems += [dma((10,)), dma((10,)), dma((2, 2)), dma((2, 2)), dma((2 + nk,))]
    vm = pl.BlockSpec(memory_space=pltpu.VMEM)
    anywhere = pl.BlockSpec(memory_space=pl.ANY)
    return pl.pallas_call(
        block_kernel,
        out_shape=(
            jax.ShapeDtypeStruct((half, d), f32),
            jax.ShapeDtypeStruct((half, d), f32),
            jax.ShapeDtypeStruct((rows, ffq), f32),
            jax.ShapeDtypeStruct((rows, ffq), f32),
            jax.ShapeDtypeStruct((npair, rows, pw), f32),
            jax.ShapeDtypeStruct((N_SUM, d), f32),
        ),
        in_specs=[pl.BlockSpec(memory_space=pltpu.SMEM), anywhere, anywhere, vm, vm, anywhere, anywhere] + [vm] * (1 + len(vectors)),
        out_specs=(anywhere, anywhere, vm, vm, vm, vm),
        scratch_shapes=scratch + sems,
        compiler_params=pltpu.CompilerParams(collective_id=0, has_side_effects=True, vmem_limit_bytes=64 << 20),
    )(lens, tokens, ograd, w_qkv, w_out, w_up, w_down, b_qv, *vectors)


def finish_kernel(res_in, tg_in, up_in, down_in, outp_in, sums_in, *rest):
    outs, (held_r, held_t, held_u, held_d, outp, sums), made, (load_sem, store_sem) = rest[:14], rest[14:20], rest[20:30], rest[30:]
    res, tg, up, down = outs[:4]
    qkv, b_qv, w_out, b_up, *rows = made
    first = [pltpu.make_async_copy(a, b, load_sem.at[i]) for i, (a, b) in enumerate(((outp_in, outp), (sums_in, sums)))]
    for cp in first:
        cp.start()
    moves = []
    for source, held, to, n in ((tg_in, held_t, tg, 4), (res_in, held_r, res, 4), (up_in, held_u, up, 1), (down_in, held_d, down, 1)):
        size = held.shape[0] // n
        for i in range(n):
            part, j = pl.ds(i * size, size), len(moves)
            load = pltpu.make_async_copy(source.at[part], held.at[part], load_sem.at[2 + j])
            load.start()
            moves.append((load, pltpu.make_async_copy(held.at[part], to.at[part], store_sem.at[j])))
    for cp in first:
        cp.wait()
    second = lax.axis_index("y") == 1

    def ordered(a):
        return jnp.where(second, jnp.concatenate([a[:, HEAD_DIM:], a[:, :HEAD_DIM]], axis=1), a)

    a = [ordered(outp[h, :, : 2 * HEAD_DIM]) for h in range(outp.shape[0])]
    b = [ordered(outp[h, :, 2 * HEAD_DIM :]) for h in range(outp.shape[0])]
    qkv[0] = jnp.concatenate([v[:, :HEAD_DIM] for v in a], axis=1)
    qkv[1] = jnp.concatenate([v[:, :HEAD_DIM] for v in b], axis=1)
    qkv[2] = jnp.concatenate([v[:, HEAD_DIM:] for v in a], axis=1)
    w_out[...] = jnp.concatenate([v[:, HEAD_DIM:] for v in b], axis=1).T
    half = sums.shape[1] // 2
    for j in (0, 1):
        v = [ordered(sums[ROW_B_QV : ROW_B_QV + 1, j * half + 128 * h : j * half + 128 * h + 128]) for h in range(outp.shape[0])]
        b_qv[j : j + 1] = jnp.concatenate([c[:, HEAD_DIM * j : HEAD_DIM * (j + 1)] for c in v], axis=1)
    b_up[...] = jnp.where(second, sums[ROW_B_UP + 1], sums[ROW_B_UP])
    for ref, row in zip(rows, (ROW_B_OUT, ROW_B_DOWN, ROW_G_ONE, ROW_C_ONE, ROW_G_TWO, ROW_C_TWO)):
        ref[...] = sums[row]
    last = [pltpu.make_async_copy(src, dst, store_sem.at[len(moves) + i]) for i, (src, dst) in enumerate(zip(made, outs[4:]))]
    for cp in last:
        cp.start()
    for load, store in moves:
        load.wait()
        store.start()
    for cp in last + [store for _, store in moves]:
        cp.wait()


def finish(res, tg, up, down, outp, sums):
    n, (rows, ffq), d = outp.shape[0], up.shape, sums.shape[1]
    anywhere = pl.BlockSpec(memory_space=pl.ANY)
    big = [res.shape, tg.shape, up.shape, down.shape]
    made = [(3, rows, n * HEAD_DIM), (2, n * HEAD_DIM), (n * HEAD_DIM, rows), (ffq,)] + [(d,)] * 6
    return pl.pallas_call(
        finish_kernel,
        out_shape=[jax.ShapeDtypeStruct(s, f32) for s in big + made],
        in_specs=[anywhere] * 6,
        out_specs=[anywhere] * 14,
        scratch_shapes=[pltpu.VMEM(s, f32) for s in big + [outp.shape, sums.shape] + made] + [pltpu.SemaphoreType.DMA((12,)), pltpu.SemaphoreType.DMA((20,))],
    )(res, tg, up, down, outp, sums)


def per_device(tokens, lengths, w_qkv, b_qv, w_out, b_out, w_up, b_up, w_down, b_down, g_one, c_one, g_two, c_two, out_grad, *, nz, sub):
    if sub > 1:
        w_qkv, w_up = lax.all_gather(w_qkv, "r", axis=1, tiled=True), lax.all_gather(w_up, "r", axis=0, tiled=True)
        w_out, w_down = [lax.all_gather(a, "r", axis=1, tiled=True) for a in (w_out, w_down)]
    vectors = (b_up, b_out, b_down, g_one, c_one, g_two, c_two)
    result, tokens_grad, up, down, outp, sums = block(lengths, tokens, out_grad, w_qkv, w_out, w_up, w_down.T, b_qv, vectors, nz)
    if sub > 1:
        up, down = [lax.psum_scatter(a, "r", scatter_dimension=0, tiled=True) for a in (up, down)]
        outp = lax.psum_scatter(outp, "r", scatter_dimension=1, tiled=True)
        sums = lax.psum(sums, "r")
    result, tokens_grad, up, down, qkv, b_qv, w_out, b_up, b_out, b_down, *norms = finish(result, tokens_grad, up, down, outp, sums)
    return (result, tokens_grad, qkv, b_qv, w_out, b_out, up, b_up, down.T, b_down, *norms)


def solution(mesh):
    dp, tensor = mesh.shape["dp"], mesh.shape["tensor"]
    line = 4 * NX
    nz, sub = line // NX, dp // line
    grid = Mesh(mesh.devices.reshape(line, sub, tensor // 2, 2), ("e", "r", "y", "c"))
    dpx, tx = ("e", "r"), ("y", "c")
    rows = P(dpx + tx, None)
    return jax.shard_map(
        functools.partial(per_device, nz=nz, sub=sub),
        mesh=grid,
        in_specs=(rows, P(dpx), P(None, dpx, tx), P(None, tx), P(tx, dpx), P(), P(dpx, tx), P(tx), P(tx, dpx), P(), P(), P(), P(), P(), rows),
        out_specs=(rows, rows, P(None, dpx, tx), P(None, tx), P(tx, dpx), P(), P(dpx, tx), P(tx), P(tx, dpx), P(), P(), P(), P(), P()),
        check_vma=False,
    )
```

```python
import functools
import math

import jax
import jax.numpy as jnp
from jax import lax
from jax.experimental import pallas as pl
from jax.experimental.pallas import tpu as pltpu
from jax.sharding import Mesh
from jax.sharding import PartitionSpec as P

HEAD_DIM = 64
EPSILON = 1e-05
MESH = pl.DeviceIdType.MESH
NX = 2
NK = 3

class Place:
    def __init__(self, nz):
        self.nz = nz
        self.e = lax.axis_index("e"); self.y = lax.axis_index("y")
        self.z = self.e // NX; self.x = self.e % NX
        self.xn = {"e": self.e + 1 - 2 * self.x}
        self.yn = {"y": 1 - self.y}
        self.up = {"e": self.e + NX}
        self.dn = {"e": self.e - NX}
        self.core = {"c": 1 - lax.axis_index("c")}

BQ = 256
NEG = -1e30
f32, bf16 = jnp.float32, jnp.bfloat16
def dot_nt(a, b): return lax.dot_general(a, b, (((1,), (1,)), ((), ())), preferred_element_type=f32)
def dot_nn(a, b): return lax.dot_general(a, b, (((1,), (0,)), ((), ())), preferred_element_type=f32)
def flip(a): return a.astype(f32).T.astype(bf16)

def pair_cols(p, group, width):
    return pl.ds(pl.multiple_of(group * width + p * 128, 128), 128)

def masked_keys(k, j, length):
    n = k.shape[0]
    lane = lax.broadcasted_iota(jnp.int32, (n, 128), 1)
    row = lax.broadcasted_iota(jnp.int32, (n, 128), 0)
    out = jnp.where((lane == 64 * (1 - j)) & (row >= length), NEG, 0.0)
    return jnp.where(lane // 64 == j, k.astype(f32), out).astype(bf16)

def with_one(q, j):
    lane = lax.broadcasted_iota(jnp.int32, q.shape, 1)
    return jnp.where(lane == 64 * (1 - j), 1.0, q.astype(f32)).astype(bf16)

def only(a, h):
    lane = lax.broadcasted_iota(jnp.int32, a.shape, 1)
    return jnp.where(lane // 64 == h, a.astype(f32), 0.0).astype(bf16)

def causal(s, i):
    n = s.shape[0] - BQ
    row = lax.broadcasted_iota(jnp.int32, (BQ, BQ), 0)
    col = lax.broadcasted_iota(jnp.int32, (BQ, BQ), 1)
    d = jnp.where(row <= col, s[n:], NEG)
    return d if n == 0 else jnp.concatenate([s[:n], d], axis=0)

def attn_fwd_pair(p, width, length, qkv, mixed, lse, hook):
    n = qkv.shape[0]
    k = qkv[:, pair_cols(p, 1, width)]
    vt = flip(qkv[:, pair_cols(p, 2, width)])
    kp = [masked_keys(k, j, length) for j in (0, 1)]
    for i in range(n // BQ):
        hi = (i + 1) * BQ
        q = qkv[i * BQ:hi, pair_cols(p, 0, width)]
        outs = []
        for j in (0, 1):
            s = causal(dot_nt(kp[j][:hi], with_one(q, j)), i)
            m = jnp.max(s, axis=0, keepdims=True)
            e = jnp.exp(s - m)
            l = jnp.sum(e, axis=0, keepdims=True)
            o = dot_nn(vt[64 * (1 - j):64 * (2 - j), :hi], e.astype(bf16))
            outs.append(o * (1.0 / l))
            lse[2 * p + j, :, i * BQ:hi] = m + jnp.log(l)
        mixed[i * BQ:hi, pair_cols(p, 0, width)] = jnp.concatenate(outs[::-1], axis=0).T.astype(bf16)
        hook(i)

def attn_bwd_pair(p, width, length, qkv, mixed, lse, dmixed, dk_acc, dv_acc, hook):
    n = qkv.shape[0]
    c0, c1, c2 = [pair_cols(p, g, width) for g in range(3)]
    k = qkv[:, c1]
    kt = flip(k)
    v = qkv[:, c2]
    kp = [masked_keys(k, j, length) for j in (0, 1)]
    dk_acc[...] = jnp.zeros_like(dk_acc); dv_acc[...] = jnp.zeros_like(dv_acc)
    for i in range(n // BQ):
        hi = (i + 1) * BQ
        q = qkv[i * BQ:hi, c0]
        do = dmixed[i * BQ:hi, c0]
        prod = (do.astype(f32) * mixed[i * BQ:hi, c0].astype(f32)).T
        dq = []
        for j in (0, 1):
            vh = 1 - j
            delta = jnp.sum(prod[64 * vh:64 * (vh + 1)], axis=0, keepdims=True)
            dom = only(do, vh)
            s = causal(dot_nt(kp[j][:hi], with_one(q, j)), i)
            w = jnp.exp(s - lse[2 * p + j, :, i * BQ:hi])
            dw = dot_nt(v[:hi], dom)
            ds = (w * (dw - delta)).astype(bf16)
            dv_acc[:hi] += dot_nn(w.astype(bf16), dom)
            dk_acc[:hi] += dot_nn(ds, only(q, j))
            dq.append(dot_nn(kt[64 * j:64 * (j + 1), :hi], ds))
        qkv[i * BQ:hi, c0] = (jnp.concatenate(dq, axis=0).T * 0.125).astype(bf16)
        hook(i)
    qkv[:, c1] = dk_acc[...].astype(bf16)
    qkv[:, c2] = dv_acc[...].astype(bf16)


class Pieces:
    def __init__(self, p, full, lo, width, ssem, rsem):
        self.p, self.full, self.lo, self.width, self.ssem, self.rsem = p, full, lo, width, ssem, rsem
        self.rows = full.shape[2] // (p.nz * NX)

    def piece(self, yq, k, e, half=None):
        n = self.rows if half is None else self.rows // 2
        at_row = e * self.rows + (half or 0) * n
        return self.full.at[yq, k, pl.ds(pl.multiple_of(at_row, 16), n), pl.ds(self.lo, self.width)]

    def span(self, k, n):
        return self.full.at[0, k, pl.ds(0, n * self.rows), pl.ds(self.lo, self.width)]

    def z(self, r):
        return (self.p.z + r + self.p.nz) % self.p.nz

    def home(self, k):
        return self.out[k] if isinstance(self.out, tuple) else self.out.at[k]

    def wire(self, s, t, dev, out_at, in_at):
        return remote(s, t, self.ssem.at[out_at], self.rsem.at[in_at], dev)

    def await_in(self, ref, in_at):
        remote(ref, ref, self.ssem.at[(0,) * len(self.ssem.shape)], self.rsem.at[in_at], self.p.xn).wait_recv()

    def await_out(self, ref, out_at):
        remote(ref, ref, self.ssem.at[out_at], self.rsem.at[(0,) * len(self.rsem.shape)], self.p.xn).wait_send()


class Gather(Pieces):
    def __init__(self, p, own, *rest):
        super().__init__(p, *rest)
        self.own = own

    def mine(self, k):
        return self.own[k].at[:, pl.ds(self.lo, self.width)]

    def copy(self, kind, k, r):
        p = self.p
        back = self.z(-r)
        if kind == 0:
            s, t, dev = self.mine(k), self.piece(p.y, k, p.e), {"e": self.z(r) * NX + p.x}
        elif kind in (1, 2):
            t = self.piece(p.y, k, back * NX + p.x)
            s, dev = (t if r else self.mine(k)), (p.xn, p.yn)[kind - 1]
        elif kind == 3:
            s = t = self.piece(p.y, k, back * NX + 1 - p.x, 0)
            dev = p.yn
        else:
            s = t = self.piece(1 - p.y, k, back * NX + p.x, 1)
            dev = p.xn
        group = (kind + 1) // 2
        return self.wire(s, t, dev, (group, k), ((r - 1, 3 + r, 7)[group], k))

    def own_z(self, k):
        nz = self.p.nz
        for r in [1, nz - 1] + list(range(2, nz - 1)):
            self.copy(0, k, r).start()

    def own_xy(self, k):
        self.copy(1, k, 0).start()
        self.copy(2, k, 0).start()

    def pass_on(self, k, r):
        self.await_in(self.span(k, 1), (r - 1, k))
        self.copy(1, k, r).start()
        self.copy(2, k, r).start()

    def turn(self, k, r):
        self.await_in(self.span(k, 2), (3 + r, k))
        self.copy(3, k, r).start()
        self.copy(4, k, r).start()

    def final(self, k):
        self.await_in(self.span(k, self.p.nz), (7, k))

    def drain(self, k):
        nz = self.p.nz
        for group, n in enumerate((nz - 1, 2 * nz, nz)):
            self.await_out(self.span(k, n), (group, k))


class PlaneGather(Pieces):
    def __init__(self, p, own, k, *rest):
        super().__init__(p, *rest)
        self.own, self.k = own, k

    def spot(self, q, z):
        p = self.p
        return self.piece(1 - p.y if q >= 2 else p.y, self.k, z * NX + (1 - p.x if q % 2 else p.x))

    def mine(self):
        return self.own[self.k].at[:, pl.ds(self.lo, self.width)]

    def copy(self, q, r):
        p = self.p
        if r:
            t = self.spot(q, p.z)
            return self.wire(t if q else self.mine(), t, {"e": self.z(r) * NX + p.x}, (1,), (3,))
        if q == 3:
            t = self.spot(1, p.z)
            return self.wire(t, t, p.yn, (0,), (2,))
        return self.wire(self.mine(), self.spot(0, p.z), (p.xn, p.yn)[q - 1], (0,), (q - 1,))

    def lined(self):
        half = (self.p.nz - 1) * 2
        return self.full.at[pl.ds(0, 2), self.k, pl.ds(0, half * self.rows), pl.ds(self.lo, self.width)]

    def spread(self, q):
        if q:
            self.await_in(self.span(self.k, 1), (q - 1,))
            if q == 1:
                self.copy(3, 0).start()
        else:
            self.copy(1, 0).start()
            self.copy(2, 0).start()
        for r in range(1, self.p.nz):
            self.copy(q, r).start()

    def final(self):
        self.await_in(self.lined(), (3,))

    def drain(self):
        self.await_out(self.span(self.k, 3), (0,))
        self.await_out(self.lined(), (1,))


class Scatter(Pieces):
    def __init__(self, p, bd, bxy, bz, out, *rest):
        super().__init__(p, *rest)
        self.bd, self.bxy, self.bz, self.out = bd, bxy, bz, out

    def slot(self, k):
        return k if self.bd.shape[1] > 1 else 0

    def copy(self, kind, k, d):
        p, b = self.p, self.slot(k)
        if kind == 0:
            s, t, dev = self.piece(1 - p.y, k, d * NX + 1 - p.x, 0), self.bd.at[0, b, d], p.yn
        elif kind == 1:
            s, t, dev = self.piece(1 - p.y, k, d * NX + 1 - p.x, 1), self.bd.at[1, b, d], p.xn
        elif kind == 2:
            s, t, dev = self.piece(p.y, k, d * NX + 1 - p.x), self.bxy.at[0, b, d], p.xn
        elif kind == 3:
            s, t, dev = self.piece(1 - p.y, k, d * NX + p.x), self.bxy.at[1, b, d], p.yn
        else:
            e = self.z(d) * NX + p.x
            s, t, dev = self.piece(p.y, k, e), self.bz.at[b, d - 1], {"e": e}
        group = kind // 2
        return self.wire(s, t, dev, (group, b), ((d, p.nz + d, 2 * p.nz)[group], b))

    def first(self, k, d):
        self.copy(0, k, d).start()
        self.copy(1, k, d).start()

    def second(self, k, r):
        p, b, d = self.p, self.slot(k), self.z(r)
        self.await_in(self.bd.at[pl.ds(0, 2), b, d], (d, b))
        ref = self.piece(p.y, k, d * NX + 1 - p.x, 0)
        ref[...] = (ref[...].astype(f32) + self.bd[0, b, d].astype(f32)).astype(bf16)
        self.copy(2, k, d).start()
        ref = self.piece(1 - p.y, k, d * NX + p.x, 1)
        ref[...] = (ref[...].astype(f32) + self.bd[1, b, d].astype(f32)).astype(bf16)
        self.copy(3, k, d).start()

    def third(self, k, r):
        p, b, d = self.p, self.slot(k), self.z(r)
        self.await_in(self.bxy.at[pl.ds(0, 2), b, d], (p.nz + d, b))
        ref = self.piece(p.y, k, d * NX + p.x)
        total = ref[...].astype(f32) + self.bxy[0, b, d].astype(f32) + self.bxy[1, b, d].astype(f32)
        if r == 0:
            self.home(k)[:, self.lo : self.lo + self.width] = total
        else:
            ref[...] = total.astype(bf16)
            self.copy(4, k, r).start()

    def final(self, k):
        b = self.slot(k)
        cols = slice(self.lo, self.lo + self.width)
        self.await_in(self.bz.at[b], (2 * self.p.nz, b))
        total = self.home(k)[:, cols]
        for r in range(1, self.p.nz):
            total = total + self.bz[b, r - 1].astype(f32)
        self.home(k)[:, cols] = total

    def drain(self, k):
        nz, b = self.p.nz, self.slot(k)
        for group, n in enumerate((nz, 2 * nz, nz - 1)):
            self.await_out(self.span(k, n), (group, b))


class PlaneScatter(Pieces):
    def __init__(self, p, k, bz, bq, out, *rest):
        super().__init__(p, *rest)
        self.k, self.bz, self.bq, self.out = k, bz, bq, out

    def spot(self, q, z):
        p = self.p
        return self.piece(1 - p.y if q >= 2 else p.y, self.k, z * NX + (1 - p.x if q % 2 else p.x))

    def copy(self, q, r):
        p = self.p
        if r:
            return self.wire(self.spot(q, self.z(r)), self.bz.at[q, r - 1], {"e": self.z(r) * NX + p.x}, (1,), (q,))
        return self.wire(self.spot(q, p.z), self.bq.at[q - 1], p.yn if q == 2 else p.xn, (0,), (3 + q,))

    def first(self):
        for r in range(1, self.p.nz):
            for q in (3, 2, 1, 0):
                self.copy(q, r).start()

    def plane_sum(self, q):
        self.await_in(self.bz.at[q], (q,))
        total = self.spot(q, self.p.z)[...].astype(f32)
        for r in range(1, self.p.nz):
            total = total + self.bz[q, r - 1].astype(f32)
        return total

    def second(self):
        for q in (3, 1):
            self.spot(q, self.p.z)[...] = self.plane_sum(q).astype(bf16)
            self.copy(q, 0).start()

    def third(self):
        total = self.plane_sum(2)
        self.await_in(self.bq.at[2], (6,))
        self.spot(2, self.p.z)[...] = (total + self.bq[2].astype(f32)).astype(bf16)
        self.copy(2, 0).start()

    def final(self):
        total = self.plane_sum(0)
        for q in (1, 2):
            self.await_in(self.bq.at[q - 1], (3 + q,))
            total = total + self.bq[q - 1].astype(f32)
        self.home(self.k)[:, self.lo : self.lo + self.width] = total

    def drain(self):
        half = (self.p.nz - 1) * 2
        self.await_out(self.span(self.k, 3), (0,))
        self.await_out(self.full.at[pl.ds(0, 2), self.k, pl.ds(0, half * self.rows), pl.ds(self.lo, self.width)], (1,))


class Sums:
    def __init__(self, p, own, plane_buf, line_buf, out, peers, column, ssem, rsem):
        self.p, self.own, self.plane_buf, self.line_buf, self.out = p, own, plane_buf, line_buf, out
        self.peers, self.column, self.ssem, self.rsem = peers, column, ssem, rsem

    def tile(self, ref, t):
        return ref.at[pl.ds(8 * t, 8)]

    def wire(self, s, t, stage, tile, dev):
        return remote(s, t, self.ssem.at[tile, stage], self.rsem.at[tile, stage], dev)

    def plane_all(self, t):
        ref = self.plane_buf.at[t, pl.ds(1, len(self.peers))]
        return self.wire(ref, ref, 0, t, self.p.xn)

    def plane(self, t):
        for i, dev in self.peers:
            self.wire(self.tile(self.own, t), self.plane_buf.at[t, i], 0, t, dev).start()

    def line(self, t):
        row = lax.broadcasted_iota(jnp.int32, self.plane_buf.shape[2:], 0)
        lo, hi = SPLIT_ROWS[t]
        self.plane_all(t).wait_recv()
        total = self.own[8 * t : 8 * t + 8]
        for i, dev in self.peers:
            part = self.plane_buf[t, i]
            total = total + (jnp.where((row >= lo) & (row < hi), 0.0, part) if i % 2 else part)
        self.out[8 * t : 8 * t + 8] = total
        for r, dev in self.column:
            self.wire(self.tile(self.out, t), self.line_buf.at[t, r], 1, t, dev).start()

    def done(self, t):
        ref = self.line_buf.at[t, pl.ds(1, len(self.column))]
        both = self.wire(ref, ref, 1, t, self.p.xn)
        both.wait_recv()
        both.wait_send()
        total = self.out[8 * t : 8 * t + 8]
        for r, dev in self.column:
            total = total + self.line_buf[t, r]
        self.out[8 * t : 8 * t + 8] = total

    def drain(self, t):
        self.plane_all(t).wait_send()


def remote(src, dst, ssem, rsem, dev):
    return pltpu.make_async_remote_copy(src, dst, ssem, rsem, device_id=dev, device_id_type=MESH)


def loop(n, fn, after=()):
    def body(i, carry):
        fn(i)
        at(i, after)
        return carry

    lax.fori_loop(0, n, body, 0)


def at(i, steps):
    for j, todo in enumerate(steps):
        if todo:

            @pl.when(i == j)
            def _(todo=todo):
                for f in todo:
                    f()


def pick(a, b):
    lane = lax.broadcasted_iota(jnp.int32, a.shape, 1)
    return jnp.where(lane % 128 < 64, a.astype(f32), b.astype(f32))


def norm_parts(v):
    center = v - jnp.mean(v, axis=-1, keepdims=True)
    r = lax.rsqrt(jnp.mean(center * center, axis=-1, keepdims=True) + EPSILON)
    return center * r, r


def norm_back(n, r, d, gain):
    q = d * gain
    return r * (q - jnp.mean(q, axis=-1, keepdims=True) - n * jnp.mean(q * n, axis=-1, keepdims=True))


def gelu_both(u):
    a, b = math.sqrt(2.0 / math.pi), 0.044715
    u2 = u * u
    t = jnp.tanh(a * u * (1.0 + b * u2))
    h = 0.5 + 0.5 * t
    return u * h, h + (0.5 * a) * u * (1.0 - t * t) * (1.0 + (3.0 * b) * u2)


def valid(shape, base, length):
    return base + lax.broadcasted_iota(jnp.int32, shape, 0) < length


N_SUM = 16
ROW_B_OUT, ROW_B_DOWN, ROW_G_TWO, ROW_C_TWO, ROW_B_UP, ROW_G_ONE, ROW_C_ONE, ROW_B_QV = 0, 1, 2, 3, 4, 8, 9, 10
SPLIT_ROWS = ((4, 6), (2, 3))
PLANE_GATHER, PLANE_SCATTER = 128, 256
AT_BEGIN, AT_NORM_A, AT_NORM_B, AT_MASK_A, AT_MASK_B, AT_WAIT_0, AT_COLLECT, AT_PROJECT, AT_ATTEND, AT_OUT_SIB, AT_OUT_OWN, AT_NORM_TWO, AT_WAIT_1, AT_UP_A, AT_UP_B, AT_DOWN_GRAD, AT_WAIT_2, AT_PRE_GRAD, AT_SECOND_SIB, AT_SECOND_OWN, AT_UP_GRAD, AT_BACK_TWO, AT_MIXED_GRAD, AT_OUT_GRAD_W, AT_ATTEND_BACK, AT_GRADS, AT_FIRST_SIB, AT_FIRST_OWN, AT_BACK_ONE, AT_DOWN_SIB, AT_DOWN_OWN, AT_FINISH, AT_END = range(33)
IN_G, IN_GD, IN_GP, IN_RD, IN_RQ, IN_RU, IN_RP, IN_AR = range(8)
DO_OWN_XY, DO_OWN_Z, DO_PASS_ON, DO_TURN, DO_SPREAD, DO_FIRST, DO_SECOND, DO_THIRD, DO_FINAL, DO_PLANE, DO_LINE, DO_DONE = range(12)
METHODS = (
    lambda part: part.own_xy,
    lambda part: part.own_z,
    lambda part: part.pass_on,
    lambda part: part.turn,
    lambda part: part.spread,
    lambda part: part.first,
    lambda part: part.second,
    lambda part: part.third,
    lambda part: part.final,
    lambda part: part.plane,
    lambda part: part.line,
    lambda part: part.done,
)
PLAN = {
    (AT_BEGIN, 0): ((IN_G, DO_OWN_Z, 0), (IN_GP, DO_SPREAD, 0),),
    (AT_NORM_A, 1): ((IN_G, DO_OWN_XY, 1), (IN_G, DO_OWN_Z, 1),),
    (AT_NORM_B, 0): ((IN_G, DO_OWN_XY, 0), (IN_GP, DO_SPREAD, 1),),
    (AT_NORM_B, 1): ((IN_GD, DO_OWN_Z, 2),),
    (AT_MASK_A, 2): ((IN_GP, DO_SPREAD, 2),),
    (AT_MASK_B, 1): ((IN_G, DO_TURN, 1, 0),),
    (AT_WAIT_0, 0): ((IN_G, DO_PASS_ON, 0, 3), (IN_G, DO_TURN, 0, 0), (IN_GP, DO_SPREAD, 3), (IN_G, DO_TURN, 0, 3), (IN_G, DO_PASS_ON, 0, 2), (IN_G, DO_PASS_ON, 0, 1), (IN_G, DO_TURN, 0, 2), (IN_G, DO_TURN, 0, 1),),
    (AT_COLLECT, 0): ((IN_G, DO_PASS_ON, 1, 3),),
    (AT_PROJECT, 0): ((IN_GD, DO_OWN_XY, 2),),
    (AT_ATTEND, 2): ((IN_G, DO_TURN, 1, 3),),
    (AT_ATTEND, 3): ((IN_G, DO_PASS_ON, 1, 2), (IN_GD, DO_TURN, 2, 0),),
    (AT_ATTEND, 6): ((IN_G, DO_PASS_ON, 1, 1),),
    (AT_ATTEND, 10): ((IN_G, DO_TURN, 1, 2),),
    (AT_OUT_SIB, 0): ((IN_GD, DO_PASS_ON, 2, 3),),
    (AT_OUT_OWN, 0): ((IN_G, DO_TURN, 1, 1),),
    (AT_NORM_TWO, 2): ((IN_GD, DO_PASS_ON, 2, 2),),
    (AT_UP_A, 0): ((IN_GD, DO_PASS_ON, 2, 1),),
    (AT_UP_A, 1): ((IN_GD, DO_TURN, 2, 3),),
    (AT_UP_B, 0): ((IN_GD, DO_TURN, 2, 2),),
    (AT_UP_B, 1): ((IN_GD, DO_TURN, 2, 1),),
    (AT_DOWN_GRAD, 1): ((IN_RD, DO_FIRST, 1, 1),),
    (AT_DOWN_GRAD, 2): ((IN_RD, DO_FIRST, 1, 2),),
    (AT_DOWN_GRAD, 3): ((IN_RQ, DO_FIRST), (IN_RD, DO_FIRST, 1, 3),),
    (AT_WAIT_2, 0): ((IN_RD, DO_FIRST, 1, 0),),
    (AT_PRE_GRAD, 2): ((IN_RD, DO_SECOND, 1, 0), (IN_RD, DO_SECOND, 1, 2), (IN_RD, DO_SECOND, 1, 1),),
    (AT_SECOND_SIB, 1): ((IN_RD, DO_SECOND, 1, 3),),
    (AT_SECOND_OWN, 0): ((IN_RD, DO_THIRD, 1, 0),),
    (AT_SECOND_OWN, 1): ((IN_RD, DO_THIRD, 1, 2),),
    (AT_UP_GRAD, 2): ((IN_RD, DO_THIRD, 1, 1),),
    (AT_BACK_TWO, 1): ((IN_RD, DO_THIRD, 1, 3),),
    (AT_MIXED_GRAD, 0): ((IN_AR, DO_PLANE, 0),),
    (AT_MIXED_GRAD, 2): ((IN_RU, DO_SECOND, 0, 0), (IN_RU, DO_SECOND, 0, 2), (IN_RU, DO_SECOND, 0, 1), (IN_RU, DO_SECOND, 0, 3),),
    (AT_ATTEND_BACK, 1): ((IN_AR, DO_LINE, 0),),
    (AT_ATTEND_BACK, 2): ((IN_RQ, DO_SECOND),),
    (AT_ATTEND_BACK, 3): ((IN_RU, DO_THIRD, 0, 0),),
    (AT_ATTEND_BACK, 4): ((IN_RU, DO_THIRD, 0, 2),),
    (AT_ATTEND_BACK, 7): ((IN_AR, DO_DONE, 0), (IN_RD, DO_FINAL, 1), (IN_RU, DO_THIRD, 0, 1),),
    (AT_GRADS, 1): ((IN_RQ, DO_THIRD), (IN_RU, DO_THIRD, 0, 3),),
    (AT_ATTEND_BACK, 10): ((IN_RP, DO_SECOND, 0, 3), (IN_RP, DO_SECOND, 0, 2),),
    (AT_ATTEND_BACK, 11): ((IN_RQ, DO_FINAL), (IN_RP, DO_SECOND, 0, 0), (IN_RP, DO_SECOND, 1, 3), (IN_RP, DO_SECOND, 1, 1), (IN_RP, DO_SECOND, 1, 0), (IN_RP, DO_SECOND, 0, 1), (IN_RP, DO_THIRD, 0, 3), (IN_RP, DO_THIRD, 0, 2),),
    (AT_GRADS, 2): ((IN_RP, DO_THIRD, 0, 0), (IN_RU, DO_FINAL, 0),),
    (AT_FIRST_OWN, 0): ((IN_RP, DO_SECOND, 1, 2), (IN_RP, DO_THIRD, 1, 1), (IN_RP, DO_THIRD, 1, 3),),
    (AT_FIRST_OWN, 1): ((IN_RP, DO_THIRD, 1, 0),),
    (AT_BACK_ONE, 0): ((IN_RP, DO_THIRD, 0, 1),),
    (AT_BACK_ONE, 1): ((IN_RP, DO_SECOND, 2, 3), (IN_RP, DO_SECOND, 2, 1), (IN_RP, DO_SECOND, 2, 2), (IN_RP, DO_SECOND, 2, 0),),
    (AT_BACK_ONE, 2): ((IN_RP, DO_THIRD, 1, 2),),
    (AT_BACK_ONE, 3): ((IN_RP, DO_THIRD, 2, 3), (IN_AR, DO_PLANE, 1), (IN_RP, DO_FINAL, 0),),
    (AT_DOWN_SIB, 0): ((IN_RP, DO_THIRD, 2, 1),),
    (AT_DOWN_OWN, 0): ((IN_RP, DO_THIRD, 2, 2), (IN_RP, DO_THIRD, 2, 0), (IN_RP, DO_FINAL, 1),),
    (AT_END, 0): ((IN_AR, DO_LINE, 1), (IN_RP, DO_FINAL, 2), (IN_AR, DO_DONE, 1),),
}


def block_kernel(
    lens, tokens, ograd, w_qkv, w_out, w_up, w_down, b_qv, b_up, b_out, b_down, g_one, c_one, g_two, c_two,
    result_hbm, tgrad_hbm, up_out, down_out, outp, sums,
    result, tgrad, tok, og, packed, w, wc, wo, x_all, sec, dr, t1, t2, ft, qkv, mixed, lse, act, gp, dmx, go,
    r1, r2, r3, r4, s1, s2, part, dk_acc, dv_acc, bias, bias_up, vec, sm, ar1, ar2,
    grf, grp, dd, dxy, dz, ud, uxy, uz, pd, pxy, pz, qz, qq,
    g_ss, g_rs, q_ss, q_rs, d_ss, d_rs, u_ss, u_rs, v_ss, v_rs, p_ss, p_rs, sib_ss, sib_rs, ar_ss, ar_rs, loc,
):
    nz = ar2.shape[1]
    p = Place(nz)
    c = lax.axis_index("c")
    half, d_model = tokens.shape
    seq = 2 * half
    hw = mixed.shape[1]
    TR = 256
    nt = half // TR
    length = lens[p.y]
    own0, sib0 = c * half, (1 - c) * half

    def rows(base, i, n=TR):
        return pl.ds(pl.multiple_of(base + i * n, n), n)

    load_t = pltpu.make_async_copy(tokens, tok, loc.at[0])
    load_g = pltpu.make_async_copy(ograd, og, loc.at[1])
    load_t.start()
    load_g.start()
    peers = []
    for dx in (0, 1):
        for dy in (0, 1):
            for dc in (0, 1):
                if dx + dy + dc:
                    peers.append((4 * dx + 2 * dy + dc, {"e": p.e + dx * (1 - 2 * p.x), "y": p.y + dy * (1 - 2 * p.y), "c": c + dc * (1 - 2 * c)}))
    column = [(r, {"e": ((p.z + r) % nz) * NX + p.x}) for r in range(1, nz)]
    bar = pltpu.get_barrier_semaphore()
    for _, dev in peers + column:
        pl.semaphore_signal(bar, 1, device_id=dev, device_id_type=MESH)
    for j, ref in enumerate((b_up, b_out, b_down, g_one, c_one, g_two, c_two)):
        vec[j] = ref[...]

    flip_lanes = p.y == 1
    for h in range(hw // 128):
        s = slice(HEAD_DIM * h, HEAD_DIM * (h + 1))
        q, k, v = [w_qkv[j][:, s].astype(f32) for j in range(3)]
        o = w_out[s, :].astype(f32).T
        for j, (lo, hi) in enumerate(((q, v), (k, o))):
            put = jnp.where(flip_lanes, jnp.concatenate([hi, lo], axis=1), jnp.concatenate([lo, hi], axis=1))
            packed[:, 256 * h + 128 * j : 256 * h + 128 * j + 128] = put.astype(bf16)
    pl.semaphore_wait(bar, len(peers) + len(column))

    def sib(i, src, dst):
        return remote(src, dst, sib_ss.at[i], sib_rs.at[i], p.core)

    DOWN, UP = 1, 0
    ffq = w.shape[3]
    gcut, rcut = ffq - PLANE_GATHER, ffq - PLANE_SCATTER
    shard = (packed, w_up, w_down)
    g = Gather(p, shard, w, 0, ffq, g_ss, g_rs)
    gd = Gather(p, shard, w, 0, gcut, g_ss, g_rs)
    gp2 = PlaneGather(p, shard, 2, w, gcut, ffq - gcut, q_ss, q_rs)
    outf = (up_out, down_out)
    ru = Scatter(p, ud, uxy, uz, outf, grf, 0, ffq, u_ss, u_rs)
    rd = Scatter(p, dd, dxy, dz, outf, grf, 0, rcut, d_ss, d_rs)
    rq = PlaneScatter(p, DOWN, qz, qq, outf, grf, rcut, ffq - rcut, v_ss, v_rs)
    rp = Scatter(p, pd, pxy, pz, outp, grp, 0, grp.shape[3], p_ss, p_rs)
    ar = Sums(p, sm, ar1, ar2, sums, peers, column, ar_ss, ar_rs)
    parts = (g, gd, gp2, rd, rq, ru, rp, ar)

    def steps(name, i=0):
        return [lambda t=t: METHODS[t[1]](parts[t[0]])(*t[2:]) for t in PLAN.get((name, i), ())]

    def mark(name):
        for f in steps(name):
            f()

    def tiled(name, n, fn):
        loop(n, fn, [steps(name, i) for i in range(n)])

    x_own, x_sib = x_all.at[rows(own0, 0, half)], x_all.at[rows(sib0, 0, half)]
    mark(AT_BEGIN)
    send_x = sib(0, tokens, x_own)
    send_x.start()
    send_dr = sib(1, ograd, dr.at[rows(own0, 0, half)])
    send_dr.start()
    send_b = remote(b_qv, bias.at[p.y], sib_ss.at[8], sib_rs.at[8], p.yn)
    send_u = remote(vec, bias_up.at[p.y], sib_ss.at[9], sib_rs.at[9], p.yn)
    send_b.start()
    send_u.start()
    keep = [pltpu.make_async_copy(shard[j], w.at[p.y, j, pl.ds(pl.multiple_of(p.e * packed.shape[0], 16), packed.shape[0])], loc.at[2 + j]) for j in range(NK)]
    for cp in keep:
        cp.start()
    bias[p.y] = b_qv[...]
    bias_up[p.y] = vec[...]
    sm[...] = jnp.zeros_like(sm)

    def norm_one(name, base, src, lo):
        def one(i):
            v = src[rows(lo, i, 128)].astype(f32)
            n, _ = norm_parts(v)
            f = n * vec[3:4] + vec[4:5]
            sec[rows(base, i, 128)] = f.astype(bf16)
            ft[:, rows(base, i, 128)] = f.astype(bf16).astype(f32).T.astype(bf16)

        tiled(name, half // 128, one)

    def mask_rows(name, base, src, lo):
        def one(i):
            v = jnp.where(valid((128, d_model), base + i * 128, length), src[rows(lo, i, 128)].astype(f32), 0.0)
            dr[rows(base, i, 128)] = v.astype(bf16)
            t1[:, rows(base, i, 128)] = v.T.astype(bf16)

        tiled(name, half // 128, one)

    load_t.wait()
    norm_one(AT_NORM_A, own0, tok, 0)
    send_x.wait_recv()
    norm_one(AT_NORM_B, sib0, x_all, sib0)
    load_g.wait()
    mask_rows(AT_MASK_A, own0, og, 0)
    send_dr.wait_recv()
    mask_rows(AT_MASK_B, sib0, dr, sib0)
    for cp in keep:
        cp.wait()
    mark(AT_WAIT_0)
    g.final(0)

    def collect(i):
        r = rows(0, i)
        for q in range(hw // 128):
            a = [w[yq, 0, r, q * 256 : q * 256 + 128] for yq in (0, 1)]
            b = [w[yq, 0, r, q * 256 + 128 : q * 256 + 256] for yq in (0, 1)]
            for group, v in enumerate((pick(a[0], a[1]), pick(b[0], b[1]), pick(a[1], a[0]), pick(b[1], b[0]))):
                wc[r, group * hw + q * 128 : group * hw + q * 128 + 128] = v.astype(bf16)
                if group == 3:
                    wo[q * 128 : q * 128 + 128, r] = v.T.astype(bf16)

    tiled(AT_COLLECT, d_model // TR, collect)
    send_b.wait_recv()
    send_u.wait_recv()

    def head_bias(row, first, second):
        s = [slice(HEAD_DIM * h, HEAD_DIM * (h + 1)) for h in range(hw // 128)]
        return jnp.concatenate([bias[j, row : row + 1, c] for c in s for j in (first, second)], axis=1)

    bq, bv = head_bias(0, 0, 1), head_bias(1, 1, 0)

    def project(i):
        h = sec[rows(0, i)]
        qkv[rows(0, i), 0:hw] = ((dot_nn(h, wc[:, 0:hw]) + bq).astype(bf16).astype(f32) * 0.125).astype(bf16)
        qkv[rows(0, i), hw : 2 * hw] = dot_nn(h, wc[:, hw : 2 * hw]).astype(bf16)
        qkv[rows(0, i), 2 * hw : 3 * hw] = (dot_nn(h, wc[:, 2 * hw : 3 * hw]) + bv).astype(bf16)

    tiled(AT_PROJECT, seq // TR, project)
    pairs, blocks = hw // 128, seq // BQ

    def attend(i):
        attn_fwd_pair(i, hw, length, qkv, mixed, lse, lambda b: at(i, [steps(AT_ATTEND, j * blocks + b) for j in range(pairs)]))

    loop(pairs, attend)

    def out_sib(i):
        s1[rows(0, i)] = dot_nn(mixed[rows(sib0, i)], wo[...]).astype(bf16)

    tiled(AT_OUT_SIB, nt, out_sib)
    send_h = sib(2, s1, r1)
    send_h.start()

    def out_own(i):
        result[rows(0, i)] = tok[rows(0, i)].astype(f32) + dot_nn(mixed[rows(own0, i)], wo[...]) + vec[1:2]

    tiled(AT_OUT_OWN, nt, out_own)
    send_h.wait_recv()

    def norm_two(i):
        h = result[rows(0, i, 128)] + r1[rows(0, i, 128)].astype(f32)
        result[rows(0, i, 128)] = h
        n, _ = norm_parts(h)
        sec[rows(own0, i, 128)] = (n * vec[5:6] + vec[6:7]).astype(bf16)

    tiled(AT_NORM_TWO, half // 128, norm_two)
    send_s = sib(3, sec.at[rows(own0, 0, half)], sec.at[rows(own0, 0, half)])
    send_s.start()
    mark(AT_WAIT_1)
    g.final(1)

    def up(name, base):
        def one(i):
            r = rows(base, i)
            h = sec[r]
            t2[:, r] = h.astype(f32).T.astype(bf16)
            for yq in (0, 1):
                u = dot_nn(h, w[yq, 1]) + bias_up[yq, 0:1]
                a, s = gelu_both(u)
                act[r, yq * ffq : (yq + 1) * ffq] = a.astype(bf16)
                gp[r, yq * ffq : (yq + 1) * ffq] = s.astype(bf16)

        tiled(name, nt, one)

    up(AT_UP_A, own0)
    send_s.wait_recv()
    up(AT_UP_B, sib0)
    ZR = d_model // nz

    def down_grad(i):
        r = rows(0, i, ZR)
        for yq in (0, 1):
            grf[yq, DOWN, r] = dot_nn(t1[r], act[:, yq * ffq : (yq + 1) * ffq]).astype(bf16)

    tiled(AT_DOWN_GRAD, nz, down_grad)
    mark(AT_WAIT_2)
    gd.final(2)
    gp2.final()

    def pre_grad(i):
        r = rows(0, i)
        for yq in (0, 1):
            cols = slice(yq * ffq, (yq + 1) * ffq)
            v = (dot_nn(dr[r], w[yq, 2]) * gp[r, cols].astype(f32)).astype(bf16)
            gp[r, cols] = v
            sm[ROW_B_UP + yq : ROW_B_UP + yq + 1] += jnp.sum(v.astype(f32), axis=0, keepdims=True)

    tiled(AT_PRE_GRAD, seq // TR, pre_grad)

    def up_back(i, base):
        return dot_nt(gp[rows(base, i), 0:ffq], w[0, 1]) + dot_nt(gp[rows(base, i), ffq : 2 * ffq], w[1, 1])

    send_h.wait_send()

    def second_sib(i):
        s1[rows(0, i)] = up_back(i, sib0).astype(bf16)

    tiled(AT_SECOND_SIB, nt, second_sib)
    send_d = sib(4, s1, r3)
    send_d.start()

    def second_own(i):
        part[rows(0, i)] = up_back(i, own0)

    tiled(AT_SECOND_OWN, nt, second_own)

    def up_grad(i):
        r = rows(0, i, ZR)
        for yq in (0, 1):
            grf[yq, UP, r] = dot_nn(t2[r], gp[:, yq * ffq : (yq + 1) * ffq]).astype(bf16)
        ru.first(UP, i)

    tiled(AT_UP_GRAD, nz, up_grad)
    send_d.wait_recv()

    def back_two(i):
        r = rows(0, i, 128)
        n, rr = norm_parts(result[r])
        ds = part[r] + r3[r].astype(f32)
        dres = jnp.where(valid((128, d_model), own0 + i * 128, length), og[r].astype(f32), 0.0)
        dh = dres + norm_back(n, rr, ds, vec[5:6])
        tgrad[r] = dh
        x_all[rows(own0, i, 128)] = dh.astype(bf16)
        for row, v in ((ROW_B_OUT, dh), (ROW_B_DOWN, dres), (ROW_G_TWO, ds * n), (ROW_C_TWO, ds)):
            sm[row : row + 1] += jnp.sum(v, axis=0, keepdims=True)

    tiled(AT_BACK_TWO, half // 128, back_two)
    send_dh = sib(5, x_own, x_own)
    send_dh.start()
    send_dh.wait_recv()

    def mixed_grad(i):
        r = rows(0, i)
        h = x_all[r]
        t1[:, r] = h.astype(f32).T.astype(bf16)
        dmx[r] = dot_nn(h, wc[:, 3 * hw : 4 * hw]).astype(bf16)

    tiled(AT_MIXED_GRAD, seq // TR, mixed_grad)

    def out_grad_w(i):
        go[rows(0, i)] = dot_nn(t1[rows(0, i)], mixed[...]).astype(bf16)

    tiled(AT_OUT_GRAD_W, d_model // TR, out_grad_w)

    def attend_back(i):
        attn_bwd_pair(
            i, hw, length, qkv, mixed, lse, dmx, dk_acc, dv_acc, lambda b: at(i, [steps(AT_ATTEND_BACK, j * blocks + b) for j in range(pairs)])
        )
        cq, ck, cv = [pair_cols(i, group, hw) for group in range(3)]

        def grads(t):
            r = rows(0, t, ZR)
            gq, gk, gv = [dot_nn(ft[r], qkv[:, cc]) for cc in (cq, ck, cv)]
            o = go[r, cq].astype(f32)
            grp[0, i, r, 0:128] = pick(gq, gv).astype(bf16)
            grp[0, i, r, 128:256] = pick(gk, o).astype(bf16)
            grp[1, i, r, 0:128] = pick(gv, gq).astype(bf16)
            grp[1, i, r, 128:256] = pick(o, gk).astype(bf16)
            rp.first(i, t)

        loop(nz, grads)
        at(i, [steps(AT_GRADS, j) for j in range(pairs)])
        for cc, lo in ((cq, 0), (cv, hw)):
            to = pl.ds(pl.multiple_of(lo + i * 128, 128), 128)
            sm[ROW_B_QV : ROW_B_QV + 1, to] = jnp.sum(qkv[:, cc].astype(f32), axis=0, keepdims=True)

    loop(pairs, attend_back)

    def first_back(i, base):
        return dot_nt(qkv[rows(base, i)], wc[:, 0 : 3 * hw])

    def first_sib(i):
        s2[rows(0, i)] = first_back(i, sib0).astype(bf16)

    tiled(AT_FIRST_SIB, nt, first_sib)
    send_f = sib(6, s2, r4)
    send_f.start()

    def first_own(i):
        part[rows(0, i)] = first_back(i, own0)

    tiled(AT_FIRST_OWN, nt, first_own)
    send_f.wait_recv()

    def back_one(i):
        r = rows(0, i, 128)
        n, rr = norm_parts(tok[r].astype(f32))
        df = part[r] + r4[r].astype(f32)
        tgrad[r] = tgrad[r] + norm_back(n, rr, df, vec[3:4])
        for row, v in ((ROW_G_ONE, df * n), (ROW_C_ONE, df)):
            sm[row : row + 1] += jnp.sum(v, axis=0, keepdims=True)

    tiled(AT_BACK_ONE, half // 128, back_one)
    store_t = pltpu.make_async_copy(tgrad, tgrad_hbm, loc.at[0])
    store_t.start()

    def down(i, base):
        return dot_nt(act[rows(base, i), 0:ffq], w[0, 2]) + dot_nt(act[rows(base, i), ffq : 2 * ffq], w[1, 2])

    send_d.wait_send()

    def down_sib(i):
        s1[rows(0, i)] = down(i, sib0).astype(bf16)

    tiled(AT_DOWN_SIB, nt, down_sib)
    send_r = sib(7, s1, r2)
    send_r.start()
    def down_own(i):
        part[rows(0, i)] = down(i, own0)

    tiled(AT_DOWN_OWN, nt, down_own)
    send_r.wait_recv()

    def finish(i):
        r = rows(0, i, 128)
        v = result[r] + part[r] + r2[r].astype(f32) + vec[2:3]
        result[r] = jnp.where(valid((128, d_model), own0 + i * 128, length), v, 0.0)

    tiled(AT_FINISH, half // 128, finish)
    store_r = pltpu.make_async_copy(result, result_hbm, loc.at[1])
    store_r.start()
    mark(AT_END)

    for k in range(2):
        g.drain(k)
    gd.drain(2)
    gp2.drain()
    ar.drain(0)
    ar.drain(1)
    rd.drain(DOWN)
    rq.drain()
    ru.drain(UP)
    for k in range(3):
        rp.drain(k)
    for cp in (send_x, send_b, send_u, send_dr, send_s, send_dh, send_f, send_r):
        cp.wait_send()
    store_t.wait()
    store_r.wait()


def block(lens, tokens, ograd, w_qkv, w_out, w_up, w_down, b_qv, vectors, nz):
    half, d = tokens.shape
    heads_w = w_qkv.shape[2]
    seq = 2 * half
    nk, (rows, ffq) = NK, w_up.shape
    hw = d // 2
    pw = 256
    npair = hw // 128

    def V(shape, t=bf16):
        return pltpu.VMEM(shape, t)

    scratch = [
        V((half, d), f32), V((half, d), f32), V((half, d)), V((half, d)), V((rows, d)),
        V((2, nk, d, ffq)), V((d, 4 * hw)), V((hw, d)), V((seq, d)), V((seq, d)), V((seq, d)), V((d, seq)), V((d, seq)), V((d, seq)),
        V((seq, 3 * hw)), V((seq, hw)), V((2 * npair, 1, seq), f32), V((seq, 2 * ffq)), V((seq, 2 * ffq)), V((seq, hw)), V((d, hw)),
        V((half, d)), V((half, d)), V((half, d)), V((half, d)), V((half, d)), V((half, d)), V((half, d), f32),
        V((seq, 128), f32), V((seq, 128), f32), V((2, 2, heads_w), f32), V((2, 8, ffq), f32), V((8, d), f32), V((N_SUM, d), f32), V((2, 8, 8, d), f32), V((2, nz, 8, d), f32),
        V((2, 2, d, ffq)), V((2, npair, d, pw)),
        V((2, 1, nz, rows // 2, ffq - PLANE_SCATTER)), V((2, 1, nz, rows, ffq - PLANE_SCATTER)), V((1, nz - 1, rows, ffq - PLANE_SCATTER)),
        V((2, 1, nz, rows // 2, ffq)), V((2, 1, nz, rows, ffq)), V((1, nz - 1, rows, ffq)),
        V((2, npair, nz, rows // 2, pw)), V((2, npair, nz, rows, pw)), V((npair, nz - 1, rows, pw)),
        V((4, nz - 1, rows, PLANE_SCATTER)), V((3, rows, PLANE_SCATTER)),
    ]
    dma = pltpu.SemaphoreType.DMA
    sems = [dma((3, nk)), dma((8, nk)), dma((2,)), dma((4,)), dma((3, 1)), dma((9, 1)), dma((3, 1)), dma((9, 1)), dma((2,)), dma((7,)), dma((3, npair)), dma((9, npair))]
    sems += [dma((10,)), dma((10,)), dma((2, 2)), dma((2, 2)), dma((2 + nk,))]
    vm = pl.BlockSpec(memory_space=pltpu.VMEM)
    anywhere = pl.BlockSpec(memory_space=pl.ANY)
    return pl.pallas_call(
        block_kernel,
        out_shape=(
            jax.ShapeDtypeStruct((half, d), f32),
            jax.ShapeDtypeStruct((half, d), f32),
            jax.ShapeDtypeStruct((rows, ffq), f32),
            jax.ShapeDtypeStruct((rows, ffq), f32),
            jax.ShapeDtypeStruct((npair, rows, pw), f32),
            jax.ShapeDtypeStruct((N_SUM, d), f32),
        ),
        in_specs=[pl.BlockSpec(memory_space=pltpu.SMEM), anywhere, anywhere, vm, vm, anywhere, anywhere] + [vm] * (1 + len(vectors)),
        out_specs=(anywhere, anywhere, vm, vm, vm, vm),
        scratch_shapes=scratch + sems,
        compiler_params=pltpu.CompilerParams(collective_id=0, has_side_effects=True, vmem_limit_bytes=64 << 20),
    )(lens, tokens, ograd, w_qkv, w_out, w_up, w_down, b_qv, *vectors)


def finish_kernel(res_in, tg_in, up_in, down_in, outp_in, sums_in, *rest):
    outs, (held_r, held_t, held_u, held_d, outp, sums), made, (load_sem, store_sem) = rest[:14], rest[14:20], rest[20:30], rest[30:]
    res, tg, up, down = outs[:4]
    qkv, b_qv, w_out, b_up, *rows = made
    first = [pltpu.make_async_copy(a, b, load_sem.at[i]) for i, (a, b) in enumerate(((outp_in, outp), (sums_in, sums)))]
    for cp in first:
        cp.start()
    moves = []
    for source, held, to, n in ((tg_in, held_t, tg, 4), (res_in, held_r, res, 4), (up_in, held_u, up, 1), (down_in, held_d, down, 1)):
        size = held.shape[0] // n
        for i in range(n):
            part, j = pl.ds(i * size, size), len(moves)
            load = pltpu.make_async_copy(source.at[part], held.at[part], load_sem.at[2 + j])
            load.start()
            moves.append((load, pltpu.make_async_copy(held.at[part], to.at[part], store_sem.at[j])))
    for cp in first:
        cp.wait()
    second = lax.axis_index("y") == 1

    def ordered(a):
        return jnp.where(second, jnp.concatenate([a[:, HEAD_DIM:], a[:, :HEAD_DIM]], axis=1), a)

    a = [ordered(outp[h, :, : 2 * HEAD_DIM]) for h in range(outp.shape[0])]
    b = [ordered(outp[h, :, 2 * HEAD_DIM :]) for h in range(outp.shape[0])]
    qkv[0] = jnp.concatenate([v[:, :HEAD_DIM] for v in a], axis=1)
    qkv[1] = jnp.concatenate([v[:, :HEAD_DIM] for v in b], axis=1)
    qkv[2] = jnp.concatenate([v[:, HEAD_DIM:] for v in a], axis=1)
    w_out[...] = jnp.concatenate([v[:, HEAD_DIM:] for v in b], axis=1).T
    half = sums.shape[1] // 2
    for j in (0, 1):
        v = [ordered(sums[ROW_B_QV : ROW_B_QV + 1, j * half + 128 * h : j * half + 128 * h + 128]) for h in range(outp.shape[0])]
        b_qv[j : j + 1] = jnp.concatenate([c[:, HEAD_DIM * j : HEAD_DIM * (j + 1)] for c in v], axis=1)
    b_up[...] = jnp.where(second, sums[ROW_B_UP + 1], sums[ROW_B_UP])
    for ref, row in zip(rows, (ROW_B_OUT, ROW_B_DOWN, ROW_G_ONE, ROW_C_ONE, ROW_G_TWO, ROW_C_TWO)):
        ref[...] = sums[row]
    last = [pltpu.make_async_copy(src, dst, store_sem.at[len(moves) + i]) for i, (src, dst) in enumerate(zip(made, outs[4:]))]
    for cp in last:
        cp.start()
    for load, store in moves:
        load.wait()
        store.start()
    for cp in last + [store for _, store in moves]:
        cp.wait()


def finish(res, tg, up, down, outp, sums):
    n, (rows, ffq), d = outp.shape[0], up.shape, sums.shape[1]
    anywhere = pl.BlockSpec(memory_space=pl.ANY)
    big = [res.shape, tg.shape, up.shape, down.shape]
    made = [(3, rows, n * HEAD_DIM), (2, n * HEAD_DIM), (n * HEAD_DIM, rows), (ffq,)] + [(d,)] * 6
    return pl.pallas_call(
        finish_kernel,
        out_shape=[jax.ShapeDtypeStruct(s, f32) for s in big + made],
        in_specs=[anywhere] * 6,
        out_specs=[anywhere] * 14,
        scratch_shapes=[pltpu.VMEM(s, f32) for s in big + [outp.shape, sums.shape] + made] + [pltpu.SemaphoreType.DMA((12,)), pltpu.SemaphoreType.DMA((20,))],
    )(res, tg, up, down, outp, sums)


def per_device(tokens, lengths, w_qkv, b_qv, w_out, b_out, w_up, b_up, w_down, b_down, g_one, c_one, g_two, c_two, out_grad, *, nz, sub):
    if sub > 1:
        w_qkv, w_up = lax.all_gather(w_qkv, "r", axis=1, tiled=True), lax.all_gather(w_up, "r", axis=0, tiled=True)
        w_out, w_down = [lax.all_gather(a, "r", axis=1, tiled=True) for a in (w_out, w_down)]
    vectors = (b_up, b_out, b_down, g_one, c_one, g_two, c_two)
    result, tokens_grad, up, down, outp, sums = block(lengths, tokens, out_grad, w_qkv, w_out, w_up, w_down.T, b_qv, vectors, nz)
    if sub > 1:
        up, down = [lax.psum_scatter(a, "r", scatter_dimension=0, tiled=True) for a in (up, down)]
        outp = lax.psum_scatter(outp, "r", scatter_dimension=1, tiled=True)
        sums = lax.psum(sums, "r")
    result, tokens_grad, up, down, qkv, b_qv, w_out, b_up, b_out, b_down, *norms = finish(result, tokens_grad, up, down, outp, sums)
    return (result, tokens_grad, qkv, b_qv, w_out, b_out, up, b_up, down.T, b_down, *norms)


def solution(mesh):
    dp, tensor = mesh.shape["dp"], mesh.shape["tensor"]
    line = 4 * NX
    nz, sub = line // NX, dp // line
    grid = Mesh(mesh.devices.reshape(line, sub, tensor // 2, 2), ("e", "r", "y", "c"))
    dpx, tx = ("e", "r"), ("y", "c")
    rows = P(dpx + tx, None)
    return jax.shard_map(
        functools.partial(per_device, nz=nz, sub=sub),
        mesh=grid,
        in_specs=(rows, P(dpx), P(None, dpx, tx), P(None, tx), P(tx, dpx), P(), P(dpx, tx), P(tx), P(tx, dpx), P(), P(), P(), P(), P(), rows),
        out_specs=(rows, rows, P(None, dpx, tx), P(None, tx), P(tx, dpx), P(), P(dpx, tx), P(tx), P(tx, dpx), P(), P(), P(), P(), P()),
        check_vma=False,
    )
```
